32 devices in a mesh: dp: 8 (over y, x, core), fsdp: 4 (over z).
Axes of the slice: x: 2, y: 2, z: 4, core: 2. Of those that a mesh axis runs over, the one named last changes fastest.
Arguments:
- tokens: bfloat16 [32768, 640], P(('dp', 'fsdp')), may hold values from -6 to 6
- cotangent: bfloat16 [32768, 640], P(('dp', 'fsdp')), may hold values from -6 to 6
- lengths: int32 [32, 4], P(('dp', 'fsdp')), may hold values from 1 to 768, 1024 in all within a row
- counts: int32 [32, 4], P(('dp', 'fsdp')), may hold values from 1 to 4
- w_qkv: float32 [1920, 640], P('fsdp', 'dp'), may hold values from -0.25 to 0.25
- w_out: float32 [640, 640], P('fsdp', 'dp'), may hold values from -2 to 2
- w_up: float32 [2560, 640], P('fsdp', 'dp'), may hold values from -0.25 to 0.25
- w_down: float32 [2560, 640], P('fsdp', 'dp'), may hold values from -0.125 to 0.125
- mom_qkv: float32 [1920, 640], P('fsdp', 'dp'), as said below
- mom_out: float32 [640, 640], P('fsdp', 'dp'), as said below
- mom_up: float32 [2560, 640], P('fsdp', 'dp'), as said below
- mom_down: float32 [2560, 640], P('fsdp', 'dp'), as said below
- vectors: float32 [13, 640], P(None, 'dp'), as said below
- vec_first: float32 [13, 640], P(None, 'dp'), as said below
- vec_second: float32 [13, 640], P(None, 'dp'), as said below
Outputs:
- layer_out: bfloat16 [32768, 640], P(('dp', 'fsdp'))
- input_grad: float32 [32768, 640], P(('dp', 'fsdp'))
- new_mom_qkv: float32 [1920, 640], P('fsdp', 'dp')
- new_mom_out: float32 [640, 640], P('fsdp', 'dp')
- new_mom_up: float32 [2560, 640], P('fsdp', 'dp')
- new_mom_down: float32 [2560, 640], P('fsdp', 'dp')
- new_w_qkv: float32 [1920, 640], P('fsdp', 'dp')
- new_w_out: float32 [640, 640], P('fsdp', 'dp')
- new_w_up: float32 [2560, 640], P('fsdp', 'dp')
- new_w_down: float32 [2560, 640], P('fsdp', 'dp')
- new_vectors: float32 [13, 640], P(None, 'dp')
- new_first: float32 [13, 640], P(None, 'dp')
- new_second: float32 [13, 640], P(None, 'dp')
The draws below stay inside these ranges and needn't reach their ends.
Inputs may be any that keep to these rules, and one draw needn't show every extreme that they name: Each row's 4 lengths sum to 1024; the longest is exactly 768. `mom_qkv`: entries of both signs, about as large as the gradient of the same matrix. `mom_out`: entries of both signs, about as large as the gradient of the same matrix. `mom_up`: entries of both signs, about as large as the gradient of the same matrix. `mom_down`: entries of both signs, about as large as the gradient of the same matrix. `vectors`: gains between 0.7 and 1.3, shifts and biases of both signs. `vec_first`: entries of both signs. `vec_second`: positive entries.
All inputs are finite; a program needn't handle non-finite values.
Results may differ from the reference program's by a relative error of at most 0.0095.
The reference program's roundings to bfloat16 on the way count: a program that leaves them out, or rounds other values in their place, can miss the bound.
Values may be sent and summed in bfloat16 or wider, within the bound.
A program may use at most 192 MiB of HBM per device.

```python
import math
from functools import partial
import jax
import jax.numpy as jnp
import numpy as np
from jax import lax

D = 640
HEAD_DIM = 32
FF = 2560
ROW_LEN = 1024
SEGS = 4
NS_ITERS = 5
STEP = 10
ROWS = 32
TOKENS = 32768
VEC_ROWS = 13


def moment_like(key, shape, factor):
    spread = factor * math.sqrt(TOKENS)
    return jnp.clip(jax.random.normal(key, shape, jnp.float32), -4.0, 4.0) * spread


def draw_mom_qkv(key, part):
    return moment_like(jax.random.fold_in(key, 101), (3 * D, D), 0.3)


def draw_mom_out(key, part):
    return moment_like(jax.random.fold_in(key, 202), (D, D), 0.3)


def draw_mom_up(key, part):
    return moment_like(jax.random.fold_in(key, 303), (FF, D), 0.3)


def draw_mom_down(key, part):
    return moment_like(jax.random.fold_in(key, 404), (FF, D), 0.3)


def draw_vectors(key, part):
    first_key, second_key = jax.random.split(jax.random.fold_in(key, 505))
    gains = 1.0 + jax.random.uniform(first_key, (VEC_ROWS, D), jnp.float32, -0.3, 0.3)
    shifts = 0.1 * jnp.clip(jax.random.normal(second_key, (VEC_ROWS, D), jnp.float32), -4.0, 4.0)
    row_index = lax.broadcasted_iota(jnp.int32, (VEC_ROWS, D), 0)
    return jnp.where((row_index == 0) | (row_index == 2), gains, shifts)


def draw_vec_first(key, part):
    return moment_like(jax.random.fold_in(key, 606), (VEC_ROWS, D), 0.05)


def draw_vec_second(key, part):
    lower = math.log(8e-05 * TOKENS)
    upper = math.log(0.0013 * TOKENS)
    return jnp.exp(jax.random.uniform(jax.random.fold_in(key, 707), (VEC_ROWS, D), jnp.float32, lower, upper))


def plant(drawn, key, least, top_value):
    shape = drawn.shape
    place = [jax.random.randint(jax.random.fold_in(key, axis), (), 0, shape[axis]) for axis in range(len(shape))]
    drawn = drawn.at[tuple(place)].set(least)
    longest = shape.index(max(shape))
    place[longest] = (place[longest] + 1) % shape[longest]
    return drawn.at[tuple(place)].set(top_value)


def shard_levels(own_key, extent, cuts, least, top_value):
    def one(dim, parts):
        draws = jax.random.uniform(jax.random.fold_in(jax.random.fold_in(own_key, 6), dim), (parts,), jnp.float32, least / len(cuts), top_value / len(cuts))
        return jnp.repeat(jnp.exp(draws), extent[dim] // parts).reshape((-1,) + (1,) * (len(extent) - dim - 1))

    factor_of = one(*cuts[0])
    for cut in cuts[1:]:
        factor_of = factor_of * one(*cut)
    return factor_of


def length_profile(amount, total, limit, slope):
    portions = [(1 << 20) // math.isqrt(standing ** slope) + 1 for standing in range(2, amount + 1)]
    surplus, holding = total - limit - (amount - 1), [1] * (amount - 1)
    while surplus > 0:
        free = [i for i in range(amount - 1) if holding[i] < limit]
        mass, left = sum([portions[i] for i in free]), surplus
        for i in free:
            more = min(limit - holding[i], max(1, left * portions[i] // mass), surplus)
            holding[i] = holding[i] + more
            surplus = surplus - more
    return np.array([limit] + holding)


def ragged(stream_key, count, total, most, slope):
    if count == 2:
        one = jax.random.randint(stream_key, (), max(1, total - most), min(most, total - 1) + 1)
        return jnp.stack([one, total - one])
    sizes = jnp.asarray(length_profile(count, total, most, slope), jnp.int32)
    pairs = (count - 1) // 2
    giver, taker = sizes[1:1 + 2 * pairs:2], sizes[2:2 + 2 * pairs:2]
    margin = jnp.minimum(giver - 1, most - taker)
    shifted = jax.random.randint(jax.random.fold_in(stream_key, 1), (pairs,), 0, 1 << 20) % (margin + 1)
    sizes = sizes.at[1:1 + 2 * pairs:2].set(giver - shifted).at[2:2 + 2 * pairs:2].set(taker + shifted)
    return sizes[jax.random.permutation(jax.random.fold_in(stream_key, 2), count)]


def scatter_about(stream_key, extent, scale, limit, pieces=(), held_as=jnp.bfloat16):
    loudness = shard_levels(stream_key, extent, pieces, -0.22, 0.18) if pieces else 1.0
    entries = jax.random.normal(stream_key, extent, jnp.float32) * scale * loudness
    return jnp.minimum(jnp.maximum(entries, -limit), limit).astype(held_as)


def setup_inputs(seed: int = 0) -> dict:
    splits = jax.random.split(jax.random.key(seed), 16)
    return {
        "tokens": scatter_about(splits[0], (TOKENS, D), 1.0, 6.0, ((0, 32),)),
        "cotangent": scatter_about(splits[1], (TOKENS, D), 1.0, 6.0, ((0, 32),)),
        "lengths": jax.vmap(lambda own: ragged(own, SEGS, ROW_LEN, 3 * ROW_LEN // 4, 2))(jax.random.split(splits[2], ROWS)).reshape((ROWS, SEGS)).astype(jnp.int32),
        "counts": plant(jax.random.randint(splits[3], (ROWS, SEGS), 1, 5), jax.random.fold_in(splits[3], 1), 1, 4).astype(jnp.int32),
        "w_qkv": scatter_about(splits[4], (3 * D, D), D ** -0.5, 0.25, ((0, 4), (1, 8)), jnp.float32),
        "w_out": scatter_about(splits[5], (D, D), (max(D // 64, 1)) ** -0.5, 2.0, ((0, 4), (1, 8)), jnp.float32),
        "w_up": scatter_about(splits[6], (FF, D), D ** -0.5, 0.25, ((0, 4), (1, 8)), jnp.float32),
        "w_down": scatter_about(splits[7], (FF, D), FF ** -0.5, 0.125, ((0, 4), (1, 8)), jnp.float32),
        "mom_qkv": draw_mom_qkv(jax.random.fold_in(splits[15], 71), 0),
        "mom_out": draw_mom_out(jax.random.fold_in(splits[15], 71), 0),
        "mom_up": draw_mom_up(jax.random.fold_in(splits[15], 71), 0),
        "mom_down": draw_mom_down(jax.random.fold_in(splits[15], 71), 0),
        "vectors": draw_vectors(jax.random.fold_in(splits[15], 71), 0),
        "vec_first": draw_vec_first(jax.random.fold_in(splits[15], 71), 0),
        "vec_second": draw_vec_second(jax.random.fold_in(splits[15], 71), 0),
    }


@jax.custom_vjp
def low(v):
    return lax.optimization_barrier(v.astype(jnp.bfloat16)).astype(jnp.float32)

@jax.custom_vjp
def low_back(v):
    return v

def low_keep(v):
    return (low(v), None)

def low_pass(kept, grad):
    return (grad,)

def back_keep(v):
    return (v, None)

def back_low(kept, grad):
    return (low(grad),)
low.defvjp(low_keep, low_pass)
low_back.defvjp(back_keep, back_low)
norm_eps = 1e-05
masked_score = -1e+30
block_rows = 2
poly_linear = 3.4445
poly_square = -4.775
poly_cubic = 2.0315
muon_rate = 0.5
muon_decay = 0.01
moment_keep = 0.5
adam_rate = 0.05
beta_first = 0.9
beta_second = 0.999
adam_eps = 1e-08
exact = lax.Precision.HIGHEST

def layer_norm(values, gain_row, shift_row):
    center = values - lax.optimization_barrier(jnp.mean(values, axis=-1, keepdims=True))
    spread = lax.optimization_barrier(jnp.mean(center * center, axis=-1, keepdims=True))
    return center * lax.rsqrt(spread + norm_eps) * gain_row + shift_row

def gelu_exact(values):
    return 0.5 * values * (1.0 + lax.erf(values * (1.0 / math.sqrt(2.0))))

def rotate(values, cosine_table, sine_table):
    half_width = values.shape[-1] // 2
    turned = jnp.concatenate([-values[..., half_width:], values[..., :half_width]], axis=-1)
    return values * cosine_table + turned * sine_table

def rotary_tables(position, head_dim):
    indices = lax.broadcasted_iota(jnp.float32, (head_dim // 2,), 0)
    inverse = jnp.exp(indices * (-2.0 * math.log(10000.0) / head_dim))
    angles = position[..., None] * inverse
    angles = jnp.concatenate([angles, angles], axis=-1)
    return (jnp.cos(angles), jnp.sin(angles))

def row_layout(lengths, counts):
    row_count, slot_count = lengths.shape
    endings = jnp.cumsum(lengths, axis=1).astype(jnp.int32)
    starting = (endings - lengths).astype(jnp.int32)
    places = lax.broadcasted_iota(jnp.int32, (row_count, ROW_LEN), 1)
    segment = lax.optimization_barrier(jnp.sum((places[:, :, None] >= endings[:, None, :]).astype(jnp.int32), axis=2)).astype(jnp.int32)
    member = segment[:, :, None] == lax.broadcasted_iota(jnp.int32, (1, 1, slot_count), 2)
    first_place = lax.optimization_barrier(jnp.sum(jnp.where(member, starting[:, None, :], 0), axis=2)).astype(jnp.int32)
    position = (places - first_place).astype(jnp.float32)
    inverse_count = 1.0 / counts.astype(jnp.float32)
    seq_share = lax.optimization_barrier(jnp.sum(jnp.where(member, inverse_count[:, None, :], 0.0), axis=2))
    return (segment, position, seq_share)

def block_forward(inputs, segment, position, weights):
    w_qkv, w_out, w_up, w_down, vectors = weights
    batch_rows, row_len, width = inputs.shape
    head_count = width // HEAD_DIM
    gain_one, shift_one, gain_two, shift_two = (vectors[0], vectors[1], vectors[2], vectors[3])
    bias_qkv = vectors[4:7].reshape(-1)
    bias_out = vectors[7]
    bias_down = vectors[8]
    bias_up = vectors[9:].reshape(-1)
    normed_one = low(layer_norm(inputs, gain_one, shift_one))
    project = low_back(jnp.einsum('ble,fe->blf', normed_one, w_qkv, precision=exact) + bias_qkv)
    query_scale = 1.0 / math.sqrt(HEAD_DIM)
    queries = project[..., :width].reshape(batch_rows, row_len, head_count, HEAD_DIM) * query_scale
    key_rows = project[..., width:2 * width].reshape(batch_rows, row_len, head_count, HEAD_DIM)
    value_rows = low(project[..., 2 * width:].reshape(batch_rows, row_len, head_count, HEAD_DIM))
    cosine_table, sine_table = rotary_tables(position, HEAD_DIM)
    cosine_table = cosine_table[:, :, None, :]
    sine_table = sine_table[:, :, None, :]
    turned_q = low(rotate(queries, cosine_table, sine_table))
    turned_k = low(rotate(key_rows, cosine_table, sine_table))
    scores = low_back(jnp.einsum('bqhd,bkhd->bhqk', turned_q, turned_k, precision=exact))
    same_segment = segment[:, None, :, None] == segment[:, None, None, :]
    scores = jnp.where(same_segment, scores, masked_score)
    row_peak = lax.optimization_barrier(jnp.max(scores, axis=-1, keepdims=True))
    raised = jnp.exp(scores - row_peak)
    softmax_full = raised / lax.optimization_barrier(jnp.sum(raised, axis=-1, keepdims=True))
    attended = jnp.einsum('bhqk,bkhd->bqhd', low(softmax_full), value_rows, precision=exact)
    attended = low(low_back(attended.reshape(batch_rows, row_len, width)))
    branch = low_back(jnp.einsum('ble,fe->blf', attended, w_out, precision=exact) + bias_out)
    after_attn = inputs + branch
    normed_two = low(layer_norm(after_attn, gain_two, shift_two))
    hidden_pre = low_back(jnp.einsum('ble,fe->blf', normed_two, w_up, precision=exact) + bias_up)
    hidden_low = low(gelu_exact(hidden_pre))
    return after_attn + low_back(jnp.einsum('blf,fe->ble', hidden_low, w_down, precision=exact) + bias_down)

def forward_all(inputs, w_qkv, w_out, w_up, w_down, vectors, segment, position):
    weights = (low(w_qkv), low(w_out), low(w_up), low(w_down), low(vectors))
    block_count = ROWS // block_rows
    token_blocks = inputs.reshape(block_count, block_rows, ROW_LEN, D)
    segment_blocks = segment.reshape(block_count, block_rows, ROW_LEN)
    position_blocks = position.reshape(block_count, block_rows, ROW_LEN)

    def one_block(block_inputs):
        return block_forward(block_inputs[0], block_inputs[1], block_inputs[2], weights)
    outcome = lax.map(jax.checkpoint(one_block), (token_blocks, segment_blocks, position_blocks))
    return outcome.reshape(TOKENS, D)

def orthogonal(moment):
    iterate = moment * lax.rsqrt(jnp.sum(moment * moment) + 1e-07)
    identity = jnp.eye(moment.shape[1], dtype=jnp.float32)
    for iteration in range(NS_ITERS):
        gram_now = jnp.dot(iterate.T, iterate, precision=exact)
        factor = poly_linear * identity + poly_square * gram_now + poly_cubic * jnp.dot(gram_now, gram_now, precision=exact)
        iterate = jnp.dot(iterate, factor, precision=exact)
    return iterate

def muon_update(weight, moment, grad_full):
    new_moment = moment_keep * moment + grad_full
    factor = muon_rate * math.sqrt(max(1.0, weight.shape[0] / weight.shape[1]))
    new_weight = weight * (1.0 - muon_rate * muon_decay) - factor * orthogonal(new_moment)
    return (new_moment, new_weight)

def reference(tokens, cotangent, lengths, counts, w_qkv, w_out, w_up, w_down, mom_qkv, mom_out, mom_up, mom_down, vectors, vec_first, vec_second):
    segment, position, seq_share = row_layout(lengths, counts)
    inputs = tokens.astype(jnp.float32)
    primal = partial(forward_all, segment=segment, position=position)
    layer_value, pullback = jax.vjp(primal, inputs, w_qkv, w_out, w_up, w_down, vectors)
    incoming = cotangent.astype(jnp.float32) * seq_share.reshape(-1)[:, None]
    grad_parts = pullback(incoming)
    new_mom_qkv, new_w_qkv = muon_update(w_qkv, mom_qkv, grad_parts[1])
    new_mom_out, new_w_out = muon_update(w_out, mom_out, grad_parts[2])
    new_mom_up, new_w_up = muon_update(w_up, mom_up, grad_parts[3])
    new_mom_down, new_w_down = muon_update(w_down, mom_down, grad_parts[4])
    vec_grad = grad_parts[5]
    new_first = beta_first * vec_first + (1.0 - beta_first) * vec_grad
    new_second = beta_second * vec_second + (1.0 - beta_second) * vec_grad * vec_grad
    first_fix = 1.0 - beta_first ** STEP
    second_fix = 1.0 - beta_second ** STEP
    new_vectors = vectors - adam_rate * (new_first / first_fix) / (jnp.sqrt(new_second / second_fix) + adam_eps)
    return (layer_value.astype(jnp.bfloat16), grad_parts[0], new_mom_qkv, new_mom_out, new_mom_up, new_mom_down, new_w_qkv, new_w_out, new_w_up, new_w_down, new_vectors, new_first, new_second)
```

```python
import functools
import math

import jax
import jax.numpy as jnp
from jax import lax
from jax.experimental import pallas as pl
from jax.experimental.pallas import tpu as pltpu
from jax.sharding import PartitionSpec as P

HEAD_DIM = 32
NS_ITERS = 5
STEP = 10
LANES = 128
LONGEST = 768

norm_eps = 1e-05
masked_score = -1e30
poly_linear = 3.4445
poly_square = -4.775
poly_cubic = 2.0315
muon_rate = 0.5
muon_decay = 0.01
moment_keep = 0.5
adam_rate = 0.05
beta_first = 0.9
beta_second = 0.999
adam_eps = 1e-08


def layer_norm(values, gain_row, shift_row):
    center = values - jnp.mean(values, axis=-1, keepdims=True)
    spread = jnp.mean(center * center, axis=-1, keepdims=True)
    return center * lax.rsqrt(spread + norm_eps) * gain_row + shift_row


def gelu_exact(values):
    return 0.5 * values * (1.0 + lax.erf(values * (1.0 / math.sqrt(2.0))))


def nn(left, right):
    return jnp.dot(left, right, preferred_element_type=jnp.float32)


def nt(left, right):
    return lax.dot_general(left, right, (((1,), (1,)), ((), ())), preferred_element_type=jnp.float32)


def tn(left, right):
    return lax.dot_general(left, right, (((0,), (0,)), ((), ())), preferred_element_type=jnp.float32)


def _half_mask(shape):
    lane = lax.broadcasted_iota(jnp.int32, shape, 1)
    return (lane % HEAD_DIM) < (HEAD_DIM // 2)


def _turn(values, first):
    half = HEAD_DIM // 2
    left = pltpu.roll(values, LANES - half, 1)
    right = pltpu.roll(values, half, 1)
    return jnp.where(first, left, right)


def attention_forward_kernel(
    q_ref, k_ref, v_ref, cos_ref, sin_ref, segc_ref, segr_ref,
    qr_ref, kr_ref, vr_ref, attn_ref, lse_ref,
    qt_s, vt_s, ot_s,
):
    first = _half_mask(cos_ref.shape)
    cosine, sine = cos_ref[...], sin_ref[...]
    queries = q_ref[...] * (1.0 / math.sqrt(HEAD_DIM))
    qr = (queries * cosine + _turn(queries, first) * sine).astype(jnp.bfloat16)
    keys = k_ref[...]
    kr = (keys * cosine + _turn(keys, first) * sine).astype(jnp.bfloat16)
    vr = v_ref[...].astype(jnp.bfloat16)
    qr_ref[...] = qr
    kr_ref[...] = kr
    vr_ref[...] = vr
    qt_s[...] = qr.T
    vt_s[...] = vr.T
    tokens = qr.shape[0]
    rest = tokens - LONGEST
    row = lax.broadcasted_iota(jnp.int32, (LANES, tokens), 0)
    same = segc_ref[LONGEST:, :] == segr_ref[:, LONGEST:]

    def head(h, carry):
        qth = jnp.where(row // HEAD_DIM == h, qt_s[...], jnp.zeros((), jnp.bfloat16))
        rows = pl.ds(pl.multiple_of(h * HEAD_DIM, HEAD_DIM), HEAD_DIM)

        def block(start, width, key_start, key_count, mask):
            scores = nn(kr_ref[key_start : key_start + key_count, :], qth[:, start : start + width])
            if mask is not None:
                scores = jnp.where(mask, scores, masked_score)
            peak = jnp.max(scores, axis=0, keepdims=True)
            raised = jnp.exp(scores - peak)
            total = jnp.sum(raised, axis=0, keepdims=True)
            out = nn(vt_s[rows, key_start : key_start + key_count], raised.astype(jnp.bfloat16))
            ot_s[rows, start : start + width] = out / total
            lse_ref[0, pl.ds(h, 1), start : start + width] = peak + jnp.log(total)

        for start in range(0, LONGEST, 256):
            block(start, 256, 0, LONGEST, None)
        block(LONGEST, rest, LONGEST, rest, same)
        return carry

    lax.fori_loop(0, LANES // HEAD_DIM, head, 0)
    attn_ref[...] = ot_s[...].T.astype(jnp.bfloat16)


def attention_forward(project, cosine, sine, seg_col, seg_row):
    tokens = project.shape[0]
    width = project.shape[1] // 3
    groups = width // LANES
    col = lambda shift: pl.BlockSpec((tokens, LANES), lambda g, shift=shift: (0, g + shift))
    whole = lambda shape: pl.BlockSpec(shape, lambda g: (0,) * len(shape))
    flops = 4 * (LONGEST**2 + (tokens - LONGEST) ** 2) * 128 * groups * 4
    return pl.pallas_call(
        attention_forward_kernel,
        grid=(groups,),
        in_specs=[col(0), col(groups), col(2 * groups), whole((tokens, LANES)), whole((tokens, LANES)),
                  whole((tokens, 1)), whole((1, tokens))],
        out_specs=[col(0)] * 4 + [pl.BlockSpec((1, 4, tokens), lambda g: (g, 0, 0))],
        out_shape=[jax.ShapeDtypeStruct((tokens, width), jnp.bfloat16)] * 4
        + [jax.ShapeDtypeStruct((groups, 4, tokens), jnp.float32)],
        scratch_shapes=[
            pltpu.VMEM((LANES, tokens), jnp.bfloat16),
            pltpu.VMEM((LANES, tokens), jnp.bfloat16),
            pltpu.VMEM((LANES, tokens), jnp.float32),
        ],
        compiler_params=pltpu.CompilerParams(vmem_limit_bytes=48 << 20),
        cost_estimate=pl.CostEstimate(flops=flops, bytes_accessed=20 << 20, transcendentals=20 << 20),
        name="attention_forward",
    )(project, project, project, cosine, sine, seg_col, seg_row)


def attention_backward_kernel(
    qr_ref, kr_ref, vr_ref, do_ref, attn_ref, lse_ref, cos_ref, sin_ref, segc_ref, segr_ref,
    dq_ref, dk_ref, dv_ref,
    qt_s, dot_s, kt_s, delta_s, dqt_s, dk_s, dv_s,
):
    tokens = qr_ref.shape[0]
    rest = tokens - LONGEST
    qt_s[...] = qr_ref[...].T
    dot_s[...] = do_ref[...].T
    kt_s[...] = kr_ref[...].T
    prod_t = (do_ref[...].astype(jnp.float32) * attn_ref[...].astype(jnp.float32)).T
    for h in range(4):
        delta_s[h : h + 1, :] = jnp.sum(prod_t[h * HEAD_DIM : (h + 1) * HEAD_DIM, :], axis=0, keepdims=True)
    dk_s[...] = jnp.zeros_like(dk_s)
    dv_s[...] = jnp.zeros_like(dv_s)
    row = lax.broadcasted_iota(jnp.int32, (LANES, tokens), 0)
    lane = lax.broadcasted_iota(jnp.int32, (tokens, LANES), 1)
    same = segc_ref[LONGEST:, :] == segr_ref[:, LONGEST:]
    zero = jnp.zeros((), jnp.bfloat16)

    def head(h, carry):
        mine_t = row // HEAD_DIM == h
        mine = lane // HEAD_DIM == h
        qth = jnp.where(mine_t, qt_s[...], zero)
        doth = jnp.where(mine_t, dot_s[...], zero)
        qh = jnp.where(mine, qr_ref[...], zero)
        doh = jnp.where(mine, do_ref[...], zero)
        rows = pl.ds(pl.multiple_of(h * HEAD_DIM, HEAD_DIM), HEAD_DIM)

        def block(start, width, key_start, key_count, mask):
            at = slice(start, start + width)
            keys = slice(key_start, key_start + key_count)
            scores = nn(kr_ref[keys, :], qth[:, at])
            if mask is not None:
                scores = jnp.where(mask, scores, masked_score)
            soft = jnp.exp(scores - lse_ref[0, pl.ds(h, 1), at])
            weight_grad = nn(vr_ref[keys, :], doth[:, at])
            score_grad = (soft * (weight_grad - delta_s[pl.ds(h, 1), at])).astype(jnp.bfloat16)
            dv_s[keys, :] += nn(soft.astype(jnp.bfloat16), doh[at, :])
            dk_s[keys, :] += nn(score_grad, qh[at, :])
            dqt_s[rows, at] = nn(kt_s[rows, keys], score_grad)

        for start in range(0, LONGEST, 256):
            block(start, 256, 0, LONGEST, None)
        block(LONGEST, rest, LONGEST, rest, same)
        return carry

    lax.fori_loop(0, LANES // HEAD_DIM, head, 0)
    first = _half_mask(cos_ref.shape)
    cosine, sine = cos_ref[...], sin_ref[...]

    def pull(values):
        return values * cosine + _turn(values * sine, first)

    dq_ref[...] = (pull(dqt_s[...].T) * (1.0 / math.sqrt(HEAD_DIM))).astype(jnp.bfloat16)
    dk_ref[...] = pull(dk_s[...]).astype(jnp.bfloat16)
    dv_ref[...] = dv_s[...].astype(jnp.bfloat16)


def attention_backward(qr, kr, vr, attn_grad, attn, lse, cosine, sine, seg_col, seg_row):
    tokens, width = qr.shape
    groups = width // LANES
    col = pl.BlockSpec((tokens, LANES), lambda g: (0, g))
    whole = lambda shape: pl.BlockSpec(shape, lambda g: (0,) * len(shape))
    flops = 10 * (LONGEST**2 + (tokens - LONGEST) ** 2) * 128 * groups * 4
    return pl.pallas_call(
        attention_backward_kernel,
        grid=(groups,),
        in_specs=[col] * 5 + [pl.BlockSpec((1, 4, tokens), lambda g: (g, 0, 0)),
                              whole((tokens, LANES)), whole((tokens, LANES)), whole((tokens, 1)), whole((1, tokens))],
        out_specs=[col] * 3,
        out_shape=[jax.ShapeDtypeStruct((tokens, width), jnp.bfloat16)] * 3,
        scratch_shapes=[
            pltpu.VMEM((LANES, tokens), jnp.bfloat16),
            pltpu.VMEM((LANES, tokens), jnp.bfloat16),
            pltpu.VMEM((LANES, tokens), jnp.bfloat16),
            pltpu.VMEM((8, tokens), jnp.float32),
            pltpu.VMEM((LANES, tokens), jnp.float32),
            pltpu.VMEM((tokens, LANES), jnp.float32),
            pltpu.VMEM((tokens, LANES), jnp.float32),
        ],
        compiler_params=pltpu.CompilerParams(vmem_limit_bytes=48 << 20),
        cost_estimate=pl.CostEstimate(flops=flops, bytes_accessed=20 << 20, transcendentals=20 << 20),
        name="attention_backward",
    )(qr, kr, vr, attn_grad, attn, lse, cosine, sine, seg_col, seg_row)


def row_layout(lengths, counts, row_len):
    lens = lengths[0]
    slots = lens.shape[0]
    order = lax.broadcasted_iota(jnp.int32, (slots, slots), 0)
    upto = lax.broadcasted_iota(jnp.int32, (slots, slots), 1)
    starting = jnp.sum(jnp.where(upto < order, lens[None, :], 0), axis=1)
    slot = lax.broadcasted_iota(jnp.int32, (slots,), 0)
    which = jnp.min(jnp.where(lens == LONGEST, slot, slots))
    offset = jnp.sum(jnp.where(slot == which, starting, 0))
    places = lax.broadcasted_iota(jnp.int32, (row_len,), 0) + offset
    places = jnp.where(places >= row_len, places - row_len, places)
    endings = starting + lens
    segment = jnp.sum((places[:, None] >= endings[None, :]).astype(jnp.int32), axis=1)
    member = segment[:, None] == slot[None, :]
    first_place = jnp.sum(jnp.where(member, starting[None, :], 0), axis=1)
    position = (places - first_place).astype(jnp.float32)
    inverse_count = 1.0 / counts[0].astype(jnp.float32)
    share = jnp.sum(jnp.where(member, inverse_count[None, :], 0.0), axis=1)
    return offset, segment, position, share


def rotary_tables(position):
    lane = lax.broadcasted_iota(jnp.int32, (1, LANES), 1)
    indices = (lane % (HEAD_DIM // 2)).astype(jnp.float32)
    inverse = jnp.exp(indices * (-2.0 * math.log(10000.0) / HEAD_DIM))
    angles = position[:, None] * inverse
    sign = jnp.where((lane % HEAD_DIM) < (HEAD_DIM // 2), -1.0, 1.0)
    return jnp.cos(angles), jnp.sin(angles) * sign


def turn_rows(values, shift):
    twice = jnp.concatenate([values, values], axis=0)
    return lax.dynamic_slice_in_dim(twice, shift, values.shape[0], 0)


def high(left, right):
    return jnp.dot(left, right, precision=lax.Precision.HIGH, preferred_element_type=jnp.float32)


def shards(
    tokens, cotangent, lengths, counts,
    w_qkv, w_out, w_up, w_down,
    mom_qkv, mom_out, mom_up, mom_down,
    vectors, vec_first, vec_second,
):
    both = ("fsdp", "dp")
    planes = lax.axis_size("fsdp")
    ranks = lax.axis_size("dp")
    row_len, width = tokens.shape
    columns = w_qkv.shape[1]
    old_weights = (w_qkv, w_out, w_up, w_down)
    old_moments = (mom_qkv, mom_out, mom_up, mom_down)
    counts_rows = [w.shape[0] for w in old_weights]
    n_vec = vectors.shape[0]

    slab_a = jnp.concatenate([w_qkv.T, w_out.T, vectors.T], axis=1).astype(jnp.bfloat16)
    slab_b = jnp.concatenate([w_up.T, w_down.T], axis=1).astype(jnp.bfloat16)
    full_a = lax.all_gather(slab_a, both, axis=0, tiled=True).reshape(planes, width, -1)
    full_b = lax.all_gather(slab_b, both, axis=0, tiled=True).reshape(planes, width, -1)
    r0, r1, r2, r3 = counts_rows
    wt_qkv = jnp.concatenate([full_a[j, :, :r0] for j in range(planes)], axis=1)
    wt_out = jnp.concatenate([full_a[j, :, r0 : r0 + r1] for j in range(planes)], axis=1)
    table = full_a[0, :, r0 + r1 :].T.astype(jnp.float32)
    wt_up = jnp.concatenate([full_b[j, :, :r2] for j in range(planes)], axis=1)
    wt_down = jnp.concatenate([full_b[j, :, r2:] for j in range(planes)], axis=1)

    offset, segment, position, share = row_layout(lengths, counts, row_len)
    cosine, sine = rotary_tables(position)
    seg_col, seg_row = segment[:, None], segment[None, :]
    inputs = turn_rows(tokens, offset).astype(jnp.float32)
    incoming = turn_rows(cotangent, offset).astype(jnp.float32) * share[:, None]

    normed_one, pull_one = jax.vjp(layer_norm, inputs, table[0], table[1])
    normed_one = normed_one.astype(jnp.bfloat16)
    project = nn(normed_one, wt_qkv) + table[4:7].reshape(-1)
    qr, kr, vr, attn, lse = attention_forward(project, cosine, sine, seg_col, seg_row)
    after = inputs + (nn(attn, wt_out) + table[7])
    normed_two, pull_two = jax.vjp(layer_norm, after, table[2], table[3])
    normed_two = normed_two.astype(jnp.bfloat16)
    hidden_pre = nn(normed_two, wt_up) + table[9:].reshape(-1)
    hidden, pull_hidden = jax.vjp(gelu_exact, hidden_pre)
    hidden = hidden.astype(jnp.bfloat16)
    layer_out = (after + (nt(hidden, wt_down) + table[8])).astype(jnp.bfloat16)

    grad_low = incoming.astype(jnp.bfloat16)
    grad_t_down = tn(grad_low, hidden)
    pre_grad = pull_hidden(nn(grad_low, wt_down))[0].astype(jnp.bfloat16)
    grad_t_up = tn(normed_two, pre_grad)
    resid_grad, gain_two, shift_two = pull_two(nt(pre_grad, wt_up))
    after_grad = incoming + resid_grad
    branch_low = after_grad.astype(jnp.bfloat16)
    grad_t_out = tn(attn, branch_low)
    attn_grad = nt(branch_low, wt_out).astype(jnp.bfloat16)
    dq, dk, dv = attention_backward(qr, kr, vr, attn_grad, attn, lse, cosine, sine, seg_col, seg_row)
    proj_grad = jnp.concatenate([dq, dk, dv], axis=1)
    grad_t_qkv = tn(normed_one, proj_grad)
    in_grad, gain_one, shift_one = pull_one(nt(proj_grad, wt_qkv))
    input_grad = after_grad + in_grad

    def column_sum(values):
        return jnp.sum(values.astype(jnp.float32), axis=0)

    vector_grad = jnp.concatenate(
        [gain_one[None], shift_one[None], gain_two[None], shift_two[None],
         column_sum(proj_grad).reshape(3, width), column_sum(branch_low)[None], column_sum(grad_low)[None],
         column_sum(pre_grad).reshape(-1, width)],
        axis=0,
    )
    back = jnp.where(offset > 0, row_len - offset, 0)
    layer_out = turn_rows(layer_out, back)
    input_grad = turn_rows(input_grad, back)

    def cut(values, j, rows):
        return values[:, j * rows : (j + 1) * rows]

    parts_b = jnp.stack([jnp.concatenate([cut(grad_t_up, j, r2), cut(grad_t_down, j, r3)], axis=1) for j in range(planes)])
    own_b = lax.psum_scatter(parts_b.reshape(planes * width, -1), both, scatter_dimension=0, tiled=True)
    parts_a = jnp.stack([jnp.concatenate([cut(grad_t_qkv, j, r0), cut(grad_t_out, j, r1), vector_grad.T], axis=1) for j in range(planes)])
    own_a = lax.psum_scatter(parts_a.reshape(planes * width, -1), both, scatter_dimension=0, tiled=True)
    grads_t = (own_a[:, :r0], own_a[:, r0 : r0 + r1], own_b[:, :r2], own_b[:, r2:])
    vector_grad = own_a[:, r0 + r1 :].T
    new_moments_t = [moment_keep * old.T + grad for old, grad in zip(old_moments, grads_t)]

    most = max(counts_rows)
    padded = [jnp.pad(m.astype(jnp.bfloat16), ((0, 0), (0, most - m.shape[1]))) for m in new_moments_t]
    sent = jnp.stack([padded[t % 4] for t in range(planes)])
    mine = lax.all_to_all(sent, "fsdp", 0, 0, tiled=True)
    mine = mine.transpose(1, 0, 2).reshape(columns, planes * most)
    whole = lax.all_gather(mine, "dp", axis=0, tiled=True)
    gram = nt(whole, whole)
    identity = jnp.eye(width, dtype=jnp.float32)
    norm_sq = jnp.trace(gram) + 1e-07
    gram = gram / norm_sq
    factor = None
    for iteration in range(NS_ITERS):
        poly = poly_linear * identity + poly_square * gram + poly_cubic * high(gram, gram)
        factor = poly if factor is None else high(factor, poly)
        if iteration + 1 < NS_ITERS:
            gram = high(high(gram, poly), poly)
    own_rows = lax.dynamic_slice_in_dim(factor, lax.axis_index("dp") * columns, columns, 0) * lax.rsqrt(norm_sq)
    own_orth = high(own_rows, whole.astype(jnp.float32))
    own_orth = own_orth.astype(jnp.bfloat16).reshape(columns, planes, most).transpose(1, 0, 2)
    pieces = lax.all_to_all(own_orth, "fsdp", 0, 0, tiled=True).astype(jnp.float32)

    new_weights = []
    for x, weight_old in enumerate(old_weights):
        rows = weight_old.shape[0]
        scale = muon_rate * math.sqrt(max(1.0, rows * planes / width))
        new_weights.append(weight_old * (1.0 - muon_rate * muon_decay) - scale * pieces[x, :, :rows].T)
    new_first = beta_first * vec_first + (1.0 - beta_first) * vector_grad
    new_second = beta_second * vec_second + (1.0 - beta_second) * vector_grad * vector_grad
    first_fix = 1.0 - beta_first**STEP
    second_fix = 1.0 - beta_second**STEP
    new_vectors = vectors - adam_rate * (new_first / first_fix) / (jnp.sqrt(new_second / second_fix) + adam_eps)
    return (layer_out, input_grad, *[m.T for m in new_moments_t], *new_weights, new_vectors, new_first, new_second)


def solution(mesh):
    rows, cells, table = P(("dp", "fsdp"), None), P("fsdp", "dp"), P(None, "dp")
    return jax.shard_map(
        shards,
        mesh=mesh,
        in_specs=(rows,) * 4 + (cells,) * 8 + (table,) * 3,
        out_specs=(rows,) * 2 + (cells,) * 8 + (table,) * 3,
        check_vma=False,
    )
```

```python
import functools
import math

import jax
import jax.numpy as jnp
from jax import lax
from jax.experimental import pallas as pl
from jax.experimental.pallas import tpu as pltpu
from jax.sharding import PartitionSpec as P

HEAD_DIM = 32
NS_ITERS = 5
STEP = 10
LANES = 128
LONGEST = 768

norm_eps = 1e-05
masked_score = -1e30
poly_linear = 3.4445
poly_square = -4.775
poly_cubic = 2.0315
muon_rate = 0.5
muon_decay = 0.01
moment_keep = 0.5
adam_rate = 0.05
beta_first = 0.9
beta_second = 0.999
adam_eps = 1e-08


def layer_norm(values, gain_row, shift_row):
    center = values - jnp.mean(values, axis=-1, keepdims=True)
    spread = jnp.mean(center * center, axis=-1, keepdims=True)
    return center * lax.rsqrt(spread + norm_eps) * gain_row + shift_row


def gelu_exact(values):
    return 0.5 * values * (1.0 + lax.erf(values * (1.0 / math.sqrt(2.0))))


def nn(left, right):
    return jnp.dot(left, right, preferred_element_type=jnp.float32)


def nt(left, right):
    return lax.dot_general(left, right, (((1,), (1,)), ((), ())), preferred_element_type=jnp.float32)


def tn(left, right):
    return lax.dot_general(left, right, (((0,), (0,)), ((), ())), preferred_element_type=jnp.float32)


def _half_mask(shape):
    lane = lax.broadcasted_iota(jnp.int32, shape, 1)
    return (lane % HEAD_DIM) < (HEAD_DIM // 2)


def _turn(values, first):
    half = HEAD_DIM // 2
    left = pltpu.roll(values, LANES - half, 1)
    right = pltpu.roll(values, half, 1)
    return jnp.where(first, left, right)


def attention_forward_kernel(
    q_ref, k_ref, v_ref, cos_ref, sin_ref, segc_ref, segr_ref,
    qr_ref, kr_ref, vr_ref, attn_ref, lse_ref,
    qt_s, vt_s, ot_s,
):
    first = _half_mask(cos_ref.shape)
    cosine, sine = cos_ref[...], sin_ref[...]
    queries = q_ref[...] * (1.0 / math.sqrt(HEAD_DIM))
    qr = (queries * cosine + _turn(queries, first) * sine).astype(jnp.bfloat16)
    keys = k_ref[...]
    kr = (keys * cosine + _turn(keys, first) * sine).astype(jnp.bfloat16)
    vr = v_ref[...].astype(jnp.bfloat16)
    qr_ref[...] = qr
    kr_ref[...] = kr
    vr_ref[...] = vr
    qt_s[...] = qr.T
    vt_s[...] = vr.T
    tokens = qr.shape[0]
    rest = tokens - LONGEST
    row = lax.broadcasted_iota(jnp.int32, (LANES, tokens), 0)
    same = segc_ref[LONGEST:, :] == segr_ref[:, LONGEST:]

    def head(h, carry):
        qth = jnp.where(row // HEAD_DIM == h, qt_s[...], jnp.zeros((), jnp.bfloat16))
        rows = pl.ds(pl.multiple_of(h * HEAD_DIM, HEAD_DIM), HEAD_DIM)

        def block(start, width, key_start, key_count, mask):
            scores = nn(kr_ref[key_start : key_start + key_count, :], qth[:, start : start + width])
            if mask is not None:
                scores = jnp.where(mask, scores, masked_score)
            peak = jnp.max(scores, axis=0, keepdims=True)
            raised = jnp.exp(scores - peak)
            total = jnp.sum(raised, axis=0, keepdims=True)
            out = nn(vt_s[rows, key_start : key_start + key_count], raised.astype(jnp.bfloat16))
            ot_s[rows, start : start + width] = out / total
            lse_ref[0, pl.ds(h, 1), start : start + width] = peak + jnp.log(total)

        for start in range(0, LONGEST, 256):
            block(start, 256, 0, LONGEST, None)
        block(LONGEST, rest, LONGEST, rest, same)
        return carry

    lax.fori_loop(0, LANES // HEAD_DIM, head, 0)
    attn_ref[...] = ot_s[...].T.astype(jnp.bfloat16)


def attention_forward(project, cosine, sine, seg_col, seg_row):
    tokens = project.shape[0]
    width = project.shape[1] // 3
    groups = width // LANES
    col = lambda shift: pl.BlockSpec((tokens, LANES), lambda g, shift=shift: (0, g + shift))
    whole = lambda shape: pl.BlockSpec(shape, lambda g: (0,) * len(shape))
    flops = 4 * (LONGEST**2 + (tokens - LONGEST) ** 2) * 128 * groups * 4
    return pl.pallas_call(
        attention_forward_kernel,
        grid=(groups,),
        in_specs=[col(0), col(groups), col(2 * groups), whole((tokens, LANES)), whole((tokens, LANES)),
                  whole((tokens, 1)), whole((1, tokens))],
        out_specs=[col(0)] * 4 + [pl.BlockSpec((1, 4, tokens), lambda g: (g, 0, 0))],
        out_shape=[jax.ShapeDtypeStruct((tokens, width), jnp.bfloat16)] * 4
        + [jax.ShapeDtypeStruct((groups, 4, tokens), jnp.float32)],
        scratch_shapes=[
            pltpu.VMEM((LANES, tokens), jnp.bfloat16),
            pltpu.VMEM((LANES, tokens), jnp.bfloat16),
            pltpu.VMEM((LANES, tokens), jnp.float32),
        ],
        compiler_params=pltpu.CompilerParams(vmem_limit_bytes=48 << 20),
        cost_estimate=pl.CostEstimate(flops=flops, bytes_accessed=20 << 20, transcendentals=20 << 20),
        name="attention_forward",
    )(project, project, project, cosine, sine, seg_col, seg_row)


def attention_backward_kernel(
    qr_ref, kr_ref, vr_ref, do_ref, attn_ref, lse_ref, cos_ref, sin_ref, segc_ref, segr_ref,
    *rest_refs,
):
    if len(rest_refs) > 10:
        parts_ref, dq_ref, dk_ref, dv_ref, own_ref = rest_refs[:5]
        scratch = rest_refs[5:]
        lanes = parts_ref.shape[-1] // 2
        halves = [stages_of(parts_ref, scratch[7 + SUM_SCRATCH * n : 7 + SUM_SCRATCH * (n + 1)], pl.ds(n * lanes, lanes))
                  for n in range(2)]
    else:
        halves = None
        dq_ref, dk_ref, dv_ref = rest_refs[:3]
        scratch = rest_refs[3:]
    qt_s, dot_s, kt_s, delta_s, dqt_s, dk_s, dv_s = scratch[:7]
    group = pl.program_id(0)
    if halves is not None:
        @pl.when(group == 0)
        def _():
            greet(all_partners())
            halves[0].core_start()
            halves[1].core_start()

        @pl.when(group == 1)
        def _():
            halves[0].core_finish()
            halves[0].chip_start()
            halves[1].core_finish()

        @pl.when(group == 2)
        def _():
            halves[1].chip_start()

        @pl.when(group == 4)
        def _():
            halves[0].chip_finish()
            halves[0].plane_start()

    tokens = qr_ref.shape[0]
    rest = tokens - LONGEST
    qt_s[...] = qr_ref[...].T
    dot_s[...] = do_ref[...].T
    kt_s[...] = kr_ref[...].T
    prod_t = (do_ref[...].astype(jnp.float32) * attn_ref[...].astype(jnp.float32)).T
    for h in range(4):
        delta_s[h : h + 1, :] = jnp.sum(prod_t[h * HEAD_DIM : (h + 1) * HEAD_DIM, :], axis=0, keepdims=True)
    dk_s[...] = jnp.zeros_like(dk_s)
    dv_s[...] = jnp.zeros_like(dv_s)
    row = lax.broadcasted_iota(jnp.int32, (LANES, tokens), 0)
    lane = lax.broadcasted_iota(jnp.int32, (tokens, LANES), 1)
    same = segc_ref[LONGEST:, :] == segr_ref[:, LONGEST:]
    zero = jnp.zeros((), jnp.bfloat16)

    def head(h, carry):
        mine_t = row // HEAD_DIM == h
        mine = lane // HEAD_DIM == h
        qth = jnp.where(mine_t, qt_s[...], zero)
        doth = jnp.where(mine_t, dot_s[...], zero)
        qh = jnp.where(mine, qr_ref[...], zero)
        doh = jnp.where(mine, do_ref[...], zero)
        rows = pl.ds(pl.multiple_of(h * HEAD_DIM, HEAD_DIM), HEAD_DIM)

        def block(start, width, key_start, key_count, mask):
            at = slice(start, start + width)
            keys = slice(key_start, key_start + key_count)
            scores = nn(kr_ref[keys, :], qth[:, at])
            if mask is not None:
                scores = jnp.where(mask, scores, masked_score)
            soft = jnp.exp(scores - lse_ref[0, pl.ds(h, 1), at])
            weight_grad = nn(vr_ref[keys, :], doth[:, at])
            score_grad = (soft * (weight_grad - delta_s[pl.ds(h, 1), at])).astype(jnp.bfloat16)
            dv_s[keys, :] += nn(soft.astype(jnp.bfloat16), doh[at, :])
            dk_s[keys, :] += nn(score_grad, qh[at, :])
            dqt_s[rows, at] = nn(kt_s[rows, keys], score_grad)

        for start in range(0, LONGEST, 256):
            block(start, 256, 0, LONGEST, None)
        block(LONGEST, rest, LONGEST, rest, same)
        return carry

    lax.fori_loop(0, LANES // HEAD_DIM, head, 0)
    first = _half_mask(cos_ref.shape)
    cosine, sine = cos_ref[...], sin_ref[...]

    def pull(values):
        return values * cosine + _turn(values * sine, first)

    dq_ref[...] = (pull(dqt_s[...].T) * (1.0 / math.sqrt(HEAD_DIM))).astype(jnp.bfloat16)
    dk_ref[...] = pull(dk_s[...]).astype(jnp.bfloat16)
    dv_ref[...] = dv_s[...].astype(jnp.bfloat16)
    if halves is not None:
        @pl.when(group == 4)
        def _():
            halves[1].chip_finish()
            halves[1].plane_start()
            own_ref[:, :lanes] = halves[0].plane_finish()
            own_ref[:, lanes:] = halves[1].plane_finish()


def attention_backward(qr, kr, vr, attn_grad, attn, lse, cosine, sine, seg_col, seg_row, parts=None):
    tokens, width = qr.shape
    groups = width // LANES
    col = pl.BlockSpec((tokens, LANES), lambda g: (0, g))
    whole = lambda shape: pl.BlockSpec(shape, lambda g: (0,) * len(shape))
    flops = 10 * (LONGEST**2 + (tokens - LONGEST) ** 2) * 128 * groups * 4
    with_sum = parts is not None
    more_in, more_out, more_shape, more_scratch, more_params, more_args = [], [], [], [], {}, ()
    if with_sum:
        rows, lanes = parts.shape[-2:]
        more_in = [pl.BlockSpec(memory_space=pl.ANY)]
        more_out = [pl.BlockSpec((rows, lanes), lambda g: (0, 0))]
        more_shape = [jax.ShapeDtypeStruct((rows, lanes), jnp.float32)]
        more_scratch = sum_scratch(rows, lanes // 2) * 2
        more_params = dict(collective_id=0, has_side_effects=True)
        more_args = (parts,)
    return pl.pallas_call(
        attention_backward_kernel,
        grid=(groups,),
        in_specs=[col] * 5 + [pl.BlockSpec((1, 4, tokens), lambda g: (g, 0, 0)),
                              whole((tokens, LANES)), whole((tokens, LANES)), whole((tokens, 1)), whole((1, tokens))]
        + more_in,
        out_specs=[col] * 3 + more_out,
        out_shape=[jax.ShapeDtypeStruct((tokens, width), jnp.bfloat16)] * 3 + more_shape,
        scratch_shapes=[
            pltpu.VMEM((LANES, tokens), jnp.bfloat16),
            pltpu.VMEM((LANES, tokens), jnp.bfloat16),
            pltpu.VMEM((LANES, tokens), jnp.bfloat16),
            pltpu.VMEM((8, tokens), jnp.float32),
            pltpu.VMEM((LANES, tokens), jnp.float32),
            pltpu.VMEM((tokens, LANES), jnp.float32),
            pltpu.VMEM((tokens, LANES), jnp.float32),
        ] + more_scratch,
        compiler_params=pltpu.CompilerParams(vmem_limit_bytes=56 << 20, **more_params),
        cost_estimate=pl.CostEstimate(flops=flops, bytes_accessed=20 << 20, transcendentals=20 << 20),
        name="attention_backward",
    )(qr, kr, vr, attn_grad, attn, lse, cosine, sine, seg_col, seg_row, *more_args)


MESH = pl.DeviceIdType.MESH


def place():
    rank, plane = lax.axis_index("dp"), lax.axis_index("fsdp")
    core = rank % 2
    chip_x = (rank // 2) % 2
    chip_y = rank // 4
    return rank, plane, core, chip_x, chip_y


def chip_at(step, chip_x, chip_y):
    other_x = 1 - chip_x if step & 1 else chip_x
    other_y = 1 - chip_y if step & 2 else chip_y
    return 2 * other_y + other_x


def greet(partners):
    barrier = pltpu.get_barrier_semaphore()
    for partner in partners:
        pl.semaphore_signal(barrier, inc=1, device_id=partner, device_id_type=MESH)
    pl.semaphore_wait(barrier, len(partners))


def all_partners():
    rank, plane, core, chip_x, chip_y = place()
    sibling = 2 * chip_at(0, chip_x, chip_y) + 1 - core
    partners = [(sibling, plane)]
    partners += [(2 * chip_at(step, chip_x, chip_y) + core, plane) for step in (1, 2, 3)]
    partners += [(rank, (plane + step) % 4) for step in (1, 2, 3)]
    return partners


class SumStages:
    def __init__(self, parts, own, from_core, from_chip, from_plane, total, sems, lanes):
        self.parts, self.own, self.from_core, self.from_chip = parts, own, from_core, from_chip
        self.from_plane, self.total, self.lanes = from_plane, total, lanes
        self.send, self.recv, self.local = sems
        self.rank, self.plane, self.core, self.chip_x, self.chip_y = place()
        self.chip = chip_at(0, self.chip_x, self.chip_y)

    def remote(self, source, target, slot, device):
        return pltpu.make_async_remote_copy(
            src_ref=source, dst_ref=target, send_sem=self.send.at[slot], recv_sem=self.recv.at[slot],
            device_id=device, device_id_type=MESH)

    def core_copies(self):
        load = pltpu.make_async_copy(self.parts.at[:, :, self.core, :, self.lanes], self.own, self.local)
        give = self.remote(self.parts.at[:, :, 1 - self.core, :, self.lanes], self.from_core, 0,
                           (2 * self.chip + 1 - self.core, self.plane))
        return load, give

    def core_start(self):
        load, give = self.core_copies()
        give.start()
        load.start()

    def core_finish(self):
        load, give = self.core_copies()
        load.wait()
        give.wait()
        for j in range(self.own.shape[0]):
            self.own[j] = (self.own[j].astype(jnp.float32) + self.from_core[j].astype(jnp.float32)).astype(self.own.dtype)

    def chip_copies(self):
        return [
            self.remote(self.own.at[:, chip_at(step, self.chip_x, self.chip_y)], self.from_chip.at[step - 1], step,
                        (2 * chip_at(step, self.chip_x, self.chip_y) + self.core, self.plane))
            for step in (1, 2, 3)
        ]

    def chip_start(self):
        for copy in self.chip_copies():
            copy.start()

    def chip_finish(self):
        for copy in self.chip_copies():
            copy.wait()
        for j in range(self.own.shape[0]):
            value = self.own[j, pl.ds(self.chip, 1)][0].astype(jnp.float32)
            for slot in range(3):
                value = value + self.from_chip[slot, j].astype(jnp.float32)
            self.total[j] = value.astype(self.total.dtype)

    def plane_copies(self):
        return [
            self.remote(self.total.at[(self.plane + step) % 4], self.from_plane.at[step - 1], 3 + step,
                        (self.rank, (self.plane + step) % 4))
            for step in (1, 2, 3)
        ]

    def plane_start(self):
        for copy in self.plane_copies():
            copy.start()

    def plane_finish(self):
        for copy in self.plane_copies():
            copy.wait()
        value = self.total[pl.ds(self.plane, 1)][0].astype(jnp.float32)
        for slot in range(3):
            value = value + self.from_plane[slot].astype(jnp.float32)
        return value


def sum_scratch(rows, lanes, dtype=jnp.bfloat16):
    return [
        pltpu.VMEM((4, 4, rows, lanes), dtype),
        pltpu.VMEM((4, 4, rows, lanes), dtype),
        pltpu.VMEM((3, 4, rows, lanes), dtype),
        pltpu.VMEM((3, rows, lanes), dtype),
        pltpu.VMEM((4, rows, lanes), dtype),
        pltpu.SemaphoreType.DMA((7,)),
        pltpu.SemaphoreType.DMA((7,)),
        pltpu.SemaphoreType.DMA,
    ]


SUM_SCRATCH = 8


def stages_of(parts, scratch, lanes):
    own, from_core, from_chip, from_plane, total, send, recv, local = scratch
    return SumStages(parts, own, from_core, from_chip, from_plane, total, (send, recv, local), lanes)


def table_sum(table_ref, table_out, from_core, from_chip, from_plane, held, send, recv):
    rank, plane, core, chip_x, chip_y = place()
    chip = chip_at(0, chip_x, chip_y)

    def remote(source, target, slot, device):
        return pltpu.make_async_remote_copy(
            src_ref=source, dst_ref=target, send_sem=send.at[slot], recv_sem=recv.at[slot],
            device_id=device, device_id_type=MESH)

    give = remote(table_ref.at[:, 1 - core], from_core, 0, (2 * chip + 1 - core, plane))
    give.start()
    yield
    give.wait()
    held[...] = table_ref[:, pl.ds(core, 1)][:, 0] + from_core[...]
    across = [remote(held.at[chip_at(step, chip_x, chip_y)], from_chip.at[step - 1], step,
                     (2 * chip_at(step, chip_x, chip_y) + core, plane)) for step in (1, 2, 3)]
    for copy in across:
        copy.start()
    yield
    for copy in across:
        copy.wait()
    own = held[pl.ds(chip, 1)][0] + from_chip[0] + from_chip[1] + from_chip[2]
    table_out[...] = own
    along = [remote(table_out, from_plane.at[step - 1], 3 + step, (rank, (plane + step) % 4)) for step in (1, 2, 3)]
    for copy in along:
        copy.start()
    yield
    for copy in along:
        copy.wait()
    table_out[...] = own + from_plane[0] + from_plane[1] + from_plane[2]
    yield


def sum_kernel(parts_ref, table_ref, own_ref, table_out, *scratch):
    stages = stages_of(parts_ref, scratch[:SUM_SCRATCH], pl.ds(0, parts_ref.shape[-1]))
    small = table_sum(table_ref, table_out, *scratch[SUM_SCRATCH:])
    greet(all_partners())
    stages.core_start()
    next(small)
    stages.core_finish()
    stages.chip_start()
    next(small)
    stages.chip_finish()
    stages.plane_start()
    next(small)
    own_ref[...] = stages.plane_finish()
    next(small)


def sum_parts(parts, table):
    rows, lanes = parts.shape[-2:]
    vmem = pl.BlockSpec(memory_space=pltpu.VMEM)
    tile = table.shape[-2:]
    return pl.pallas_call(
        sum_kernel,
        in_specs=[pl.BlockSpec(memory_space=pl.ANY), vmem],
        out_specs=[vmem, vmem],
        out_shape=[jax.ShapeDtypeStruct((rows, lanes), jnp.float32), jax.ShapeDtypeStruct(tile, jnp.float32)],
        scratch_shapes=sum_scratch(rows, lanes)
        + [pltpu.VMEM((4, *tile), jnp.float32), pltpu.VMEM((3, *tile), jnp.float32), pltpu.VMEM((3, *tile), jnp.float32),
           pltpu.VMEM((4, *tile), jnp.float32), pltpu.SemaphoreType.DMA((7,)), pltpu.SemaphoreType.DMA((7,))],
        compiler_params=pltpu.CompilerParams(collective_id=1, has_side_effects=True, vmem_limit_bytes=40 << 20),
        name="sum_parts",
    )(parts, table)


def row_layout(lengths, counts, row_len):
    lens = lengths[0]
    slots = lens.shape[0]
    order = lax.broadcasted_iota(jnp.int32, (slots, slots), 0)
    upto = lax.broadcasted_iota(jnp.int32, (slots, slots), 1)
    starting = jnp.sum(jnp.where(upto < order, lens[None, :], 0), axis=1)
    slot = lax.broadcasted_iota(jnp.int32, (slots,), 0)
    which = jnp.min(jnp.where(lens == LONGEST, slot, slots))
    offset = jnp.sum(jnp.where(slot == which, starting, 0))
    places = lax.broadcasted_iota(jnp.int32, (row_len,), 0) + offset
    places = jnp.where(places >= row_len, places - row_len, places)
    endings = starting + lens
    segment = jnp.sum((places[:, None] >= endings[None, :]).astype(jnp.int32), axis=1)
    member = segment[:, None] == slot[None, :]
    first_place = jnp.sum(jnp.where(member, starting[None, :], 0), axis=1)
    position = (places - first_place).astype(jnp.float32)
    inverse_count = 1.0 / counts[0].astype(jnp.float32)
    share = jnp.sum(jnp.where(member, inverse_count[None, :], 0.0), axis=1)
    return offset, segment, position, share


def rotary_tables(position):
    lane = lax.broadcasted_iota(jnp.int32, (1, LANES), 1)
    indices = (lane % (HEAD_DIM // 2)).astype(jnp.float32)
    inverse = jnp.exp(indices * (-2.0 * math.log(10000.0) / HEAD_DIM))
    angles = position[:, None] * inverse
    sign = jnp.where((lane % HEAD_DIM) < (HEAD_DIM // 2), -1.0, 1.0)
    return jnp.cos(angles), jnp.sin(angles) * sign


def turn_rows(values, shift):
    twice = jnp.concatenate([values, values], axis=0)
    return lax.dynamic_slice_in_dim(twice, shift, values.shape[0], 0)


def high(left, right):
    return jnp.dot(left, right, precision=lax.Precision.HIGH, preferred_element_type=jnp.float32)


def shards(
    tokens, cotangent, lengths, counts,
    w_qkv, w_out, w_up, w_down,
    mom_qkv, mom_out, mom_up, mom_down,
    vectors, vec_first, vec_second,
):
    both = ("fsdp", "dp")
    planes = lax.axis_size("fsdp")
    ranks = lax.axis_size("dp")
    row_len, width = tokens.shape
    columns = w_qkv.shape[1]
    old_weights = (w_qkv, w_out, w_up, w_down)
    old_moments = (mom_qkv, mom_out, mom_up, mom_down)
    counts_rows = [w.shape[0] for w in old_weights]
    n_vec = vectors.shape[0]

    slab_a = jnp.concatenate([w_qkv.T, w_out.T, vectors.T], axis=1).astype(jnp.bfloat16)
    slab_b = jnp.concatenate([w_up.T, w_down.T], axis=1).astype(jnp.bfloat16)
    full_a = lax.all_gather(slab_a, both, axis=0, tiled=True).reshape(planes, width, -1)
    full_b = lax.all_gather(slab_b, both, axis=0, tiled=True).reshape(planes, width, -1)
    r0, r1, r2, r3 = counts_rows
    wt_qkv = jnp.concatenate([full_a[j, :, :r0] for j in range(planes)], axis=1)
    wt_out = jnp.concatenate([full_a[j, :, r0 : r0 + r1] for j in range(planes)], axis=1)
    table = full_a[0, :, r0 + r1 :].T.astype(jnp.float32)
    wt_up = jnp.concatenate([full_b[j, :, :r2] for j in range(planes)], axis=1)
    wt_down = jnp.concatenate([full_b[j, :, r2:] for j in range(planes)], axis=1)

    offset, segment, position, share = row_layout(lengths, counts, row_len)
    cosine, sine = rotary_tables(position)
    seg_col, seg_row = segment[:, None], segment[None, :]
    inputs = turn_rows(tokens, offset).astype(jnp.float32)
    incoming = turn_rows(cotangent, offset).astype(jnp.float32) * share[:, None]

    normed_one, pull_one = jax.vjp(layer_norm, inputs, table[0], table[1])
    normed_one = normed_one.astype(jnp.bfloat16)
    project = nn(normed_one, wt_qkv) + table[4:7].reshape(-1)
    qr, kr, vr, attn, lse = attention_forward(project, cosine, sine, seg_col, seg_row)
    after = inputs + (nn(attn, wt_out) + table[7])
    normed_two, pull_two = jax.vjp(layer_norm, after, table[2], table[3])
    normed_two = normed_two.astype(jnp.bfloat16)
    hidden_pre = nn(normed_two, wt_up) + table[9:].reshape(-1)
    hidden, pull_hidden = jax.vjp(gelu_exact, hidden_pre)
    hidden = hidden.astype(jnp.bfloat16)
    layer_out = (after + (nt(hidden, wt_down) + table[8])).astype(jnp.bfloat16)

    grad_low = incoming.astype(jnp.bfloat16)
    grad_t_down = tn(grad_low, hidden)
    pre_grad = pull_hidden(nn(grad_low, wt_down))[0].astype(jnp.bfloat16)
    grad_t_up = tn(normed_two, pre_grad)
    resid_grad, gain_two, shift_two = pull_two(nt(pre_grad, wt_up))
    after_grad = incoming + resid_grad
    branch_low = after_grad.astype(jnp.bfloat16)
    grad_t_out = tn(attn, branch_low)
    attn_grad = nt(branch_low, wt_out).astype(jnp.bfloat16)
    near = (ranks, planes) == (8, 4)

    def cut(values, j, rows):
        return values[:, j * rows : (j + 1) * rows]

    parts_b = jnp.stack([jnp.concatenate([cut(grad_t_up, j, r2), cut(grad_t_down, j, r3)], axis=1) for j in range(planes)])
    if near:
        parts_b = parts_b.astype(jnp.bfloat16).reshape(planes, 4, 2, columns, -1)
        dq, dk, dv, own_b = attention_backward(
            qr, kr, vr, attn_grad, attn, lse, cosine, sine, seg_col, seg_row, parts_b)
    else:
        dq, dk, dv = attention_backward(qr, kr, vr, attn_grad, attn, lse, cosine, sine, seg_col, seg_row)
        own_b = lax.psum_scatter(parts_b.reshape(planes * width, -1), both, scatter_dimension=0, tiled=True)
    proj_grad = jnp.concatenate([dq, dk, dv], axis=1)
    grad_t_qkv = tn(normed_one, proj_grad)
    in_grad, gain_one, shift_one = pull_one(nt(proj_grad, wt_qkv))
    input_grad = after_grad + in_grad

    def column_sum(values):
        return jnp.sum(values.astype(jnp.float32), axis=0)

    vector_grad = jnp.concatenate(
        [gain_one[None], shift_one[None], gain_two[None], shift_two[None],
         column_sum(proj_grad).reshape(3, width), column_sum(branch_low)[None], column_sum(grad_low)[None],
         column_sum(pre_grad).reshape(-1, width)],
        axis=0,
    )
    back = jnp.where(offset > 0, row_len - offset, 0)
    layer_out = turn_rows(layer_out, back)
    input_grad = turn_rows(input_grad, back)

    if near:
        parts_a = jnp.stack([jnp.concatenate([cut(grad_t_qkv, j, r0), cut(grad_t_out, j, r1)], axis=1) for j in range(planes)])
        tiles = jnp.pad(vector_grad.reshape(n_vec, ranks, columns).transpose(1, 0, 2),
                        ((0, 0), (0, 16 - n_vec), (0, LANES - columns))).reshape(4, 2, 16, LANES)
        own_a, tile = sum_parts(parts_a.astype(jnp.bfloat16).reshape(planes, 4, 2, columns, -1), tiles)
        vector_grad = tile[:n_vec, :columns]
    else:
        parts_a = jnp.stack([jnp.concatenate([cut(grad_t_qkv, j, r0), cut(grad_t_out, j, r1), vector_grad.T], axis=1)
                             for j in range(planes)])
        own_a = lax.psum_scatter(parts_a.reshape(planes * width, -1), both, scatter_dimension=0, tiled=True)
        vector_grad = own_a[:, r0 + r1 :].T
    grads_t = (own_a[:, :r0], own_a[:, r0 : r0 + r1], own_b[:, :r2], own_b[:, r2:])
    new_moments_t = [moment_keep * old.T + grad for old, grad in zip(old_moments, grads_t)]

    most = max(counts_rows)
    padded = [jnp.pad(m.astype(jnp.bfloat16), ((0, 0), (0, most - m.shape[1]))) for m in new_moments_t]
    sent = jnp.stack([padded[t % 4] for t in range(planes)])
    mine = lax.all_to_all(sent, "fsdp", 0, 0, tiled=True)
    mine = mine.transpose(1, 0, 2).reshape(columns, planes * most)
    whole = lax.all_gather(mine, "dp", axis=0, tiled=True)
    gram = nt(whole, whole)
    identity = jnp.eye(width, dtype=jnp.float32)
    norm_sq = jnp.trace(gram) + 1e-07
    gram = gram / norm_sq
    factor = None
    for iteration in range(NS_ITERS):
        poly = poly_linear * identity + poly_square * gram + poly_cubic * high(gram, gram)
        factor = poly if factor is None else high(factor, poly)
        if iteration + 1 < NS_ITERS:
            gram = high(high(gram, poly), poly)
    own_rows = lax.dynamic_slice_in_dim(factor, lax.axis_index("dp") * columns, columns, 0) * lax.rsqrt(norm_sq)
    own_orth = high(own_rows, whole.astype(jnp.float32))
    own_orth = own_orth.astype(jnp.bfloat16).reshape(columns, planes, most).transpose(1, 0, 2)
    pieces = lax.all_to_all(own_orth, "fsdp", 0, 0, tiled=True).astype(jnp.float32)

    new_weights = []
    for x, weight_old in enumerate(old_weights):
        rows = weight_old.shape[0]
        scale = muon_rate * math.sqrt(max(1.0, rows * planes / width))
        new_weights.append(weight_old * (1.0 - muon_rate * muon_decay) - scale * pieces[x, :, :rows].T)
    new_first = beta_first * vec_first + (1.0 - beta_first) * vector_grad
    new_second = beta_second * vec_second + (1.0 - beta_second) * vector_grad * vector_grad
    first_fix = 1.0 - beta_first**STEP
    second_fix = 1.0 - beta_second**STEP
    new_vectors = vectors - adam_rate * (new_first / first_fix) / (jnp.sqrt(new_second / second_fix) + adam_eps)
    return (layer_out, input_grad, *[m.T for m in new_moments_t], *new_weights, new_vectors, new_first, new_second)


def solution(mesh):
    rows, cells, table = P(("dp", "fsdp"), None), P("fsdp", "dp"), P(None, "dp")
    return jax.shard_map(
        shards,
        mesh=mesh,
        in_specs=(rows,) * 4 + (cells,) * 8 + (table,) * 3,
        out_specs=(rows,) * 2 + (cells,) * 8 + (table,) * 3,
        check_vma=False,
    )
```

```python
import functools
import math

import jax
import jax.numpy as jnp
from jax import lax
from jax.experimental import pallas as pl
from jax.experimental.pallas import tpu as pltpu
from jax.sharding import PartitionSpec as P

HEAD_DIM = 32
NS_ITERS = 5
STEP = 10
LANES = 128
LONGEST = 768

norm_eps = 1e-05
masked_score = -1e30
poly_linear = 3.4445
poly_square = -4.775
poly_cubic = 2.0315
muon_rate = 0.5
muon_decay = 0.01
moment_keep = 0.5
adam_rate = 0.05
beta_first = 0.9
beta_second = 0.999
adam_eps = 1e-08


def layer_norm(values, gain_row, shift_row):
    center = values - jnp.mean(values, axis=-1, keepdims=True)
    spread = jnp.mean(center * center, axis=-1, keepdims=True)
    return center * lax.rsqrt(spread + norm_eps) * gain_row + shift_row


def gelu_exact(values):
    return 0.5 * values * (1.0 + lax.erf(values * (1.0 / math.sqrt(2.0))))


def nn(left, right):
    return jnp.dot(left, right, preferred_element_type=jnp.float32)


def nt(left, right):
    return lax.dot_general(left, right, (((1,), (1,)), ((), ())), preferred_element_type=jnp.float32)


def tn(left, right):
    return lax.dot_general(left, right, (((0,), (0,)), ((), ())), preferred_element_type=jnp.float32)


def _half_mask(shape):
    lane = lax.broadcasted_iota(jnp.int32, shape, 1)
    return (lane % HEAD_DIM) < (HEAD_DIM // 2)


def _turn(values, first):
    half = HEAD_DIM // 2
    left = pltpu.roll(values, LANES - half, 1)
    right = pltpu.roll(values, half, 1)
    return jnp.where(first, left, right)


def attention_forward_kernel(
    q_ref, k_ref, v_ref, cos_ref, sin_ref, segc_ref, segr_ref,
    qr_ref, kr_ref, vr_ref, attn_ref, lse_ref,
    qt_s, vt_s, ot_s,
):
    first = _half_mask(cos_ref.shape)
    cosine, sine = cos_ref[...], sin_ref[...]
    queries = q_ref[...] * (1.0 / math.sqrt(HEAD_DIM))
    qr = (queries * cosine + _turn(queries, first) * sine).astype(jnp.bfloat16)
    keys = k_ref[...]
    kr = (keys * cosine + _turn(keys, first) * sine).astype(jnp.bfloat16)
    vr = v_ref[...].astype(jnp.bfloat16)
    qr_ref[...] = qr
    kr_ref[...] = kr
    vr_ref[...] = vr
    qt_s[...] = qr.T
    vt_s[...] = vr.T
    tokens = qr.shape[0]
    rest = tokens - LONGEST
    row = lax.broadcasted_iota(jnp.int32, (LANES, tokens), 0)
    same = segc_ref[LONGEST:, :] == segr_ref[:, LONGEST:]

    def head(h, carry):
        qth = jnp.where(row // HEAD_DIM == h, qt_s[...], jnp.zeros((), jnp.bfloat16))
        rows = pl.ds(pl.multiple_of(h * HEAD_DIM, HEAD_DIM), HEAD_DIM)

        def block(start, width, key_start, key_count, mask):
            scores = nn(kr_ref[key_start : key_start + key_count, :], qth[:, start : start + width])
            if mask is not None:
                scores = jnp.where(mask, scores, masked_score)
            peak = jnp.max(scores, axis=0, keepdims=True)
            raised = jnp.exp(scores - peak)
            total = jnp.sum(raised, axis=0, keepdims=True)
            out = nn(vt_s[rows, key_start : key_start + key_count], raised.astype(jnp.bfloat16))
            ot_s[rows, start : start + width] = out / total
            lse_ref[0, pl.ds(h, 1), start : start + width] = peak + jnp.log(total)

        for start in range(0, LONGEST, 256):
            block(start, 256, 0, LONGEST, None)
        block(LONGEST, rest, LONGEST, rest, same)
        return carry

    lax.fori_loop(0, LANES // HEAD_DIM, head, 0)
    attn_ref[...] = ot_s[...].T.astype(jnp.bfloat16)


def attention_forward(project, cosine, sine, seg_col, seg_row):
    tokens = project.shape[0]
    width = project.shape[1] // 3
    groups = width // LANES
    col = lambda shift: pl.BlockSpec((tokens, LANES), lambda g, shift=shift: (0, g + shift))
    whole = lambda shape: pl.BlockSpec(shape, lambda g: (0,) * len(shape))
    flops = 4 * (LONGEST**2 + (tokens - LONGEST) ** 2) * 128 * groups * 4
    return pl.pallas_call(
        attention_forward_kernel,
        grid=(groups,),
        in_specs=[col(0), col(groups), col(2 * groups), whole((tokens, LANES)), whole((tokens, LANES)),
                  whole((tokens, 1)), whole((1, tokens))],
        out_specs=[col(0)] * 4 + [pl.BlockSpec((1, 4, tokens), lambda g: (g, 0, 0))],
        out_shape=[jax.ShapeDtypeStruct((tokens, width), jnp.bfloat16)] * 4
        + [jax.ShapeDtypeStruct((groups, 4, tokens), jnp.float32)],
        scratch_shapes=[
            pltpu.VMEM((LANES, tokens), jnp.bfloat16),
            pltpu.VMEM((LANES, tokens), jnp.bfloat16),
            pltpu.VMEM((LANES, tokens), jnp.float32),
        ],
        compiler_params=pltpu.CompilerParams(vmem_limit_bytes=48 << 20),
        cost_estimate=pl.CostEstimate(flops=flops, bytes_accessed=20 << 20, transcendentals=20 << 20),
        name="attention_forward",
    )(project, project, project, cosine, sine, seg_col, seg_row)


def attention_backward_kernel(
    qr_ref, kr_ref, vr_ref, do_ref, attn_ref, lse_ref, cos_ref, sin_ref, segc_ref, segr_ref,
    *rest_refs,
):
    dq_ref, dk_ref, dv_ref = rest_refs[:3]
    qt_s, dot_s, kt_s, delta_s, dqt_s, dk_s, dv_s = rest_refs[3:]
    tokens = qr_ref.shape[0]
    rest = tokens - LONGEST
    qt_s[...] = qr_ref[...].T
    dot_s[...] = do_ref[...].T
    kt_s[...] = kr_ref[...].T
    prod_t = (do_ref[...].astype(jnp.float32) * attn_ref[...].astype(jnp.float32)).T
    for h in range(4):
        delta_s[h : h + 1, :] = jnp.sum(prod_t[h * HEAD_DIM : (h + 1) * HEAD_DIM, :], axis=0, keepdims=True)
    dk_s[...] = jnp.zeros_like(dk_s)
    dv_s[...] = jnp.zeros_like(dv_s)
    row = lax.broadcasted_iota(jnp.int32, (LANES, tokens), 0)
    lane = lax.broadcasted_iota(jnp.int32, (tokens, LANES), 1)
    same = segc_ref[LONGEST:, :] == segr_ref[:, LONGEST:]
    zero = jnp.zeros((), jnp.bfloat16)

    def head(h, carry):
        mine_t = row // HEAD_DIM == h
        mine = lane // HEAD_DIM == h
        qth = jnp.where(mine_t, qt_s[...], zero)
        doth = jnp.where(mine_t, dot_s[...], zero)
        qh = jnp.where(mine, qr_ref[...], zero)
        doh = jnp.where(mine, do_ref[...], zero)
        rows = pl.ds(pl.multiple_of(h * HEAD_DIM, HEAD_DIM), HEAD_DIM)

        def block(start, width, key_start, key_count, mask):
            at = slice(start, start + width)
            keys = slice(key_start, key_start + key_count)
            scores = nn(kr_ref[keys, :], qth[:, at])
            if mask is not None:
                scores = jnp.where(mask, scores, masked_score)
            soft = jnp.exp(scores - lse_ref[0, pl.ds(h, 1), at])
            weight_grad = nn(vr_ref[keys, :], doth[:, at])
            score_grad = (soft * (weight_grad - delta_s[pl.ds(h, 1), at])).astype(jnp.bfloat16)
            dv_s[keys, :] += nn(soft.astype(jnp.bfloat16), doh[at, :])
            dk_s[keys, :] += nn(score_grad, qh[at, :])
            dqt_s[rows, at] = nn(kt_s[rows, keys], score_grad)

        for start in range(0, LONGEST, 256):
            block(start, 256, 0, LONGEST, None)
        block(LONGEST, rest, LONGEST, rest, same)
        return carry

    lax.fori_loop(0, LANES // HEAD_DIM, head, 0)
    first = _half_mask(cos_ref.shape)
    cosine, sine = cos_ref[...], sin_ref[...]

    def pull(values):
        return values * cosine + _turn(values * sine, first)

    dq_ref[...] = (pull(dqt_s[...].T) * (1.0 / math.sqrt(HEAD_DIM))).astype(jnp.bfloat16)
    dk_ref[...] = pull(dk_s[...]).astype(jnp.bfloat16)
    dv_ref[...] = dv_s[...].astype(jnp.bfloat16)


def attention_backward(qr, kr, vr, attn_grad, attn, lse, cosine, sine, seg_col, seg_row):
    tokens, width = qr.shape
    groups = width // LANES
    col = pl.BlockSpec((tokens, LANES), lambda g: (0, g))
    whole = lambda shape: pl.BlockSpec(shape, lambda g: (0,) * len(shape))
    flops = 10 * (LONGEST**2 + (tokens - LONGEST) ** 2) * 128 * groups * 4
    return pl.pallas_call(
        attention_backward_kernel,
        grid=(groups,),
        in_specs=[col] * 5 + [pl.BlockSpec((1, 4, tokens), lambda g: (g, 0, 0)),
                              whole((tokens, LANES)), whole((tokens, LANES)), whole((tokens, 1)), whole((1, tokens))],
        out_specs=[col] * 3,
        out_shape=[jax.ShapeDtypeStruct((tokens, width), jnp.bfloat16)] * 3,
        scratch_shapes=[
            pltpu.VMEM((LANES, tokens), jnp.bfloat16),
            pltpu.VMEM((LANES, tokens), jnp.bfloat16),
            pltpu.VMEM((LANES, tokens), jnp.bfloat16),
            pltpu.VMEM((8, tokens), jnp.float32),
            pltpu.VMEM((LANES, tokens), jnp.float32),
            pltpu.VMEM((tokens, LANES), jnp.float32),
            pltpu.VMEM((tokens, LANES), jnp.float32),
        ],
        compiler_params=pltpu.CompilerParams(vmem_limit_bytes=56 << 20),
        cost_estimate=pl.CostEstimate(flops=flops, bytes_accessed=20 << 20, transcendentals=20 << 20),
        name="attention_backward",
    )(qr, kr, vr, attn_grad, attn, lse, cosine, sine, seg_col, seg_row)


MESH = pl.DeviceIdType.MESH


def place():
    rank, plane = lax.axis_index("dp"), lax.axis_index("fsdp")
    core = rank % 2
    chip_x = (rank // 2) % 2
    chip_y = rank // 4
    return rank, plane, core, chip_x, chip_y


def chip_at(step, chip_x, chip_y):
    other_x = 1 - chip_x if step & 1 else chip_x
    other_y = 1 - chip_y if step & 2 else chip_y
    return 2 * other_y + other_x


def greet(partners):
    barrier = pltpu.get_barrier_semaphore()
    for partner in partners:
        pl.semaphore_signal(barrier, inc=1, device_id=partner, device_id_type=MESH)
    pl.semaphore_wait(barrier, len(partners))


def all_partners():
    rank, plane, core, chip_x, chip_y = place()
    sibling = 2 * chip_at(0, chip_x, chip_y) + 1 - core
    partners = [(sibling, plane)]
    partners += [(2 * chip_at(step, chip_x, chip_y) + core, plane) for step in (1, 2, 3)]
    partners += [(rank, (plane + step) % 4) for step in (1, 2, 3)]
    return partners


class SumStages:
    def __init__(self, parts, own, from_core, from_chip, from_plane, total, sems, lanes):
        self.parts, self.own, self.from_core, self.from_chip = parts, own, from_core, from_chip
        self.from_plane, self.total, self.lanes = from_plane, total, lanes
        self.send, self.recv, self.local = sems
        self.rank, self.plane, self.core, self.chip_x, self.chip_y = place()
        self.chip = chip_at(0, self.chip_x, self.chip_y)

    def remote(self, source, target, slot, device):
        return pltpu.make_async_remote_copy(
            src_ref=source, dst_ref=target, send_sem=self.send.at[slot], recv_sem=self.recv.at[slot],
            device_id=device, device_id_type=MESH)

    def core_copies(self):
        load = pltpu.make_async_copy(self.parts.at[:, :, self.core, :, self.lanes], self.own, self.local)
        give = self.remote(self.parts.at[:, :, 1 - self.core, :, self.lanes], self.from_core, 0,
                           (2 * self.chip + 1 - self.core, self.plane))
        return load, give

    def core_start(self):
        load, give = self.core_copies()
        give.start()
        load.start()

    def core_finish(self):
        load, give = self.core_copies()
        load.wait()
        give.wait()
        for j in range(self.own.shape[0]):
            self.own[j] = (self.own[j].astype(jnp.float32) + self.from_core[j].astype(jnp.float32)).astype(self.own.dtype)

    def chip_copies(self):
        return [
            self.remote(self.own.at[:, chip_at(step, self.chip_x, self.chip_y)], self.from_chip.at[step - 1], step,
                        (2 * chip_at(step, self.chip_x, self.chip_y) + self.core, self.plane))
            for step in (1, 2, 3)
        ]

    def chip_start(self):
        for copy in self.chip_copies():
            copy.start()

    def chip_finish(self):
        for copy in self.chip_copies():
            copy.wait()
        for j in range(self.own.shape[0]):
            value = self.own[j, pl.ds(self.chip, 1)][0].astype(jnp.float32)
            for slot in range(3):
                value = value + self.from_chip[slot, j].astype(jnp.float32)
            self.total[j] = value.astype(self.total.dtype)

    def plane_copies(self):
        return [
            self.remote(self.total.at[(self.plane + step) % 4], self.from_plane.at[step - 1], 3 + step,
                        (self.rank, (self.plane + step) % 4))
            for step in (1, 2, 3)
        ]

    def plane_start(self):
        for copy in self.plane_copies():
            copy.start()

    def plane_finish(self):
        for copy in self.plane_copies():
            copy.wait()
        value = self.total[pl.ds(self.plane, 1)][0].astype(jnp.float32)
        for slot in range(3):
            value = value + self.from_plane[slot].astype(jnp.float32)
        return value


def sum_scratch(rows, lanes, dtype=jnp.bfloat16):
    return [
        pltpu.VMEM((4, 4, rows, lanes), dtype),
        pltpu.VMEM((4, 4, rows, lanes), dtype),
        pltpu.VMEM((3, 4, rows, lanes), dtype),
        pltpu.VMEM((3, rows, lanes), dtype),
        pltpu.VMEM((4, rows, lanes), dtype),
        pltpu.SemaphoreType.DMA((7,)),
        pltpu.SemaphoreType.DMA((7,)),
        pltpu.SemaphoreType.DMA,
    ]


SUM_SCRATCH = 8


def stages_of(parts, scratch, lanes):
    own, from_core, from_chip, from_plane, total, send, recv, local = scratch
    return SumStages(parts, own, from_core, from_chip, from_plane, total, (send, recv, local), lanes)


def table_sum(table_ref, table_out, from_core, from_chip, from_plane, held, send, recv):
    rank, plane, core, chip_x, chip_y = place()
    chip = chip_at(0, chip_x, chip_y)

    def remote(source, target, slot, device):
        return pltpu.make_async_remote_copy(
            src_ref=source, dst_ref=target, send_sem=send.at[slot], recv_sem=recv.at[slot],
            device_id=device, device_id_type=MESH)

    give = remote(table_ref.at[:, 1 - core], from_core, 0, (2 * chip + 1 - core, plane))
    give.start()
    yield
    give.wait()
    held[...] = table_ref[:, pl.ds(core, 1)][:, 0] + from_core[...]
    across = [remote(held.at[chip_at(step, chip_x, chip_y)], from_chip.at[step - 1], step,
                     (2 * chip_at(step, chip_x, chip_y) + core, plane)) for step in (1, 2, 3)]
    for copy in across:
        copy.start()
    yield
    for copy in across:
        copy.wait()
    own = held[pl.ds(chip, 1)][0] + from_chip[0] + from_chip[1] + from_chip[2]
    table_out[...] = own
    along = [remote(table_out, from_plane.at[step - 1], 3 + step, (rank, (plane + step) % 4)) for step in (1, 2, 3)]
    for copy in along:
        copy.start()
    yield
    for copy in along:
        copy.wait()
    table_out[...] = own + from_plane[0] + from_plane[1] + from_plane[2]
    yield


class Gather:
    def __init__(self, at, send, recv, base, start, size):
        rank, plane, core, chip_x, chip_y = place()
        half = size // 2
        every, low, high = pl.ds(start, size), pl.ds(start, half), pl.ds(start + half, half)
        chips = [chip_at(step, chip_x, chip_y) for step in range(4)]
        over = [2 * chip + core for chip in chips]

        def copy(chip, lanes, slot, device):
            block = at(chip, core, lanes)
            return pltpu.make_async_remote_copy(
                src_ref=block, dst_ref=block, send_sem=send.at[base + slot], recv_sem=recv.at[base + slot],
                device_id=(device, plane), device_id_type=MESH)

        self.to_x, self.to_y = copy(chips[0], every, 0, over[1]), copy(chips[0], every, 1, over[2])
        self.on_y, self.on_x = copy(chips[1], low, 2, over[2]), copy(chips[2], high, 3, over[1])
        self.beside = [copy(chip, every, 4 + step, 2 * chips[0] + 1 - core) for step, chip in enumerate(chips)]

    def first(self):
        self.to_x.start()
        self.to_y.start()
        self.beside[0].start()

    def second(self):
        self.to_x.wait_recv()
        self.on_y.start()
        self.beside[1].start()
        self.to_y.wait_recv()
        self.on_x.start()
        self.beside[2].start()

    def third(self):
        self.on_y.wait_recv()
        self.on_x.wait_recv()
        self.beside[3].start()

    def finish(self):
        for copy in (self.to_x, self.to_y, self.on_y, self.on_x):
            copy.wait_send()
        for copy in self.beside:
            copy.wait()


def split(values):
    top = values.astype(jnp.bfloat16)
    return top, (values - top.astype(jnp.float32)).astype(jnp.bfloat16)


def put_left(ref, values):
    width = values.shape[1]
    top, low = split(values)
    ref[:, :width] = top
    ref[:, width : 2 * width] = top
    ref[:, 2 * width :] = low


def put_right(ref, values):
    width = values.shape[0]
    top, low = split(values)
    ref[:width, :] = top
    ref[width : 2 * width, :] = low
    ref[2 * width :, :] = top


def tiles_of(width):
    first = width % 256
    edges = ([0] if first else []) + list(range(first, width + 1, 256))
    return list(zip(edges[:-1], edges[1:]))


def symmetric_product(out, left, right, tiles):
    for start, stop in tiles:
        block = nn(left[:stop, :], right[:, start:stop])
        out[:stop, start:stop] = block
        if start:
            out[start:stop, :start] = block[:start, :].T


def orthogonal_rows(whole, mine, gram, poly, temp, factor, left_gram, left_temp, right, write):
    width = gram.shape[0]
    tiles = tiles_of(width)
    flat = whole[...].reshape(width, whole.shape[-1])
    for start, stop in tiles:
        block = nt(flat[:stop, :], flat[start:stop, :])
        gram[:stop, start:stop] = block
        if start:
            gram[start:stop, :start] = block[:start, :].T
    diagonal = lax.broadcasted_iota(jnp.int32, (width, width), 0) == lax.broadcasted_iota(jnp.int32, (width, width), 1)
    norm_sq = jnp.sum(jnp.sum(jnp.where(diagonal, gram[...], 0.0), axis=1, keepdims=True), axis=0, keepdims=True) + 1e-07
    gram[...] = gram[...] / norm_sq

    def polynomial():
        put_left(left_gram, gram[...])
        put_right(right, gram[...])
        symmetric_product(temp, left_gram, right, tiles)
        poly[...] = jnp.where(diagonal, poly_linear, 0.0) + poly_square * gram[...] + poly_cubic * temp[...]
        put_right(right, poly[...])

    def next_gram():
        symmetric_product(temp, left_gram, right, tiles)
        put_left(left_temp, temp[...])
        symmetric_product(gram, left_temp, right, tiles)

    polynomial()
    factor[...] = poly[...]

    def iteration(step, carry):
        next_gram()
        polynomial()
        put_left(left_temp, factor[...])
        symmetric_product(factor, left_temp, right, tiles)
        return carry

    lax.fori_loop(0, NS_ITERS - 2, iteration, 0)
    next_gram()
    put_right(right, gram[...])
    rows = factor[mine, :]

    def thin(values):
        put_left(left_temp.at[: values.shape[0], :], values)
        return nn(left_temp[: values.shape[0], :], right[...])

    once = thin(rows)
    twice = thin(once)
    rows = (poly_linear * rows + poly_square * once + poly_cubic * twice) * lax.rsqrt(norm_sq)
    top, low = split(rows)
    lanes = whole.shape[-1] // 4
    for j in range(4):
        part = flat[:, j * lanes : (j + 1) * lanes]
        write(j, nn(top, part) + nn(low, part))


class PlaneStage:
    def __init__(self, total, from_plane, send, recv):
        rank, self.plane = place()[:2]
        self.total, self.from_plane = total, from_plane
        self.copies = [
            pltpu.make_async_remote_copy(
                src_ref=total.at[(self.plane + step) % 4], dst_ref=from_plane.at[step - 1],
                send_sem=send.at[step - 1], recv_sem=recv.at[step - 1],
                device_id=(rank, (self.plane + step) % 4), device_id_type=MESH)
            for step in (1, 2, 3)
        ]

    def start(self):
        for copy in self.copies:
            copy.start()

    def finish(self):
        for copy in self.copies:
            copy.wait()
        value = self.total[pl.ds(self.plane, 1)][0].astype(jnp.float32)
        for slot in range(3):
            value = value + self.from_plane[slot].astype(jnp.float32)
        return value


def tail_kernel(parts_ref, table_ref, total_b_ref, mom_qkv, mom_out, mom_up, mom_down,
                own_a_ref, own_b_ref, table_out, pieces, *refs):
    moments = (mom_qkv, mom_out, mom_up, mom_down)
    stages = stages_of(parts_ref, refs[:SUM_SCRATCH], pl.ds(0, parts_ref.shape[-1]))
    refs = refs[SUM_SCRATCH:]
    table_scratch, refs = refs[:6], refs[6:]
    blocks, whole, gram, poly, temp, factor, left_gram, left_temp, right, from_plane_b = refs[:10]
    plane_send, plane_recv, gather_send, gather_recv, back_send, back_recv, b_send, b_recv = refs[10:]
    adding = table_sum(table_ref, table_out, *table_scratch)
    rank, plane, core, chip_x, chip_y = place()
    chip = chip_at(0, chip_x, chip_y)
    columns = own_b_ref.shape[0]
    lanes = blocks.shape[-1]
    last_b = PlaneStage(total_b_ref, from_plane_b, b_send, b_recv)

    greet(all_partners())
    stages.core_start()
    last_b.start()
    next(adding)
    stages.core_finish()
    stages.chip_start()
    next(adding)

    def momentum(x, gradient):
        rows = gradient.shape[1]
        blocks[x, :, :rows] = (moment_keep * moments[x][...] + gradient).astype(jnp.bfloat16)
        if rows < lanes:
            blocks[x, :, rows:] = jnp.zeros((columns, lanes - rows), jnp.bfloat16)

    own_b_ref[...] = last_b.finish()
    at = 0
    for x in (2, 3):
        rows = moments[x].shape[1]
        momentum(x, own_b_ref[:, at : at + rows])
        at += rows
    stages.chip_finish()
    stages.plane_start()
    next(adding)
    own_a_ref[...] = stages.plane_finish()
    at = 0
    for x in (0, 1):
        rows = moments[x].shape[1]
        momentum(x, own_a_ref[:, at : at + rows])
        at += rows

    own_lanes = pl.ds(pl.multiple_of(plane * lanes, lanes), lanes)
    out = [
        pltpu.make_async_remote_copy(
            src_ref=blocks.at[(plane + step) % 4], dst_ref=whole.at[chip, core, :, own_lanes],
            send_sem=plane_send.at[step - 1], recv_sem=plane_recv.at[step - 1],
            device_id=(rank, (plane + step) % 4), device_id_type=MESH)
        for step in (1, 2, 3)
    ]
    for copy in out:
        copy.start()
    whole[pl.ds(chip, 1), pl.ds(core, 1), :, own_lanes] = blocks[pl.ds(plane, 1)][None]
    next(adding)
    for copy in out:
        copy.wait()
    gather = Gather(lambda m, c, lane: whole.at[m, c, :, lane], gather_send, gather_recv, 0, 0, whole.shape[-1])
    gather.first()
    gather.second()
    gather.third()
    gather.finish()

    def write(j, values):
        blocks[j] = values.astype(jnp.bfloat16)

    orthogonal_rows(whole, pl.ds(pl.multiple_of(rank * columns, 8), columns), gram, poly, temp, factor,
                    left_gram, left_temp, right, write)
    home = [
        pltpu.make_async_remote_copy(
            src_ref=blocks.at[(plane + step) % 4], dst_ref=pieces.at[plane],
            send_sem=back_send.at[step - 1], recv_sem=back_recv.at[step - 1],
            device_id=(rank, (plane + step) % 4), device_id_type=MESH)
        for step in (1, 2, 3)
    ]
    for copy in home:
        copy.start()
    pieces[pl.ds(plane, 1)] = blocks[pl.ds(plane, 1)]
    for copy in home:
        copy.wait()


def tail(parts, table, total_b, moments):
    rows, lanes = parts.shape[-2:]
    width = rows * 8
    vmem = pl.BlockSpec(memory_space=pltpu.VMEM)
    tile = table.shape[-2:]
    most = max(m.shape[1] for m in moments)
    shape = jax.ShapeDtypeStruct
    f32, bf16 = jnp.float32, jnp.bfloat16
    square = pltpu.VMEM((width, width), f32)
    sems = lambda n: pltpu.SemaphoreType.DMA((n,))
    lanes_b = total_b.shape[-1]
    return pl.pallas_call(
        tail_kernel,
        in_specs=[pl.BlockSpec(memory_space=pl.ANY)] + [vmem] * 6,
        out_specs=[vmem] * 4,
        out_shape=[shape((rows, lanes), f32), shape((rows, lanes_b), f32), shape(tile, f32), shape((4, rows, most), bf16)],
        scratch_shapes=sum_scratch(rows, lanes)
        + [pltpu.VMEM((4, *tile), f32), pltpu.VMEM((3, *tile), f32),
           pltpu.VMEM((3, *tile), f32), pltpu.VMEM((4, *tile), f32), sems(7), sems(7)]
        + [pltpu.VMEM((4, rows, most), bf16), pltpu.VMEM((4, 2, rows, 4 * most), bf16),
           square, square, square, square,
           pltpu.VMEM((width, 3 * width), bf16), pltpu.VMEM((width, 3 * width), bf16),
           pltpu.VMEM((3 * width, width), bf16), pltpu.VMEM((3, rows, lanes_b), bf16)]
        + [sems(3), sems(3), sems(8), sems(8), sems(3), sems(3), sems(3), sems(3)],
        compiler_params=pltpu.CompilerParams(collective_id=1, has_side_effects=True, vmem_limit_bytes=60 << 20),
        name="tail",
    )(parts, table, total_b, *moments)


def finish_kernel(own_a_ref, own_b_ref, tile_ref, pieces_ref, *refs):
    moments, weights, small = refs[0:4], refs[4:8], refs[8:11]
    new_moments, new_weights, new_small = refs[11:15], refs[15:19], refs[19:22]
    columns, width = own_b_ref.shape[0], own_b_ref.shape[0] * 8
    starts = {0: (own_a_ref, 0), 1: (own_a_ref, moments[0].shape[1]), 2: (own_b_ref, 0), 3: (own_b_ref, moments[2].shape[1])}
    for x in range(4):
        rows = moments[x].shape[1]
        source, at = starts[x]
        new_moments[x][...] = moment_keep * moments[x][...] + source[:, at : at + rows]
        scale = muon_rate * math.sqrt(max(1.0, rows * 4 / width))
        new_weights[x][...] = (weights[x][...] * (1.0 - muon_rate * muon_decay)
                               - scale * pieces_ref[x, :, :rows].astype(jnp.float32))
    first_fix = 1.0 - beta_first**STEP
    second_fix = 1.0 - beta_second**STEP
    n_vec = small[0].shape[0]
    vector_grad = tile_ref[:n_vec, :columns]
    vectors, vec_first, vec_second = (ref[...] for ref in small)
    new_first = beta_first * vec_first + (1.0 - beta_first) * vector_grad
    new_second = beta_second * vec_second + (1.0 - beta_second) * vector_grad * vector_grad
    new_small[0][...] = vectors - adam_rate * (new_first / first_fix) / (jnp.sqrt(new_second / second_fix) + adam_eps)
    new_small[1][...] = new_first
    new_small[2][...] = new_second


def finish(own_a, own_b, tile, pieces, moments, weights, small):
    vmem = pl.BlockSpec(memory_space=pltpu.VMEM)
    outs = pl.pallas_call(
        finish_kernel,
        in_specs=[vmem] * 15,
        out_specs=[vmem] * 11,
        out_shape=[jax.ShapeDtypeStruct(x.shape, jnp.float32) for x in (*moments, *weights, *small)],
        compiler_params=pltpu.CompilerParams(vmem_limit_bytes=32 << 20),
        name="finish",
    )(own_a, own_b, tile, pieces, *moments, *weights, *small)
    return outs[:4], outs[4:8], outs[8:]


ROW_LEN = 1024
GATHERED = 512
LATER = 1536
CHUNK_A = 256
CHUNK_B = 512


def row_marks(len_ref):
    ends = [len_ref[0, 0]]
    for slot in (1, 2):
        ends.append(ends[-1] + len_ref[0, slot])
    starts = [0, *ends]
    offset = starts[3]
    for slot in (2, 1, 0):
        offset = jnp.where(len_ref[0, slot] == LONGEST, starts[slot], offset)
    return ends, offset


def segment_of(index, ends, offset):
    where = index + offset
    where = jnp.where(where >= ROW_LEN, where - ROW_LEN, where)
    segment = sum((where >= end).astype(jnp.int32) for end in ends)
    return where, segment


def turned_rows(values, offset):
    return pltpu.roll(values.astype(jnp.float32), jnp.where(offset > 0, ROW_LEN - offset, 0), 0)


def same_rest(ends, offset):
    rest = ROW_LEN - LONGEST
    columns = lax.broadcasted_iota(jnp.int32, (rest, rest), 0) + LONGEST
    rows = lax.broadcasted_iota(jnp.int32, (rest, rest), 1) + LONGEST
    return segment_of(columns, ends, offset)[1] == segment_of(rows, ends, offset)[1]


def attention_jobs(tokens):
    blocks = [(start, 256, 0, LONGEST) for start in range(0, LONGEST, 256)] + [(LONGEST, tokens - LONGEST, LONGEST, tokens - LONGEST)]
    return [(h, *block) for h in range(LANES // HEAD_DIM) for block in blocks]


def attention_group(q, k_ref, v, same, ot_s, vt_s, lse_ref):
    tokens = q.shape[0]
    qt = q.T
    vt_s[...] = v.T
    row = lax.broadcasted_iota(jnp.int32, qt.shape, 0)
    jobs = attention_jobs(tokens)
    queries, scores, soft = {}, {}, {}

    def score(job):
        h, start, width, key_start, key_count = job
        if h not in queries:
            queries[h] = jnp.where(row // HEAD_DIM == h, qt, jnp.zeros((), jnp.bfloat16))
        out = nn(k_ref[key_start : key_start + key_count, :], queries[h][:, start : start + width])
        return jnp.where(same, out, masked_score) if start == LONGEST else out

    def soften(values):
        peak = jnp.max(values, axis=0, keepdims=True)
        raised = jnp.exp(values - peak)
        return raised.astype(jnp.bfloat16), peak, jnp.sum(raised, axis=0, keepdims=True)

    def collect(job, raised, peak, total):
        h, start, width, key_start, key_count = job
        rows = slice(h * HEAD_DIM, (h + 1) * HEAD_DIM)
        out = nn(vt_s[rows, key_start : key_start + key_count], raised)
        ot_s[rows, start : start + width] = out / total
        lse_ref[0, h : h + 1, start : start + width] = peak + jnp.log(total)

    count = len(jobs)
    for t in range(count + 2):
        if t < count:
            scores[t] = score(jobs[t])
        if 0 <= t - 1 < count:
            soft[t - 1] = soften(scores.pop(t - 1))
        if 0 <= t - 2:
            collect(jobs[t - 2], *soft.pop(t - 2))
    return ot_s[...].T.astype(jnp.bfloat16)


def head_kernel(
    len_ref, tokens_ref, slab_a_ref, slab_b_ref, vec_ref,
    qr_ref, kr_ref, vr_ref, attn_ref, lse_ref, h1_ref, x_ref, cos_ref, sin_ref, wt_ref, table_ref, full_b,
    full_a, full_v, twice_s, q_s, k_s, v_s, ot_s, vt_s,
    a_send, a_recv, az_send, az_recv, b_send, b_recv, bz_send, bz_recv, v_send, v_recv, local,
):
    group = pl.program_id(0)
    rank, plane, core, chip_x, chip_y = place()
    chip = chip_at(0, chip_x, chip_y)
    chunks_a, chunks_b = GATHERED // CHUNK_A, LATER // CHUNK_B
    gather_a = [Gather(lambda m, c, lane: full_a.at[:, m, c, :, lane], a_send, a_recv, 8 * n, CHUNK_A * n, CHUNK_A)
                for n in range(chunks_a)]
    gather_b = [Gather(lambda m, c, lane: full_b.at[:, m, c, :, lane], b_send, b_recv, 8 * n, CHUNK_B * n, CHUNK_B)
                for n in range(chunks_b)]

    def along(slab, full, send, recv, n, size):
        lanes = pl.ds(size * n, size)
        return [
            pltpu.make_async_remote_copy(
                src_ref=slab.at[:, lanes], dst_ref=full.at[plane, chip, core, :, lanes],
                send_sem=send.at[3 * n + step - 1], recv_sem=recv.at[3 * n + step - 1],
                device_id=(rank, (plane + step) % 4), device_id_type=MESH)
            for step in (1, 2, 3)
        ]

    along_a = [along(slab_a_ref, full_a, az_send, az_recv, n, CHUNK_A) for n in range(chunks_a)]
    along_b = [along(slab_b_ref, full_b, bz_send, bz_recv, n, CHUNK_B) for n in range(chunks_b)]
    own_b = pltpu.make_async_copy(slab_b_ref, full_b.at[plane, chip, core], local)
    ends, offset = row_marks(len_ref)

    @pl.when(group == 0)
    def _():
        greet(all_partners())
        for copy in along_a[0]:
            copy.start()
        own_b.start()
        full_v[pl.ds(chip, 1), pl.ds(core, 1)] = vec_ref[...][None, None]
        full_a[pl.ds(plane, 1), pl.ds(chip, 1), pl.ds(core, 1)] = slab_a_ref[...][None, None, None]

        def vec_copy(m, slot, device):
            block = full_v.at[m, core]
            return pltpu.make_async_remote_copy(
                src_ref=block, dst_ref=block, send_sem=v_send.at[slot], recv_sem=v_recv.at[slot],
                device_id=(device, plane), device_id_type=MESH)

        chips = [chip_at(step, chip_x, chip_y) for step in range(4)]
        vec_over = [vec_copy(chip, step - 1, 2 * chips[step] + core) for step in (1, 2, 3)]
        vec_beside = [vec_copy(m, 3 + step, 2 * chip + 1 - core) for step, m in enumerate(chips)]
        for copy in (*vec_over, vec_beside[0]):
            copy.start()
        twice_s[...] = turned_rows(tokens_ref[...], offset)
        for copy in along_a[0]:
            copy.wait()
        for copy in along_a[1]:
            copy.start()
        gather_a[0].first()
        index = lax.broadcasted_iota(jnp.int32, (ROW_LEN, LANES), 0)
        where, segment = segment_of(index, ends, offset)
        start = jnp.where(segment == 0, 0, jnp.where(segment == 1, ends[0], jnp.where(segment == 2, ends[1], ends[2])))
        position = (where - start).astype(jnp.float32)
        lane = lax.broadcasted_iota(jnp.int32, (1, LANES), 1)
        inverse = jnp.exp((lane % (HEAD_DIM // 2)).astype(jnp.float32) * (-2.0 * math.log(10000.0) / HEAD_DIM))
        sign = jnp.where((lane % HEAD_DIM) < (HEAD_DIM // 2), -1.0, 1.0)
        angles = position * inverse
        for copy in along_a[1]:
            copy.wait()
        gather_a[1].first()
        for copies in along_b:
            for copy in copies:
                copy.start()
        cos_ref[...] = jnp.cos(angles)
        for step in range(3):
            vec_over[step].wait()
            vec_beside[step + 1].start()
        gather_a[0].second()
        sin_ref[...] = jnp.sin(angles) * sign
        for copy in vec_beside:
            copy.wait()
        table_t = jnp.concatenate([full_v[m, c] for m in range(4) for c in range(2)], axis=0)
        table_ref[...] = table_t.T[: table_ref.shape[0], :]
        gather_a[1].second()
        gain, shift = table_ref[0:1, :], table_ref[1:2, :]
        for r in range(0, ROW_LEN, 256):
            values = twice_s[r : r + 256, :]
            x_ref[r : r + 256, :] = values.astype(jnp.bfloat16)
            h1_ref[r : r + 256, :] = layer_norm(values, gain, shift).astype(jnp.bfloat16)
        gather_a[0].third()
        gather_a[1].third()
        for gather in gather_a:
            gather.finish()
        own_b.wait()
        for copy in along_b[0]:
            copy.wait()
        gather_b[0].first()
        width = wt_ref.shape[0]
        rows = wt_ref.shape[1] // 4
        wt_ref[...] = jnp.concatenate(
            [full_a[j].reshape(width, GATHERED)[:, :rows] for j in range(4)], axis=1)
        first = _half_mask((256, LANES))
        bias = [table_ref[4 + part : 5 + part, :] for part in range(3)]
        for r in range(0, ROW_LEN, 256):
            at = slice(r, r + 256)
            project = nn(h1_ref[at, :], wt_ref[...])
            cosine, sine = cos_ref[at, :], sin_ref[at, :]
            for g in range(width // LANES):
                lanes = slice(g * LANES, (g + 1) * LANES)
                queries = (project[:, lanes] + bias[0][:, lanes]) * (1.0 / math.sqrt(HEAD_DIM))
                keys = project[:, width + g * LANES : width + (g + 1) * LANES] + bias[1][:, lanes]
                q_s[g, at, :] = (queries * cosine + _turn(queries, first) * sine).astype(jnp.bfloat16)
                k_s[g, at, :] = (keys * cosine + _turn(keys, first) * sine).astype(jnp.bfloat16)
                v_s[g, at, :] = (project[:, 2 * width + g * LANES : 2 * width + (g + 1) * LANES]
                                 + bias[2][:, lanes]).astype(jnp.bfloat16)
            if r == 256:
                for copy in along_b[1]:
                    copy.wait()
                gather_b[1].first()
        for copy in along_b[2]:
            copy.wait()
        gather_b[2].first()

    @pl.when(group == 1)
    def _():
        gather_b[0].second()

    @pl.when(group == 2)
    def _():
        gather_b[1].second()
        gather_b[0].third()

    @pl.when(group == 4)
    def _():
        gather_b[2].second()
        gather_b[1].third()

    qr_ref[...] = q_s[group]
    kr_ref[...] = k_s[group]
    vr_ref[...] = v_s[group]
    attn_ref[...] = attention_group(q_s[group], kr_ref, v_s[group], same_rest(ends, offset), ot_s, vt_s, lse_ref)

    @pl.when(group == 4)
    def _():
        gather_b[2].third()
        for gather in gather_b:
            gather.finish()


def head(lengths, tokens, slab_a, slab_b, vec):
    tokens_count, width = tokens.shape
    groups = width // LANES
    columns = slab_a.shape[0]
    col = pl.BlockSpec((tokens_count, LANES), lambda g: (0, g))
    whole = lambda *shape: pl.BlockSpec(shape, lambda g: (0,) * len(shape))
    shape = jax.ShapeDtypeStruct
    bf16, f32 = jnp.bfloat16, jnp.float32
    sems = lambda n: pltpu.SemaphoreType.DMA((n,))
    na, nb = GATHERED // CHUNK_A, LATER // CHUNK_B
    return pl.pallas_call(
        head_kernel,
        grid=(groups,),
        in_specs=[pl.BlockSpec(memory_space=pltpu.SMEM), whole(tokens_count, width), whole(columns, GATHERED),
                  whole(columns, LATER), whole(columns, LANES)],
        out_specs=[col] * 4 + [pl.BlockSpec((1, 4, tokens_count), lambda g: (g, 0, 0)),
                               whole(tokens_count, width), whole(tokens_count, width),
                               whole(tokens_count, LANES), whole(tokens_count, LANES),
                               whole(width, 3 * width), whole(16, width), pl.BlockSpec(memory_space=pl.ANY)],
        out_shape=[shape((tokens_count, width), bf16)] * 4 + [shape((groups, 4, tokens_count), f32)]
        + [shape((tokens_count, width), bf16)] * 2 + [shape((tokens_count, LANES), f32)] * 2
        + [shape((width, 3 * width), bf16), shape((16, width), f32), shape((4, 4, 2, columns, LATER), bf16)],
        scratch_shapes=[
            pltpu.VMEM((4, 4, 2, columns, GATHERED), bf16),
            pltpu.VMEM((4, 2, columns, LANES), f32),
            pltpu.VMEM((tokens_count, width), f32),
            pltpu.VMEM((groups, tokens_count, LANES), bf16),
            pltpu.VMEM((groups, tokens_count, LANES), bf16),
            pltpu.VMEM((groups, tokens_count, LANES), bf16),
            pltpu.VMEM((LANES, tokens_count), f32),
            pltpu.VMEM((LANES, tokens_count), bf16),
            sems(8 * na), sems(8 * na), sems(3 * na), sems(3 * na),
            sems(8 * nb), sems(8 * nb), sems(3 * nb), sems(3 * nb), sems(7), sems(7), pltpu.SemaphoreType.DMA,
        ],
        compiler_params=pltpu.CompilerParams(collective_id=2, has_side_effects=True, vmem_limit_bytes=58 << 20),
        name="head",
    )(lengths, tokens, slab_a, slab_b, vec)


def middle_kernel(
    len_ref, count_ref, x_ref, attn_ref, cot_ref, table_ref, out_lanes_ref, block_ref,
    layer_ref, after_grad_ref, attn_grad_ref, parts_ref, out_grad_ref, sums_ref,
    xhat_s, rstd_s, h2_s, h2t_s, dy_s, dyt_s, acc_s, back_s, act_s, pre_s, wt_out_s,
):
    j = pl.program_id(0)
    tokens, width = x_ref.shape
    ends, offset = row_marks(len_ref)
    chunk = 256
    cuts = [slice(r, r + chunk) for r in range(0, tokens, chunk)]

    @pl.when(j == 0)
    def _():
        rows = width // 4
        wt_out_s[...] = jnp.concatenate([out_lanes_ref[p, :, :rows] for p in range(4)], axis=1)
        index = lax.broadcasted_iota(jnp.int32, (tokens, 1), 0)
        _, segment = segment_of(index, ends, offset)
        number = jnp.where(segment == 0, count_ref[0, 0], jnp.where(
            segment == 1, count_ref[0, 1], jnp.where(segment == 2, count_ref[0, 2], count_ref[0, 3])))
        incoming = turned_rows(cot_ref[...], offset) * (1.0 / number.astype(jnp.float32))
        after_grad_ref[...] = incoming
        dy_s[...] = incoming.astype(jnp.bfloat16)
        dyt_s[...] = dy_s[...].T
        sums_ref[...] = jnp.zeros_like(sums_ref)
        sums_ref[8:9, :] = jnp.sum(dy_s[...].astype(jnp.float32), axis=0, keepdims=True)
        gain, shift = table_ref[2:3, :], table_ref[3:4, :]
        for at in cuts:
            after = x_ref[at, :].astype(jnp.float32) + (nn(attn_ref[at, :], wt_out_s[...]) + table_ref[7:8, :])
            acc_s[at, :] = after + table_ref[8:9, :]
            center = after - jnp.mean(after, axis=-1, keepdims=True)
            rstd = lax.rsqrt(jnp.mean(center * center, axis=-1, keepdims=True) + norm_eps)
            xhat = center * rstd
            xhat_s[at, :] = xhat
            rstd_s[at, :] = rstd
            h2_s[at, :] = (xhat * gain + shift).astype(jnp.bfloat16)
        h2t_s[...] = h2_s[...].T
        back_s[...] = jnp.zeros_like(back_s)

    up, down = block_ref.at[0, :, :width], block_ref.at[0, :, width:]
    bias = table_ref[pl.ds(9 + j, 1), :]

    def products(at):
        return nn(h2_s[at, :], up[...]), nn(dy_s[at, :], down[...])

    def pointwise(at, pre, act_grad):
        pre = pre + bias
        cdf = 0.5 * (1.0 + lax.erf(pre * (1.0 / math.sqrt(2.0))))
        slope = cdf + pre * (jnp.exp(-0.5 * pre * pre) * (1.0 / math.sqrt(2.0 * math.pi)))
        act_s[at, :] = (pre * cdf).astype(jnp.bfloat16)
        pre_s[at, :] = (act_grad * slope).astype(jnp.bfloat16)

    def collect(at):
        acc_s[at, :] += nt(act_s[at, :], down[...])
        back_s[at, :] += nt(pre_s[at, :], up[...])

    held = {}
    for t in range(len(cuts) + 1):
        if t < len(cuts):
            held[t] = products(cuts[t])
        if t >= 1:
            pointwise(cuts[t - 1], *held.pop(t - 1))
            collect(cuts[t - 1])
    parts_ref[0, :, :width] = nn(h2t_s[...], pre_s[...]).astype(jnp.bfloat16)
    parts_ref[0, :, width:] = nn(dyt_s[...], act_s[...]).astype(jnp.bfloat16)
    sums_ref[pl.ds(9 + j, 1), :] = jnp.sum(pre_s[...].astype(jnp.float32), axis=0, keepdims=True)

    @pl.when(j == 3)
    def _():
        layer_ref[...] = pltpu.roll(acc_s[...], offset, 0).astype(jnp.bfloat16)
        gain = table_ref[2:3, :]
        gain_sum = jnp.zeros((1, width), jnp.float32)
        shift_sum = jnp.zeros((1, width), jnp.float32)
        branch_sum = jnp.zeros((1, width), jnp.float32)
        for at in cuts:
            grad, xhat = back_s[at, :], xhat_s[at, :]
            gain_sum += jnp.sum(grad * xhat, axis=0, keepdims=True)
            shift_sum += jnp.sum(grad, axis=0, keepdims=True)
            scaled = grad * gain
            resid = rstd_s[at, :] * (
                scaled - jnp.mean(scaled, axis=-1, keepdims=True)
                - xhat * jnp.mean(scaled * xhat, axis=-1, keepdims=True))
            after_grad = after_grad_ref[at, :] + resid
            after_grad_ref[at, :] = after_grad
            low = after_grad.astype(jnp.bfloat16)
            dy_s[at, :] = low
            branch_sum += jnp.sum(low.astype(jnp.float32), axis=0, keepdims=True)
            attn_grad_ref[at, :] = nt(low, wt_out_s[...]).astype(jnp.bfloat16)
        sums_ref[2:3, :] = gain_sum
        sums_ref[3:4, :] = shift_sum
        sums_ref[7:8, :] = branch_sum
        h2t_s[...] = attn_ref[...].T
        out_grad_ref[...] = nn(h2t_s[...], dy_s[...]).astype(jnp.bfloat16)


def middle(lengths, counts, x, attn, cotangent, table, full_b):
    tokens, width = x.shape
    later = full_b.shape[-1]
    whole = lambda *shape: pl.BlockSpec(shape, lambda j: (0,) * len(shape))
    smem = pl.BlockSpec(memory_space=pltpu.SMEM)
    shape = jax.ShapeDtypeStruct
    bf16, f32 = jnp.bfloat16, jnp.float32
    flat = pltpu.VMEM((tokens, width), bf16)
    wide = pltpu.VMEM((tokens, width), f32)
    turned = pltpu.VMEM((width, tokens), bf16)
    return pl.pallas_call(
        middle_kernel,
        grid=(4,),
        in_specs=[smem, smem, whole(tokens, width), whole(tokens, width), whole(tokens, width), whole(16, width),
                  pl.BlockSpec((4, width, later - 2 * width), lambda j: (0, 0, 2 * width // (later - 2 * width))),
                  pl.BlockSpec((1, width, 2 * width), lambda j: (j, 0, 0))],
        out_specs=[whole(tokens, width), whole(tokens, width), whole(tokens, width),
                   pl.BlockSpec((1, width, 2 * width), lambda j: (j, 0, 0)), whole(width, width), whole(16, width)],
        out_shape=[shape((tokens, width), bf16), shape((tokens, width), f32), shape((tokens, width), bf16),
                   shape((4, width, 2 * width), bf16), shape((width, width), bf16), shape((16, width), f32)],
        scratch_shapes=[wide, pltpu.VMEM((tokens, 1), f32), flat, turned, flat, turned, wide, wide, flat, flat,
                        pltpu.VMEM((width, width), bf16)],
        compiler_params=pltpu.CompilerParams(vmem_limit_bytes=60 << 20),
        name="middle",
    )(lengths, counts, x, attn, cotangent, table, full_b, full_b)


def backward_group(qr_ref, kr_ref, vr_ref, do_ref, attn_ref, lse_ref, same, qt_s, dot_s, kt_s, delta_s, dqt_s, dk_s, dv_s):
    tokens = qr_ref.shape[0]
    qt_s[...] = qr_ref[...].T
    dot_s[...] = do_ref[...].T
    kt_s[...] = kr_ref[...].T
    prod_t = (do_ref[...].astype(jnp.float32) * attn_ref[...].astype(jnp.float32)).T
    for h in range(4):
        delta_s[h : h + 1, :] = jnp.sum(prod_t[h * HEAD_DIM : (h + 1) * HEAD_DIM, :], axis=0, keepdims=True)
    dk_s[...] = jnp.zeros_like(dk_s)
    dv_s[...] = jnp.zeros_like(dv_s)
    row = lax.broadcasted_iota(jnp.int32, (LANES, tokens), 0)
    lane = lax.broadcasted_iota(jnp.int32, (tokens, LANES), 1)
    zero = jnp.zeros((), jnp.bfloat16)
    jobs = attention_jobs(tokens)
    masked, held = {}, {}

    def products(job):
        h, start, width, key_start, key_count = job
        if h not in masked:
            masked[h] = (
                jnp.where(row // HEAD_DIM == h, qt_s[...], zero), jnp.where(row // HEAD_DIM == h, dot_s[...], zero),
                jnp.where(lane // HEAD_DIM == h, qr_ref[...], zero), jnp.where(lane // HEAD_DIM == h, do_ref[...], zero))
        at, keys = slice(start, start + width), slice(key_start, key_start + key_count)
        scores = nn(kr_ref[keys, :], masked[h][0][:, at])
        if start == LONGEST:
            scores = jnp.where(same, scores, masked_score)
        return scores, nn(vr_ref[keys, :], masked[h][1][:, at])

    def finish(job, scores, weight_grad):
        h, start, width, key_start, key_count = job
        at, keys = slice(start, start + width), slice(key_start, key_start + key_count)
        rows = slice(h * HEAD_DIM, (h + 1) * HEAD_DIM)
        soft = jnp.exp(scores - lse_ref[0, h : h + 1, at])
        score_grad = (soft * (weight_grad - delta_s[h : h + 1, at])).astype(jnp.bfloat16)
        dv_s[keys, :] += nn(soft.astype(jnp.bfloat16), masked[h][3][at, :])
        dk_s[keys, :] += nn(score_grad, masked[h][2][at, :])
        dqt_s[rows, at] = nn(kt_s[rows, keys], score_grad)

    for t in range(len(jobs) + 1):
        if t < len(jobs):
            held[t] = products(jobs[t])
        if t >= 1:
            finish(jobs[t - 1], *held.pop(t - 1))


def backward_kernel(
    len_ref, qr_ref, kr_ref, vr_ref, do_ref, attn_ref, lse_ref, cos_ref, sin_ref, parts_ref,
    dq_ref, dk_ref, dv_ref, total_ref, *scratch,
):
    group = pl.program_id(0)
    lanes = parts_ref.shape[-1] // 2
    halves = [stages_of(parts_ref, scratch[7 + SUM_SCRATCH * n : 7 + SUM_SCRATCH * (n + 1)], pl.ds(n * lanes, lanes))
              for n in range(2)]
    dqt_s, dk_s, dv_s = scratch[4:7]

    @pl.when(group == 0)
    def _():
        greet(all_partners())
        halves[0].core_start()
        halves[1].core_start()

    @pl.when(group == 1)
    def _():
        halves[0].core_finish()
        halves[0].chip_start()
        halves[1].core_finish()
        halves[1].chip_start()

    ends, offset = row_marks(len_ref)
    backward_group(qr_ref, kr_ref, vr_ref, do_ref, attn_ref, lse_ref, same_rest(ends, offset), *scratch[:7])
    first = _half_mask(cos_ref.shape)
    cosine, sine = cos_ref[...], sin_ref[...]

    def pull(values):
        return values * cosine + _turn(values * sine, first)

    dq_ref[...] = (pull(dqt_s[...].T) * (1.0 / math.sqrt(HEAD_DIM))).astype(jnp.bfloat16)
    dk_ref[...] = pull(dk_s[...]).astype(jnp.bfloat16)
    dv_ref[...] = dv_s[...].astype(jnp.bfloat16)

    @pl.when(group == 4)
    def _():
        for n in range(2):
            halves[n].chip_finish()
            total_ref[:, :, n * lanes : (n + 1) * lanes] = halves[n].total[...]


def backward(lengths, qr, kr, vr, attn_grad, attn, lse, cosine, sine, parts):
    tokens, width = qr.shape
    groups = width // LANES
    rows, lanes = parts.shape[-2:]
    col = pl.BlockSpec((tokens, LANES), lambda g: (0, g))
    whole = lambda *shape: pl.BlockSpec(shape, lambda g: (0,) * len(shape))
    shape = jax.ShapeDtypeStruct
    bf16, f32 = jnp.bfloat16, jnp.float32
    return pl.pallas_call(
        backward_kernel,
        grid=(groups,),
        in_specs=[pl.BlockSpec(memory_space=pltpu.SMEM)] + [col] * 5
        + [pl.BlockSpec((1, 4, tokens), lambda g: (g, 0, 0)), whole(tokens, LANES), whole(tokens, LANES),
           pl.BlockSpec(memory_space=pl.ANY)],
        out_specs=[col] * 3 + [whole(4, rows, lanes)],
        out_shape=[shape((tokens, width), bf16)] * 3 + [shape((4, rows, lanes), bf16)],
        scratch_shapes=[pltpu.VMEM((LANES, tokens), bf16)] * 3
        + [pltpu.VMEM((8, tokens), f32), pltpu.VMEM((LANES, tokens), f32), pltpu.VMEM((tokens, LANES), f32),
           pltpu.VMEM((tokens, LANES), f32)] + sum_scratch(rows, lanes // 2) * 2,
        compiler_params=pltpu.CompilerParams(collective_id=0, has_side_effects=True, vmem_limit_bytes=58 << 20),
        name="backward",
    )(lengths, qr, kr, vr, attn_grad, attn, lse, cosine, sine, parts)


def row_layout(lengths, counts, row_len):
    lens = lengths[0]
    slots = lens.shape[0]
    order = lax.broadcasted_iota(jnp.int32, (slots, slots), 0)
    upto = lax.broadcasted_iota(jnp.int32, (slots, slots), 1)
    starting = jnp.sum(jnp.where(upto < order, lens[None, :], 0), axis=1)
    slot = lax.broadcasted_iota(jnp.int32, (slots,), 0)
    which = jnp.min(jnp.where(lens == LONGEST, slot, slots))
    offset = jnp.sum(jnp.where(slot == which, starting, 0))
    places = lax.broadcasted_iota(jnp.int32, (row_len,), 0) + offset
    places = jnp.where(places >= row_len, places - row_len, places)
    endings = starting + lens
    segment = jnp.sum((places[:, None] >= endings[None, :]).astype(jnp.int32), axis=1)
    member = segment[:, None] == slot[None, :]
    first_place = jnp.sum(jnp.where(member, starting[None, :], 0), axis=1)
    position = (places - first_place).astype(jnp.float32)
    inverse_count = 1.0 / counts[0].astype(jnp.float32)
    share = jnp.sum(jnp.where(member, inverse_count[None, :], 0.0), axis=1)
    return offset, segment, position, share


def rotary_tables(position):
    lane = lax.broadcasted_iota(jnp.int32, (1, LANES), 1)
    indices = (lane % (HEAD_DIM // 2)).astype(jnp.float32)
    inverse = jnp.exp(indices * (-2.0 * math.log(10000.0) / HEAD_DIM))
    angles = position[:, None] * inverse
    sign = jnp.where((lane % HEAD_DIM) < (HEAD_DIM // 2), -1.0, 1.0)
    return jnp.cos(angles), jnp.sin(angles) * sign


def turn_rows(values, shift):
    twice = jnp.concatenate([values, values], axis=0)
    return lax.dynamic_slice_in_dim(twice, shift, values.shape[0], 0)


def high(left, right):
    return jnp.dot(left, right, precision=lax.Precision.HIGH, preferred_element_type=jnp.float32)


def shards_near(
    tokens, cotangent, lengths, counts,
    w_qkv, w_out, w_up, w_down,
    mom_qkv, mom_out, mom_up, mom_down,
    vectors, vec_first, vec_second,
):
    row_len, width = tokens.shape
    columns = w_qkv.shape[1]
    n_vec = vectors.shape[0]
    weights_t = [w.T for w in (w_qkv, w_out, w_up, w_down)]
    moments_t = [m.T for m in (mom_qkv, mom_out, mom_up, mom_down)]
    r0, r1, r2, r3 = [w.shape[1] for w in weights_t]
    pad = lambda x, n: jnp.pad(x, ((0, 0), (0, n - x.shape[1])))
    slab_a = pad(weights_t[0].astype(jnp.bfloat16), GATHERED)
    slab_b = pad(jnp.concatenate([weights_t[2], weights_t[3], weights_t[1]], axis=1).astype(jnp.bfloat16), LATER)
    vec = pad(vectors.T.astype(jnp.bfloat16).astype(jnp.float32), LANES)
    qr, kr, vr, attn, lse, normed_one, turned, cosine, sine, wt_qkv, table, full_b = head(
        lengths, tokens, slab_a, slab_b, vec)
    layer_out, after_grad, attn_grad, parts_b, out_grad, sums = middle(
        lengths, counts, turned, attn, cotangent, table, full_b.reshape(4, width, -1))
    dq, dk, dv, total_b = backward(
        lengths, qr, kr, vr, attn_grad, attn, lse, cosine, sine, parts_b.reshape(4, 4, 2, columns, -1))
    proj_grad = jnp.concatenate([dq, dk, dv], axis=1)
    grad_t_qkv = tn(normed_one, proj_grad).astype(jnp.bfloat16)
    inputs = turned.astype(jnp.float32)
    _, pull_one = jax.vjp(layer_norm, inputs, table[0], table[1])
    in_grad, gain_one, shift_one = pull_one(nt(proj_grad, wt_qkv))
    _, _, _, offset = row_layout(lengths, counts, row_len)[::-1]
    input_grad = turn_rows(after_grad + in_grad, jnp.where(offset > 0, row_len - offset, 0))
    qkv_sum = jnp.sum(proj_grad.astype(jnp.float32), axis=0).reshape(3, width)
    vector_grad = jnp.concatenate([gain_one[None], shift_one[None], sums[2:4], qkv_sum, sums[7:n_vec]], axis=0)
    tiles = jnp.pad(vector_grad.reshape(n_vec, 8, columns).transpose(1, 0, 2),
                    ((0, 0), (0, 16 - n_vec), (0, LANES - columns))).reshape(4, 2, 16, LANES)
    parts_a = jnp.stack([jnp.concatenate([grad_t_qkv[:, j * r0 : (j + 1) * r0], out_grad[:, j * r1 : (j + 1) * r1]], axis=1)
                         for j in range(4)]).reshape(4, 4, 2, columns, -1)
    own_a, own_b, tile, pieces = tail(parts_a, tiles, total_b, moments_t)
    new_moments, new_weights, new_small = finish(
        own_a, own_b, tile, pieces, moments_t, weights_t, (vectors, vec_first, vec_second))
    return (layer_out, input_grad, *[m.T for m in new_moments], *[w.T for w in new_weights], *new_small)


def shards_far(
    tokens, cotangent, lengths, counts,
    w_qkv, w_out, w_up, w_down,
    mom_qkv, mom_out, mom_up, mom_down,
    vectors, vec_first, vec_second,
):
    both = ("fsdp", "dp")
    planes = lax.axis_size("fsdp")
    ranks = lax.axis_size("dp")
    row_len, width = tokens.shape
    columns = w_qkv.shape[1]
    old_weights = (w_qkv, w_out, w_up, w_down)
    old_moments = (mom_qkv, mom_out, mom_up, mom_down)
    counts_rows = [w.shape[0] for w in old_weights]
    n_vec = vectors.shape[0]

    slab_a = jnp.concatenate([w_qkv.T, w_out.T, vectors.T], axis=1).astype(jnp.bfloat16)
    slab_b = jnp.concatenate([w_up.T, w_down.T], axis=1).astype(jnp.bfloat16)
    full_a = lax.all_gather(slab_a, both, axis=0, tiled=True).reshape(planes, width, -1)
    full_b = lax.all_gather(slab_b, both, axis=0, tiled=True).reshape(planes, width, -1)
    r0, r1, r2, r3 = counts_rows
    wt_qkv = jnp.concatenate([full_a[j, :, :r0] for j in range(planes)], axis=1)
    wt_out = jnp.concatenate([full_a[j, :, r0 : r0 + r1] for j in range(planes)], axis=1)
    table = full_a[0, :, r0 + r1 :].T.astype(jnp.float32)
    wt_up = jnp.concatenate([full_b[j, :, :r2] for j in range(planes)], axis=1)
    wt_down = jnp.concatenate([full_b[j, :, r2:] for j in range(planes)], axis=1)

    offset, segment, position, share = row_layout(lengths, counts, row_len)
    cosine, sine = rotary_tables(position)
    seg_col, seg_row = segment[:, None], segment[None, :]
    inputs = turn_rows(tokens, offset).astype(jnp.float32)
    incoming = turn_rows(cotangent, offset).astype(jnp.float32) * share[:, None]

    normed_one, pull_one = jax.vjp(layer_norm, inputs, table[0], table[1])
    normed_one = normed_one.astype(jnp.bfloat16)
    project = nn(normed_one, wt_qkv) + table[4:7].reshape(-1)
    qr, kr, vr, attn, lse = attention_forward(project, cosine, sine, seg_col, seg_row)
    after = inputs + (nn(attn, wt_out) + table[7])
    normed_two, pull_two = jax.vjp(layer_norm, after, table[2], table[3])
    normed_two = normed_two.astype(jnp.bfloat16)
    hidden_pre = nn(normed_two, wt_up) + table[9:].reshape(-1)
    hidden, pull_hidden = jax.vjp(gelu_exact, hidden_pre)
    hidden = hidden.astype(jnp.bfloat16)
    layer_out = (after + (nt(hidden, wt_down) + table[8])).astype(jnp.bfloat16)

    grad_low = incoming.astype(jnp.bfloat16)
    grad_t_down = tn(grad_low, hidden)
    pre_grad = pull_hidden(nn(grad_low, wt_down))[0].astype(jnp.bfloat16)
    grad_t_up = tn(normed_two, pre_grad)
    resid_grad, gain_two, shift_two = pull_two(nt(pre_grad, wt_up))
    after_grad = incoming + resid_grad
    branch_low = after_grad.astype(jnp.bfloat16)
    grad_t_out = tn(attn, branch_low)
    attn_grad = nt(branch_low, wt_out).astype(jnp.bfloat16)
    dq, dk, dv = attention_backward(qr, kr, vr, attn_grad, attn, lse, cosine, sine, seg_col, seg_row)
    proj_grad = jnp.concatenate([dq, dk, dv], axis=1)
    grad_t_qkv = tn(normed_one, proj_grad)
    in_grad, gain_one, shift_one = pull_one(nt(proj_grad, wt_qkv))
    input_grad = after_grad + in_grad

    def column_sum(values):
        return jnp.sum(values.astype(jnp.float32), axis=0)

    vector_grad = jnp.concatenate(
        [gain_one[None], shift_one[None], gain_two[None], shift_two[None],
         column_sum(proj_grad).reshape(3, width), column_sum(branch_low)[None], column_sum(grad_low)[None],
         column_sum(pre_grad).reshape(-1, width)],
        axis=0,
    )
    back = jnp.where(offset > 0, row_len - offset, 0)
    layer_out = turn_rows(layer_out, back)
    input_grad = turn_rows(input_grad, back)

    def cut(values, j, rows):
        return values[:, j * rows : (j + 1) * rows]

    parts_b = jnp.stack([jnp.concatenate([cut(grad_t_up, j, r2), cut(grad_t_down, j, r3)], axis=1) for j in range(planes)])
    own_b = lax.psum_scatter(parts_b.reshape(planes * width, -1), both, scatter_dimension=0, tiled=True)
    parts_a = jnp.stack([jnp.concatenate([cut(grad_t_qkv, j, r0), cut(grad_t_out, j, r1), vector_grad.T], axis=1) for j in range(planes)])
    own_a = lax.psum_scatter(parts_a.reshape(planes * width, -1), both, scatter_dimension=0, tiled=True)
    grads_t = (own_a[:, :r0], own_a[:, r0 : r0 + r1], own_b[:, :r2], own_b[:, r2:])
    vector_grad = own_a[:, r0 + r1 :].T
    new_moments_t = [moment_keep * old.T + grad for old, grad in zip(old_moments, grads_t)]

    most = max(counts_rows)
    padded = [jnp.pad(m.astype(jnp.bfloat16), ((0, 0), (0, most - m.shape[1]))) for m in new_moments_t]
    sent = jnp.stack([padded[t % 4] for t in range(planes)])
    mine = lax.all_to_all(sent, "fsdp", 0, 0, tiled=True)
    mine = mine.transpose(1, 0, 2).reshape(columns, planes * most)
    whole = lax.all_gather(mine, "dp", axis=0, tiled=True)
    gram = nt(whole, whole)
    identity = jnp.eye(width, dtype=jnp.float32)
    norm_sq = jnp.trace(gram) + 1e-07
    gram = gram / norm_sq
    factor = None
    for iteration in range(NS_ITERS):
        poly = poly_linear * identity + poly_square * gram + poly_cubic * high(gram, gram)
        factor = poly if factor is None else high(factor, poly)
        if iteration + 1 < NS_ITERS:
            gram = high(high(gram, poly), poly)
    own_rows = lax.dynamic_slice_in_dim(factor, lax.axis_index("dp") * columns, columns, 0) * lax.rsqrt(norm_sq)
    own_orth = high(own_rows, whole.astype(jnp.float32))
    own_orth = own_orth.astype(jnp.bfloat16).reshape(columns, planes, most).transpose(1, 0, 2)
    pieces = lax.all_to_all(own_orth, "fsdp", 0, 0, tiled=True).astype(jnp.float32)

    new_weights = []
    for x, weight_old in enumerate(old_weights):
        rows = weight_old.shape[0]
        scale = muon_rate * math.sqrt(max(1.0, rows * planes / width))
        new_weights.append(weight_old * (1.0 - muon_rate * muon_decay) - scale * pieces[x, :, :rows].T)
    new_first = beta_first * vec_first + (1.0 - beta_first) * vector_grad
    new_second = beta_second * vec_second + (1.0 - beta_second) * vector_grad * vector_grad
    first_fix = 1.0 - beta_first**STEP
    second_fix = 1.0 - beta_second**STEP
    new_vectors = vectors - adam_rate * (new_first / first_fix) / (jnp.sqrt(new_second / second_fix) + adam_eps)
    return (layer_out, input_grad, *[m.T for m in new_moments_t], *new_weights, new_vectors, new_first, new_second)


def solution(mesh):
    rows, cells, table = P(("dp", "fsdp"), None), P("fsdp", "dp"), P(None, "dp")
    near = dict(mesh.shape) == {"dp": 8, "fsdp": 4}
    return jax.shard_map(
        shards_near if near else shards_far,
        mesh=mesh,
        in_specs=(rows,) * 4 + (cells,) * 8 + (table,) * 3,
        out_specs=(rows,) * 2 + (cells,) * 8 + (table,) * 3,
        check_vma=False,
    )
```

```python
import functools
import math

import jax
import jax.numpy as jnp
from jax import lax
from jax.experimental import pallas as pl
from jax.experimental.pallas import tpu as pltpu
from jax.sharding import PartitionSpec as P

HEAD_DIM = 32
NS_ITERS = 5
STEP = 10
LANES = 128
LONGEST = 768

norm_eps = 1e-05
masked_score = -1e30
poly_linear = 3.4445
poly_square = -4.775
poly_cubic = 2.0315
muon_rate = 0.5
muon_decay = 0.01
moment_keep = 0.5
adam_rate = 0.05
beta_first = 0.9
beta_second = 0.999
adam_eps = 1e-08


def layer_norm(values, gain_row, shift_row):
    center = values - jnp.mean(values, axis=-1, keepdims=True)
    spread = jnp.mean(center * center, axis=-1, keepdims=True)
    return center * lax.rsqrt(spread + norm_eps) * gain_row + shift_row


def gelu_exact(values):
    return 0.5 * values * (1.0 + lax.erf(values * (1.0 / math.sqrt(2.0))))


def nn(left, right):
    return jnp.dot(left, right, preferred_element_type=jnp.float32)


def nt(left, right):
    return lax.dot_general(left, right, (((1,), (1,)), ((), ())), preferred_element_type=jnp.float32)


def tn(left, right):
    return lax.dot_general(left, right, (((0,), (0,)), ((), ())), preferred_element_type=jnp.float32)


def _half_mask(shape):
    lane = lax.broadcasted_iota(jnp.int32, shape, 1)
    return (lane % HEAD_DIM) < (HEAD_DIM // 2)


def _turn(values, first):
    half = HEAD_DIM // 2
    left = pltpu.roll(values, LANES - half, 1)
    right = pltpu.roll(values, half, 1)
    return jnp.where(first, left, right)


def attention_forward_kernel(
    q_ref, k_ref, v_ref, cos_ref, sin_ref, segc_ref, segr_ref,
    qr_ref, kr_ref, vr_ref, attn_ref, lse_ref,
    qt_s, vt_s, ot_s,
):
    first = _half_mask(cos_ref.shape)
    cosine, sine = cos_ref[...], sin_ref[...]
    queries = q_ref[...] * (1.0 / math.sqrt(HEAD_DIM))
    qr = (queries * cosine + _turn(queries, first) * sine).astype(jnp.bfloat16)
    keys = k_ref[...]
    kr = (keys * cosine + _turn(keys, first) * sine).astype(jnp.bfloat16)
    vr = v_ref[...].astype(jnp.bfloat16)
    qr_ref[...] = qr
    kr_ref[...] = kr
    vr_ref[...] = vr
    qt_s[...] = qr.T
    vt_s[...] = vr.T
    tokens = qr.shape[0]
    rest = tokens - LONGEST
    row = lax.broadcasted_iota(jnp.int32, (LANES, tokens), 0)
    same = segc_ref[LONGEST:, :] == segr_ref[:, LONGEST:]

    def head(h, carry):
        qth = jnp.where(row // HEAD_DIM == h, qt_s[...], jnp.zeros((), jnp.bfloat16))
        rows = pl.ds(pl.multiple_of(h * HEAD_DIM, HEAD_DIM), HEAD_DIM)

        def block(start, width, key_start, key_count, mask):
            scores = nn(kr_ref[key_start : key_start + key_count, :], qth[:, start : start + width])
            if mask is not None:
                scores = jnp.where(mask, scores, masked_score)
            peak = jnp.max(scores, axis=0, keepdims=True)
            raised = jnp.exp(scores - peak)
            total = jnp.sum(raised, axis=0, keepdims=True)
            out = nn(vt_s[rows, key_start : key_start + key_count], raised.astype(jnp.bfloat16))
            ot_s[rows, start : start + width] = out / total
            lse_ref[0, pl.ds(h, 1), start : start + width] = peak + jnp.log(total)

        for start in range(0, LONGEST, 256):
            block(start, 256, 0, LONGEST, None)
        block(LONGEST, rest, LONGEST, rest, same)
        return carry

    lax.fori_loop(0, LANES // HEAD_DIM, head, 0)
    attn_ref[...] = ot_s[...].T.astype(jnp.bfloat16)


def attention_forward(project, cosine, sine, seg_col, seg_row):
    tokens = project.shape[0]
    width = project.shape[1] // 3
    groups = width // LANES
    col = lambda shift: pl.BlockSpec((tokens, LANES), lambda g, shift=shift: (0, g + shift))
    whole = lambda shape: pl.BlockSpec(shape, lambda g: (0,) * len(shape))
    flops = 4 * (LONGEST**2 + (tokens - LONGEST) ** 2) * 128 * groups * 4
    return pl.pallas_call(
        attention_forward_kernel,
        grid=(groups,),
        in_specs=[col(0), col(groups), col(2 * groups), whole((tokens, LANES)), whole((tokens, LANES)),
                  whole((tokens, 1)), whole((1, tokens))],
        out_specs=[col(0)] * 4 + [pl.BlockSpec((1, 4, tokens), lambda g: (g, 0, 0))],
        out_shape=[jax.ShapeDtypeStruct((tokens, width), jnp.bfloat16)] * 4
        + [jax.ShapeDtypeStruct((groups, 4, tokens), jnp.float32)],
        scratch_shapes=[
            pltpu.VMEM((LANES, tokens), jnp.bfloat16),
            pltpu.VMEM((LANES, tokens), jnp.bfloat16),
            pltpu.VMEM((LANES, tokens), jnp.float32),
        ],
        compiler_params=pltpu.CompilerParams(vmem_limit_bytes=48 << 20),
        cost_estimate=pl.CostEstimate(flops=flops, bytes_accessed=20 << 20, transcendentals=20 << 20),
        name="attention_forward",
    )(project, project, project, cosine, sine, seg_col, seg_row)


def attention_backward_kernel(
    qr_ref, kr_ref, vr_ref, do_ref, attn_ref, lse_ref, cos_ref, sin_ref, segc_ref, segr_ref,
    *rest_refs,
):
    dq_ref, dk_ref, dv_ref = rest_refs[:3]
    qt_s, dot_s, kt_s, delta_s, dqt_s, dk_s, dv_s = rest_refs[3:]
    tokens = qr_ref.shape[0]
    rest = tokens - LONGEST
    qt_s[...] = qr_ref[...].T
    dot_s[...] = do_ref[...].T
    kt_s[...] = kr_ref[...].T
    prod_t = (do_ref[...].astype(jnp.float32) * attn_ref[...].astype(jnp.float32)).T
    for h in range(4):
        delta_s[h : h + 1, :] = jnp.sum(prod_t[h * HEAD_DIM : (h + 1) * HEAD_DIM, :], axis=0, keepdims=True)
    dk_s[...] = jnp.zeros_like(dk_s)
    dv_s[...] = jnp.zeros_like(dv_s)
    row = lax.broadcasted_iota(jnp.int32, (LANES, tokens), 0)
    lane = lax.broadcasted_iota(jnp.int32, (tokens, LANES), 1)
    same = segc_ref[LONGEST:, :] == segr_ref[:, LONGEST:]
    zero = jnp.zeros((), jnp.bfloat16)

    def head(h, carry):
        mine_t = row // HEAD_DIM == h
        mine = lane // HEAD_DIM == h
        qth = jnp.where(mine_t, qt_s[...], zero)
        doth = jnp.where(mine_t, dot_s[...], zero)
        qh = jnp.where(mine, qr_ref[...], zero)
        doh = jnp.where(mine, do_ref[...], zero)
        rows = pl.ds(pl.multiple_of(h * HEAD_DIM, HEAD_DIM), HEAD_DIM)

        def block(start, width, key_start, key_count, mask):
            at = slice(start, start + width)
            keys = slice(key_start, key_start + key_count)
            scores = nn(kr_ref[keys, :], qth[:, at])
            if mask is not None:
                scores = jnp.where(mask, scores, masked_score)
            soft = jnp.exp(scores - lse_ref[0, pl.ds(h, 1), at])
            weight_grad = nn(vr_ref[keys, :], doth[:, at])
            score_grad = (soft * (weight_grad - delta_s[pl.ds(h, 1), at])).astype(jnp.bfloat16)
            dv_s[keys, :] += nn(soft.astype(jnp.bfloat16), doh[at, :])
            dk_s[keys, :] += nn(score_grad, qh[at, :])
            dqt_s[rows, at] = nn(kt_s[rows, keys], score_grad)

        for start in range(0, LONGEST, 256):
            block(start, 256, 0, LONGEST, None)
        block(LONGEST, rest, LONGEST, rest, same)
        return carry

    lax.fori_loop(0, LANES // HEAD_DIM, head, 0)
    first = _half_mask(cos_ref.shape)
    cosine, sine = cos_ref[...], sin_ref[...]

    def pull(values):
        return values * cosine + _turn(values * sine, first)

    dq_ref[...] = (pull(dqt_s[...].T) * (1.0 / math.sqrt(HEAD_DIM))).astype(jnp.bfloat16)
    dk_ref[...] = pull(dk_s[...]).astype(jnp.bfloat16)
    dv_ref[...] = dv_s[...].astype(jnp.bfloat16)


def attention_backward(qr, kr, vr, attn_grad, attn, lse, cosine, sine, seg_col, seg_row):
    tokens, width = qr.shape
    groups = width // LANES
    col = pl.BlockSpec((tokens, LANES), lambda g: (0, g))
    whole = lambda shape: pl.BlockSpec(shape, lambda g: (0,) * len(shape))
    flops = 10 * (LONGEST**2 + (tokens - LONGEST) ** 2) * 128 * groups * 4
    return pl.pallas_call(
        attention_backward_kernel,
        grid=(groups,),
        in_specs=[col] * 5 + [pl.BlockSpec((1, 4, tokens), lambda g: (g, 0, 0)),
                              whole((tokens, LANES)), whole((tokens, LANES)), whole((tokens, 1)), whole((1, tokens))],
        out_specs=[col] * 3,
        out_shape=[jax.ShapeDtypeStruct((tokens, width), jnp.bfloat16)] * 3,
        scratch_shapes=[
            pltpu.VMEM((LANES, tokens), jnp.bfloat16),
            pltpu.VMEM((LANES, tokens), jnp.bfloat16),
            pltpu.VMEM((LANES, tokens), jnp.bfloat16),
            pltpu.VMEM((8, tokens), jnp.float32),
            pltpu.VMEM((LANES, tokens), jnp.float32),
            pltpu.VMEM((tokens, LANES), jnp.float32),
            pltpu.VMEM((tokens, LANES), jnp.float32),
        ],
        compiler_params=pltpu.CompilerParams(vmem_limit_bytes=56 << 20),
        cost_estimate=pl.CostEstimate(flops=flops, bytes_accessed=20 << 20, transcendentals=20 << 20),
        name="attention_backward",
    )(qr, kr, vr, attn_grad, attn, lse, cosine, sine, seg_col, seg_row)


MESH = pl.DeviceIdType.MESH


def place():
    rank, plane = lax.axis_index("dp"), lax.axis_index("fsdp")
    core = rank % 2
    chip_x = (rank // 2) % 2
    chip_y = rank // 4
    return rank, plane, core, chip_x, chip_y


def chip_at(step, chip_x, chip_y):
    other_x = 1 - chip_x if step & 1 else chip_x
    other_y = 1 - chip_y if step & 2 else chip_y
    return 2 * other_y + other_x


def greet(partners):
    barrier = pltpu.get_barrier_semaphore()
    for partner in partners:
        pl.semaphore_signal(barrier, inc=1, device_id=partner, device_id_type=MESH)
    pl.semaphore_wait(barrier, len(partners))


def all_partners():
    rank, plane, core, chip_x, chip_y = place()
    sibling = 2 * chip_at(0, chip_x, chip_y) + 1 - core
    partners = [(sibling, plane)]
    partners += [(2 * chip_at(step, chip_x, chip_y) + core, plane) for step in (1, 2, 3)]
    partners += [(rank, (plane + step) % 4) for step in (1, 2, 3)]
    return partners


class SumStages:
    def __init__(self, parts, own, from_core, from_chip, from_plane, total, sems, lanes):
        self.parts, self.own, self.from_core, self.from_chip = parts, own, from_core, from_chip
        self.from_plane, self.total, self.lanes = from_plane, total, lanes
        self.send, self.recv, self.local = sems
        self.rank, self.plane, self.core, self.chip_x, self.chip_y = place()
        self.chip = chip_at(0, self.chip_x, self.chip_y)

    def remote(self, source, target, slot, device):
        return pltpu.make_async_remote_copy(
            src_ref=source, dst_ref=target, send_sem=self.send.at[slot], recv_sem=self.recv.at[slot],
            device_id=device, device_id_type=MESH)

    def give_copy(self, source):
        return self.remote(source, self.from_core, 0, (2 * self.chip + 1 - self.core, self.plane))

    def core_add(self, give):
        give.wait()
        for j in range(self.own.shape[0]):
            self.own[j] = (self.own[j].astype(jnp.float32) + self.from_core[j].astype(jnp.float32)).astype(self.own.dtype)

    def core_copies(self):
        load = pltpu.make_async_copy(self.parts.at[:, :, self.core, :, self.lanes], self.own, self.local)
        give = self.remote(self.parts.at[:, :, 1 - self.core, :, self.lanes], self.from_core, 0,
                           (2 * self.chip + 1 - self.core, self.plane))
        return load, give

    def core_start(self):
        load, give = self.core_copies()
        give.start()
        load.start()

    def core_finish(self):
        load, give = self.core_copies()
        load.wait()
        self.core_add(give)

    def chip_copies(self):
        return [
            self.remote(self.own.at[:, chip_at(step, self.chip_x, self.chip_y)], self.from_chip.at[step - 1], step,
                        (2 * chip_at(step, self.chip_x, self.chip_y) + self.core, self.plane))
            for step in (1, 2, 3)
        ]

    def chip_start(self):
        for copy in self.chip_copies():
            copy.start()

    def chip_finish(self):
        for copy in self.chip_copies():
            copy.wait()
        for j in range(self.own.shape[0]):
            value = self.own[j, pl.ds(self.chip, 1)][0].astype(jnp.float32)
            for slot in range(3):
                value = value + self.from_chip[slot, j].astype(jnp.float32)
            self.total[j] = value.astype(self.total.dtype)

    def plane_copies(self):
        return [
            self.remote(self.total.at[(self.plane + step) % 4], self.from_plane.at[step - 1], 3 + step,
                        (self.rank, (self.plane + step) % 4))
            for step in (1, 2, 3)
        ]

    def plane_start(self):
        for copy in self.plane_copies():
            copy.start()

    def plane_finish(self):
        for copy in self.plane_copies():
            copy.wait()
        value = self.total[pl.ds(self.plane, 1)][0].astype(jnp.float32)
        for slot in range(3):
            value = value + self.from_plane[slot].astype(jnp.float32)
        return value


def sum_scratch(rows, lanes, dtype=jnp.bfloat16):
    return [
        pltpu.VMEM((4, 4, rows, lanes), dtype),
        pltpu.VMEM((4, 4, rows, lanes), dtype),
        pltpu.VMEM((3, 4, rows, lanes), dtype),
        pltpu.VMEM((3, rows, lanes), dtype),
        pltpu.VMEM((4, rows, lanes), dtype),
        pltpu.SemaphoreType.DMA((7,)),
        pltpu.SemaphoreType.DMA((7,)),
        pltpu.SemaphoreType.DMA,
    ]


SUM_SCRATCH = 8


def stages_of(parts, scratch, lanes):
    own, from_core, from_chip, from_plane, total, send, recv, local = scratch
    return SumStages(parts, own, from_core, from_chip, from_plane, total, (send, recv, local), lanes)


def table_sum(table_ref, table_out, from_core, from_chip, from_plane, held, send, recv):
    rank, plane, core, chip_x, chip_y = place()
    chip = chip_at(0, chip_x, chip_y)

    def remote(source, target, slot, device):
        return pltpu.make_async_remote_copy(
            src_ref=source, dst_ref=target, send_sem=send.at[slot], recv_sem=recv.at[slot],
            device_id=device, device_id_type=MESH)

    give = remote(table_ref.at[:, 1 - core], from_core, 0, (2 * chip + 1 - core, plane))
    give.start()
    yield
    give.wait()
    held[...] = table_ref[:, pl.ds(core, 1)][:, 0] + from_core[...]
    across = [remote(held.at[chip_at(step, chip_x, chip_y)], from_chip.at[step - 1], step,
                     (2 * chip_at(step, chip_x, chip_y) + core, plane)) for step in (1, 2, 3)]
    for copy in across:
        copy.start()
    yield
    for copy in across:
        copy.wait()
    own = held[pl.ds(chip, 1)][0] + from_chip[0] + from_chip[1] + from_chip[2]
    table_out[...] = own
    along = [remote(table_out, from_plane.at[step - 1], 3 + step, (rank, (plane + step) % 4)) for step in (1, 2, 3)]
    for copy in along:
        copy.start()
    yield
    for copy in along:
        copy.wait()
    table_out[...] = own + from_plane[0] + from_plane[1] + from_plane[2]
    yield


class Gather:
    def __init__(self, at, send, recv, base, start, size):
        rank, plane, core, chip_x, chip_y = place()
        half = size // 2
        every, low, high = pl.ds(start, size), pl.ds(start, half), pl.ds(start + half, half)
        chips = [chip_at(step, chip_x, chip_y) for step in range(4)]
        over = [2 * chip + core for chip in chips]

        def copy(chip, lanes, slot, device):
            block = at(chip, core, lanes)
            return pltpu.make_async_remote_copy(
                src_ref=block, dst_ref=block, send_sem=send.at[base + slot], recv_sem=recv.at[base + slot],
                device_id=(device, plane), device_id_type=MESH)

        self.to_x, self.to_y = copy(chips[0], every, 0, over[1]), copy(chips[0], every, 1, over[2])
        self.on_y, self.on_x = copy(chips[1], low, 2, over[2]), copy(chips[2], high, 3, over[1])
        self.beside = [copy(chip, every, 4 + step, 2 * chips[0] + 1 - core) for step, chip in enumerate(chips)]

    def first(self):
        self.to_x.start()
        self.to_y.start()
        self.beside[0].start()

    def second(self):
        self.to_x.wait_recv()
        self.on_y.start()
        self.beside[1].start()
        self.to_y.wait_recv()
        self.on_x.start()
        self.beside[2].start()

    def third(self):
        self.on_y.wait_recv()
        self.on_x.wait_recv()
        self.beside[3].start()

    def finish(self):
        for copy in (self.to_x, self.to_y, self.on_y, self.on_x):
            copy.wait_send()
        for copy in self.beside:
            copy.wait()


def split(values):
    top = values.astype(jnp.bfloat16)
    return top, (values - top.astype(jnp.float32)).astype(jnp.bfloat16)


def put_left(ref, values):
    width = values.shape[1]
    top, low = split(values)
    ref[:, :width] = top
    ref[:, width : 2 * width] = top
    ref[:, 2 * width :] = low


def put_right(ref, values):
    width = values.shape[0]
    top, low = split(values)
    ref[:width, :] = top
    ref[width : 2 * width, :] = low
    ref[2 * width :, :] = top


def tiles_of(width):
    first = width % 256
    edges = ([0] if first else []) + list(range(first, width + 1, 256))
    return list(zip(edges[:-1], edges[1:]))


def symmetric_product(out, left, right, tiles):
    for start, stop in tiles:
        block = nn(left[:stop, :], right[:, start:stop])
        out[:stop, start:stop] = block
        if start:
            out[start:stop, :start] = block[:start, :].T


def orthogonal_rows(whole, mine, gram, poly, temp, factor, left_gram, left_temp, right, write):
    width = gram.shape[0]
    tiles = tiles_of(width)
    flat = whole[...].reshape(width, whole.shape[-1])
    for start, stop in tiles:
        block = nt(flat[:stop, :], flat[start:stop, :])
        gram[:stop, start:stop] = block
        if start:
            gram[start:stop, :start] = block[:start, :].T
    diagonal = lax.broadcasted_iota(jnp.int32, (width, width), 0) == lax.broadcasted_iota(jnp.int32, (width, width), 1)
    norm_sq = jnp.sum(jnp.sum(jnp.where(diagonal, gram[...], 0.0), axis=1, keepdims=True), axis=0, keepdims=True) + 1e-07
    gram[...] = gram[...] / norm_sq

    def polynomial():
        put_left(left_gram, gram[...])
        put_right(right, gram[...])
        symmetric_product(temp, left_gram, right, tiles)
        poly[...] = jnp.where(diagonal, poly_linear, 0.0) + poly_square * gram[...] + poly_cubic * temp[...]
        put_right(right, poly[...])

    def next_gram():
        symmetric_product(temp, left_gram, right, tiles)
        put_left(left_temp, temp[...])
        symmetric_product(gram, left_temp, right, tiles)

    polynomial()
    factor[...] = poly[...]

    def iteration(step, carry):
        next_gram()
        polynomial()
        put_left(left_temp, factor[...])
        symmetric_product(factor, left_temp, right, tiles)
        return carry

    lax.fori_loop(0, NS_ITERS - 2, iteration, 0)
    next_gram()
    put_right(right, gram[...])
    rows = factor[mine, :]

    def thin(values):
        put_left(left_temp.at[: values.shape[0], :], values)
        return nn(left_temp[: values.shape[0], :], right[...])

    once = thin(rows)
    twice = thin(once)
    rows = (poly_linear * rows + poly_square * once + poly_cubic * twice) * lax.rsqrt(norm_sq)
    top, low = split(rows)
    lanes = whole.shape[-1] // 4
    for j in range(4):
        part = flat[:, j * lanes : (j + 1) * lanes]
        write(j, nn(top, part) + nn(low, part))


class PlaneStage:
    def __init__(self, total, from_plane, send, recv):
        rank, self.plane = place()[:2]
        self.total, self.from_plane = total, from_plane
        self.copies = [
            pltpu.make_async_remote_copy(
                src_ref=total.at[(self.plane + step) % 4], dst_ref=from_plane.at[step - 1],
                send_sem=send.at[step - 1], recv_sem=recv.at[step - 1],
                device_id=(rank, (self.plane + step) % 4), device_id_type=MESH)
            for step in (1, 2, 3)
        ]

    def start(self):
        for copy in self.copies:
            copy.start()

    def finish(self):
        for copy in self.copies:
            copy.wait()
        value = self.total[pl.ds(self.plane, 1)][0].astype(jnp.float32)
        for slot in range(3):
            value = value + self.from_plane[slot].astype(jnp.float32)
        return value


def tail_kernel(
    h1_ref, dq_ref, dk_ref, dv_ref, out_grad_ref, sums_ref, table_ref, total_b_ref, len_ref,
    *refs,
):
    moments, weights, small, (wt_hbm, after_hbm, x_hbm) = refs[0:4], refs[4:8], refs[8:11], refs[11:14]
    new_moments, new_weights, new_small, input_grad_ref = refs[14:18], refs[18:22], refs[22:25], refs[25]
    table_out, pieces, own_b_ref, own_a_ref = refs[26:30]
    refs = refs[30:]
    stages = stages_of(None, refs[:SUM_SCRATCH], None)
    refs = refs[SUM_SCRATCH:]
    table_scratch, refs = refs[:6], refs[6:]
    blocks, whole, gram, poly, temp, factor, left_gram, left_temp, right, from_plane_b = refs[:10]
    plane_send, plane_recv, gather_send, gather_recv, back_send, back_recv, b_send, b_recv, loads = refs[10:19]
    give_s, tiles_s, h1t_s, wt_s, after_s, x_s = refs[19:]
    rank, plane, core, chip_x, chip_y = place()
    chip = chip_at(0, chip_x, chip_y)
    columns = own_b_ref.shape[0]
    lanes = blocks.shape[-1]
    tokens, width = h1_ref.shape
    rows_qkv, rows_out = moments[0].shape[1], moments[1].shape[0]
    last_b = PlaneStage(total_b_ref, from_plane_b, b_send, b_recv)
    loading = [pltpu.make_async_copy(source, target, loads.at[n])
               for n, (source, target) in enumerate(((wt_hbm, wt_s), (after_hbm, after_s), (x_hbm, x_s)))]
    for copy in loading:
        copy.start()
    h1t_s[...] = h1_ref[...].T
    greet(all_partners())
    last_b.start()

    def half(which, target):
        starts = [pl.multiple_of(columns * (2 * m + which), 16) for m in range(4)]
        left = jnp.concatenate([h1t_s[pl.ds(start, columns), :] for start in starts], axis=0)
        qkv = jnp.concatenate([nn(left, ref[...]).astype(jnp.bfloat16) for ref in (dq_ref, dk_ref, dv_ref)], axis=1)
        out = jnp.concatenate([out_grad_ref[pl.ds(start, columns), :] for start in starts], axis=0)
        for j in range(4):
            both = jnp.concatenate(
                [qkv[:, j * rows_qkv : (j + 1) * rows_qkv], out[:, j * rows_out : (j + 1) * rows_out]], axis=1)
            target[j] = both.reshape(4, columns, lanes)

    half(1 - core, give_s)
    give = stages.give_copy(give_s)
    give.start()
    half(core, stages.own)
    stages.core_add(give)
    stages.chip_start()

    for copy in loading:
        copy.wait()
    ends, offset = row_marks(len_ref)
    gain = table_ref[0:1, :]
    gain_sum = jnp.zeros((1, width), jnp.float32)
    shift_sum = jnp.zeros((1, width), jnp.float32)
    for r in range(0, tokens, 256):
        at = slice(r, r + 256)
        grad = sum(nt(ref[at, :], wt_s[:, part * width : (part + 1) * width])
                   for part, ref in enumerate((dq_ref, dk_ref, dv_ref)))
        values = x_s[at, :].astype(jnp.float32)
        center = values - jnp.mean(values, axis=-1, keepdims=True)
        rstd = lax.rsqrt(jnp.mean(center * center, axis=-1, keepdims=True) + norm_eps)
        xhat = center * rstd
        gain_sum += jnp.sum(grad * xhat, axis=0, keepdims=True)
        shift_sum += jnp.sum(grad, axis=0, keepdims=True)
        scaled = grad * gain
        after_s[at, :] += rstd * (scaled - jnp.mean(scaled, axis=-1, keepdims=True)
                                  - xhat * jnp.mean(scaled * xhat, axis=-1, keepdims=True))
    vector = jnp.concatenate(
        [gain_sum, shift_sum, sums_ref[2:4, :]]
        + [jnp.sum(ref[...].astype(jnp.float32), axis=0, keepdims=True) for ref in (dq_ref, dk_ref, dv_ref)]
        + [sums_ref[7:16, :]], axis=0)
    for block in range(8):
        part = vector[:, block * columns : (block + 1) * columns]
        tiles_s[block // 2, block % 2] = jnp.concatenate(
            [part, jnp.zeros((16, LANES - columns), jnp.float32)], axis=1)
    adding = table_sum(tiles_s, table_out, *table_scratch)
    next(adding)
    input_grad_ref[...] = pltpu.roll(after_s[...], offset, 0)

    def momentum(x, gradient):
        rows = gradient.shape[1]
        if x == 1:
            new = moment_keep * moments[x][...].T + gradient
            new_moments[x][...] = new.T
        else:
            new = moment_keep * moments[x][...] + gradient
            new_moments[x][...] = new
        blocks[x, :, :rows] = new.astype(jnp.bfloat16)
        if rows < lanes:
            blocks[x, :, rows:] = jnp.zeros((columns, lanes - rows), jnp.bfloat16)

    own_lanes = pl.ds(pl.multiple_of(plane * lanes, lanes), lanes)
    out = [
        pltpu.make_async_remote_copy(
            src_ref=blocks.at[(plane + step) % 4], dst_ref=whole.at[chip, core, :, own_lanes],
            send_sem=plane_send.at[step - 1], recv_sem=plane_recv.at[step - 1],
            device_id=(rank, (plane + step) % 4), device_id_type=MESH)
        for step in (1, 2, 3)
    ]
    next(adding)
    own_b_ref[...] = last_b.finish()
    at = 0
    for x in (2, 3):
        rows = moments[x].shape[1]
        momentum(x, own_b_ref[:, at : at + rows])
        at += rows
    for step in (1, 2, 3):
        @pl.when((plane + step) % 4 >= 2)
        def _():
            out[step - 1].start()

    stages.chip_finish()
    stages.plane_start()
    next(adding)
    own_a_ref[...] = stages.plane_finish()
    momentum(0, own_a_ref[:, :rows_qkv])
    momentum(1, own_a_ref[:, rows_qkv : rows_qkv + rows_out])
    for step in (1, 2, 3):
        @pl.when((plane + step) % 4 < 2)
        def _():
            out[step - 1].start()

    whole[pl.ds(chip, 1), pl.ds(core, 1), :, own_lanes] = blocks[pl.ds(plane, 1)][None]
    next(adding)
    first_fix = 1.0 - beta_first**STEP
    second_fix = 1.0 - beta_second**STEP
    n_vec = small[0].shape[0]
    vector_grad = table_out[:n_vec, :columns]
    vectors, vec_first, vec_second = (ref[...] for ref in small)
    new_first = beta_first * vec_first + (1.0 - beta_first) * vector_grad
    new_second = beta_second * vec_second + (1.0 - beta_second) * vector_grad * vector_grad
    new_small[0][...] = vectors - adam_rate * (new_first / first_fix) / (jnp.sqrt(new_second / second_fix) + adam_eps)
    new_small[1][...] = new_first
    new_small[2][...] = new_second
    for copy in out:
        copy.wait()
    gather = Gather(lambda m, c, lane: whole.at[m, c, :, lane], gather_send, gather_recv, 0, 0, whole.shape[-1])
    gather.first()
    gather.second()
    gather.third()
    gather.finish()

    def write(j, values):
        blocks[j] = values.astype(jnp.bfloat16)

    orthogonal_rows(whole, pl.ds(pl.multiple_of(rank * columns, 8), columns), gram, poly, temp, factor,
                    left_gram, left_temp, right, write)
    home = [
        pltpu.make_async_remote_copy(
            src_ref=blocks.at[(plane + step) % 4], dst_ref=pieces.at[plane],
            send_sem=back_send.at[step - 1], recv_sem=back_recv.at[step - 1],
            device_id=(rank, (plane + step) % 4), device_id_type=MESH)
        for step in (1, 2, 3)
    ]
    for copy in home:
        copy.start()
    pieces[pl.ds(plane, 1)] = blocks[pl.ds(plane, 1)]
    for copy in home:
        copy.wait()
    for x in range(4):
        rows = moments[x].shape[0 if x == 1 else 1]
        scale = muon_rate * math.sqrt(max(1.0, rows * 4 / width))
        change = pieces[x, :, :rows].astype(jnp.float32)
        new_weights[x][...] = (weights[x][...] * (1.0 - muon_rate * muon_decay)
                               - scale * (change.T if x == 1 else change))


def tail(h1, dq, dk, dv, out_grad, sums, table, total_b, lengths, moments, weights, small, wt_qkv, after_grad, x):
    tokens, width = h1.shape
    rows = width // 8
    vmem = pl.BlockSpec(memory_space=pltpu.VMEM)
    hbm = pl.BlockSpec(memory_space=pl.ANY)
    tile = (16, LANES)
    most = max(moments[n].shape[1] for n in (0, 2, 3))
    shape = jax.ShapeDtypeStruct
    f32, bf16 = jnp.float32, jnp.bfloat16
    square = pltpu.VMEM((width, width), f32)
    sems = lambda n: pltpu.SemaphoreType.DMA((n,))
    lanes_b = total_b.shape[-1]
    return pl.pallas_call(
        tail_kernel,
        in_specs=[vmem] * 8 + [pl.BlockSpec(memory_space=pltpu.SMEM)] + [vmem] * 11 + [hbm] * 3,
        out_specs=[vmem] * 12,
        out_shape=[shape(v.shape, f32) for v in (*moments, *weights, *small)] + [shape((tokens, width), f32)],
        scratch_shapes=[pltpu.VMEM(tile, f32), pltpu.VMEM((4, rows, most), bf16), pltpu.VMEM((rows, lanes_b), f32),
                        pltpu.VMEM((rows, most), f32)] + sum_scratch(rows, most)
        + [pltpu.VMEM((4, *tile), f32), pltpu.VMEM((3, *tile), f32),
           pltpu.VMEM((3, *tile), f32), pltpu.VMEM((4, *tile), f32), sems(7), sems(7)]
        + [pltpu.VMEM((4, rows, most), bf16), pltpu.VMEM((4, 2, rows, 4 * most), bf16),
           square, square, square, square,
           pltpu.VMEM((width, 3 * width), bf16), pltpu.VMEM((width, 3 * width), bf16),
           pltpu.VMEM((3 * width, width), bf16), pltpu.VMEM((3, rows, lanes_b), bf16)]
        + [sems(3), sems(3), sems(8), sems(8), sems(3), sems(3), sems(3), sems(3), sems(3)]
        + [pltpu.VMEM((4, 4, rows, most), bf16), pltpu.VMEM((4, 2, *tile), f32), pltpu.VMEM((width, tokens), bf16),
           pltpu.VMEM((width, 3 * width), bf16), pltpu.VMEM((tokens, width), f32), pltpu.VMEM((tokens, width), bf16)],
        compiler_params=pltpu.CompilerParams(collective_id=1, has_side_effects=True, vmem_limit_bytes=60 << 20),
        name="tail",
    )(h1, dq, dk, dv, out_grad, sums, table, total_b, lengths, *moments, *weights, *small, wt_qkv, after_grad, x)


def finish_kernel(*refs):
    count = len(refs) // 3
    sources, targets, held, loads, stores = refs[:count], refs[count : 2 * count], refs[2 * count : -2], refs[-2], refs[-1]
    loading, storing = [], []
    for n in range(count):
        rows = sources[n].shape[0]
        parts = 4 if rows >= ROW_LEN else 1
        for p in range(parts):
            at = pl.ds(p * (rows // parts), rows // parts)
            slot = len(loading)
            loading.append(pltpu.make_async_copy(sources[n].at[at], held[n].at[at], loads.at[slot]))
            storing.append(pltpu.make_async_copy(held[n].at[at], targets[n].at[at], stores.at[slot]))
    for copy in loading:
        copy.start()
    for load, store in zip(loading, storing):
        load.wait()
        store.start()
    for copy in storing:
        copy.wait()


def finish(values):
    hbm = pl.BlockSpec(memory_space=pl.ANY)
    count = len(values)
    copies = sum(4 if x.shape[0] >= ROW_LEN else 1 for x in values)
    return pl.pallas_call(
        finish_kernel,
        in_specs=[hbm] * count,
        out_specs=[hbm] * count,
        out_shape=[jax.ShapeDtypeStruct(x.shape, x.dtype) for x in values],
        scratch_shapes=[pltpu.VMEM(x.shape, x.dtype) for x in values]
        + [pltpu.SemaphoreType.DMA((copies,)), pltpu.SemaphoreType.DMA((copies,))],
        compiler_params=pltpu.CompilerParams(vmem_limit_bytes=62 << 20),
        name="finish",
    )(*values)


ROW_LEN = 1024
GATHERED = 512
CHUNK_A = 256
OUT_LANES = 256
CUTS_B = ((0, 512), (512, 768))


def row_marks(len_ref):
    ends = [len_ref[0, 0]]
    for slot in (1, 2):
        ends.append(ends[-1] + len_ref[0, slot])
    starts = [0, *ends]
    offset = starts[3]
    for slot in (2, 1, 0):
        offset = jnp.where(len_ref[0, slot] == LONGEST, starts[slot], offset)
    return ends, offset


def segment_of(index, ends, offset):
    where = index + offset
    where = jnp.where(where >= ROW_LEN, where - ROW_LEN, where)
    segment = sum((where >= end).astype(jnp.int32) for end in ends)
    return where, segment


def turned_rows(values, offset):
    return pltpu.roll(values.astype(jnp.float32), jnp.where(offset > 0, ROW_LEN - offset, 0), 0)


def same_rest(ends, offset):
    rest = ROW_LEN - LONGEST
    columns = lax.broadcasted_iota(jnp.int32, (rest, rest), 0) + LONGEST
    rows = lax.broadcasted_iota(jnp.int32, (rest, rest), 1) + LONGEST
    return segment_of(columns, ends, offset)[1] == segment_of(rows, ends, offset)[1]


def attention_jobs(tokens):
    blocks = [(start, 256, 0, LONGEST) for start in range(0, LONGEST, 256)] + [(LONGEST, tokens - LONGEST, LONGEST, tokens - LONGEST)]
    return [(h, *block) for h in range(LANES // HEAD_DIM) for block in blocks]


def attention_group(q, k_ref, v, same, ot_s, vt_s, lse_ref):
    tokens = q.shape[0]
    qt = q.T
    vt_s[...] = v.T
    row = lax.broadcasted_iota(jnp.int32, qt.shape, 0)
    jobs = attention_jobs(tokens)
    queries, scores, soft = {}, {}, {}

    def score(job):
        h, start, width, key_start, key_count = job
        if h not in queries:
            queries[h] = jnp.where(row // HEAD_DIM == h, qt, jnp.zeros((), jnp.bfloat16))
        out = nn(k_ref[key_start : key_start + key_count, :], queries[h][:, start : start + width])
        return jnp.where(same, out, masked_score) if start == LONGEST else out

    def soften(values):
        peak = jnp.max(values, axis=0, keepdims=True)
        raised = jnp.exp(values - peak)
        return raised.astype(jnp.bfloat16), peak, jnp.sum(raised, axis=0, keepdims=True)

    def collect(job, raised, peak, total):
        h, start, width, key_start, key_count = job
        rows = slice(h * HEAD_DIM, (h + 1) * HEAD_DIM)
        out = nn(vt_s[rows, key_start : key_start + key_count], raised)
        ot_s[rows, start : start + width] = out / total
        lse_ref[0, h : h + 1, start : start + width] = peak + jnp.log(total)

    count = len(jobs)
    for t in range(count + 2):
        if t < count:
            scores[t] = score(jobs[t])
        if 0 <= t - 1 < count:
            soft[t - 1] = soften(scores.pop(t - 1))
        if 0 <= t - 2:
            collect(jobs[t - 2], *soft.pop(t - 2))
    return ot_s[...].T.astype(jnp.bfloat16)


def head_kernel(
    len_ref, tokens_ref, w_qkv_ref, w_up_ref, w_down_ref, w_out_ref, vectors_ref,
    qr_ref, kr_ref, vr_ref, attn_ref, lse_ref, h1_ref, x_ref, cos_ref, sin_ref, wt_ref, table_ref, full_b, full_o,
    full_a, full_v, twice_s, q_s, k_s, v_s, ot_s, vt_s, slab_a, slab_b, slab_o,
    a_send, a_recv, az_send, az_recv, b_send, b_recv, bz_send, bz_recv, v_send, v_recv, local,
):
    group = pl.program_id(0)
    rank, plane, core, chip_x, chip_y = place()
    chip = chip_at(0, chip_x, chip_y)
    columns = slab_a.shape[0]
    chunks_a = GATHERED // CHUNK_A
    gather_a = [Gather(lambda m, c, lane: full_a.at[:, m, c, :, lane], a_send, a_recv, 8 * n, CHUNK_A * n, CHUNK_A)
                for n in range(chunks_a)]
    gather_o = Gather(lambda m, c, lane: full_o.at[:, m, c, :, lane], b_send, b_recv, 0, 0, OUT_LANES)
    gather_b = [Gather(lambda m, c, lane: full_b.at[pl.ds(0, 2), m, c, :, lane], b_send, b_recv, 8 + 8 * n, *cut)
                for n, cut in enumerate(CUTS_B)]

    def along(slab, full, send, recv, n, start, size):
        lanes = pl.ds(start, size)
        return [
            pltpu.make_async_remote_copy(
                src_ref=slab.at[:, lanes], dst_ref=full.at[plane, chip, core, :, lanes],
                send_sem=send.at[3 * n + step - 1], recv_sem=recv.at[3 * n + step - 1],
                device_id=(rank, (plane + step) % 4), device_id_type=MESH)
            for step in (1, 2, 3)
        ]

    along_a = [along(slab_a, full_a, az_send, az_recv, n, CHUNK_A * n, CHUNK_A) for n in range(chunks_a)]
    along_o = along(slab_o, full_o, bz_send, bz_recv, 0, 0, OUT_LANES)
    along_b = [along(slab_b, full_b, bz_send, bz_recv, 1 + n, *cut) for n, cut in enumerate(CUTS_B)]
    own_b = [pltpu.make_async_copy(slab_b, full_b.at[plane, chip, core], local.at[0]),
             pltpu.make_async_copy(slab_o, full_o.at[plane, chip, core], local.at[1])]
    ends, offset = row_marks(len_ref)

    def widen(values, lanes):
        return jnp.concatenate([values, jnp.zeros((values.shape[0], lanes - values.shape[1]), values.dtype)], axis=1)

    @pl.when(group == 0)
    def _():
        slab_a[...] = widen(w_qkv_ref[...].astype(jnp.bfloat16), GATHERED)
        n_vec, width = vectors_ref.shape[0], tokens_ref.shape[1]
        vectors = jnp.concatenate([vectors_ref[...], jnp.zeros((LANES - n_vec, columns), jnp.float32)], axis=0)
        vectors = vectors.astype(jnp.bfloat16).astype(jnp.float32)
        full_v[pl.ds(chip, 1), pl.ds(core, 1)] = widen(vectors, LANES).T[:columns, :][None, None]
        full_a[pl.ds(plane, 1), pl.ds(chip, 1), pl.ds(core, 1)] = slab_a[...][None, None, None]
        greet(all_partners())
        for copy in along_a[0]:
            copy.start()
        slab_b[:, :width] = w_up_ref[...].astype(jnp.bfloat16)
        slab_b[:, width:] = w_down_ref[...].astype(jnp.bfloat16)
        slab_o[...] = widen(w_out_ref[...].T.astype(jnp.bfloat16), OUT_LANES)
        for copy in own_b:
            copy.start()

        def vec_copy(m, slot, device):
            block = full_v.at[m, core]
            return pltpu.make_async_remote_copy(
                src_ref=block, dst_ref=block, send_sem=v_send.at[slot], recv_sem=v_recv.at[slot],
                device_id=(device, plane), device_id_type=MESH)

        chips = [chip_at(step, chip_x, chip_y) for step in range(4)]
        vec_over = [vec_copy(chip, step - 1, 2 * chips[step] + core) for step in (1, 2, 3)]
        vec_beside = [vec_copy(m, 3 + step, 2 * chip + 1 - core) for step, m in enumerate(chips)]
        for copy in (*vec_over, vec_beside[0]):
            copy.start()
        twice_s[...] = turned_rows(tokens_ref[...], offset)
        for copy in along_a[0]:
            copy.wait()
        for copy in along_a[1]:
            copy.start()
        gather_a[0].first()
        index = lax.broadcasted_iota(jnp.int32, (ROW_LEN, LANES), 0)
        where, segment = segment_of(index, ends, offset)
        start = jnp.where(segment == 0, 0, jnp.where(segment == 1, ends[0], jnp.where(segment == 2, ends[1], ends[2])))
        position = (where - start).astype(jnp.float32)
        lane = lax.broadcasted_iota(jnp.int32, (1, LANES), 1)
        inverse = jnp.exp((lane % (HEAD_DIM // 2)).astype(jnp.float32) * (-2.0 * math.log(10000.0) / HEAD_DIM))
        sign = jnp.where((lane % HEAD_DIM) < (HEAD_DIM // 2), -1.0, 1.0)
        angles = position * inverse
        for copy in along_a[1]:
            copy.wait()
        gather_a[1].first()
        for copies in (along_o, *along_b):
            for copy in copies:
                copy.start()
        cos_ref[...] = jnp.cos(angles)
        for step in range(3):
            vec_over[step].wait()
            vec_beside[step + 1].start()
        gather_a[0].second()
        sin_ref[...] = jnp.sin(angles) * sign
        for copy in vec_beside:
            copy.wait()
        table_t = jnp.concatenate([full_v[m, c] for m in range(4) for c in range(2)], axis=0)
        table_ref[...] = table_t.T[: table_ref.shape[0], :]
        gather_a[1].second()
        gain, shift = table_ref[0:1, :], table_ref[1:2, :]
        for r in range(0, ROW_LEN, 256):
            values = twice_s[r : r + 256, :]
            x_ref[r : r + 256, :] = values.astype(jnp.bfloat16)
            h1_ref[r : r + 256, :] = layer_norm(values, gain, shift).astype(jnp.bfloat16)
        gather_a[0].third()
        gather_a[1].third()
        for gather in gather_a:
            gather.finish()
        for copy in (*own_b, *along_o):
            copy.wait()
        gather_o.first()
        rows = wt_ref.shape[1] // 4
        wt_ref[...] = jnp.concatenate(
            [full_a[j].reshape(width, GATHERED)[:, :rows] for j in range(4)], axis=1)
        first = _half_mask((256, LANES))
        bias = [table_ref[4 + part : 5 + part, :] for part in range(3)]
        for r in range(0, ROW_LEN, 256):
            at = slice(r, r + 256)
            project = nn(h1_ref[at, :], wt_ref[...])
            cosine, sine = cos_ref[at, :], sin_ref[at, :]
            for g in range(width // LANES):
                lanes = slice(g * LANES, (g + 1) * LANES)
                queries = (project[:, lanes] + bias[0][:, lanes]) * (1.0 / math.sqrt(HEAD_DIM))
                keys = project[:, width + g * LANES : width + (g + 1) * LANES] + bias[1][:, lanes]
                q_s[g, at, :] = (queries * cosine + _turn(queries, first) * sine).astype(jnp.bfloat16)
                k_s[g, at, :] = (keys * cosine + _turn(keys, first) * sine).astype(jnp.bfloat16)
                v_s[g, at, :] = (project[:, 2 * width + g * LANES : 2 * width + (g + 1) * LANES]
                                 + bias[2][:, lanes]).astype(jnp.bfloat16)
        for copy in along_b[0]:
            copy.wait()
        gather_b[0].first()
        gather_o.second()

    @pl.when(group == 1)
    def _():
        for copy in along_b[1]:
            copy.wait()
        gather_b[1].first()
        gather_o.third()

    @pl.when(group == 2)
    def _():
        gather_b[0].second()

    @pl.when(group == 4)
    def _():
        gather_b[1].second()
        gather_b[0].third()

    qr_ref[...] = q_s[group]
    kr_ref[...] = k_s[group]
    vr_ref[...] = v_s[group]
    attn_ref[...] = attention_group(q_s[group], kr_ref, v_s[group], same_rest(ends, offset), ot_s, vt_s, lse_ref)

    @pl.when(group == 4)
    def _():
        gather_b[1].third()
        for gather in (gather_o, *gather_b):
            gather.finish()


def head(lengths, tokens, w_qkv_t, w_up_t, w_down_t, w_out, vectors):
    tokens_count, width = tokens.shape
    groups = width // LANES
    columns = w_qkv_t.shape[0]
    col = pl.BlockSpec((tokens_count, LANES), lambda g: (0, g))
    whole = lambda *shape: pl.BlockSpec(shape, lambda g: (0,) * len(shape))
    shape = jax.ShapeDtypeStruct
    bf16, f32 = jnp.bfloat16, jnp.float32
    sems = lambda n: pltpu.SemaphoreType.DMA((n,))
    na, nb = GATHERED // CHUNK_A, 1 + len(CUTS_B)
    return pl.pallas_call(
        head_kernel,
        grid=(groups,),
        in_specs=[pl.BlockSpec(memory_space=pltpu.SMEM), whole(tokens_count, width), whole(*w_qkv_t.shape),
                  whole(columns, width), whole(columns, width), whole(*w_out.shape), whole(*vectors.shape)],
        out_specs=[col] * 4 + [pl.BlockSpec((1, 4, tokens_count), lambda g: (g, 0, 0)),
                               whole(tokens_count, width), whole(tokens_count, width),
                               whole(tokens_count, LANES), whole(tokens_count, LANES),
                               whole(width, 3 * width), whole(16, width), pl.BlockSpec(memory_space=pl.ANY),
                               pl.BlockSpec(memory_space=pl.ANY)],
        out_shape=[shape((tokens_count, width), bf16)] * 4 + [shape((groups, 4, tokens_count), f32)]
        + [shape((tokens_count, width), bf16)] * 2 + [shape((tokens_count, LANES), f32)] * 2
        + [shape((width, 3 * width), bf16), shape((16, width), f32), shape((4, 4, 2, columns, 2 * width), bf16),
           shape((4, 4, 2, columns, OUT_LANES), bf16)],
        scratch_shapes=[
            pltpu.VMEM((4, 4, 2, columns, GATHERED), bf16),
            pltpu.VMEM((4, 2, columns, LANES), f32),
            pltpu.VMEM((tokens_count, width), f32),
            pltpu.VMEM((groups, tokens_count, LANES), bf16),
            pltpu.VMEM((groups, tokens_count, LANES), bf16),
            pltpu.VMEM((groups, tokens_count, LANES), bf16),
            pltpu.VMEM((LANES, tokens_count), f32),
            pltpu.VMEM((LANES, tokens_count), bf16),
            pltpu.VMEM((columns, GATHERED), bf16),
            pltpu.VMEM((columns, 2 * width), bf16),
            pltpu.VMEM((columns, OUT_LANES), bf16),
            sems(8 * na), sems(8 * na), sems(3 * na), sems(3 * na),
            sems(8 * nb), sems(8 * nb), sems(3 * nb), sems(3 * nb), sems(7), sems(7), sems(2),
        ],
        compiler_params=pltpu.CompilerParams(collective_id=2, has_side_effects=True, vmem_limit_bytes=58 << 20),
        name="head",
    )(lengths, tokens, w_qkv_t, w_up_t, w_down_t, w_out, vectors)


def middle_kernel(
    len_ref, count_ref, x_ref, attn_ref, cot_ref, table_ref, full_o_ref, full_b,
    layer_ref, after_grad_ref, attn_grad_ref, parts_ref, out_grad_ref, sums_ref,
    xhat_s, rstd_s, h2_s, h2t_s, dy_s, dyt_s, acc_s, back_s, act_s, pre_s, wt_out_s, w_s, send, recv, local,
):
    step = pl.program_id(0)
    tokens, width = x_ref.shape
    rank, plane, core, chip_x, chip_y = place()
    chip = chip_at(0, chip_x, chip_y)
    late = Gather(lambda m, c, lane: w_s.at[1, :, m, c, :, lane], send, recv, 0, 0, 2 * width)
    loads = [pltpu.make_async_copy(full_b.at[pl.ds(2, 2), chip, core], w_s.at[1, :, chip, core], local.at[0]),
             pltpu.make_async_copy(full_b.at[pl.ds(0, 2)], w_s.at[0], local.at[1])]
    ends, offset = row_marks(len_ref)
    chunk = 256
    cuts = [slice(r, r + chunk) for r in range(0, tokens, chunk)]

    @pl.when(step == 0)
    def _():
        for load in loads:
            load.start()
        greet([(2 * chip + 1 - core, plane)]
              + [(2 * chip_at(other, chip_x, chip_y) + core, plane) for other in (1, 2)])
        loads[0].wait()
        late.first()
        rows = width // 4
        wt_out_s[...] = jnp.concatenate([full_o_ref[p].reshape(width, OUT_LANES)[:, :rows] for p in range(4)], axis=1)
        index = lax.broadcasted_iota(jnp.int32, (tokens, 1), 0)
        _, segment = segment_of(index, ends, offset)
        number = jnp.where(segment == 0, count_ref[0, 0], jnp.where(
            segment == 1, count_ref[0, 1], jnp.where(segment == 2, count_ref[0, 2], count_ref[0, 3])))
        incoming = turned_rows(cot_ref[...], offset) * (1.0 / number.astype(jnp.float32))
        after_grad_ref[...] = incoming
        dy_s[...] = incoming.astype(jnp.bfloat16)
        dyt_s[...] = dy_s[...].T
        sums_ref[...] = jnp.zeros_like(sums_ref)
        sums_ref[8:9, :] = jnp.sum(dy_s[...].astype(jnp.float32), axis=0, keepdims=True)
        gain, shift = table_ref[2:3, :], table_ref[3:4, :]
        for at in cuts:
            after = x_ref[at, :].astype(jnp.float32) + (nn(attn_ref[at, :], wt_out_s[...]) + table_ref[7:8, :])
            acc_s[at, :] = after + table_ref[8:9, :]
            center = after - jnp.mean(after, axis=-1, keepdims=True)
            rstd = lax.rsqrt(jnp.mean(center * center, axis=-1, keepdims=True) + norm_eps)
            xhat = center * rstd
            xhat_s[at, :] = xhat
            rstd_s[at, :] = rstd
            h2_s[at, :] = (xhat * gain + shift).astype(jnp.bfloat16)
        h2t_s[...] = h2_s[...].T
        back_s[...] = jnp.zeros_like(back_s)

    @pl.when(step == 0)
    def _():
        loads[1].wait()
        late.second()

    @pl.when(step == 1)
    def _():
        late.finish()

    def weights(lanes):
        return jnp.concatenate([w_s[step, p, :, :, :, lanes].reshape(width, width) for p in range(2)], axis=1)

    up, down = (weights(slice(part * width, (part + 1) * width)) for part in range(2))
    bias = jnp.concatenate([table_ref[pl.ds(9 + 2 * step + p, 1), :] for p in range(2)], axis=1)

    def products(at):
        return nn(h2_s[at, :], up), nn(dy_s[at, :], down)

    def pointwise(at, pre, act_grad):
        pre = pre + bias
        cdf = 0.5 * (1.0 + lax.erf(pre * (1.0 / math.sqrt(2.0))))
        slope = cdf + pre * (jnp.exp(-0.5 * pre * pre) * (1.0 / math.sqrt(2.0 * math.pi)))
        act_s[at, :] = (pre * cdf).astype(jnp.bfloat16)
        pre_s[at, :] = (act_grad * slope).astype(jnp.bfloat16)

    def collect(at):
        acc_s[at, :] += nt(act_s[at, :], down)
        back_s[at, :] += nt(pre_s[at, :], up)

    held = {}
    for t in range(len(cuts) + 1):
        if t < len(cuts):
            held[t] = products(cuts[t])
        if t >= 1:
            pointwise(cuts[t - 1], *held.pop(t - 1))
            collect(cuts[t - 1])

    @pl.when(step == 0)
    def _():
        late.third()

    for part, (left, right) in enumerate(((h2t_s, pre_s), (dyt_s, act_s))):
        grad = nn(left[...], right[...]).astype(jnp.bfloat16)
        for p in range(2):
            parts_ref[p, :, part * width : (part + 1) * width] = grad[:, p * width : (p + 1) * width]
    bias_sum = jnp.sum(pre_s[...].astype(jnp.float32), axis=0, keepdims=True)
    for p in range(2):
        sums_ref[pl.ds(9 + 2 * step + p, 1), :] = bias_sum[:, p * width : (p + 1) * width]

    @pl.when(step == 1)
    def _():
        layer_ref[...] = pltpu.roll(acc_s[...], offset, 0).astype(jnp.bfloat16)
        gain = table_ref[2:3, :]
        gain_sum = jnp.zeros((1, width), jnp.float32)
        shift_sum = jnp.zeros((1, width), jnp.float32)
        branch_sum = jnp.zeros((1, width), jnp.float32)
        for at in cuts:
            grad, xhat = back_s[at, :], xhat_s[at, :]
            gain_sum += jnp.sum(grad * xhat, axis=0, keepdims=True)
            shift_sum += jnp.sum(grad, axis=0, keepdims=True)
            scaled = grad * gain
            resid = rstd_s[at, :] * (
                scaled - jnp.mean(scaled, axis=-1, keepdims=True)
                - xhat * jnp.mean(scaled * xhat, axis=-1, keepdims=True))
            after_grad = after_grad_ref[at, :] + resid
            after_grad_ref[at, :] = after_grad
            low = after_grad.astype(jnp.bfloat16)
            dy_s[at, :] = low
            branch_sum += jnp.sum(low.astype(jnp.float32), axis=0, keepdims=True)
            attn_grad_ref[at, :] = nt(low, wt_out_s[...]).astype(jnp.bfloat16)
        sums_ref[2:3, :] = gain_sum
        sums_ref[3:4, :] = shift_sum
        sums_ref[7:8, :] = branch_sum
        h2t_s[...] = attn_ref[...].T
        out_grad_ref[...] = nn(h2t_s[...], dy_s[...]).astype(jnp.bfloat16)


def middle(lengths, counts, x, attn, cotangent, table, full_o, full_b):
    tokens, width = x.shape
    columns = full_b.shape[3]
    whole = lambda *shape: pl.BlockSpec(shape, lambda j: (0,) * len(shape))
    smem = pl.BlockSpec(memory_space=pltpu.SMEM)
    shape = jax.ShapeDtypeStruct
    bf16, f32 = jnp.bfloat16, jnp.float32
    flat = pltpu.VMEM((tokens, width), bf16)
    double = pltpu.VMEM((tokens, 2 * width), bf16)
    wide = pltpu.VMEM((tokens, width), f32)
    turned = pltpu.VMEM((width, tokens), bf16)
    sems = lambda n: pltpu.SemaphoreType.DMA((n,))
    return pl.pallas_call(
        middle_kernel,
        grid=(2,),
        in_specs=[smem, smem, whole(tokens, width), whole(tokens, width), whole(tokens, width), whole(16, width),
                  whole(*full_o.shape), pl.BlockSpec(memory_space=pl.ANY)],
        out_specs=[whole(tokens, width), whole(tokens, width), whole(tokens, width),
                   pl.BlockSpec((2, width, 2 * width), lambda j: (j, 0, 0)), whole(width, width), whole(16, width)],
        out_shape=[shape((tokens, width), bf16), shape((tokens, width), f32), shape((tokens, width), bf16),
                   shape((4, width, 2 * width), bf16), shape((width, width), bf16), shape((16, width), f32)],
        scratch_shapes=[wide, pltpu.VMEM((tokens, 1), f32), flat, turned, flat, turned, wide, wide, double, double,
                        pltpu.VMEM((width, width), bf16), pltpu.VMEM((2, 2, 4, 2, columns, 2 * width), bf16),
                        sems(8), sems(8), sems(2)],
        compiler_params=pltpu.CompilerParams(collective_id=3, has_side_effects=True, vmem_limit_bytes=62 << 20),
        name="middle",
    )(lengths, counts, x, attn, cotangent, table, full_o, full_b)


def backward_group(qr_ref, kr_ref, vr_ref, do_ref, attn_ref, lse_ref, same, qt_s, dot_s, kt_s, delta_s, dqt_s, dk_s, dv_s):
    tokens = qr_ref.shape[0]
    qt_s[...] = qr_ref[...].T
    dot_s[...] = do_ref[...].T
    kt_s[...] = kr_ref[...].T
    prod_t = (do_ref[...].astype(jnp.float32) * attn_ref[...].astype(jnp.float32)).T
    for h in range(4):
        delta_s[h : h + 1, :] = jnp.sum(prod_t[h * HEAD_DIM : (h + 1) * HEAD_DIM, :], axis=0, keepdims=True)
    dk_s[...] = jnp.zeros_like(dk_s)
    dv_s[...] = jnp.zeros_like(dv_s)
    row = lax.broadcasted_iota(jnp.int32, (LANES, tokens), 0)
    lane = lax.broadcasted_iota(jnp.int32, (tokens, LANES), 1)
    zero = jnp.zeros((), jnp.bfloat16)
    jobs = attention_jobs(tokens)
    masked, held = {}, {}

    def products(job):
        h, start, width, key_start, key_count = job
        if h not in masked:
            masked[h] = (
                jnp.where(row // HEAD_DIM == h, qt_s[...], zero), jnp.where(row // HEAD_DIM == h, dot_s[...], zero),
                jnp.where(lane // HEAD_DIM == h, qr_ref[...], zero), jnp.where(lane // HEAD_DIM == h, do_ref[...], zero))
        at, keys = slice(start, start + width), slice(key_start, key_start + key_count)
        scores = nn(kr_ref[keys, :], masked[h][0][:, at])
        if start == LONGEST:
            scores = jnp.where(same, scores, masked_score)
        return scores, nn(vr_ref[keys, :], masked[h][1][:, at])

    def finish(job, scores, weight_grad):
        h, start, width, key_start, key_count = job
        at, keys = slice(start, start + width), slice(key_start, key_start + key_count)
        rows = slice(h * HEAD_DIM, (h + 1) * HEAD_DIM)
        soft = jnp.exp(scores - lse_ref[0, h : h + 1, at])
        score_grad = (soft * (weight_grad - delta_s[h : h + 1, at])).astype(jnp.bfloat16)
        dv_s[keys, :] += nn(soft.astype(jnp.bfloat16), masked[h][3][at, :])
        dk_s[keys, :] += nn(score_grad, masked[h][2][at, :])
        dqt_s[rows, at] = nn(kt_s[rows, keys], score_grad)

    for t in range(len(jobs) + 1):
        if t < len(jobs):
            held[t] = products(jobs[t])
        if t >= 1:
            finish(jobs[t - 1], *held.pop(t - 1))


def backward_kernel(
    len_ref, qr_ref, kr_ref, vr_ref, do_ref, attn_ref, lse_ref, cos_ref, sin_ref, parts_ref,
    dq_ref, dk_ref, dv_ref, total_ref, *scratch,
):
    group = pl.program_id(0)
    lanes = parts_ref.shape[-1] // 2
    halves = [stages_of(parts_ref, scratch[7 + SUM_SCRATCH * n : 7 + SUM_SCRATCH * (n + 1)], pl.ds(n * lanes, lanes))
              for n in range(2)]
    dqt_s, dk_s, dv_s = scratch[4:7]

    @pl.when(group == 0)
    def _():
        greet(all_partners())
        halves[0].core_start()
        halves[1].core_start()

    @pl.when(group == 1)
    def _():
        halves[0].core_finish()
        halves[0].chip_start()
        halves[1].core_finish()
        halves[1].chip_start()

    ends, offset = row_marks(len_ref)
    backward_group(qr_ref, kr_ref, vr_ref, do_ref, attn_ref, lse_ref, same_rest(ends, offset), *scratch[:7])
    first = _half_mask(cos_ref.shape)
    cosine, sine = cos_ref[...], sin_ref[...]

    def pull(values):
        return values * cosine + _turn(values * sine, first)

    dq_ref[...] = (pull(dqt_s[...].T) * (1.0 / math.sqrt(HEAD_DIM))).astype(jnp.bfloat16)
    dk_ref[...] = pull(dk_s[...]).astype(jnp.bfloat16)
    dv_ref[...] = dv_s[...].astype(jnp.bfloat16)

    @pl.when(group == 4)
    def _():
        for n in range(2):
            halves[n].chip_finish()
            total_ref[:, :, n * lanes : (n + 1) * lanes] = halves[n].total[...]


def backward(lengths, qr, kr, vr, attn_grad, attn, lse, cosine, sine, parts):
    tokens, width = qr.shape
    groups = width // LANES
    rows, lanes = parts.shape[-2:]
    col = pl.BlockSpec((tokens, LANES), lambda g: (0, g))
    whole = lambda *shape: pl.BlockSpec(shape, lambda g: (0,) * len(shape))
    shape = jax.ShapeDtypeStruct
    bf16, f32 = jnp.bfloat16, jnp.float32
    return pl.pallas_call(
        backward_kernel,
        grid=(groups,),
        in_specs=[pl.BlockSpec(memory_space=pltpu.SMEM)] + [col] * 5
        + [pl.BlockSpec((1, 4, tokens), lambda g: (g, 0, 0)), whole(tokens, LANES), whole(tokens, LANES),
           pl.BlockSpec(memory_space=pl.ANY)],
        out_specs=[col] * 3 + [whole(4, rows, lanes)],
        out_shape=[shape((tokens, width), bf16)] * 3 + [shape((4, rows, lanes), bf16)],
        scratch_shapes=[pltpu.VMEM((LANES, tokens), bf16)] * 3
        + [pltpu.VMEM((8, tokens), f32), pltpu.VMEM((LANES, tokens), f32), pltpu.VMEM((tokens, LANES), f32),
           pltpu.VMEM((tokens, LANES), f32)] + sum_scratch(rows, lanes // 2) * 2,
        compiler_params=pltpu.CompilerParams(collective_id=0, has_side_effects=True, vmem_limit_bytes=58 << 20),
        name="backward",
    )(lengths, qr, kr, vr, attn_grad, attn, lse, cosine, sine, parts)


def row_layout(lengths, counts, row_len):
    lens = lengths[0]
    slots = lens.shape[0]
    order = lax.broadcasted_iota(jnp.int32, (slots, slots), 0)
    upto = lax.broadcasted_iota(jnp.int32, (slots, slots), 1)
    starting = jnp.sum(jnp.where(upto < order, lens[None, :], 0), axis=1)
    slot = lax.broadcasted_iota(jnp.int32, (slots,), 0)
    which = jnp.min(jnp.where(lens == LONGEST, slot, slots))
    offset = jnp.sum(jnp.where(slot == which, starting, 0))
    places = lax.broadcasted_iota(jnp.int32, (row_len,), 0) + offset
    places = jnp.where(places >= row_len, places - row_len, places)
    endings = starting + lens
    segment = jnp.sum((places[:, None] >= endings[None, :]).astype(jnp.int32), axis=1)
    member = segment[:, None] == slot[None, :]
    first_place = jnp.sum(jnp.where(member, starting[None, :], 0), axis=1)
    position = (places - first_place).astype(jnp.float32)
    inverse_count = 1.0 / counts[0].astype(jnp.float32)
    share = jnp.sum(jnp.where(member, inverse_count[None, :], 0.0), axis=1)
    return offset, segment, position, share


def rotary_tables(position):
    lane = lax.broadcasted_iota(jnp.int32, (1, LANES), 1)
    indices = (lane % (HEAD_DIM // 2)).astype(jnp.float32)
    inverse = jnp.exp(indices * (-2.0 * math.log(10000.0) / HEAD_DIM))
    angles = position[:, None] * inverse
    sign = jnp.where((lane % HEAD_DIM) < (HEAD_DIM // 2), -1.0, 1.0)
    return jnp.cos(angles), jnp.sin(angles) * sign


def turn_rows(values, shift):
    twice = jnp.concatenate([values, values], axis=0)
    return lax.dynamic_slice_in_dim(twice, shift, values.shape[0], 0)


def high(left, right):
    return jnp.dot(left, right, precision=lax.Precision.HIGH, preferred_element_type=jnp.float32)


def shards_near(
    tokens, cotangent, lengths, counts,
    w_qkv, w_out, w_up, w_down,
    mom_qkv, mom_out, mom_up, mom_down,
    vectors, vec_first, vec_second,
):
    columns = w_qkv.shape[1]
    weights_t = [w_qkv.T, w_out, w_up.T, w_down.T]
    moments_t = [mom_qkv.T, mom_out, mom_up.T, mom_down.T]
    qr, kr, vr, attn, lse, normed_one, turned, cosine, sine, wt_qkv, table, full_b, full_o = head(
        lengths, tokens, weights_t[0], weights_t[2], weights_t[3], w_out, vectors)
    layer_out, after_grad, attn_grad, parts_b, out_grad, sums = middle(
        lengths, counts, turned, attn, cotangent, table, full_o, full_b)
    dq, dk, dv, total_b = backward(
        lengths, qr, kr, vr, attn_grad, attn, lse, cosine, sine, parts_b.reshape(4, 4, 2, columns, -1))
    results = tail(
        normed_one, dq, dk, dv, out_grad, sums, table, total_b, lengths, moments_t, weights_t,
        (vectors, vec_first, vec_second), wt_qkv, after_grad, turned)
    results = finish([*results, layer_out])
    matrices = [v if x % 4 == 1 else v.T for x, v in enumerate(results[:8])]
    return (results[12], results[11], *matrices, *results[8:11])


def shards_far(
    tokens, cotangent, lengths, counts,
    w_qkv, w_out, w_up, w_down,
    mom_qkv, mom_out, mom_up, mom_down,
    vectors, vec_first, vec_second,
):
    both = ("fsdp", "dp")
    planes = lax.axis_size("fsdp")
    ranks = lax.axis_size("dp")
    row_len, width = tokens.shape
    columns = w_qkv.shape[1]
    old_weights = (w_qkv, w_out, w_up, w_down)
    old_moments = (mom_qkv, mom_out, mom_up, mom_down)
    counts_rows = [w.shape[0] for w in old_weights]
    n_vec = vectors.shape[0]

    slab_a = jnp.concatenate([w_qkv.T, w_out.T, vectors.T], axis=1).astype(jnp.bfloat16)
    slab_b = jnp.concatenate([w_up.T, w_down.T], axis=1).astype(jnp.bfloat16)
    full_a = lax.all_gather(slab_a, both, axis=0, tiled=True).reshape(planes, width, -1)
    full_b = lax.all_gather(slab_b, both, axis=0, tiled=True).reshape(planes, width, -1)
    r0, r1, r2, r3 = counts_rows
    wt_qkv = jnp.concatenate([full_a[j, :, :r0] for j in range(planes)], axis=1)
    wt_out = jnp.concatenate([full_a[j, :, r0 : r0 + r1] for j in range(planes)], axis=1)
    table = full_a[0, :, r0 + r1 :].T.astype(jnp.float32)
    wt_up = jnp.concatenate([full_b[j, :, :r2] for j in range(planes)], axis=1)
    wt_down = jnp.concatenate([full_b[j, :, r2:] for j in range(planes)], axis=1)

    offset, segment, position, share = row_layout(lengths, counts, row_len)
    cosine, sine = rotary_tables(position)
    seg_col, seg_row = segment[:, None], segment[None, :]
    inputs = turn_rows(tokens, offset).astype(jnp.float32)
    incoming = turn_rows(cotangent, offset).astype(jnp.float32) * share[:, None]

    normed_one, pull_one = jax.vjp(layer_norm, inputs, table[0], table[1])
    normed_one = normed_one.astype(jnp.bfloat16)
    project = nn(normed_one, wt_qkv) + table[4:7].reshape(-1)
    qr, kr, vr, attn, lse = attention_forward(project, cosine, sine, seg_col, seg_row)
    after = inputs + (nn(attn, wt_out) + table[7])
    normed_two, pull_two = jax.vjp(layer_norm, after, table[2], table[3])
    normed_two = normed_two.astype(jnp.bfloat16)
    hidden_pre = nn(normed_two, wt_up) + table[9:].reshape(-1)
    hidden, pull_hidden = jax.vjp(gelu_exact, hidden_pre)
    hidden = hidden.astype(jnp.bfloat16)
    layer_out = (after + (nt(hidden, wt_down) + table[8])).astype(jnp.bfloat16)

    grad_low = incoming.astype(jnp.bfloat16)
    grad_t_down = tn(grad_low, hidden)
    pre_grad = pull_hidden(nn(grad_low, wt_down))[0].astype(jnp.bfloat16)
    grad_t_up = tn(normed_two, pre_grad)
    resid_grad, gain_two, shift_two = pull_two(nt(pre_grad, wt_up))
    after_grad = incoming + resid_grad
    branch_low = after_grad.astype(jnp.bfloat16)
    grad_t_out = tn(attn, branch_low)
    attn_grad = nt(branch_low, wt_out).astype(jnp.bfloat16)
    dq, dk, dv = attention_backward(qr, kr, vr, attn_grad, attn, lse, cosine, sine, seg_col, seg_row)
    proj_grad = jnp.concatenate([dq, dk, dv], axis=1)
    grad_t_qkv = tn(normed_one, proj_grad)
    in_grad, gain_one, shift_one = pull_one(nt(proj_grad, wt_qkv))
    input_grad = after_grad + in_grad

    def column_sum(values):
        return jnp.sum(values.astype(jnp.float32), axis=0)

    vector_grad = jnp.concatenate(
        [gain_one[None], shift_one[None], gain_two[None], shift_two[None],
         column_sum(proj_grad).reshape(3, width), column_sum(branch_low)[None], column_sum(grad_low)[None],
         column_sum(pre_grad).reshape(-1, width)],
        axis=0,
    )
    back = jnp.where(offset > 0, row_len - offset, 0)
    layer_out = turn_rows(layer_out, back)
    input_grad = turn_rows(input_grad, back)

    def cut(values, j, rows):
        return values[:, j * rows : (j + 1) * rows]

    parts_b = jnp.stack([jnp.concatenate([cut(grad_t_up, j, r2), cut(grad_t_down, j, r3)], axis=1) for j in range(planes)])
    own_b = lax.psum_scatter(parts_b.reshape(planes * width, -1), both, scatter_dimension=0, tiled=True)
    parts_a = jnp.stack([jnp.concatenate([cut(grad_t_qkv, j, r0), cut(grad_t_out, j, r1), vector_grad.T], axis=1) for j in range(planes)])
    own_a = lax.psum_scatter(parts_a.reshape(planes * width, -1), both, scatter_dimension=0, tiled=True)
    grads_t = (own_a[:, :r0], own_a[:, r0 : r0 + r1], own_b[:, :r2], own_b[:, r2:])
    vector_grad = own_a[:, r0 + r1 :].T
    new_moments_t = [moment_keep * old.T + grad for old, grad in zip(old_moments, grads_t)]

    most = max(counts_rows)
    padded = [jnp.pad(m.astype(jnp.bfloat16), ((0, 0), (0, most - m.shape[1]))) for m in new_moments_t]
    sent = jnp.stack([padded[t % 4] for t in range(planes)])
    mine = lax.all_to_all(sent, "fsdp", 0, 0, tiled=True)
    mine = mine.transpose(1, 0, 2).reshape(columns, planes * most)
    whole = lax.all_gather(mine, "dp", axis=0, tiled=True)
    gram = nt(whole, whole)
    identity = jnp.eye(width, dtype=jnp.float32)
    norm_sq = jnp.trace(gram) + 1e-07
    gram = gram / norm_sq
    factor = None
    for iteration in range(NS_ITERS):
        poly = poly_linear * identity + poly_square * gram + poly_cubic * high(gram, gram)
        factor = poly if factor is None else high(factor, poly)
        if iteration + 1 < NS_ITERS:
            gram = high(high(gram, poly), poly)
    own_rows = lax.dynamic_slice_in_dim(factor, lax.axis_index("dp") * columns, columns, 0) * lax.rsqrt(norm_sq)
    own_orth = high(own_rows, whole.astype(jnp.float32))
    own_orth = own_orth.astype(jnp.bfloat16).reshape(columns, planes, most).transpose(1, 0, 2)
    pieces = lax.all_to_all(own_orth, "fsdp", 0, 0, tiled=True).astype(jnp.float32)

    new_weights = []
    for x, weight_old in enumerate(old_weights):
        rows = weight_old.shape[0]
        scale = muon_rate * math.sqrt(max(1.0, rows * planes / width))
        new_weights.append(weight_old * (1.0 - muon_rate * muon_decay) - scale * pieces[x, :, :rows].T)
    new_first = beta_first * vec_first + (1.0 - beta_first) * vector_grad
    new_second = beta_second * vec_second + (1.0 - beta_second) * vector_grad * vector_grad
    first_fix = 1.0 - beta_first**STEP
    second_fix = 1.0 - beta_second**STEP
    new_vectors = vectors - adam_rate * (new_first / first_fix) / (jnp.sqrt(new_second / second_fix) + adam_eps)
    return (layer_out, input_grad, *[m.T for m in new_moments_t], *new_weights, new_vectors, new_first, new_second)


def solution(mesh):
    rows, cells, table = P(("dp", "fsdp"), None), P("fsdp", "dp"), P(None, "dp")
    near = dict(mesh.shape) == {"dp": 8, "fsdp": 4}
    return jax.shard_map(
        shards_near if near else shards_far,
        mesh=mesh,
        in_specs=(rows,) * 4 + (cells,) * 8 + (table,) * 3,
        out_specs=(rows,) * 2 + (cells,) * 8 + (table,) * 3,
        check_vma=False,
    )
```

```python
import functools
import math

import jax
import jax.numpy as jnp
from jax import lax
from jax.experimental import pallas as pl
from jax.experimental.pallas import tpu as pltpu
from jax.sharding import PartitionSpec as P

HEAD_DIM = 32
NS_ITERS = 5
STEP = 10
LANES = 128
LONGEST = 768

norm_eps = 1e-05
masked_score = -1e30
poly_linear = 3.4445
poly_square = -4.775
poly_cubic = 2.0315
muon_rate = 0.5
muon_decay = 0.01
moment_keep = 0.5
adam_rate = 0.05
beta_first = 0.9
beta_second = 0.999
adam_eps = 1e-08


def layer_norm(values, gain_row, shift_row):
    center = values - jnp.mean(values, axis=-1, keepdims=True)
    spread = jnp.mean(center * center, axis=-1, keepdims=True)
    return center * lax.rsqrt(spread + norm_eps) * gain_row + shift_row


def gelu_exact(values):
    return 0.5 * values * (1.0 + lax.erf(values * (1.0 / math.sqrt(2.0))))


def nn(left, right):
    return jnp.dot(left, right, preferred_element_type=jnp.float32)


def nt(left, right):
    return lax.dot_general(left, right, (((1,), (1,)), ((), ())), preferred_element_type=jnp.float32)


def tn(left, right):
    return lax.dot_general(left, right, (((0,), (0,)), ((), ())), preferred_element_type=jnp.float32)


def _half_mask(shape):
    lane = lax.broadcasted_iota(jnp.int32, shape, 1)
    return (lane % HEAD_DIM) < (HEAD_DIM // 2)


def _turn(values, first):
    half = HEAD_DIM // 2
    left = pltpu.roll(values, LANES - half, 1)
    right = pltpu.roll(values, half, 1)
    return jnp.where(first, left, right)


def attention_forward_kernel(
    q_ref, k_ref, v_ref, cos_ref, sin_ref, segc_ref, segr_ref,
    qr_ref, kr_ref, vr_ref, attn_ref, lse_ref,
    qt_s, vt_s, ot_s,
):
    first = _half_mask(cos_ref.shape)
    cosine, sine = cos_ref[...], sin_ref[...]
    queries = q_ref[...] * (1.0 / math.sqrt(HEAD_DIM))
    qr = (queries * cosine + _turn(queries, first) * sine).astype(jnp.bfloat16)
    keys = k_ref[...]
    kr = (keys * cosine + _turn(keys, first) * sine).astype(jnp.bfloat16)
    vr = v_ref[...].astype(jnp.bfloat16)
    qr_ref[...] = qr
    kr_ref[...] = kr
    vr_ref[...] = vr
    qt_s[...] = qr.T
    vt_s[...] = vr.T
    tokens = qr.shape[0]
    rest = tokens - LONGEST
    row = lax.broadcasted_iota(jnp.int32, (LANES, tokens), 0)
    same = segc_ref[LONGEST:, :] == segr_ref[:, LONGEST:]

    def head(h, carry):
        qth = jnp.where(row // HEAD_DIM == h, qt_s[...], jnp.zeros((), jnp.bfloat16))
        rows = pl.ds(pl.multiple_of(h * HEAD_DIM, HEAD_DIM), HEAD_DIM)

        def block(start, width, key_start, key_count, mask):
            scores = nn(kr_ref[key_start : key_start + key_count, :], qth[:, start : start + width])
            if mask is not None:
                scores = jnp.where(mask, scores, masked_score)
            peak = jnp.max(scores, axis=0, keepdims=True)
            raised = jnp.exp(scores - peak)
            total = jnp.sum(raised, axis=0, keepdims=True)
            out = nn(vt_s[rows, key_start : key_start + key_count], raised.astype(jnp.bfloat16))
            ot_s[rows, start : start + width] = out / total
            lse_ref[0, pl.ds(h, 1), start : start + width] = peak + jnp.log(total)

        for start in range(0, LONGEST, 256):
            block(start, 256, 0, LONGEST, None)
        block(LONGEST, rest, LONGEST, rest, same)
        return carry

    lax.fori_loop(0, LANES // HEAD_DIM, head, 0)
    attn_ref[...] = ot_s[...].T.astype(jnp.bfloat16)


def attention_forward(project, cosine, sine, seg_col, seg_row):
    tokens = project.shape[0]
    width = project.shape[1] // 3
    groups = width // LANES
    col = lambda shift: pl.BlockSpec((tokens, LANES), lambda g, shift=shift: (0, g + shift))
    whole = lambda shape: pl.BlockSpec(shape, lambda g: (0,) * len(shape))
    flops = 4 * (LONGEST**2 + (tokens - LONGEST) ** 2) * 128 * groups * 4
    return pl.pallas_call(
        attention_forward_kernel,
        grid=(groups,),
        in_specs=[col(0), col(groups), col(2 * groups), whole((tokens, LANES)), whole((tokens, LANES)),
                  whole((tokens, 1)), whole((1, tokens))],
        out_specs=[col(0)] * 4 + [pl.BlockSpec((1, 4, tokens), lambda g: (g, 0, 0))],
        out_shape=[jax.ShapeDtypeStruct((tokens, width), jnp.bfloat16)] * 4
        + [jax.ShapeDtypeStruct((groups, 4, tokens), jnp.float32)],
        scratch_shapes=[
            pltpu.VMEM((LANES, tokens), jnp.bfloat16),
            pltpu.VMEM((LANES, tokens), jnp.bfloat16),
            pltpu.VMEM((LANES, tokens), jnp.float32),
        ],
        compiler_params=pltpu.CompilerParams(vmem_limit_bytes=48 << 20),
        cost_estimate=pl.CostEstimate(flops=flops, bytes_accessed=20 << 20, transcendentals=20 << 20),
        name="attention_forward",
    )(project, project, project, cosine, sine, seg_col, seg_row)


def attention_backward_kernel(
    qr_ref, kr_ref, vr_ref, do_ref, attn_ref, lse_ref, cos_ref, sin_ref, segc_ref, segr_ref,
    *rest_refs,
):
    dq_ref, dk_ref, dv_ref = rest_refs[:3]
    qt_s, dot_s, kt_s, delta_s, dqt_s, dk_s, dv_s = rest_refs[3:]
    tokens = qr_ref.shape[0]
    rest = tokens - LONGEST
    qt_s[...] = qr_ref[...].T
    dot_s[...] = do_ref[...].T
    kt_s[...] = kr_ref[...].T
    prod_t = (do_ref[...].astype(jnp.float32) * attn_ref[...].astype(jnp.float32)).T
    for h in range(4):
        delta_s[h : h + 1, :] = jnp.sum(prod_t[h * HEAD_DIM : (h + 1) * HEAD_DIM, :], axis=0, keepdims=True)
    dk_s[...] = jnp.zeros_like(dk_s)
    dv_s[...] = jnp.zeros_like(dv_s)
    row = lax.broadcasted_iota(jnp.int32, (LANES, tokens), 0)
    lane = lax.broadcasted_iota(jnp.int32, (tokens, LANES), 1)
    same = segc_ref[LONGEST:, :] == segr_ref[:, LONGEST:]
    zero = jnp.zeros((), jnp.bfloat16)

    def head(h, carry):
        mine_t = row // HEAD_DIM == h
        mine = lane // HEAD_DIM == h
        qth = jnp.where(mine_t, qt_s[...], zero)
        doth = jnp.where(mine_t, dot_s[...], zero)
        qh = jnp.where(mine, qr_ref[...], zero)
        doh = jnp.where(mine, do_ref[...], zero)
        rows = pl.ds(pl.multiple_of(h * HEAD_DIM, HEAD_DIM), HEAD_DIM)

        def block(start, width, key_start, key_count, mask):
            at = slice(start, start + width)
            keys = slice(key_start, key_start + key_count)
            scores = nn(kr_ref[keys, :], qth[:, at])
            if mask is not None:
                scores = jnp.where(mask, scores, masked_score)
            soft = jnp.exp(scores - lse_ref[0, pl.ds(h, 1), at])
            weight_grad = nn(vr_ref[keys, :], doth[:, at])
            score_grad = (soft * (weight_grad - delta_s[pl.ds(h, 1), at])).astype(jnp.bfloat16)
            dv_s[keys, :] += nn(soft.astype(jnp.bfloat16), doh[at, :])
            dk_s[keys, :] += nn(score_grad, qh[at, :])
            dqt_s[rows, at] = nn(kt_s[rows, keys], score_grad)

        for start in range(0, LONGEST, 256):
            block(start, 256, 0, LONGEST, None)
        block(LONGEST, rest, LONGEST, rest, same)
        return carry

    lax.fori_loop(0, LANES // HEAD_DIM, head, 0)
    first = _half_mask(cos_ref.shape)
    cosine, sine = cos_ref[...], sin_ref[...]

    def pull(values):
        return values * cosine + _turn(values * sine, first)

    dq_ref[...] = (pull(dqt_s[...].T) * (1.0 / math.sqrt(HEAD_DIM))).astype(jnp.bfloat16)
    dk_ref[...] = pull(dk_s[...]).astype(jnp.bfloat16)
    dv_ref[...] = dv_s[...].astype(jnp.bfloat16)


def attention_backward(qr, kr, vr, attn_grad, attn, lse, cosine, sine, seg_col, seg_row):
    tokens, width = qr.shape
    groups = width // LANES
    col = pl.BlockSpec((tokens, LANES), lambda g: (0, g))
    whole = lambda shape: pl.BlockSpec(shape, lambda g: (0,) * len(shape))
    flops = 10 * (LONGEST**2 + (tokens - LONGEST) ** 2) * 128 * groups * 4
    return pl.pallas_call(
        attention_backward_kernel,
        grid=(groups,),
        in_specs=[col] * 5 + [pl.BlockSpec((1, 4, tokens), lambda g: (g, 0, 0)),
                              whole((tokens, LANES)), whole((tokens, LANES)), whole((tokens, 1)), whole((1, tokens))],
        out_specs=[col] * 3,
        out_shape=[jax.ShapeDtypeStruct((tokens, width), jnp.bfloat16)] * 3,
        scratch_shapes=[
            pltpu.VMEM((LANES, tokens), jnp.bfloat16),
            pltpu.VMEM((LANES, tokens), jnp.bfloat16),
            pltpu.VMEM((LANES, tokens), jnp.bfloat16),
            pltpu.VMEM((8, tokens), jnp.float32),
            pltpu.VMEM((LANES, tokens), jnp.float32),
            pltpu.VMEM((tokens, LANES), jnp.float32),
            pltpu.VMEM((tokens, LANES), jnp.float32),
        ],
        compiler_params=pltpu.CompilerParams(vmem_limit_bytes=56 << 20),
        cost_estimate=pl.CostEstimate(flops=flops, bytes_accessed=20 << 20, transcendentals=20 << 20),
        name="attention_backward",
    )(qr, kr, vr, attn_grad, attn, lse, cosine, sine, seg_col, seg_row)


MESH = pl.DeviceIdType.MESH


def place():
    rank, plane = lax.axis_index("dp"), lax.axis_index("fsdp")
    core = rank % 2
    chip_x = (rank // 2) % 2
    chip_y = rank // 4
    return rank, plane, core, chip_x, chip_y


def chip_at(step, chip_x, chip_y):
    other_x = 1 - chip_x if step & 1 else chip_x
    other_y = 1 - chip_y if step & 2 else chip_y
    return 2 * other_y + other_x


def greet(partners):
    barrier = pltpu.get_barrier_semaphore()
    for partner in partners:
        pl.semaphore_signal(barrier, inc=1, device_id=partner, device_id_type=MESH)
    pl.semaphore_wait(barrier, len(partners))


def all_partners():
    rank, plane, core, chip_x, chip_y = place()
    sibling = 2 * chip_at(0, chip_x, chip_y) + 1 - core
    partners = [(sibling, plane)]
    partners += [(2 * chip_at(step, chip_x, chip_y) + core, plane) for step in (1, 2, 3)]
    partners += [(rank, (plane + step) % 4) for step in (1, 2, 3)]
    return partners


class SumStages:
    def __init__(self, parts, scratch, lanes):
        (self.own, self.from_core, self.from_first, self.middle, self.from_second, self.total, self.from_plane,
         self.send, self.recv, self.local) = scratch
        self.parts, self.lanes = parts, lanes
        self.rank, self.plane, self.core, self.chip_x, self.chip_y = place()

    def remote(self, source, target, slot, device):
        return pltpu.make_async_remote_copy(
            src_ref=source, dst_ref=target, send_sem=self.send.at[slot], recv_sem=self.recv.at[slot],
            device_id=device, device_id_type=MESH)

    def device(self, step):
        return (2 * chip_at(step, self.chip_x, self.chip_y) + self.core, self.plane)

    def add(self, left, right):
        return left.astype(jnp.float32) + right.astype(jnp.float32)

    def give_copy(self, source):
        return self.remote(source, self.from_core, 0, (2 * chip_at(0, self.chip_x, self.chip_y) + 1 - self.core, self.plane))

    def core_add(self, give):
        give.wait()
        for j in range(4):
            self.own[j] = self.add(self.own[j], self.from_core[j]).astype(self.own.dtype)

    def core_copies(self):
        load = pltpu.make_async_copy(self.parts.at[:, :, :, self.core, :, self.lanes], self.own, self.local)
        return load, self.give_copy(self.parts.at[:, :, :, 1 - self.core, :, self.lanes])

    def core_start(self):
        load, give = self.core_copies()
        give.start()
        load.start()

    def core_finish(self):
        load, give = self.core_copies()
        load.wait()
        self.core_add(give)

    def first_copies(self):
        return [
            self.remote(self.own.at[pl.ds(0, 2), :, 1 - self.chip_x], self.from_first.at[0], 1, self.device(1)),
            self.remote(self.own.at[pl.ds(2, 2), 1 - self.chip_y], self.from_first.at[1], 2, self.device(2)),
        ]

    def second_copies(self):
        return [
            self.remote(self.middle.at[0, :, 1 - self.chip_y], self.from_second.at[0], 3, self.device(2)),
            self.remote(self.middle.at[1, :, 1 - self.chip_x], self.from_second.at[1], 4, self.device(1)),
        ]

    def chip_start(self):
        for copy in self.first_copies():
            copy.start()

    def chip_turn(self):
        for copy in self.first_copies():
            copy.wait()
        for j in range(2):
            mine = self.own[j, :, pl.ds(self.chip_x, 1)][:, 0]
            self.middle[0, j] = self.add(mine, self.from_first[0, j]).astype(self.middle.dtype)
            mine = self.own[2 + j, pl.ds(self.chip_y, 1)][0]
            self.middle[1, j] = self.add(mine, self.from_first[1, j]).astype(self.middle.dtype)
        for copy in self.second_copies():
            copy.start()

    def chip_finish(self):
        for copy in self.second_copies():
            copy.wait()
        for half, index in ((0, self.chip_y), (1, self.chip_x)):
            for j in range(2):
                mine = self.middle[half, j, pl.ds(index, 1)][0]
                self.total[2 * half + j] = self.add(mine, self.from_second[half, j]).astype(self.total.dtype)

    def plane_copies(self):
        return [
            self.remote(self.total.at[(self.plane + step) % 4], self.from_plane.at[step - 1], 4 + step,
                        (self.rank, (self.plane + step) % 4))
            for step in (1, 2, 3)
        ]

    def plane_start(self):
        for copy in self.plane_copies():
            copy.start()

    def plane_finish(self):
        for copy in self.plane_copies():
            copy.wait()
        value = self.total[pl.ds(self.plane, 1)][0].astype(jnp.float32)
        for slot in range(3):
            value = value + self.from_plane[slot].astype(jnp.float32)
        return value


def sum_scratch(rows, lanes, dtype=jnp.bfloat16):
    return [
        pltpu.VMEM((4, 2, 2, rows, lanes), dtype),
        pltpu.VMEM((4, 2, 2, rows, lanes), dtype),
        pltpu.VMEM((2, 2, 2, rows, lanes), dtype),
        pltpu.VMEM((2, 2, 2, rows, lanes), dtype),
        pltpu.VMEM((2, 2, rows, lanes), dtype),
        pltpu.VMEM((4, rows, lanes), dtype),
        pltpu.VMEM((3, rows, lanes), dtype),
        pltpu.SemaphoreType.DMA((8,)),
        pltpu.SemaphoreType.DMA((8,)),
        pltpu.SemaphoreType.DMA,
    ]


SUM_SCRATCH = 10


def table_sum(table_ref, table_out, from_core, from_chip, from_plane, held, send, recv):
    rank, plane, core, chip_x, chip_y = place()
    chip = chip_at(0, chip_x, chip_y)

    def remote(source, target, slot, device):
        return pltpu.make_async_remote_copy(
            src_ref=source, dst_ref=target, send_sem=send.at[slot], recv_sem=recv.at[slot],
            device_id=device, device_id_type=MESH)

    give = remote(table_ref.at[:, 1 - core], from_core, 0, (2 * chip + 1 - core, plane))
    give.start()
    yield
    give.wait()
    held[...] = table_ref[:, pl.ds(core, 1)][:, 0] + from_core[...]
    across = [remote(held.at[chip_at(step, chip_x, chip_y)], from_chip.at[step - 1], step,
                     (2 * chip_at(step, chip_x, chip_y) + core, plane)) for step in (1, 2, 3)]
    for copy in across:
        copy.start()
    yield
    for copy in across:
        copy.wait()
    own = held[pl.ds(chip, 1)][0] + from_chip[0] + from_chip[1] + from_chip[2]
    table_out[...] = own
    along = [remote(table_out, from_plane.at[step - 1], 3 + step, (rank, (plane + step) % 4)) for step in (1, 2, 3)]
    for copy in along:
        copy.start()
    yield
    for copy in along:
        copy.wait()
    table_out[...] = own + from_plane[0] + from_plane[1] + from_plane[2]
    yield


class Gather:
    def __init__(self, at, send, recv, base, parts):
        rank, plane, core, chip_x, chip_y = place()
        every, low, high = parts
        chips = [chip_at(step, chip_x, chip_y) for step in range(4)]
        over = [2 * chip + core for chip in chips]

        def copy(chip, lanes, slot, device):
            block = at(chip, core, lanes)
            return pltpu.make_async_remote_copy(
                src_ref=block, dst_ref=block, send_sem=send.at[base + slot], recv_sem=recv.at[base + slot],
                device_id=(device, plane), device_id_type=MESH)

        self.to_x, self.to_y = copy(chips[0], every, 0, over[1]), copy(chips[0], every, 1, over[2])
        self.on_y, self.on_x = copy(chips[1], low, 2, over[2]), copy(chips[2], high, 3, over[1])
        self.beside = [copy(chip, every, 4 + step, 2 * chips[0] + 1 - core) for step, chip in enumerate(chips)]

    def first(self):
        self.to_x.start()
        self.to_y.start()
        self.beside[0].start()

    def second(self):
        self.to_x.wait_recv()
        self.on_y.start()
        self.beside[1].start()
        self.to_y.wait_recv()
        self.on_x.start()
        self.beside[2].start()

    def third(self):
        self.on_y.wait_recv()
        self.on_x.wait_recv()
        self.beside[3].start()

    def finish(self):
        for copy in (self.to_x, self.to_y, self.on_y, self.on_x):
            copy.wait_send()
        for copy in self.beside:
            copy.wait()


def split(values):
    top = values.astype(jnp.bfloat16)
    return top, (values - top.astype(jnp.float32)).astype(jnp.bfloat16)


def put_left(ref, values):
    width = values.shape[1]
    top, low = split(values)
    ref[:, :width] = top
    ref[:, width : 2 * width] = top
    ref[:, 2 * width :] = low


def put_right(ref, values):
    width = values.shape[0]
    top, low = split(values)
    ref[:width, :] = top
    ref[width : 2 * width, :] = low
    ref[2 * width :, :] = top


def tiles_of(width):
    first = width % 256
    edges = ([0] if first else []) + list(range(first, width + 1, 256))
    return list(zip(edges[:-1], edges[1:]))


def symmetric_product(out, left, right, tiles):
    for start, stop in tiles:
        block = nn(left[:stop, :], right[:, start:stop])
        out[:stop, start:stop] = block
        if start:
            out[start:stop, :start] = block[:start, :].T


def orthogonal_rows(whole, mine, gram, poly, temp, factor, left_gram, left_temp, right, write):
    width = gram.shape[0]
    tiles = tiles_of(width)
    parts = [whole[j].reshape(width, whole.shape[-1]) for j in range(4)]
    for start, stop in tiles:
        block = sum(nt(part[:stop, :], part[start:stop, :]) for part in parts)
        gram[:stop, start:stop] = block
        if start:
            gram[start:stop, :start] = block[:start, :].T
    diagonal = lax.broadcasted_iota(jnp.int32, (width, width), 0) == lax.broadcasted_iota(jnp.int32, (width, width), 1)
    norm_sq = jnp.sum(jnp.sum(jnp.where(diagonal, gram[...], 0.0), axis=1, keepdims=True), axis=0, keepdims=True) + 1e-07
    gram[...] = gram[...] / norm_sq

    def polynomial():
        put_left(left_gram, gram[...])
        put_right(right, gram[...])
        symmetric_product(temp, left_gram, right, tiles)
        poly[...] = jnp.where(diagonal, poly_linear, 0.0) + poly_square * gram[...] + poly_cubic * temp[...]
        put_right(right, poly[...])

    def next_gram():
        symmetric_product(temp, left_gram, right, tiles)
        put_left(left_temp, temp[...])
        symmetric_product(gram, left_temp, right, tiles)

    polynomial()
    factor[...] = poly[...]

    def iteration(step, carry):
        next_gram()
        polynomial()
        put_left(left_temp, factor[...])
        symmetric_product(factor, left_temp, right, tiles)
        return carry

    lax.fori_loop(0, NS_ITERS - 2, iteration, 0)
    next_gram()
    put_right(right, gram[...])
    rows = factor[mine, :]

    def thin(values):
        put_left(left_temp.at[: values.shape[0], :], values)
        return nn(left_temp[: values.shape[0], :], right[...])

    once = thin(rows)
    twice = thin(once)
    rows = (poly_linear * rows + poly_square * once + poly_cubic * twice) * lax.rsqrt(norm_sq)
    top, low = split(rows)
    for j, part in enumerate(parts):
        write(j, nn(top, part) + nn(low, part))


class PlaneStage:
    def __init__(self, total, from_plane, send, recv):
        rank, self.plane = place()[:2]
        self.total, self.from_plane = total, from_plane
        self.copies = [
            pltpu.make_async_remote_copy(
                src_ref=total.at[(self.plane + step) % 4], dst_ref=from_plane.at[step - 1],
                send_sem=send.at[step - 1], recv_sem=recv.at[step - 1],
                device_id=(rank, (self.plane + step) % 4), device_id_type=MESH)
            for step in (1, 2, 3)
        ]

    def start(self):
        for copy in self.copies:
            copy.start()

    def finish(self):
        for copy in self.copies:
            copy.wait()
        value = self.total[pl.ds(self.plane, 1)][0].astype(jnp.float32)
        for slot in range(3):
            value = value + self.from_plane[slot].astype(jnp.float32)
        return value


MATRIX_OF = (1, 0, 2, 3)
LANES_OF = (256, 512, 640, 640)


def tail_kernel(
    h1_ref, dq_ref, dk_ref, dv_ref, out_grad_ref, sums_ref, table_ref, own_up_ref, total_b_ref, len_ref,
    *refs,
):
    moments, weights, small, (wt_hbm, after_hbm, x_hbm) = refs[0:4], refs[4:8], refs[8:11], refs[11:14]
    new_moments, new_weights, new_small, input_grad_ref = refs[14:18], refs[18:22], refs[22:25], refs[25]
    table_out, pieces = refs[26:28]
    refs = refs[28:]
    stages = SumStages(None, refs[:SUM_SCRATCH], None)
    refs = refs[SUM_SCRATCH:]
    table_scratch, refs = refs[:6], refs[6:]
    blocks, whole, gram, poly, temp, factor, left_gram, left_temp, right, from_plane_b = refs[:10]
    plane_send, plane_recv, gather_send, gather_recv, back_send, back_recv, b_send, b_recv, loads = refs[10:19]
    give_s, tiles_s, h1t_s, wt_s, after_s, x_s = refs[19:]
    rank, plane, core, chip_x, chip_y = place()
    chip = chip_at(0, chip_x, chip_y)
    columns, lanes = blocks.shape[1:]
    tokens, width = h1_ref.shape
    rows_qkv, rows_out = moments[0].shape[1], moments[1].shape[0]
    last_b = PlaneStage(total_b_ref, from_plane_b, b_send, b_recv)
    loading = [pltpu.make_async_copy(source, target, loads.at[n])
               for n, (source, target) in enumerate(((wt_hbm, wt_s), (after_hbm, after_s), (x_hbm, x_s)))]
    for copy in loading:
        copy.start()
    h1t_s[...] = h1_ref[...].T

    @pl.when(plane < 2)
    def _():
        whole[...] = jnp.zeros_like(whole)

    greet(all_partners())
    last_b.start()

    def half(which, target):
        starts = [pl.multiple_of(columns * (2 * m + which), 16) for m in range(4)]
        left = jnp.concatenate([h1t_s[pl.ds(start, columns), :] for start in starts], axis=0)
        qkv = jnp.concatenate([nn(left, ref[...]).astype(jnp.bfloat16) for ref in (dq_ref, dk_ref, dv_ref)], axis=1)
        out = jnp.concatenate([out_grad_ref[pl.ds(start, columns), :] for start in starts], axis=0)
        for j in range(4):
            both = jnp.concatenate(
                [qkv[:, j * rows_qkv : (j + 1) * rows_qkv], out[:, j * rows_out : (j + 1) * rows_out]], axis=1)
            target[j] = both.reshape(2, 2, columns, lanes)

    half(1 - core, give_s)
    give = stages.give_copy(give_s)
    give.start()
    half(core, stages.own)
    stages.core_add(give)
    stages.chip_start()

    def momentum(x, gradient):
        rows = gradient.shape[1]
        slot = MATRIX_OF.index(x)
        if x == 1:
            new = moment_keep * moments[x][...].T + gradient
            new_moments[x][...] = new.T
        else:
            new = moment_keep * moments[x][...] + gradient
            new_moments[x][...] = new
        blocks[slot, :, :rows] = new.astype(jnp.bfloat16)
        if rows < lanes:
            blocks[slot, :, rows:] = jnp.zeros((columns, lanes - rows), jnp.bfloat16)

    def out_copy(step, target):
        part = pl.ds(0, LANES_OF[target])
        return pltpu.make_async_remote_copy(
            src_ref=blocks.at[target, :, part], dst_ref=whole.at[plane, chip, core, :, part],
            send_sem=plane_send.at[step - 1], recv_sem=plane_recv.at[step - 1],
            device_id=(rank, (plane + step) % 4), device_id_type=MESH)

    def when_target(targets, act):
        for step in (1, 2, 3):
            for target in targets:
                @pl.when((plane + step) % 4 == target)
                def _():
                    act(out_copy(step, target))

    def place_own(target):
        part = LANES_OF[target]
        whole[target, pl.ds(chip, 1), pl.ds(core, 1), :, :part] = blocks[target, :, :part][None, None]

    def gather_of(target):
        part = pl.ds(0, LANES_OF[target])
        return Gather(lambda m, c, planes: whole.at[planes, m, c, :, part], gather_send, gather_recv, 0, lane_parts(0, 4))

    def arrived(target):
        for step in (1, 2, 3):
            out_copy(step, target).wait_recv()

    for copy in loading:
        copy.wait()
    ends, offset = row_marks(len_ref)
    gain = table_ref[0:1, :]
    gain_sum = jnp.zeros((1, width), jnp.float32)
    shift_sum = jnp.zeros((1, width), jnp.float32)
    for r in range(0, tokens, 256):
        at = slice(r, r + 256)
        grad = sum(nt(ref[at, :], wt_s[:, part * width : (part + 1) * width])
                   for part, ref in enumerate((dq_ref, dk_ref, dv_ref)))
        values = x_s[at, :].astype(jnp.float32)
        center = values - jnp.mean(values, axis=-1, keepdims=True)
        rstd = lax.rsqrt(jnp.mean(center * center, axis=-1, keepdims=True) + norm_eps)
        xhat = center * rstd
        gain_sum += jnp.sum(grad * xhat, axis=0, keepdims=True)
        shift_sum += jnp.sum(grad, axis=0, keepdims=True)
        scaled = grad * gain
        after_s[at, :] += rstd * (scaled - jnp.mean(scaled, axis=-1, keepdims=True)
                                  - xhat * jnp.mean(scaled * xhat, axis=-1, keepdims=True))
        if r == 256:
            momentum(2, own_up_ref[...])
            momentum(3, last_b.finish())
            when_target((2, 3), lambda copy: copy.start())
    vector = jnp.concatenate(
        [gain_sum, shift_sum, sums_ref[2:4, :]]
        + [jnp.sum(ref[...].astype(jnp.float32), axis=0, keepdims=True) for ref in (dq_ref, dk_ref, dv_ref)]
        + [sums_ref[7:16, :]], axis=0)
    for block in range(8):
        part = vector[:, block * columns : (block + 1) * columns]
        tiles_s[block // 2, block % 2] = jnp.concatenate(
            [part, jnp.zeros((16, LANES - columns), jnp.float32)], axis=1)
    adding = table_sum(tiles_s, table_out, *table_scratch)
    stages.chip_turn()
    next(adding)
    input_grad_ref[...] = pltpu.roll(after_s[...], offset, 0)
    stages.chip_finish()
    stages.plane_start()
    next(adding)
    for target in (2, 3):
        @pl.when(plane == target)
        def _():
            place_own(target)
            arrived(target)
            gather_of(target).first()
    next(adding)
    gradient = stages.plane_finish()
    momentum(0, gradient[:, :rows_qkv])
    momentum(1, gradient[:, rows_qkv : rows_qkv + rows_out])
    when_target((0, 1), lambda copy: copy.start())
    for target in (2, 3):
        @pl.when(plane == target)
        def _():
            gather = gather_of(target)
            gather.second()
            gather.third()
            gather.finish()
    next(adding)
    first_fix = 1.0 - beta_first**STEP
    second_fix = 1.0 - beta_second**STEP
    n_vec = small[0].shape[0]
    vector_grad = table_out[:n_vec, :columns]
    vectors, vec_first, vec_second = (ref[...] for ref in small)
    new_first = beta_first * vec_first + (1.0 - beta_first) * vector_grad
    new_second = beta_second * vec_second + (1.0 - beta_second) * vector_grad * vector_grad
    new_small[0][...] = vectors - adam_rate * (new_first / first_fix) / (jnp.sqrt(new_second / second_fix) + adam_eps)
    new_small[1][...] = new_first
    new_small[2][...] = new_second
    for target in (0, 1):
        @pl.when(plane == target)
        def _():
            place_own(target)
            arrived(target)
            gather = gather_of(target)
            gather.first()
            gather.second()
            gather.third()
            gather.finish()
    when_target((0, 1, 2, 3), lambda copy: copy.wait_send())

    def write(j, values):
        blocks[j] = values.astype(jnp.bfloat16)

    orthogonal_rows(whole, pl.ds(pl.multiple_of(rank * columns, 8), columns), gram, poly, temp, factor,
                    left_gram, left_temp, right, write)

    def home_copy(step, source):
        part = pl.ds(0, LANES_OF[source])
        return pltpu.make_async_remote_copy(
            src_ref=blocks.at[(plane + step) % 4, :, part], dst_ref=pieces.at[source, :, part],
            send_sem=back_send.at[step - 1], recv_sem=back_recv.at[step - 1],
            device_id=(rank, (plane + step) % 4), device_id_type=MESH)

    for source in range(4):
        @pl.when(plane == source)
        def _():
            for step in (1, 2, 3):
                home_copy(step, source).start()
            pieces[source] = blocks[source]

    def update(x):
        rows = moments[x].shape[0 if x == 1 else 1]
        scale = muon_rate * math.sqrt(max(1.0, rows * 4 / width))
        change = pieces[MATRIX_OF.index(x), :, :rows].astype(jnp.float32)
        new_weights[x][...] = (weights[x][...] * (1.0 - muon_rate * muon_decay)
                               - scale * (change.T if x == 1 else change))

    for source in (2, 3, 0, 1):
        for step in (1, 2, 3):
            @pl.when((plane + 4 - source) % 4 == step)
            def _():
                home_copy(step, source).wait_recv()
        update(MATRIX_OF[source])
    for source in range(4):
        @pl.when(plane == source)
        def _():
            for step in (1, 2, 3):
                home_copy(step, source).wait_send()


def tail(h1, dq, dk, dv, out_grad, sums, table, own_up, total_b, lengths, moments, weights, small, wt_qkv, after_grad, x):
    tokens, width = h1.shape
    rows = width // 8
    vmem = pl.BlockSpec(memory_space=pltpu.VMEM)
    hbm = pl.BlockSpec(memory_space=pl.ANY)
    tile = (16, LANES)
    most = max(moments[n].shape[1] for n in (0, 2, 3))
    shape = jax.ShapeDtypeStruct
    f32, bf16 = jnp.float32, jnp.bfloat16
    square = pltpu.VMEM((width, width), f32)
    sems = lambda n: pltpu.SemaphoreType.DMA((n,))
    lanes_b = total_b.shape[-1]
    return pl.pallas_call(
        tail_kernel,
        in_specs=[vmem] * 9 + [pl.BlockSpec(memory_space=pltpu.SMEM)] + [vmem] * 11 + [hbm] * 3,
        out_specs=[vmem] * 12,
        out_shape=[shape(v.shape, f32) for v in (*moments, *weights, *small)] + [shape((tokens, width), f32)],
        scratch_shapes=[pltpu.VMEM(tile, f32), pltpu.VMEM((4, rows, most), bf16)] + sum_scratch(rows, most)
        + [pltpu.VMEM((4, *tile), f32), pltpu.VMEM((3, *tile), f32),
           pltpu.VMEM((3, *tile), f32), pltpu.VMEM((4, *tile), f32), sems(7), sems(7)]
        + [pltpu.VMEM((4, rows, most), bf16), pltpu.VMEM((4, 4, 2, rows, most), bf16),
           square, square, square, square,
           pltpu.VMEM((width, 3 * width), bf16), pltpu.VMEM((width, 3 * width), bf16),
           pltpu.VMEM((3 * width, width), bf16), pltpu.VMEM((3, rows, lanes_b), bf16)]
        + [sems(3), sems(3), sems(8), sems(8), sems(3), sems(3), sems(3), sems(3), sems(3)]
        + [pltpu.VMEM((4, 2, 2, rows, most), bf16), pltpu.VMEM((4, 2, *tile), f32), pltpu.VMEM((width, tokens), bf16),
           pltpu.VMEM((width, 3 * width), bf16), pltpu.VMEM((tokens, width), f32), pltpu.VMEM((tokens, width), bf16)],
        compiler_params=pltpu.CompilerParams(collective_id=1, has_side_effects=True, vmem_limit_bytes=60 << 20),
        name="tail",
    )(h1, dq, dk, dv, out_grad, sums, table, own_up, total_b, lengths, *moments, *weights, *small, wt_qkv, after_grad, x)


def finish_kernel(*refs):
    count = len(refs) // 3
    sources, targets, held, loads, stores = refs[:count], refs[count : 2 * count], refs[2 * count : -2], refs[-2], refs[-1]
    loading, storing = [], []
    for n in range(count):
        rows = sources[n].shape[0]
        parts = 4 if rows >= ROW_LEN else 1
        for p in range(parts):
            at = pl.ds(p * (rows // parts), rows // parts)
            slot = len(loading)
            loading.append(pltpu.make_async_copy(sources[n].at[at], held[n].at[at], loads.at[slot]))
            storing.append(pltpu.make_async_copy(held[n].at[at], targets[n].at[at], stores.at[slot]))
    for copy in loading:
        copy.start()
    for load, store in zip(loading, storing):
        load.wait()
        store.start()
    for copy in storing:
        copy.wait()


def finish(values):
    hbm = pl.BlockSpec(memory_space=pl.ANY)
    count = len(values)
    copies = sum(4 if x.shape[0] >= ROW_LEN else 1 for x in values)
    return pl.pallas_call(
        finish_kernel,
        in_specs=[hbm] * count,
        out_specs=[hbm] * count,
        out_shape=[jax.ShapeDtypeStruct(x.shape, x.dtype) for x in values],
        scratch_shapes=[pltpu.VMEM(x.shape, x.dtype) for x in values]
        + [pltpu.SemaphoreType.DMA((copies,)), pltpu.SemaphoreType.DMA((copies,))],
        compiler_params=pltpu.CompilerParams(vmem_limit_bytes=62 << 20),
        name="finish",
    )(*values)


def lane_parts(start, size):
    half = size // 2
    return pl.ds(start, size), pl.ds(start, half), pl.ds(start + half, half)


ROW_LEN = 1024
GATHERED = 512
CHUNK_A = 256
OUT_LANES = 256
CUTS_B = ((0, 512), (512, 768))


def row_marks(len_ref):
    ends = [len_ref[0, 0]]
    for slot in (1, 2):
        ends.append(ends[-1] + len_ref[0, slot])
    starts = [0, *ends]
    offset = starts[3]
    for slot in (2, 1, 0):
        offset = jnp.where(len_ref[0, slot] == LONGEST, starts[slot], offset)
    return ends, offset


def segment_of(index, ends, offset):
    where = index + offset
    where = jnp.where(where >= ROW_LEN, where - ROW_LEN, where)
    segment = sum((where >= end).astype(jnp.int32) for end in ends)
    return where, segment


def turned_rows(values, offset):
    return pltpu.roll(values.astype(jnp.float32), jnp.where(offset > 0, ROW_LEN - offset, 0), 0)


def same_rest(ends, offset):
    rest = ROW_LEN - LONGEST
    columns = lax.broadcasted_iota(jnp.int32, (rest, rest), 0) + LONGEST
    rows = lax.broadcasted_iota(jnp.int32, (rest, rest), 1) + LONGEST
    return segment_of(columns, ends, offset)[1] == segment_of(rows, ends, offset)[1]


def attention_jobs(tokens):
    blocks = [(start, 256, 0, LONGEST) for start in range(0, LONGEST, 256)] + [(LONGEST, tokens - LONGEST, LONGEST, tokens - LONGEST)]
    return [(h, *block) for h in range(LANES // HEAD_DIM) for block in blocks]


def attention_group(q, k_ref, v, same, ot_s, vt_s, lse_ref):
    tokens = q.shape[0]
    qt = q.T
    vt_s[...] = v.T
    row = lax.broadcasted_iota(jnp.int32, qt.shape, 0)
    jobs = attention_jobs(tokens)
    queries, scores, soft = {}, {}, {}

    def score(job):
        h, start, width, key_start, key_count = job
        if h not in queries:
            queries[h] = jnp.where(row // HEAD_DIM == h, qt, jnp.zeros((), jnp.bfloat16))
        out = nn(k_ref[key_start : key_start + key_count, :], queries[h][:, start : start + width])
        return jnp.where(same, out, masked_score) if start == LONGEST else out

    def soften(values):
        peak = jnp.max(values, axis=0, keepdims=True)
        raised = jnp.exp(values - peak)
        return raised.astype(jnp.bfloat16), peak, jnp.sum(raised, axis=0, keepdims=True)

    def collect(job, raised, peak, total):
        h, start, width, key_start, key_count = job
        rows = slice(h * HEAD_DIM, (h + 1) * HEAD_DIM)
        out = nn(vt_s[rows, key_start : key_start + key_count], raised)
        ot_s[rows, start : start + width] = out / total
        lse_ref[0, h : h + 1, start : start + width] = peak + jnp.log(total)

    count = len(jobs)
    for t in range(count + 2):
        if t < count:
            scores[t] = score(jobs[t])
        if 0 <= t - 1 < count:
            soft[t - 1] = soften(scores.pop(t - 1))
        if 0 <= t - 2:
            collect(jobs[t - 2], *soft.pop(t - 2))
    return ot_s[...].T.astype(jnp.bfloat16)


def head_kernel(
    len_ref, tokens_ref, w_qkv_ref, w_up_ref, w_down_ref, w_out_ref, vectors_ref,
    qr_ref, kr_ref, vr_ref, attn_ref, lse_ref, h1_ref, x_ref, cos_ref, sin_ref, wt_ref, table_ref, full_b, full_o,
    full_a, full_v, twice_s, q_s, k_s, v_s, ot_s, vt_s, slab_a, slab_b, slab_o,
    a_send, a_recv, az_send, az_recv, b_send, b_recv, bz_send, bz_recv, v_send, v_recv, local,
):
    group = pl.program_id(0)
    rank, plane, core, chip_x, chip_y = place()
    chip = chip_at(0, chip_x, chip_y)
    columns = slab_a.shape[0]
    chunks_a = GATHERED // CHUNK_A
    gather_a = [Gather(lambda m, c, lane: full_a.at[:, m, c, :, lane], a_send, a_recv, 8 * n,
                       lane_parts(CHUNK_A * n, CHUNK_A))
                for n in range(chunks_a)]
    gather_o = Gather(lambda m, c, lane: full_o.at[:, m, c, :, lane], b_send, b_recv, 0, lane_parts(0, OUT_LANES))
    gather_b = [Gather(lambda m, c, lane: full_b.at[pl.ds(0, 2), m, c, :, lane], b_send, b_recv, 8 + 8 * n,
                       lane_parts(*cut))
                for n, cut in enumerate(CUTS_B)]

    def along(slab, full, send, recv, n, start, size):
        lanes = pl.ds(start, size)
        return [
            pltpu.make_async_remote_copy(
                src_ref=slab.at[:, lanes], dst_ref=full.at[plane, chip, core, :, lanes],
                send_sem=send.at[3 * n + step - 1], recv_sem=recv.at[3 * n + step - 1],
                device_id=(rank, (plane + step) % 4), device_id_type=MESH)
            for step in (1, 2, 3)
        ]

    along_a = [along(slab_a, full_a, az_send, az_recv, n, CHUNK_A * n, CHUNK_A) for n in range(chunks_a)]
    along_o = along(slab_o, full_o, bz_send, bz_recv, 0, 0, OUT_LANES)
    along_b = [along(slab_b, full_b, bz_send, bz_recv, 1 + n, *cut) for n, cut in enumerate(CUTS_B)]
    own_b = [pltpu.make_async_copy(slab_b, full_b.at[plane, chip, core], local.at[0]),
             pltpu.make_async_copy(slab_o, full_o.at[plane, chip, core], local.at[1])]
    ends, offset = row_marks(len_ref)

    def widen(values, lanes):
        return jnp.concatenate([values, jnp.zeros((values.shape[0], lanes - values.shape[1]), values.dtype)], axis=1)

    @pl.when(group == 0)
    def _():
        slab_a[...] = widen(w_qkv_ref[...].astype(jnp.bfloat16), GATHERED)
        n_vec, width = vectors_ref.shape[0], tokens_ref.shape[1]
        vectors = jnp.concatenate([vectors_ref[...], jnp.zeros((LANES - n_vec, columns), jnp.float32)], axis=0)
        vectors = vectors.astype(jnp.bfloat16).astype(jnp.float32)
        full_v[pl.ds(chip, 1), pl.ds(core, 1)] = widen(vectors, LANES).T[:columns, :][None, None]
        full_a[pl.ds(plane, 1), pl.ds(chip, 1), pl.ds(core, 1)] = slab_a[...][None, None, None]
        greet(all_partners())
        for copy in along_a[0]:
            copy.start()
        slab_b[:, :width] = w_up_ref[...].astype(jnp.bfloat16)
        slab_b[:, width:] = w_down_ref[...].astype(jnp.bfloat16)
        slab_o[...] = widen(w_out_ref[...].T.astype(jnp.bfloat16), OUT_LANES)
        for copy in own_b:
            copy.start()

        def vec_copy(m, slot, device):
            block = full_v.at[m, core]
            return pltpu.make_async_remote_copy(
                src_ref=block, dst_ref=block, send_sem=v_send.at[slot], recv_sem=v_recv.at[slot],
                device_id=(device, plane), device_id_type=MESH)

        chips = [chip_at(step, chip_x, chip_y) for step in range(4)]
        vec_over = [vec_copy(chip, step - 1, 2 * chips[step] + core) for step in (1, 2, 3)]
        vec_beside = [vec_copy(m, 3 + step, 2 * chip + 1 - core) for step, m in enumerate(chips)]
        for copy in (*vec_over, vec_beside[0]):
            copy.start()
        twice_s[...] = turned_rows(tokens_ref[...], offset)
        for copy in along_a[0]:
            copy.wait()
        for copy in along_a[1]:
            copy.start()
        gather_a[0].first()
        index = lax.broadcasted_iota(jnp.int32, (ROW_LEN, LANES), 0)
        where, segment = segment_of(index, ends, offset)
        start = jnp.where(segment == 0, 0, jnp.where(segment == 1, ends[0], jnp.where(segment == 2, ends[1], ends[2])))
        position = (where - start).astype(jnp.float32)
        lane = lax.broadcasted_iota(jnp.int32, (1, LANES), 1)
        inverse = jnp.exp((lane % (HEAD_DIM // 2)).astype(jnp.float32) * (-2.0 * math.log(10000.0) / HEAD_DIM))
        sign = jnp.where((lane % HEAD_DIM) < (HEAD_DIM // 2), -1.0, 1.0)
        angles = position * inverse
        for copy in along_a[1]:
            copy.wait()
        gather_a[1].first()
        for copies in (along_o, *along_b):
            for copy in copies:
                copy.start()
        cos_ref[...] = jnp.cos(angles)
        for step in range(3):
            vec_over[step].wait()
            vec_beside[step + 1].start()
        gather_a[0].second()
        sin_ref[...] = jnp.sin(angles) * sign
        for copy in vec_beside:
            copy.wait()
        table_t = jnp.concatenate([full_v[m, c] for m in range(4) for c in range(2)], axis=0)
        table_ref[...] = table_t.T[: table_ref.shape[0], :]
        gather_a[1].second()
        gain, shift = table_ref[0:1, :], table_ref[1:2, :]
        for r in range(0, ROW_LEN, 256):
            values = twice_s[r : r + 256, :]
            x_ref[r : r + 256, :] = values.astype(jnp.bfloat16)
            h1_ref[r : r + 256, :] = layer_norm(values, gain, shift).astype(jnp.bfloat16)
        gather_a[0].third()
        gather_a[1].third()
        for gather in gather_a:
            gather.finish()
        for copy in (*own_b, *along_o):
            copy.wait()
        gather_o.first()
        rows = wt_ref.shape[1] // 4
        wt_ref[...] = jnp.concatenate(
            [full_a[j].reshape(width, GATHERED)[:, :rows] for j in range(4)], axis=1)
        first = _half_mask((256, LANES))
        bias = [table_ref[4 + part : 5 + part, :] for part in range(3)]
        for r in range(0, ROW_LEN, 256):
            at = slice(r, r + 256)
            project = nn(h1_ref[at, :], wt_ref[...])
            cosine, sine = cos_ref[at, :], sin_ref[at, :]
            for g in range(width // LANES):
                lanes = slice(g * LANES, (g + 1) * LANES)
                queries = (project[:, lanes] + bias[0][:, lanes]) * (1.0 / math.sqrt(HEAD_DIM))
                keys = project[:, width + g * LANES : width + (g + 1) * LANES] + bias[1][:, lanes]
                q_s[g, at, :] = (queries * cosine + _turn(queries, first) * sine).astype(jnp.bfloat16)
                k_s[g, at, :] = (keys * cosine + _turn(keys, first) * sine).astype(jnp.bfloat16)
                v_s[g, at, :] = (project[:, 2 * width + g * LANES : 2 * width + (g + 1) * LANES]
                                 + bias[2][:, lanes]).astype(jnp.bfloat16)
        for copy in along_b[0]:
            copy.wait()
        gather_b[0].first()
        gather_o.second()

    @pl.when(group == 1)
    def _():
        for copy in along_b[1]:
            copy.wait()
        gather_b[1].first()
        gather_o.third()

    @pl.when(group == 2)
    def _():
        gather_b[0].second()

    @pl.when(group == 4)
    def _():
        gather_b[1].second()
        gather_b[0].third()

    qr_ref[...] = q_s[group]
    kr_ref[...] = k_s[group]
    vr_ref[...] = v_s[group]
    attn_ref[...] = attention_group(q_s[group], kr_ref, v_s[group], same_rest(ends, offset), ot_s, vt_s, lse_ref)

    @pl.when(group == 4)
    def _():
        gather_b[1].third()
        for gather in (gather_o, *gather_b):
            gather.finish()


def head(lengths, tokens, w_qkv_t, w_up_t, w_down_t, w_out, vectors):
    tokens_count, width = tokens.shape
    groups = width // LANES
    columns = w_qkv_t.shape[0]
    col = pl.BlockSpec((tokens_count, LANES), lambda g: (0, g))
    whole = lambda *shape: pl.BlockSpec(shape, lambda g: (0,) * len(shape))
    shape = jax.ShapeDtypeStruct
    bf16, f32 = jnp.bfloat16, jnp.float32
    sems = lambda n: pltpu.SemaphoreType.DMA((n,))
    na, nb = GATHERED // CHUNK_A, 1 + len(CUTS_B)
    return pl.pallas_call(
        head_kernel,
        grid=(groups,),
        in_specs=[pl.BlockSpec(memory_space=pltpu.SMEM), whole(tokens_count, width), whole(*w_qkv_t.shape),
                  whole(columns, width), whole(columns, width), whole(*w_out.shape), whole(*vectors.shape)],
        out_specs=[col] * 4 + [pl.BlockSpec((1, 4, tokens_count), lambda g: (g, 0, 0)),
                               whole(tokens_count, width), whole(tokens_count, width),
                               whole(tokens_count, LANES), whole(tokens_count, LANES),
                               whole(width, 3 * width), whole(16, width), pl.BlockSpec(memory_space=pl.ANY),
                               pl.BlockSpec(memory_space=pl.ANY)],
        out_shape=[shape((tokens_count, width), bf16)] * 4 + [shape((groups, 4, tokens_count), f32)]
        + [shape((tokens_count, width), bf16)] * 2 + [shape((tokens_count, LANES), f32)] * 2
        + [shape((width, 3 * width), bf16), shape((16, width), f32), shape((4, 4, 2, columns, 2 * width), bf16),
           shape((4, 4, 2, columns, OUT_LANES), bf16)],
        scratch_shapes=[
            pltpu.VMEM((4, 4, 2, columns, GATHERED), bf16),
            pltpu.VMEM((4, 2, columns, LANES), f32),
            pltpu.VMEM((tokens_count, width), f32),
            pltpu.VMEM((groups, tokens_count, LANES), bf16),
            pltpu.VMEM((groups, tokens_count, LANES), bf16),
            pltpu.VMEM((groups, tokens_count, LANES), bf16),
            pltpu.VMEM((LANES, tokens_count), f32),
            pltpu.VMEM((LANES, tokens_count), bf16),
            pltpu.VMEM((columns, GATHERED), bf16),
            pltpu.VMEM((columns, 2 * width), bf16),
            pltpu.VMEM((columns, OUT_LANES), bf16),
            sems(8 * na), sems(8 * na), sems(3 * na), sems(3 * na),
            sems(8 * nb), sems(8 * nb), sems(3 * nb), sems(3 * nb), sems(7), sems(7), sems(2),
        ],
        compiler_params=pltpu.CompilerParams(collective_id=2, has_side_effects=True, vmem_limit_bytes=58 << 20),
        name="head",
    )(lengths, tokens, w_qkv_t, w_up_t, w_down_t, w_out, vectors)


def middle_kernel(
    len_ref, count_ref, x_ref, attn_ref, cot_ref, table_ref, full_o_ref, full_b,
    layer_ref, after_grad_ref, attn_grad_ref, parts_ref, out_grad_ref, sums_ref,
    xhat_s, rstd_s, h2_s, h2t_s, dy_s, dyt_s, acc_s, back_s, act_s, pre_s, wt_out_s, w_s, send, recv, local,
):
    step = pl.program_id(0)
    tokens, width = x_ref.shape
    rank, plane, core, chip_x, chip_y = place()
    chip = chip_at(0, chip_x, chip_y)
    late = Gather(lambda m, c, lane: w_s.at[1, :, m, c, :, lane], send, recv, 0, lane_parts(0, 2 * width))
    loads = [pltpu.make_async_copy(full_b.at[pl.ds(2, 2), chip, core], w_s.at[1, :, chip, core], local.at[0]),
             pltpu.make_async_copy(full_b.at[pl.ds(0, 2)], w_s.at[0], local.at[1])]
    ends, offset = row_marks(len_ref)
    chunk = 256
    cuts = [slice(r, r + chunk) for r in range(0, tokens, chunk)]

    @pl.when(step == 0)
    def _():
        for load in loads:
            load.start()
        greet([(2 * chip + 1 - core, plane)]
              + [(2 * chip_at(other, chip_x, chip_y) + core, plane) for other in (1, 2)])
        loads[0].wait()
        late.first()
        rows = width // 4
        wt_out_s[...] = jnp.concatenate([full_o_ref[p].reshape(width, OUT_LANES)[:, :rows] for p in range(4)], axis=1)
        index = lax.broadcasted_iota(jnp.int32, (tokens, 1), 0)
        _, segment = segment_of(index, ends, offset)
        number = jnp.where(segment == 0, count_ref[0, 0], jnp.where(
            segment == 1, count_ref[0, 1], jnp.where(segment == 2, count_ref[0, 2], count_ref[0, 3])))
        incoming = turned_rows(cot_ref[...], offset) * (1.0 / number.astype(jnp.float32))
        after_grad_ref[...] = incoming
        dy_s[...] = incoming.astype(jnp.bfloat16)
        dyt_s[...] = dy_s[...].T
        sums_ref[...] = jnp.zeros_like(sums_ref)
        sums_ref[8:9, :] = jnp.sum(dy_s[...].astype(jnp.float32), axis=0, keepdims=True)
        gain, shift = table_ref[2:3, :], table_ref[3:4, :]
        for at in cuts:
            after = x_ref[at, :].astype(jnp.float32) + (nn(attn_ref[at, :], wt_out_s[...]) + table_ref[7:8, :])
            acc_s[at, :] = after + table_ref[8:9, :]
            center = after - jnp.mean(after, axis=-1, keepdims=True)
            rstd = lax.rsqrt(jnp.mean(center * center, axis=-1, keepdims=True) + norm_eps)
            xhat = center * rstd
            xhat_s[at, :] = xhat
            rstd_s[at, :] = rstd
            h2_s[at, :] = (xhat * gain + shift).astype(jnp.bfloat16)
        h2t_s[...] = h2_s[...].T
        back_s[...] = jnp.zeros_like(back_s)

    @pl.when(step == 0)
    def _():
        loads[1].wait()
        late.second()

    @pl.when(step == 1)
    def _():
        late.finish()

    def weights(lanes):
        return jnp.concatenate([w_s[step, p, :, :, :, lanes].reshape(width, width) for p in range(2)], axis=1)

    up, down = (weights(slice(part * width, (part + 1) * width)) for part in range(2))
    bias = jnp.concatenate([table_ref[pl.ds(9 + 2 * step + p, 1), :] for p in range(2)], axis=1)

    def products(at):
        return nn(h2_s[at, :], up), nn(dy_s[at, :], down)

    def pointwise(at, pre, act_grad):
        pre = pre + bias
        cdf = 0.5 * (1.0 + lax.erf(pre * (1.0 / math.sqrt(2.0))))
        slope = cdf + pre * (jnp.exp(-0.5 * pre * pre) * (1.0 / math.sqrt(2.0 * math.pi)))
        act_s[at, :] = (pre * cdf).astype(jnp.bfloat16)
        pre_s[at, :] = (act_grad * slope).astype(jnp.bfloat16)

    def collect(at):
        acc_s[at, :] += nt(act_s[at, :], down)
        back_s[at, :] += nt(pre_s[at, :], up)

    held = {}
    for t in range(len(cuts) + 1):
        if t < len(cuts):
            held[t] = products(cuts[t])
        if t >= 1:
            pointwise(cuts[t - 1], *held.pop(t - 1))
            collect(cuts[t - 1])

    @pl.when(step == 0)
    def _():
        late.third()

    for part, (left, right) in enumerate(((h2t_s, pre_s), (dyt_s, act_s))):
        grad = nn(left[...], right[...]).astype(jnp.bfloat16)
        for p in range(2):
            parts_ref[p, :, part * width : (part + 1) * width] = grad[:, p * width : (p + 1) * width]
    bias_sum = jnp.sum(pre_s[...].astype(jnp.float32), axis=0, keepdims=True)
    for p in range(2):
        sums_ref[pl.ds(9 + 2 * step + p, 1), :] = bias_sum[:, p * width : (p + 1) * width]

    @pl.when(step == 1)
    def _():
        layer_ref[...] = pltpu.roll(acc_s[...], offset, 0).astype(jnp.bfloat16)
        gain = table_ref[2:3, :]
        gain_sum = jnp.zeros((1, width), jnp.float32)
        shift_sum = jnp.zeros((1, width), jnp.float32)
        branch_sum = jnp.zeros((1, width), jnp.float32)
        for at in cuts:
            grad, xhat = back_s[at, :], xhat_s[at, :]
            gain_sum += jnp.sum(grad * xhat, axis=0, keepdims=True)
            shift_sum += jnp.sum(grad, axis=0, keepdims=True)
            scaled = grad * gain
            resid = rstd_s[at, :] * (
                scaled - jnp.mean(scaled, axis=-1, keepdims=True)
                - xhat * jnp.mean(scaled * xhat, axis=-1, keepdims=True))
            after_grad = after_grad_ref[at, :] + resid
            after_grad_ref[at, :] = after_grad
            low = after_grad.astype(jnp.bfloat16)
            dy_s[at, :] = low
            branch_sum += jnp.sum(low.astype(jnp.float32), axis=0, keepdims=True)
            attn_grad_ref[at, :] = nt(low, wt_out_s[...]).astype(jnp.bfloat16)
        sums_ref[2:3, :] = gain_sum
        sums_ref[3:4, :] = shift_sum
        sums_ref[7:8, :] = branch_sum
        h2t_s[...] = attn_ref[...].T
        out_grad_ref[...] = nn(h2t_s[...], dy_s[...]).astype(jnp.bfloat16)


def middle(lengths, counts, x, attn, cotangent, table, full_o, full_b):
    tokens, width = x.shape
    columns = full_b.shape[3]
    whole = lambda *shape: pl.BlockSpec(shape, lambda j: (0,) * len(shape))
    smem = pl.BlockSpec(memory_space=pltpu.SMEM)
    shape = jax.ShapeDtypeStruct
    bf16, f32 = jnp.bfloat16, jnp.float32
    flat = pltpu.VMEM((tokens, width), bf16)
    double = pltpu.VMEM((tokens, 2 * width), bf16)
    wide = pltpu.VMEM((tokens, width), f32)
    turned = pltpu.VMEM((width, tokens), bf16)
    sems = lambda n: pltpu.SemaphoreType.DMA((n,))
    return pl.pallas_call(
        middle_kernel,
        grid=(2,),
        in_specs=[smem, smem, whole(tokens, width), whole(tokens, width), whole(tokens, width), whole(16, width),
                  whole(*full_o.shape), pl.BlockSpec(memory_space=pl.ANY)],
        out_specs=[whole(tokens, width), whole(tokens, width), whole(tokens, width),
                   pl.BlockSpec((2, width, 2 * width), lambda j: (j, 0, 0)), whole(width, width), whole(16, width)],
        out_shape=[shape((tokens, width), bf16), shape((tokens, width), f32), shape((tokens, width), bf16),
                   shape((4, width, 2 * width), bf16), shape((width, width), bf16), shape((16, width), f32)],
        scratch_shapes=[wide, pltpu.VMEM((tokens, 1), f32), flat, turned, flat, turned, wide, wide, double, double,
                        pltpu.VMEM((width, width), bf16), pltpu.VMEM((2, 2, 4, 2, columns, 2 * width), bf16),
                        sems(8), sems(8), sems(2)],
        compiler_params=pltpu.CompilerParams(collective_id=3, has_side_effects=True, vmem_limit_bytes=62 << 20),
        name="middle",
    )(lengths, counts, x, attn, cotangent, table, full_o, full_b)


def backward_group(qr_ref, kr_ref, vr_ref, do_ref, attn_ref, lse_ref, same, qt_s, dot_s, kt_s, delta_s, dqt_s, dk_s, dv_s):
    tokens = qr_ref.shape[0]
    qt_s[...] = qr_ref[...].T
    dot_s[...] = do_ref[...].T
    kt_s[...] = kr_ref[...].T
    prod_t = (do_ref[...].astype(jnp.float32) * attn_ref[...].astype(jnp.float32)).T
    for h in range(4):
        delta_s[h : h + 1, :] = jnp.sum(prod_t[h * HEAD_DIM : (h + 1) * HEAD_DIM, :], axis=0, keepdims=True)
    dk_s[...] = jnp.zeros_like(dk_s)
    dv_s[...] = jnp.zeros_like(dv_s)
    row = lax.broadcasted_iota(jnp.int32, (LANES, tokens), 0)
    lane = lax.broadcasted_iota(jnp.int32, (tokens, LANES), 1)
    zero = jnp.zeros((), jnp.bfloat16)
    jobs = attention_jobs(tokens)
    masked, held = {}, {}

    def products(job):
        h, start, width, key_start, key_count = job
        if h not in masked:
            masked[h] = (
                jnp.where(row // HEAD_DIM == h, qt_s[...], zero), jnp.where(row // HEAD_DIM == h, dot_s[...], zero),
                jnp.where(lane // HEAD_DIM == h, qr_ref[...], zero), jnp.where(lane // HEAD_DIM == h, do_ref[...], zero))
        at, keys = slice(start, start + width), slice(key_start, key_start + key_count)
        scores = nn(kr_ref[keys, :], masked[h][0][:, at])
        if start == LONGEST:
            scores = jnp.where(same, scores, masked_score)
        return scores, nn(vr_ref[keys, :], masked[h][1][:, at])

    def finish(job, scores, weight_grad):
        h, start, width, key_start, key_count = job
        at, keys = slice(start, start + width), slice(key_start, key_start + key_count)
        rows = slice(h * HEAD_DIM, (h + 1) * HEAD_DIM)
        soft = jnp.exp(scores - lse_ref[0, h : h + 1, at])
        score_grad = (soft * (weight_grad - delta_s[h : h + 1, at])).astype(jnp.bfloat16)
        dv_s[keys, :] += nn(soft.astype(jnp.bfloat16), masked[h][3][at, :])
        dk_s[keys, :] += nn(score_grad, masked[h][2][at, :])
        dqt_s[rows, at] = nn(kt_s[rows, keys], score_grad)

    for t in range(len(jobs) + 1):
        if t < len(jobs):
            held[t] = products(jobs[t])
        if t >= 1:
            finish(jobs[t - 1], *held.pop(t - 1))


def backward_kernel(
    len_ref, qr_ref, kr_ref, vr_ref, do_ref, attn_ref, lse_ref, cos_ref, sin_ref, parts_ref,
    dq_ref, dk_ref, dv_ref, own_ref, total_ref, *scratch,
):
    group = pl.program_id(0)
    lanes = parts_ref.shape[-1] // 2
    halves = [SumStages(parts_ref, scratch[7 + SUM_SCRATCH * n : 7 + SUM_SCRATCH * (n + 1)], pl.ds(n * lanes, lanes))
              for n in range(2)]
    dqt_s, dk_s, dv_s = scratch[4:7]

    @pl.when(group == 0)
    def _():
        greet(all_partners())
        halves[0].core_start()
        halves[1].core_start()

    @pl.when(group == 1)
    def _():
        halves[0].core_finish()
        halves[0].chip_start()
        halves[1].core_finish()

    @pl.when(group == 2)
    def _():
        halves[1].chip_start()

    @pl.when(group == 3)
    def _():
        halves[0].chip_turn()

    @pl.when(group == 4)
    def _():
        halves[0].chip_finish()
        halves[0].plane_start()
        halves[1].chip_turn()

    ends, offset = row_marks(len_ref)
    backward_group(qr_ref, kr_ref, vr_ref, do_ref, attn_ref, lse_ref, same_rest(ends, offset), *scratch[:7])
    first = _half_mask(cos_ref.shape)
    cosine, sine = cos_ref[...], sin_ref[...]

    def pull(values):
        return values * cosine + _turn(values * sine, first)

    dq_ref[...] = (pull(dqt_s[...].T) * (1.0 / math.sqrt(HEAD_DIM))).astype(jnp.bfloat16)
    dk_ref[...] = pull(dk_s[...]).astype(jnp.bfloat16)
    dv_ref[...] = dv_s[...].astype(jnp.bfloat16)

    @pl.when(group == 4)
    def _():
        halves[1].chip_finish()
        total_ref[...] = halves[1].total[...]
        own_ref[...] = halves[0].plane_finish()


def backward(lengths, qr, kr, vr, attn_grad, attn, lse, cosine, sine, parts):
    tokens, width = qr.shape
    groups = width // LANES
    rows, lanes = parts.shape[-2:]
    col = pl.BlockSpec((tokens, LANES), lambda g: (0, g))
    whole = lambda *shape: pl.BlockSpec(shape, lambda g: (0,) * len(shape))
    shape = jax.ShapeDtypeStruct
    bf16, f32 = jnp.bfloat16, jnp.float32
    return pl.pallas_call(
        backward_kernel,
        grid=(groups,),
        in_specs=[pl.BlockSpec(memory_space=pltpu.SMEM)] + [col] * 5
        + [pl.BlockSpec((1, 4, tokens), lambda g: (g, 0, 0)), whole(tokens, LANES), whole(tokens, LANES),
           pl.BlockSpec(memory_space=pl.ANY)],
        out_specs=[col] * 3 + [whole(rows, lanes // 2), whole(4, rows, lanes // 2)],
        out_shape=[shape((tokens, width), bf16)] * 3 + [shape((rows, lanes // 2), f32), shape((4, rows, lanes // 2), bf16)],
        scratch_shapes=[pltpu.VMEM((LANES, tokens), bf16)] * 3
        + [pltpu.VMEM((8, tokens), f32), pltpu.VMEM((LANES, tokens), f32), pltpu.VMEM((tokens, LANES), f32),
           pltpu.VMEM((tokens, LANES), f32)] + sum_scratch(rows, lanes // 2) * 2,
        compiler_params=pltpu.CompilerParams(collective_id=0, has_side_effects=True, vmem_limit_bytes=58 << 20),
        name="backward",
    )(lengths, qr, kr, vr, attn_grad, attn, lse, cosine, sine, parts)


def row_layout(lengths, counts, row_len):
    lens = lengths[0]
    slots = lens.shape[0]
    order = lax.broadcasted_iota(jnp.int32, (slots, slots), 0)
    upto = lax.broadcasted_iota(jnp.int32, (slots, slots), 1)
    starting = jnp.sum(jnp.where(upto < order, lens[None, :], 0), axis=1)
    slot = lax.broadcasted_iota(jnp.int32, (slots,), 0)
    which = jnp.min(jnp.where(lens == LONGEST, slot, slots))
    offset = jnp.sum(jnp.where(slot == which, starting, 0))
    places = lax.broadcasted_iota(jnp.int32, (row_len,), 0) + offset
    places = jnp.where(places >= row_len, places - row_len, places)
    endings = starting + lens
    segment = jnp.sum((places[:, None] >= endings[None, :]).astype(jnp.int32), axis=1)
    member = segment[:, None] == slot[None, :]
    first_place = jnp.sum(jnp.where(member, starting[None, :], 0), axis=1)
    position = (places - first_place).astype(jnp.float32)
    inverse_count = 1.0 / counts[0].astype(jnp.float32)
    share = jnp.sum(jnp.where(member, inverse_count[None, :], 0.0), axis=1)
    return offset, segment, position, share


def rotary_tables(position):
    lane = lax.broadcasted_iota(jnp.int32, (1, LANES), 1)
    indices = (lane % (HEAD_DIM // 2)).astype(jnp.float32)
    inverse = jnp.exp(indices * (-2.0 * math.log(10000.0) / HEAD_DIM))
    angles = position[:, None] * inverse
    sign = jnp.where((lane % HEAD_DIM) < (HEAD_DIM // 2), -1.0, 1.0)
    return jnp.cos(angles), jnp.sin(angles) * sign


def turn_rows(values, shift):
    twice = jnp.concatenate([values, values], axis=0)
    return lax.dynamic_slice_in_dim(twice, shift, values.shape[0], 0)


def high(left, right):
    return jnp.dot(left, right, precision=lax.Precision.HIGH, preferred_element_type=jnp.float32)


def shards_near(
    tokens, cotangent, lengths, counts,
    w_qkv, w_out, w_up, w_down,
    mom_qkv, mom_out, mom_up, mom_down,
    vectors, vec_first, vec_second,
):
    columns = w_qkv.shape[1]
    weights_t = [w_qkv.T, w_out, w_up.T, w_down.T]
    moments_t = [mom_qkv.T, mom_out, mom_up.T, mom_down.T]
    qr, kr, vr, attn, lse, normed_one, turned, cosine, sine, wt_qkv, table, full_b, full_o = head(
        lengths, tokens, weights_t[0], weights_t[2], weights_t[3], w_out, vectors)
    layer_out, after_grad, attn_grad, parts_b, out_grad, sums = middle(
        lengths, counts, turned, attn, cotangent, table, full_o, full_b)
    dq, dk, dv, own_up, total_down = backward(
        lengths, qr, kr, vr, attn_grad, attn, lse, cosine, sine, parts_b.reshape(4, 2, 2, 2, columns, -1))
    results = tail(
        normed_one, dq, dk, dv, out_grad, sums, table, own_up, total_down, lengths, moments_t, weights_t,
        (vectors, vec_first, vec_second), wt_qkv, after_grad, turned)
    results = finish([*results, layer_out])
    matrices = [v if x % 4 == 1 else v.T for x, v in enumerate(results[:8])]
    return (results[12], results[11], *matrices, *results[8:11])


def shards_far(
    tokens, cotangent, lengths, counts,
    w_qkv, w_out, w_up, w_down,
    mom_qkv, mom_out, mom_up, mom_down,
    vectors, vec_first, vec_second,
):
    both = ("fsdp", "dp")
    planes = lax.axis_size("fsdp")
    ranks = lax.axis_size("dp")
    row_len, width = tokens.shape
    columns = w_qkv.shape[1]
    old_weights = (w_qkv, w_out, w_up, w_down)
    old_moments = (mom_qkv, mom_out, mom_up, mom_down)
    counts_rows = [w.shape[0] for w in old_weights]
    n_vec = vectors.shape[0]

    slab_a = jnp.concatenate([w_qkv.T, w_out.T, vectors.T], axis=1).astype(jnp.bfloat16)
    slab_b = jnp.concatenate([w_up.T, w_down.T], axis=1).astype(jnp.bfloat16)
    full_a = lax.all_gather(slab_a, both, axis=0, tiled=True).reshape(planes, width, -1)
    full_b = lax.all_gather(slab_b, both, axis=0, tiled=True).reshape(planes, width, -1)
    r0, r1, r2, r3 = counts_rows
    wt_qkv = jnp.concatenate([full_a[j, :, :r0] for j in range(planes)], axis=1)
    wt_out = jnp.concatenate([full_a[j, :, r0 : r0 + r1] for j in range(planes)], axis=1)
    table = full_a[0, :, r0 + r1 :].T.astype(jnp.float32)
    wt_up = jnp.concatenate([full_b[j, :, :r2] for j in range(planes)], axis=1)
    wt_down = jnp.concatenate([full_b[j, :, r2:] for j in range(planes)], axis=1)

    offset, segment, position, share = row_layout(lengths, counts, row_len)
    cosine, sine = rotary_tables(position)
    seg_col, seg_row = segment[:, None], segment[None, :]
    inputs = turn_rows(tokens, offset).astype(jnp.float32)
    incoming = turn_rows(cotangent, offset).astype(jnp.float32) * share[:, None]

    normed_one, pull_one = jax.vjp(layer_norm, inputs, table[0], table[1])
    normed_one = normed_one.astype(jnp.bfloat16)
    project = nn(normed_one, wt_qkv) + table[4:7].reshape(-1)
    qr, kr, vr, attn, lse = attention_forward(project, cosine, sine, seg_col, seg_row)
    after = inputs + (nn(attn, wt_out) + table[7])
    normed_two, pull_two = jax.vjp(layer_norm, after, table[2], table[3])
    normed_two = normed_two.astype(jnp.bfloat16)
    hidden_pre = nn(normed_two, wt_up) + table[9:].reshape(-1)
    hidden, pull_hidden = jax.vjp(gelu_exact, hidden_pre)
    hidden = hidden.astype(jnp.bfloat16)
    layer_out = (after + (nt(hidden, wt_down) + table[8])).astype(jnp.bfloat16)

    grad_low = incoming.astype(jnp.bfloat16)
    grad_t_down = tn(grad_low, hidden)
    pre_grad = pull_hidden(nn(grad_low, wt_down))[0].astype(jnp.bfloat16)
    grad_t_up = tn(normed_two, pre_grad)
    resid_grad, gain_two, shift_two = pull_two(nt(pre_grad, wt_up))
    after_grad = incoming + resid_grad
    branch_low = after_grad.astype(jnp.bfloat16)
    grad_t_out = tn(attn, branch_low)
    attn_grad = nt(branch_low, wt_out).astype(jnp.bfloat16)
    dq, dk, dv = attention_backward(qr, kr, vr, attn_grad, attn, lse, cosine, sine, seg_col, seg_row)
    proj_grad = jnp.concatenate([dq, dk, dv], axis=1)
    grad_t_qkv = tn(normed_one, proj_grad)
    in_grad, gain_one, shift_one = pull_one(nt(proj_grad, wt_qkv))
    input_grad = after_grad + in_grad

    def column_sum(values):
        return jnp.sum(values.astype(jnp.float32), axis=0)

    vector_grad = jnp.concatenate(
        [gain_one[None], shift_one[None], gain_two[None], shift_two[None],
         column_sum(proj_grad).reshape(3, width), column_sum(branch_low)[None], column_sum(grad_low)[None],
         column_sum(pre_grad).reshape(-1, width)],
        axis=0,
    )
    back = jnp.where(offset > 0, row_len - offset, 0)
    layer_out = turn_rows(layer_out, back)
    input_grad = turn_rows(input_grad, back)

    def cut(values, j, rows):
        return values[:, j * rows : (j + 1) * rows]

    parts_b = jnp.stack([jnp.concatenate([cut(grad_t_up, j, r2), cut(grad_t_down, j, r3)], axis=1) for j in range(planes)])
    own_b = lax.psum_scatter(parts_b.reshape(planes * width, -1), both, scatter_dimension=0, tiled=True)
    parts_a = jnp.stack([jnp.concatenate([cut(grad_t_qkv, j, r0), cut(grad_t_out, j, r1), vector_grad.T], axis=1) for j in range(planes)])
    own_a = lax.psum_scatter(parts_a.reshape(planes * width, -1), both, scatter_dimension=0, tiled=True)
    grads_t = (own_a[:, :r0], own_a[:, r0 : r0 + r1], own_b[:, :r2], own_b[:, r2:])
    vector_grad = own_a[:, r0 + r1 :].T
    new_moments_t = [moment_keep * old.T + grad for old, grad in zip(old_moments, grads_t)]

    most = max(counts_rows)
    padded = [jnp.pad(m.astype(jnp.bfloat16), ((0, 0), (0, most - m.shape[1]))) for m in new_moments_t]
    sent = jnp.stack([padded[t % 4] for t in range(planes)])
    mine = lax.all_to_all(sent, "fsdp", 0, 0, tiled=True)
    mine = mine.transpose(1, 0, 2).reshape(columns, planes * most)
    whole = lax.all_gather(mine, "dp", axis=0, tiled=True)
    gram = nt(whole, whole)
    identity = jnp.eye(width, dtype=jnp.float32)
    norm_sq = jnp.trace(gram) + 1e-07
    gram = gram / norm_sq
    factor = None
    for iteration in range(NS_ITERS):
        poly = poly_linear * identity + poly_square * gram + poly_cubic * high(gram, gram)
        factor = poly if factor is None else high(factor, poly)
        if iteration + 1 < NS_ITERS:
            gram = high(high(gram, poly), poly)
    own_rows = lax.dynamic_slice_in_dim(factor, lax.axis_index("dp") * columns, columns, 0) * lax.rsqrt(norm_sq)
    own_orth = high(own_rows, whole.astype(jnp.float32))
    own_orth = own_orth.astype(jnp.bfloat16).reshape(columns, planes, most).transpose(1, 0, 2)
    pieces = lax.all_to_all(own_orth, "fsdp", 0, 0, tiled=True).astype(jnp.float32)

    new_weights = []
    for x, weight_old in enumerate(old_weights):
        rows = weight_old.shape[0]
        scale = muon_rate * math.sqrt(max(1.0, rows * planes / width))
        new_weights.append(weight_old * (1.0 - muon_rate * muon_decay) - scale * pieces[x, :, :rows].T)
    new_first = beta_first * vec_first + (1.0 - beta_first) * vector_grad
    new_second = beta_second * vec_second + (1.0 - beta_second) * vector_grad * vector_grad
    first_fix = 1.0 - beta_first**STEP
    second_fix = 1.0 - beta_second**STEP
    new_vectors = vectors - adam_rate * (new_first / first_fix) / (jnp.sqrt(new_second / second_fix) + adam_eps)
    return (layer_out, input_grad, *[m.T for m in new_moments_t], *new_weights, new_vectors, new_first, new_second)


def solution(mesh):
    rows, cells, table = P(("dp", "fsdp"), None), P("fsdp", "dp"), P(None, "dp")
    near = dict(mesh.shape) == {"dp": 8, "fsdp": 4}
    return jax.shard_map(
        shards_near if near else shards_far,
        mesh=mesh,
        in_specs=(rows,) * 4 + (cells,) * 8 + (table,) * 3,
        out_specs=(rows,) * 2 + (cells,) * 8 + (table,) * 3,
        check_vma=False,
    )
```

```python
import functools
import math

import jax
import jax.numpy as jnp
from jax import lax
from jax.experimental import pallas as pl
from jax.experimental.pallas import tpu as pltpu
from jax.sharding import PartitionSpec as P

HEAD_DIM = 32
NS_ITERS = 5
STEP = 10
LANES = 128
LONGEST = 768

norm_eps = 1e-05
masked_score = -1e30
poly_linear = 3.4445
poly_square = -4.775
poly_cubic = 2.0315
muon_rate = 0.5
muon_decay = 0.01
moment_keep = 0.5
adam_rate = 0.05
beta_first = 0.9
beta_second = 0.999
adam_eps = 1e-08


def layer_norm(values, gain_row, shift_row):
    center = values - jnp.mean(values, axis=-1, keepdims=True)
    spread = jnp.mean(center * center, axis=-1, keepdims=True)
    return center * lax.rsqrt(spread + norm_eps) * gain_row + shift_row


def gelu_exact(values):
    return 0.5 * values * (1.0 + lax.erf(values * (1.0 / math.sqrt(2.0))))


def nn(left, right):
    return jnp.dot(left, right, preferred_element_type=jnp.float32)


def nt(left, right):
    return lax.dot_general(left, right, (((1,), (1,)), ((), ())), preferred_element_type=jnp.float32)


def tn(left, right):
    return lax.dot_general(left, right, (((0,), (0,)), ((), ())), preferred_element_type=jnp.float32)


def _half_mask(shape):
    lane = lax.broadcasted_iota(jnp.int32, shape, 1)
    return (lane % HEAD_DIM) < (HEAD_DIM // 2)


def _turn(values, first):
    half = HEAD_DIM // 2
    left = pltpu.roll(values, LANES - half, 1)
    right = pltpu.roll(values, half, 1)
    return jnp.where(first, left, right)


def attention_forward_kernel(
    q_ref, k_ref, v_ref, cos_ref, sin_ref, segc_ref, segr_ref,
    qr_ref, kr_ref, vr_ref, attn_ref, lse_ref,
    qt_s, vt_s, ot_s,
):
    first = _half_mask(cos_ref.shape)
    cosine, sine = cos_ref[...], sin_ref[...]
    queries = q_ref[...] * (1.0 / math.sqrt(HEAD_DIM))
    qr = (queries * cosine + _turn(queries, first) * sine).astype(jnp.bfloat16)
    keys = k_ref[...]
    kr = (keys * cosine + _turn(keys, first) * sine).astype(jnp.bfloat16)
    vr = v_ref[...].astype(jnp.bfloat16)
    qr_ref[...] = qr
    kr_ref[...] = kr
    vr_ref[...] = vr
    qt_s[...] = qr.T
    vt_s[...] = vr.T
    tokens = qr.shape[0]
    rest = tokens - LONGEST
    row = lax.broadcasted_iota(jnp.int32, (LANES, tokens), 0)
    same = segc_ref[LONGEST:, :] == segr_ref[:, LONGEST:]

    def head(h, carry):
        qth = jnp.where(row // HEAD_DIM == h, qt_s[...], jnp.zeros((), jnp.bfloat16))
        rows = pl.ds(pl.multiple_of(h * HEAD_DIM, HEAD_DIM), HEAD_DIM)

        def block(start, width, key_start, key_count, mask):
            scores = nn(kr_ref[key_start : key_start + key_count, :], qth[:, start : start + width])
            if mask is not None:
                scores = jnp.where(mask, scores, masked_score)
            peak = jnp.max(scores, axis=0, keepdims=True)
            raised = jnp.exp(scores - peak)
            total = jnp.sum(raised, axis=0, keepdims=True)
            out = nn(vt_s[rows, key_start : key_start + key_count], raised.astype(jnp.bfloat16))
            ot_s[rows, start : start + width] = out / total
            lse_ref[0, pl.ds(h, 1), start : start + width] = peak + jnp.log(total)

        for start in range(0, LONGEST, 256):
            block(start, 256, 0, LONGEST, None)
        block(LONGEST, rest, LONGEST, rest, same)
        return carry

    lax.fori_loop(0, LANES // HEAD_DIM, head, 0)
    attn_ref[...] = ot_s[...].T.astype(jnp.bfloat16)


def attention_forward(project, cosine, sine, seg_col, seg_row):
    tokens = project.shape[0]
    width = project.shape[1] // 3
    groups = width // LANES
    col = lambda shift: pl.BlockSpec((tokens, LANES), lambda g, shift=shift: (0, g + shift))
    whole = lambda shape: pl.BlockSpec(shape, lambda g: (0,) * len(shape))
    flops = 4 * (LONGEST**2 + (tokens - LONGEST) ** 2) * 128 * groups * 4
    return pl.pallas_call(
        attention_forward_kernel,
        grid=(groups,),
        in_specs=[col(0), col(groups), col(2 * groups), whole((tokens, LANES)), whole((tokens, LANES)),
                  whole((tokens, 1)), whole((1, tokens))],
        out_specs=[col(0)] * 4 + [pl.BlockSpec((1, 4, tokens), lambda g: (g, 0, 0))],
        out_shape=[jax.ShapeDtypeStruct((tokens, width), jnp.bfloat16)] * 4
        + [jax.ShapeDtypeStruct((groups, 4, tokens), jnp.float32)],
        scratch_shapes=[
            pltpu.VMEM((LANES, tokens), jnp.bfloat16),
            pltpu.VMEM((LANES, tokens), jnp.bfloat16),
            pltpu.VMEM((LANES, tokens), jnp.float32),
        ],
        compiler_params=pltpu.CompilerParams(vmem_limit_bytes=48 << 20),
        cost_estimate=pl.CostEstimate(flops=flops, bytes_accessed=20 << 20, transcendentals=20 << 20),
        name="attention_forward",
    )(project, project, project, cosine, sine, seg_col, seg_row)


def attention_backward_kernel(
    qr_ref, kr_ref, vr_ref, do_ref, attn_ref, lse_ref, cos_ref, sin_ref, segc_ref, segr_ref,
    *rest_refs,
):
    dq_ref, dk_ref, dv_ref = rest_refs[:3]
    qt_s, dot_s, kt_s, delta_s, dqt_s, dk_s, dv_s = rest_refs[3:]
    tokens = qr_ref.shape[0]
    rest = tokens - LONGEST
    qt_s[...] = qr_ref[...].T
    dot_s[...] = do_ref[...].T
    kt_s[...] = kr_ref[...].T
    prod_t = (do_ref[...].astype(jnp.float32) * attn_ref[...].astype(jnp.float32)).T
    for h in range(4):
        delta_s[h : h + 1, :] = jnp.sum(prod_t[h * HEAD_DIM : (h + 1) * HEAD_DIM, :], axis=0, keepdims=True)
    dk_s[...] = jnp.zeros_like(dk_s)
    dv_s[...] = jnp.zeros_like(dv_s)
    row = lax.broadcasted_iota(jnp.int32, (LANES, tokens), 0)
    lane = lax.broadcasted_iota(jnp.int32, (tokens, LANES), 1)
    same = segc_ref[LONGEST:, :] == segr_ref[:, LONGEST:]
    zero = jnp.zeros((), jnp.bfloat16)

    def head(h, carry):
        mine_t = row // HEAD_DIM == h
        mine = lane // HEAD_DIM == h
        qth = jnp.where(mine_t, qt_s[...], zero)
        doth = jnp.where(mine_t, dot_s[...], zero)
        qh = jnp.where(mine, qr_ref[...], zero)
        doh = jnp.where(mine, do_ref[...], zero)
        rows = pl.ds(pl.multiple_of(h * HEAD_DIM, HEAD_DIM), HEAD_DIM)

        def block(start, width, key_start, key_count, mask):
            at = slice(start, start + width)
            keys = slice(key_start, key_start + key_count)
            scores = nn(kr_ref[keys, :], qth[:, at])
            if mask is not None:
                scores = jnp.where(mask, scores, masked_score)
            soft = jnp.exp(scores - lse_ref[0, pl.ds(h, 1), at])
            weight_grad = nn(vr_ref[keys, :], doth[:, at])
            score_grad = (soft * (weight_grad - delta_s[pl.ds(h, 1), at])).astype(jnp.bfloat16)
            dv_s[keys, :] += nn(soft.astype(jnp.bfloat16), doh[at, :])
            dk_s[keys, :] += nn(score_grad, qh[at, :])
            dqt_s[rows, at] = nn(kt_s[rows, keys], score_grad)

        for start in range(0, LONGEST, 256):
            block(start, 256, 0, LONGEST, None)
        block(LONGEST, rest, LONGEST, rest, same)
        return carry

    lax.fori_loop(0, LANES // HEAD_DIM, head, 0)
    first = _half_mask(cos_ref.shape)
    cosine, sine = cos_ref[...], sin_ref[...]

    def pull(values):
        return values * cosine + _turn(values * sine, first)

    dq_ref[...] = (pull(dqt_s[...].T) * (1.0 / math.sqrt(HEAD_DIM))).astype(jnp.bfloat16)
    dk_ref[...] = pull(dk_s[...]).astype(jnp.bfloat16)
    dv_ref[...] = dv_s[...].astype(jnp.bfloat16)


def attention_backward(qr, kr, vr, attn_grad, attn, lse, cosine, sine, seg_col, seg_row):
    tokens, width = qr.shape
    groups = width // LANES
    col = pl.BlockSpec((tokens, LANES), lambda g: (0, g))
    whole = lambda shape: pl.BlockSpec(shape, lambda g: (0,) * len(shape))
    flops = 10 * (LONGEST**2 + (tokens - LONGEST) ** 2) * 128 * groups * 4
    return pl.pallas_call(
        attention_backward_kernel,
        grid=(groups,),
        in_specs=[col] * 5 + [pl.BlockSpec((1, 4, tokens), lambda g: (g, 0, 0)),
                              whole((tokens, LANES)), whole((tokens, LANES)), whole((tokens, 1)), whole((1, tokens))],
        out_specs=[col] * 3,
        out_shape=[jax.ShapeDtypeStruct((tokens, width), jnp.bfloat16)] * 3,
        scratch_shapes=[
            pltpu.VMEM((LANES, tokens), jnp.bfloat16),
            pltpu.VMEM((LANES, tokens), jnp.bfloat16),
            pltpu.VMEM((LANES, tokens), jnp.bfloat16),
            pltpu.VMEM((8, tokens), jnp.float32),
            pltpu.VMEM((LANES, tokens), jnp.float32),
            pltpu.VMEM((tokens, LANES), jnp.float32),
            pltpu.VMEM((tokens, LANES), jnp.float32),
        ],
        compiler_params=pltpu.CompilerParams(vmem_limit_bytes=56 << 20),
        cost_estimate=pl.CostEstimate(flops=flops, bytes_accessed=20 << 20, transcendentals=20 << 20),
        name="attention_backward",
    )(qr, kr, vr, attn_grad, attn, lse, cosine, sine, seg_col, seg_row)


MESH = pl.DeviceIdType.MESH


def place():
    rank, plane = lax.axis_index("dp"), lax.axis_index("fsdp")
    core = rank % 2
    chip_x = (rank // 2) % 2
    chip_y = rank // 4
    return rank, plane, core, chip_x, chip_y


def chip_at(step, chip_x, chip_y):
    other_x = 1 - chip_x if step & 1 else chip_x
    other_y = 1 - chip_y if step & 2 else chip_y
    return 2 * other_y + other_x


def greet(partners):
    barrier = pltpu.get_barrier_semaphore()
    for partner in partners:
        pl.semaphore_signal(barrier, inc=1, device_id=partner, device_id_type=MESH)
    pl.semaphore_wait(barrier, len(partners))


def all_partners():
    rank, plane, core, chip_x, chip_y = place()
    sibling = 2 * chip_at(0, chip_x, chip_y) + 1 - core
    partners = [(sibling, plane)]
    partners += [(2 * chip_at(step, chip_x, chip_y) + core, plane) for step in (1, 2, 3)]
    partners += [(rank, (plane + step) % 4) for step in (1, 2, 3)]
    return partners


class SumStages:
    def __init__(self, parts, scratch, lanes):
        (self.own, self.from_core, self.from_first, self.middle, self.from_second, self.total, self.from_plane,
         self.send, self.recv, self.local) = scratch
        self.parts, self.lanes = parts, lanes
        self.rank, self.plane, self.core, self.chip_x, self.chip_y = place()

    def remote(self, source, target, slot, device):
        return pltpu.make_async_remote_copy(
            src_ref=source, dst_ref=target, send_sem=self.send.at[slot], recv_sem=self.recv.at[slot],
            device_id=device, device_id_type=MESH)

    def device(self, step):
        return (2 * chip_at(step, self.chip_x, self.chip_y) + self.core, self.plane)

    def add(self, left, right):
        return left.astype(jnp.float32) + right.astype(jnp.float32)

    def give_copy(self, source):
        return self.remote(source, self.from_core, 0, (2 * chip_at(0, self.chip_x, self.chip_y) + 1 - self.core, self.plane))

    def core_add(self, give):
        give.wait()
        for j in range(4):
            self.own[j] = self.add(self.own[j], self.from_core[j]).astype(self.own.dtype)

    def core_copies(self):
        load = pltpu.make_async_copy(self.parts.at[:, :, :, self.core, :, self.lanes], self.own, self.local)
        return load, self.give_copy(self.parts.at[:, :, :, 1 - self.core, :, self.lanes])

    def core_start(self):
        load, give = self.core_copies()
        give.start()
        load.start()

    def core_finish(self):
        load, give = self.core_copies()
        load.wait()
        self.core_add(give)

    def first_copies(self):
        return [
            self.remote(self.own.at[pl.ds(0, 2), :, 1 - self.chip_x], self.from_first.at[0], 1, self.device(1)),
            self.remote(self.own.at[pl.ds(2, 2), 1 - self.chip_y], self.from_first.at[1], 2, self.device(2)),
        ]

    def second_copies(self):
        return [
            self.remote(self.middle.at[0, :, 1 - self.chip_y], self.from_second.at[0], 3, self.device(2)),
            self.remote(self.middle.at[1, :, 1 - self.chip_x], self.from_second.at[1], 4, self.device(1)),
        ]

    def chip_start(self):
        for copy in self.first_copies():
            copy.start()

    def chip_turn(self):
        for copy in self.first_copies():
            copy.wait()
        for j in range(2):
            mine = self.own[j, :, pl.ds(self.chip_x, 1)][:, 0]
            self.middle[0, j] = self.add(mine, self.from_first[0, j]).astype(self.middle.dtype)
            mine = self.own[2 + j, pl.ds(self.chip_y, 1)][0]
            self.middle[1, j] = self.add(mine, self.from_first[1, j]).astype(self.middle.dtype)
        for copy in self.second_copies():
            copy.start()

    def chip_finish(self):
        for copy in self.second_copies():
            copy.wait()
        for half, index in ((0, self.chip_y), (1, self.chip_x)):
            for j in range(2):
                mine = self.middle[half, j, pl.ds(index, 1)][0]
                self.total[2 * half + j] = self.add(mine, self.from_second[half, j]).astype(self.total.dtype)

    def plane_copies(self):
        return [
            self.remote(self.total.at[(self.plane + step) % 4], self.from_plane.at[step - 1], 4 + step,
                        (self.rank, (self.plane + step) % 4))
            for step in (1, 2, 3)
        ]

    def plane_start(self):
        for copy in self.plane_copies():
            copy.start()

    def plane_finish(self):
        for copy in self.plane_copies():
            copy.wait()
        value = self.total[pl.ds(self.plane, 1)][0].astype(jnp.float32)
        for slot in range(3):
            value = value + self.from_plane[slot].astype(jnp.float32)
        return value


def sum_scratch(rows, lanes, dtype=jnp.bfloat16):
    return [
        pltpu.VMEM((4, 2, 2, rows, lanes), dtype),
        pltpu.VMEM((4, 2, 2, rows, lanes), dtype),
        pltpu.VMEM((2, 2, 2, rows, lanes), dtype),
        pltpu.VMEM((2, 2, 2, rows, lanes), dtype),
        pltpu.VMEM((2, 2, rows, lanes), dtype),
        pltpu.VMEM((4, rows, lanes), dtype),
        pltpu.VMEM((3, rows, lanes), dtype),
        pltpu.SemaphoreType.DMA((8,)),
        pltpu.SemaphoreType.DMA((8,)),
        pltpu.SemaphoreType.DMA,
    ]


SUM_SCRATCH = 10


def table_sum(table_ref, table_out, from_core, from_chip, from_plane, held, send, recv):
    rank, plane, core, chip_x, chip_y = place()
    chip = chip_at(0, chip_x, chip_y)

    def remote(source, target, slot, device):
        return pltpu.make_async_remote_copy(
            src_ref=source, dst_ref=target, send_sem=send.at[slot], recv_sem=recv.at[slot],
            device_id=device, device_id_type=MESH)

    give = remote(table_ref.at[:, 1 - core], from_core, 0, (2 * chip + 1 - core, plane))
    give.start()
    yield
    give.wait()
    held[...] = table_ref[:, pl.ds(core, 1)][:, 0] + from_core[...]
    across = [remote(held.at[chip_at(step, chip_x, chip_y)], from_chip.at[step - 1], step,
                     (2 * chip_at(step, chip_x, chip_y) + core, plane)) for step in (1, 2, 3)]
    for copy in across:
        copy.start()
    yield
    for copy in across:
        copy.wait()
    own = held[pl.ds(chip, 1)][0] + from_chip[0] + from_chip[1] + from_chip[2]
    table_out[...] = own
    along = [remote(table_out, from_plane.at[step - 1], 3 + step, (rank, (plane + step) % 4)) for step in (1, 2, 3)]
    for copy in along:
        copy.start()
    yield
    for copy in along:
        copy.wait()
    table_out[...] = own + from_plane[0] + from_plane[1] + from_plane[2]
    yield


class Gather:
    def __init__(self, at, send, recv, base, parts):
        rank, plane, core, chip_x, chip_y = place()
        every, low, high = parts
        chips = [chip_at(step, chip_x, chip_y) for step in range(4)]
        over = [2 * chip + core for chip in chips]

        def copy(chip, lanes, slot, device):
            block = at(chip, core, lanes)
            return pltpu.make_async_remote_copy(
                src_ref=block, dst_ref=block, send_sem=send.at[base + slot], recv_sem=recv.at[base + slot],
                device_id=(device, plane), device_id_type=MESH)

        self.to_x, self.to_y = copy(chips[0], every, 0, over[1]), copy(chips[0], every, 1, over[2])
        self.on_y, self.on_x = copy(chips[1], low, 2, over[2]), copy(chips[2], high, 3, over[1])
        self.beside = [copy(chip, every, 4 + step, 2 * chips[0] + 1 - core) for step, chip in enumerate(chips)]

    def first(self):
        self.to_x.start()
        self.to_y.start()
        self.beside[0].start()

    def second(self):
        self.to_x.wait_recv()
        self.on_y.start()
        self.beside[1].start()
        self.to_y.wait_recv()
        self.on_x.start()
        self.beside[2].start()

    def third(self):
        self.on_y.wait_recv()
        self.on_x.wait_recv()
        self.beside[3].start()

    def finish(self):
        for copy in (self.to_x, self.to_y, self.on_y, self.on_x):
            copy.wait_send()
        for copy in self.beside:
            copy.wait()


def split(values):
    top = values.astype(jnp.bfloat16)
    return top, (values - top.astype(jnp.float32)).astype(jnp.bfloat16)


def put_left(ref, values):
    width = values.shape[1]
    top, low = split(values)
    ref[:, :width] = top
    ref[:, width : 2 * width] = top
    ref[:, 2 * width :] = low


def put_right(ref, values):
    width = values.shape[0]
    top, low = split(values)
    ref[:width, :] = top
    ref[width : 2 * width, :] = low
    ref[2 * width :, :] = top


def tiles_of(width):
    first = width % 256
    edges = ([0] if first else []) + list(range(first, width + 1, 256))
    return list(zip(edges[:-1], edges[1:]))


def symmetric_product(out, left, right, tiles):
    for start, stop in tiles:
        block = nn(left[:stop, :], right[:, start:stop])
        out[:stop, start:stop] = block
        if start:
            out[start:stop, :start] = block[:start, :].T


def orthogonal_rows(whole, mine, gram, poly, temp, rows_s, left_gram, left_temp, right, write):
    width = gram.shape[0]
    tiles = tiles_of(width)
    parts = [whole[j].reshape(width, whole.shape[-1]) for j in range(4)]
    for start, stop in tiles:
        block = sum(nt(part[:stop, :], part[start:stop, :]) for part in parts)
        gram[:stop, start:stop] = block
        if start:
            gram[start:stop, :start] = block[:start, :].T
    diagonal = lax.broadcasted_iota(jnp.int32, (width, width), 0) == lax.broadcasted_iota(jnp.int32, (width, width), 1)
    norm_sq = jnp.sum(jnp.sum(jnp.where(diagonal, gram[...], 0.0), axis=1, keepdims=True), axis=0, keepdims=True) + 1e-07
    gram[...] = gram[...] / norm_sq

    def polynomial():
        put_left(left_gram, gram[...])
        put_right(right, gram[...])
        symmetric_product(temp, left_gram, right, tiles)
        poly[...] = jnp.where(diagonal, poly_linear, 0.0) + poly_square * gram[...] + poly_cubic * temp[...]
        put_right(right, poly[...])

    def next_gram():
        symmetric_product(temp, left_gram, right, tiles)
        put_left(left_temp, temp[...])
        symmetric_product(gram, left_temp, right, tiles)

    def thin(values):
        count = values.shape[0]
        top, low = split(values)
        both = nn(jnp.concatenate([top, low], axis=0), right[:width, :])
        return both[:count, :] + both[count:, :] + nn(top, right[width : 2 * width, :])

    polynomial()
    rows_s[...] = poly[mine, :]

    def iteration(step, carry):
        next_gram()
        polynomial()
        rows_s[...] = thin(rows_s[...])
        return carry

    lax.fori_loop(0, NS_ITERS - 2, iteration, 0)
    next_gram()
    put_right(right, gram[...])
    rows = rows_s[...]
    once = thin(rows)
    twice = thin(once)
    rows = (poly_linear * rows + poly_square * once + poly_cubic * twice) * lax.rsqrt(norm_sq)
    top, low = split(rows)
    for j, part in enumerate(parts):
        write(j, nn(top, part) + nn(low, part))


class PlaneStage:
    def __init__(self, total, from_plane, send, recv):
        rank, self.plane = place()[:2]
        self.total, self.from_plane = total, from_plane
        self.copies = [
            pltpu.make_async_remote_copy(
                src_ref=total.at[(self.plane + step) % 4], dst_ref=from_plane.at[step - 1],
                send_sem=send.at[step - 1], recv_sem=recv.at[step - 1],
                device_id=(rank, (self.plane + step) % 4), device_id_type=MESH)
            for step in (1, 2, 3)
        ]

    def start(self):
        for copy in self.copies:
            copy.start()

    def finish(self):
        for copy in self.copies:
            copy.wait()
        value = self.total[pl.ds(self.plane, 1)][0].astype(jnp.float32)
        for slot in range(3):
            value = value + self.from_plane[slot].astype(jnp.float32)
        return value


MATRIX_OF = (1, 0, 2, 3)
LANES_OF = (256, 512, 640, 640)
CUTS_A = ((0, 256), (256, 384))


def tail_kernel(
    sums_ref, table_ref, own_up_ref, total_b_ref, len_ref, *refs,
):
    moments, weights, small, large = refs[0:4], refs[4:8], refs[8:11], refs[11:19]
    refs = refs[19:]
    new_moments, new_weights, new_small, input_grad_hbm = refs[0:4], refs[4:8], refs[8:11], refs[11]
    table_out, pieces = refs[12:14]
    refs = refs[14:]
    early, late = (SumStages(None, refs[SUM_SCRATCH * n : SUM_SCRATCH * (n + 1)], None) for n in range(2))
    refs = refs[2 * SUM_SCRATCH :]
    table_scratch, refs = refs[:6], refs[6:]
    blocks, whole, gram, poly, temp, rows_s, left_gram, left_temp, right, from_plane_b = refs[:10]
    plane_send, plane_recv, gather_send, gather_recv, back_send, back_recv, b_send, b_recv, loads = refs[10:19]
    gives_s, (tiles_s, h1t_s, turned_s, stored), held = refs[19:21], refs[21:25], refs[25:]
    h1_ref, dq_ref, dk_ref, dv_ref, out_grad_ref, wt_s, after_s, x_s = held
    rank, plane, core, chip_x, chip_y = place()
    chip = chip_at(0, chip_x, chip_y)
    columns, lanes = blocks.shape[1:]
    tokens, width = h1_ref.shape
    rows_qkv, rows_out = moments[0].shape[1], moments[1].shape[0]
    last_b = PlaneStage(total_b_ref, from_plane_b, b_send, b_recv)
    loading = [pltpu.make_async_copy(source, target, loads.at[n]) for n, (source, target) in enumerate(zip(large, held))]
    for copy in loading:
        copy.start()

    @pl.when(plane < 2)
    def _():
        whole[...] = jnp.zeros_like(whole)

    greet(all_partners())
    last_b.start()
    loading[0].wait()
    h1t_s[...] = h1_ref[...].T
    for copy in loading[1:5]:
        copy.wait()

    def half(which, targets):
        starts = [pl.multiple_of(columns * (2 * m + which), 16) for m in range(4)]
        left = jnp.concatenate([h1t_s[pl.ds(start, columns), :] for start in starts], axis=0)
        qkv = jnp.concatenate([nn(left, ref[...]).astype(jnp.bfloat16) for ref in (dq_ref, dk_ref, dv_ref)], axis=1)
        out = jnp.concatenate([out_grad_ref[pl.ds(start, columns), :] for start in starts], axis=0)
        for j in range(4):
            both = jnp.concatenate(
                [qkv[:, j * rows_qkv : (j + 1) * rows_qkv], out[:, j * rows_out : (j + 1) * rows_out]], axis=1)
            for target, (start, size) in zip(targets, CUTS_A):
                target[j] = both[:, start : start + size].reshape(2, 2, columns, size)

    half(1 - core, gives_s)
    gives = [stages.give_copy(source) for stages, source in zip((early, late), gives_s)]
    for give in gives:
        give.start()
    half(core, (early.own, late.own))
    early.core_add(gives[0])
    early.chip_start()
    late.core_add(gives[1])

    def momentum(x, gradient):
        rows = gradient.shape[1]
        slot = MATRIX_OF.index(x)
        if x == 1:
            new = moment_keep * moments[x][...].T + gradient
            new_moments[x][...] = new.T
        else:
            new = moment_keep * moments[x][...] + gradient
            new_moments[x][...] = new
        blocks[slot, :, :rows] = new.astype(jnp.bfloat16)
        if rows < lanes:
            blocks[slot, :, rows:] = jnp.zeros((columns, lanes - rows), jnp.bfloat16)

    def out_copy(step, target):
        part = pl.ds(0, LANES_OF[target])
        return pltpu.make_async_remote_copy(
            src_ref=blocks.at[target, :, part], dst_ref=whole.at[plane, chip, core, :, part],
            send_sem=plane_send.at[step - 1], recv_sem=plane_recv.at[step - 1],
            device_id=(rank, (plane + step) % 4), device_id_type=MESH)

    def when_target(targets, act):
        for step in (1, 2, 3):
            for target in targets:
                @pl.when((plane + step) % 4 == target)
                def _():
                    act(out_copy(step, target))

    def place_own(target):
        part = LANES_OF[target]
        whole[target, pl.ds(chip, 1), pl.ds(core, 1), :, :part] = blocks[target, :, :part][None, None]

    def gather_of(target):
        part = pl.ds(0, LANES_OF[target])
        return Gather(lambda m, c, planes: whole.at[planes, m, c, :, part], gather_send, gather_recv, 0, lane_parts(0, 4))

    def arrived(target):
        for step in (1, 2, 3):
            out_copy(step, target).wait_recv()

    for copy in loading[5:]:
        copy.wait()
    ends, offset = row_marks(len_ref)
    gain = table_ref[0:1, :]
    gain_sum = jnp.zeros((1, width), jnp.float32)
    shift_sum = jnp.zeros((1, width), jnp.float32)
    for r in range(0, tokens, 256):
        at = slice(r, r + 256)
        grad = sum(nt(ref[at, :], wt_s[:, part * width : (part + 1) * width])
                   for part, ref in enumerate((dq_ref, dk_ref, dv_ref)))
        values = x_s[at, :].astype(jnp.float32)
        center = values - jnp.mean(values, axis=-1, keepdims=True)
        rstd = lax.rsqrt(jnp.mean(center * center, axis=-1, keepdims=True) + norm_eps)
        xhat = center * rstd
        gain_sum += jnp.sum(grad * xhat, axis=0, keepdims=True)
        shift_sum += jnp.sum(grad, axis=0, keepdims=True)
        scaled = grad * gain
        after_s[at, :] += rstd * (scaled - jnp.mean(scaled, axis=-1, keepdims=True)
                                  - xhat * jnp.mean(scaled * xhat, axis=-1, keepdims=True))
        if r == 0:
            early.chip_turn()
            late.chip_start()
        if r == 512:
            early.chip_finish()
            early.plane_start()
        if r == 256:
            momentum(2, own_up_ref[...])
            momentum(3, last_b.finish())
            when_target((2, 3), lambda copy: copy.start())
    vector = jnp.concatenate(
        [gain_sum, shift_sum, sums_ref[2:4, :]]
        + [jnp.sum(ref[...].astype(jnp.float32), axis=0, keepdims=True) for ref in (dq_ref, dk_ref, dv_ref)]
        + [sums_ref[7:16, :]], axis=0)
    for block in range(8):
        part = vector[:, block * columns : (block + 1) * columns]
        tiles_s[block // 2, block % 2] = jnp.concatenate(
            [part, jnp.zeros((16, LANES - columns), jnp.float32)], axis=1)
    adding = table_sum(tiles_s, table_out, *table_scratch)
    late.chip_turn()
    next(adding)
    turned_s[...] = pltpu.roll(after_s[...], offset, 0)
    storing = pltpu.make_async_copy(turned_s, input_grad_hbm, stored)
    storing.start()
    late.chip_finish()
    late.plane_start()
    next(adding)
    for target in (2, 3):
        @pl.when(plane == target)
        def _():
            place_own(target)
            arrived(target)
            gather_of(target).first()
    next(adding)
    gradient = jnp.concatenate([early.plane_finish(), late.plane_finish()], axis=1)
    momentum(0, gradient[:, :rows_qkv])
    momentum(1, gradient[:, rows_qkv : rows_qkv + rows_out])
    when_target((0, 1), lambda copy: copy.start())
    for target in (2, 3):
        @pl.when(plane == target)
        def _():
            gather = gather_of(target)
            gather.second()
            gather.third()
            gather.finish()
    next(adding)
    first_fix = 1.0 - beta_first**STEP
    second_fix = 1.0 - beta_second**STEP
    n_vec = small[0].shape[0]
    vector_grad = table_out[:n_vec, :columns]
    vectors, vec_first, vec_second = (ref[...] for ref in small)
    new_first = beta_first * vec_first + (1.0 - beta_first) * vector_grad
    new_second = beta_second * vec_second + (1.0 - beta_second) * vector_grad * vector_grad
    new_small[0][...] = vectors - adam_rate * (new_first / first_fix) / (jnp.sqrt(new_second / second_fix) + adam_eps)
    new_small[1][...] = new_first
    new_small[2][...] = new_second
    for target in (0, 1):
        @pl.when(plane == target)
        def _():
            place_own(target)
            arrived(target)
            gather = gather_of(target)
            gather.first()
            gather.second()
            gather.third()
            gather.finish()
    when_target((0, 1, 2, 3), lambda copy: copy.wait_send())

    def write(j, values):
        blocks[j] = values.astype(jnp.bfloat16)

    orthogonal_rows(whole, pl.ds(pl.multiple_of(rank * columns, 8), columns), gram, poly, temp, rows_s,
                    left_gram, left_temp, right, write)

    def home_copy(step, source):
        part = pl.ds(0, LANES_OF[source])
        return pltpu.make_async_remote_copy(
            src_ref=blocks.at[(plane + step) % 4, :, part], dst_ref=pieces.at[source, :, part],
            send_sem=back_send.at[step - 1], recv_sem=back_recv.at[step - 1],
            device_id=(rank, (plane + step) % 4), device_id_type=MESH)

    for source in range(4):
        @pl.when(plane == source)
        def _():
            for step in (1, 2, 3):
                home_copy(step, source).start()
            pieces[source] = blocks[source]

    def update(x):
        rows = moments[x].shape[0 if x == 1 else 1]
        scale = muon_rate * math.sqrt(max(1.0, rows * 4 / width))
        change = pieces[MATRIX_OF.index(x), :, :rows].astype(jnp.float32)
        new_weights[x][...] = (weights[x][...] * (1.0 - muon_rate * muon_decay)
                               - scale * (change.T if x == 1 else change))

    for source in (2, 3, 0, 1):
        for step in (1, 2, 3):
            @pl.when((plane + 4 - source) % 4 == step)
            def _():
                home_copy(step, source).wait_recv()
        update(MATRIX_OF[source])
    for source in range(4):
        @pl.when(plane == source)
        def _():
            for step in (1, 2, 3):
                home_copy(step, source).wait_send()
    storing.wait()


def tail(h1, dq, dk, dv, out_grad, sums, table, own_up, total_b, lengths, moments, weights, small, wt_qkv, after_grad, x):
    tokens, width = h1.shape
    rows = width // 8
    large = (h1, dq, dk, dv, out_grad, wt_qkv, after_grad, x)
    vmem = pl.BlockSpec(memory_space=pltpu.VMEM)
    hbm = pl.BlockSpec(memory_space=pl.ANY)
    tile = (16, LANES)
    most = max(moments[n].shape[1] for n in (0, 2, 3))
    shape = jax.ShapeDtypeStruct
    f32, bf16 = jnp.float32, jnp.bfloat16
    square = pltpu.VMEM((width, width), f32)
    sems = lambda n: pltpu.SemaphoreType.DMA((n,))
    lanes_b = total_b.shape[-1]
    return pl.pallas_call(
        tail_kernel,
        in_specs=[vmem] * 4 + [pl.BlockSpec(memory_space=pltpu.SMEM)] + [vmem] * 11 + [hbm] * 8,
        out_specs=[vmem] * 11 + [hbm],
        out_shape=[shape(v.shape, f32) for v in (*moments, *weights, *small)] + [shape((tokens, width), f32)],
        scratch_shapes=[pltpu.VMEM(tile, f32), pltpu.VMEM((4, rows, most), bf16)]
        + [scratch for _, size in CUTS_A for scratch in sum_scratch(rows, size)]
        + [pltpu.VMEM((4, *tile), f32), pltpu.VMEM((3, *tile), f32),
           pltpu.VMEM((3, *tile), f32), pltpu.VMEM((4, *tile), f32), sems(7), sems(7)]
        + [pltpu.VMEM((4, rows, most), bf16), pltpu.VMEM((4, 4, 2, rows, most), bf16),
           square, square, square, pltpu.VMEM((rows, width), f32),
           pltpu.VMEM((width, 3 * width), bf16), pltpu.VMEM((width, 3 * width), bf16),
           pltpu.VMEM((3 * width, width), bf16), pltpu.VMEM((3, rows, lanes_b), bf16)]
        + [sems(3), sems(3), sems(8), sems(8), sems(3), sems(3), sems(3), sems(3), sems(8)]
        + [pltpu.VMEM((4, 2, 2, rows, size), bf16) for _, size in CUTS_A]
        + [pltpu.VMEM((4, 2, *tile), f32), pltpu.VMEM((width, tokens), bf16),
           pltpu.VMEM((tokens, width), f32), pltpu.SemaphoreType.DMA]
        + [pltpu.VMEM(v.shape, v.dtype) for v in large],
        compiler_params=pltpu.CompilerParams(collective_id=1, has_side_effects=True, vmem_limit_bytes=60 << 20),
        name="tail",
    )(sums, table, own_up, total_b, lengths, *moments, *weights, *small, *large)


def finish_kernel(*refs):
    count = len(refs) // 3
    sources, targets, held, loads, stores = refs[:count], refs[count : 2 * count], refs[2 * count : -2], refs[-2], refs[-1]
    loading, storing = [], []
    for n in range(count):
        rows = sources[n].shape[0]
        parts = 4 if rows >= ROW_LEN else 1
        for p in range(parts):
            at = pl.ds(p * (rows // parts), rows // parts)
            slot = len(loading)
            loading.append(pltpu.make_async_copy(sources[n].at[at], held[n].at[at], loads.at[slot]))
            storing.append(pltpu.make_async_copy(held[n].at[at], targets[n].at[at], stores.at[slot]))
    for copy in loading:
        copy.start()
    for load, store in zip(loading, storing):
        load.wait()
        store.start()
    for copy in storing:
        copy.wait()


def finish(values):
    hbm = pl.BlockSpec(memory_space=pl.ANY)
    count = len(values)
    copies = sum(4 if x.shape[0] >= ROW_LEN else 1 for x in values)
    return pl.pallas_call(
        finish_kernel,
        in_specs=[hbm] * count,
        out_specs=[hbm] * count,
        out_shape=[jax.ShapeDtypeStruct(x.shape, x.dtype) for x in values],
        scratch_shapes=[pltpu.VMEM(x.shape, x.dtype) for x in values]
        + [pltpu.SemaphoreType.DMA((copies,)), pltpu.SemaphoreType.DMA((copies,))],
        compiler_params=pltpu.CompilerParams(vmem_limit_bytes=62 << 20),
        name="finish",
    )(*values)


def lane_parts(start, size):
    half = size // 2
    return pl.ds(start, size), pl.ds(start, half), pl.ds(start + half, half)


ROW_LEN = 1024
GATHERED = 512
CHUNK_A = 256
OUT_LANES = 256
CUTS_B = ((0, 512), (512, 768))


def row_marks(len_ref):
    ends = [len_ref[0, 0]]
    for slot in (1, 2):
        ends.append(ends[-1] + len_ref[0, slot])
    starts = [0, *ends]
    offset = starts[3]
    for slot in (2, 1, 0):
        offset = jnp.where(len_ref[0, slot] == LONGEST, starts[slot], offset)
    return ends, offset


def segment_of(index, ends, offset):
    where = index + offset
    where = jnp.where(where >= ROW_LEN, where - ROW_LEN, where)
    segment = sum((where >= end).astype(jnp.int32) for end in ends)
    return where, segment


def turned_rows(values, offset):
    return pltpu.roll(values.astype(jnp.float32), jnp.where(offset > 0, ROW_LEN - offset, 0), 0)


def same_rest(ends, offset):
    rest = ROW_LEN - LONGEST
    columns = lax.broadcasted_iota(jnp.int32, (rest, rest), 0) + LONGEST
    rows = lax.broadcasted_iota(jnp.int32, (rest, rest), 1) + LONGEST
    return segment_of(columns, ends, offset)[1] == segment_of(rows, ends, offset)[1]


def attention_jobs(tokens):
    blocks = [(start, 256, 0, LONGEST) for start in range(0, LONGEST, 256)] + [(LONGEST, tokens - LONGEST, LONGEST, tokens - LONGEST)]
    return [(h, *block) for h in range(LANES // HEAD_DIM) for block in blocks]


def attention_group(q, k_ref, v, same, ot_s, vt_s, lse_ref):
    tokens = q.shape[0]
    qt = q.T
    vt_s[...] = v.T
    row = lax.broadcasted_iota(jnp.int32, qt.shape, 0)
    jobs = attention_jobs(tokens)
    queries, scores, soft = {}, {}, {}

    def score(job):
        h, start, width, key_start, key_count = job
        if h not in queries:
            queries[h] = jnp.where(row // HEAD_DIM == h, qt, jnp.zeros((), jnp.bfloat16))
        out = nn(k_ref[key_start : key_start + key_count, :], queries[h][:, start : start + width])
        return jnp.where(same, out, masked_score) if start == LONGEST else out

    def soften(values):
        peak = jnp.max(values, axis=0, keepdims=True)
        raised = jnp.exp(values - peak)
        return raised.astype(jnp.bfloat16), peak, jnp.sum(raised, axis=0, keepdims=True)

    def collect(job, raised, peak, total):
        h, start, width, key_start, key_count = job
        rows = slice(h * HEAD_DIM, (h + 1) * HEAD_DIM)
        out = nn(vt_s[rows, key_start : key_start + key_count], raised)
        ot_s[rows, start : start + width] = out / total
        lse_ref[0, h : h + 1, start : start + width] = peak + jnp.log(total)

    count = len(jobs)
    for t in range(count + 2):
        if t < count:
            scores[t] = score(jobs[t])
        if 0 <= t - 1 < count:
            soft[t - 1] = soften(scores.pop(t - 1))
        if 0 <= t - 2:
            collect(jobs[t - 2], *soft.pop(t - 2))
    return ot_s[...].T.astype(jnp.bfloat16)


def head_kernel(
    len_ref, count_ref, tokens_ref, w_qkv_ref, w_up_ref, w_down_ref, w_out_ref, vectors_ref, cot_hbm,
    qr_ref, kr_ref, vr_ref, attn_ref, lse_ref, h1_hbm, x_hbm, cos_hbm, sin_hbm, wt_hbm, table_ref, full_b, full_o,
    incoming_hbm, dy_hbm, dyt_hbm, incoming_s, dy_s, dyt_s, cot_s,
    h1_ref, x_ref, cos_ref, sin_ref, wt_ref, stores, full_a, full_v, twice_s, q_s, k_s, v_s, ot_s, vt_s, slab_a, slab_b, slab_o,
    a_send, a_recv, az_send, az_recv, b_send, b_recv, bz_send, bz_recv, v_send, v_recv, local,
):
    group = pl.program_id(0)
    rank, plane, core, chip_x, chip_y = place()
    chip = chip_at(0, chip_x, chip_y)
    columns = slab_a.shape[0]
    chunks_a = GATHERED // CHUNK_A
    gather_a = [Gather(lambda m, c, lane: full_a.at[:, m, c, :, lane], a_send, a_recv, 8 * n,
                       lane_parts(CHUNK_A * n, CHUNK_A))
                for n in range(chunks_a)]
    gather_o = Gather(lambda m, c, lane: full_o.at[:, m, c, :, lane], b_send, b_recv, 0, lane_parts(0, OUT_LANES))
    gather_b = [Gather(lambda m, c, lane: full_b.at[pl.ds(0, 2), m, c, :, lane], b_send, b_recv, 8 + 8 * n,
                       lane_parts(*cut))
                for n, cut in enumerate(CUTS_B)]

    def along(slab, full, send, recv, n, start, size):
        lanes = pl.ds(start, size)
        return [
            pltpu.make_async_remote_copy(
                src_ref=slab.at[:, lanes], dst_ref=full.at[plane, chip, core, :, lanes],
                send_sem=send.at[3 * n + step - 1], recv_sem=recv.at[3 * n + step - 1],
                device_id=(rank, (plane + step) % 4), device_id_type=MESH)
            for step in (1, 2, 3)
        ]

    along_a = [along(slab_a, full_a, az_send, az_recv, n, CHUNK_A * n, CHUNK_A) for n in range(chunks_a)]
    along_o = along(slab_o, full_o, bz_send, bz_recv, 0, 0, OUT_LANES)
    along_b = [along(slab_b, full_b, bz_send, bz_recv, 1 + n, *cut) for n, cut in enumerate(CUTS_B)]
    own_b = [pltpu.make_async_copy(slab_b, full_b.at[plane, chip, core], local.at[0]),
             pltpu.make_async_copy(slab_o, full_o.at[plane, chip, core], local.at[1])]
    storing = [pltpu.make_async_copy(source, target, stores.at[n]) for n, (source, target) in enumerate(
        ((h1_ref, h1_hbm), (x_ref, x_hbm), (cos_ref, cos_hbm), (sin_ref, sin_hbm), (wt_ref, wt_hbm),
         (incoming_s, incoming_hbm), (dy_s, dy_hbm), (dyt_s, dyt_hbm)))]
    load_cot = pltpu.make_async_copy(cot_hbm, cot_s, local.at[2])
    ends, offset = row_marks(len_ref)

    def widen(values, lanes):
        return jnp.concatenate([values, jnp.zeros((values.shape[0], lanes - values.shape[1]), values.dtype)], axis=1)

    @pl.when(group == 0)
    def _():
        load_cot.start()
        slab_a[...] = widen(w_qkv_ref[...].astype(jnp.bfloat16), GATHERED)
        n_vec, width = vectors_ref.shape[0], tokens_ref.shape[1]
        vectors = jnp.concatenate([vectors_ref[...], jnp.zeros((LANES - n_vec, columns), jnp.float32)], axis=0)
        vectors = vectors.astype(jnp.bfloat16).astype(jnp.float32)
        full_v[pl.ds(chip, 1), pl.ds(core, 1)] = widen(vectors, LANES).T[:columns, :][None, None]
        full_a[pl.ds(plane, 1), pl.ds(chip, 1), pl.ds(core, 1)] = slab_a[...][None, None, None]
        greet(all_partners())
        for copy in along_a[0]:
            copy.start()
        slab_b[:, :width] = w_up_ref[...].astype(jnp.bfloat16)
        slab_b[:, width:] = w_down_ref[...].astype(jnp.bfloat16)
        slab_o[...] = widen(w_out_ref[...].T.astype(jnp.bfloat16), OUT_LANES)
        for copy in own_b:
            copy.start()

        def vec_copy(m, slot, device):
            block = full_v.at[m, core]
            return pltpu.make_async_remote_copy(
                src_ref=block, dst_ref=block, send_sem=v_send.at[slot], recv_sem=v_recv.at[slot],
                device_id=(device, plane), device_id_type=MESH)

        chips = [chip_at(step, chip_x, chip_y) for step in range(4)]
        vec_over = [vec_copy(chip, step - 1, 2 * chips[step] + core) for step in (1, 2, 3)]
        vec_beside = [vec_copy(m, 3 + step, 2 * chip + 1 - core) for step, m in enumerate(chips)]
        for copy in (*vec_over, vec_beside[0]):
            copy.start()
        twice_s[...] = turned_rows(tokens_ref[...], offset)
        for copy in along_a[0]:
            copy.wait()
        for copy in along_a[1]:
            copy.start()
        gather_a[0].first()
        index = lax.broadcasted_iota(jnp.int32, (ROW_LEN, LANES), 0)
        where, segment = segment_of(index, ends, offset)
        start = jnp.where(segment == 0, 0, jnp.where(segment == 1, ends[0], jnp.where(segment == 2, ends[1], ends[2])))
        position = (where - start).astype(jnp.float32)
        lane = lax.broadcasted_iota(jnp.int32, (1, LANES), 1)
        inverse = jnp.exp((lane % (HEAD_DIM // 2)).astype(jnp.float32) * (-2.0 * math.log(10000.0) / HEAD_DIM))
        sign = jnp.where((lane % HEAD_DIM) < (HEAD_DIM // 2), -1.0, 1.0)
        angles = position * inverse
        for copy in along_a[1]:
            copy.wait()
        gather_a[1].first()
        for copies in (along_o, *along_b):
            for copy in copies:
                copy.start()
        cos_ref[...] = jnp.cos(angles)
        for step in range(3):
            vec_over[step].wait()
            vec_beside[step + 1].start()
        gather_a[0].second()
        sin_ref[...] = jnp.sin(angles) * sign
        for copy in vec_beside:
            copy.wait()
        table_t = jnp.concatenate([full_v[m, c] for m in range(4) for c in range(2)], axis=0)
        table_ref[...] = table_t.T[: table_ref.shape[0], :]
        gather_a[1].second()
        load_cot.wait()
        _, segment = segment_of(lax.broadcasted_iota(jnp.int32, (ROW_LEN, 1), 0), ends, offset)
        number = jnp.where(segment == 0, count_ref[0, 0], jnp.where(
            segment == 1, count_ref[0, 1], jnp.where(segment == 2, count_ref[0, 2], count_ref[0, 3])))
        incoming_s[...] = turned_rows(cot_s[...], offset) * (1.0 / number.astype(jnp.float32))
        dy_s[...] = incoming_s[...].astype(jnp.bfloat16)
        dyt_s[...] = dy_s[...].T
        gather_a[0].third()
        gather_a[1].third()
        gain, shift = table_ref[0:1, :], table_ref[1:2, :]
        for r in range(0, ROW_LEN, 256):
            values = twice_s[r : r + 256, :]
            x_ref[r : r + 256, :] = values.astype(jnp.bfloat16)
            h1_ref[r : r + 256, :] = layer_norm(values, gain, shift).astype(jnp.bfloat16)
        for gather in gather_a:
            gather.finish()
        for copy in (*own_b, *along_o):
            copy.wait()
        gather_o.first()
        rows = wt_ref.shape[1] // 4
        wt_ref[...] = jnp.concatenate(
            [full_a[j].reshape(width, GATHERED)[:, :rows] for j in range(4)], axis=1)
        first = _half_mask((256, LANES))
        bias = [table_ref[4 + part : 5 + part, :] for part in range(3)]
        for r in range(0, ROW_LEN, 256):
            at = slice(r, r + 256)
            project = nn(h1_ref[at, :], wt_ref[...])
            cosine, sine = cos_ref[at, :], sin_ref[at, :]
            for g in range(width // LANES):
                lanes = slice(g * LANES, (g + 1) * LANES)
                queries = (project[:, lanes] + bias[0][:, lanes]) * (1.0 / math.sqrt(HEAD_DIM))
                keys = project[:, width + g * LANES : width + (g + 1) * LANES] + bias[1][:, lanes]
                q_s[g, at, :] = (queries * cosine + _turn(queries, first) * sine).astype(jnp.bfloat16)
                k_s[g, at, :] = (keys * cosine + _turn(keys, first) * sine).astype(jnp.bfloat16)
                v_s[g, at, :] = (project[:, 2 * width + g * LANES : 2 * width + (g + 1) * LANES]
                                 + bias[2][:, lanes]).astype(jnp.bfloat16)
        for copy in storing:
            copy.start()
        for copy in along_b[0]:
            copy.wait()
        gather_b[0].first()
        gather_o.second()

    @pl.when(group == 1)
    def _():
        for copy in along_b[1]:
            copy.wait()
        gather_b[1].first()
        gather_o.third()

    @pl.when(group == 2)
    def _():
        gather_b[0].second()

    @pl.when(group == 4)
    def _():
        gather_b[1].second()
        gather_b[0].third()

    qr_ref[...] = q_s[group]
    kr_ref[...] = k_s[group]
    vr_ref[...] = v_s[group]
    attn_ref[...] = attention_group(q_s[group], kr_ref, v_s[group], same_rest(ends, offset), ot_s, vt_s, lse_ref)

    @pl.when(group == 4)
    def _():
        gather_b[1].third()
        for gather in (gather_o, *gather_b):
            gather.finish()
        for copy in storing:
            copy.wait()


def head(lengths, counts, tokens, cotangent, w_qkv_t, w_up_t, w_down_t, w_out, vectors):
    tokens_count, width = tokens.shape
    groups = width // LANES
    columns = w_qkv_t.shape[0]
    col = pl.BlockSpec((tokens_count, LANES), lambda g: (0, g))
    whole = lambda *shape: pl.BlockSpec(shape, lambda g: (0,) * len(shape))
    shape = jax.ShapeDtypeStruct
    bf16, f32 = jnp.bfloat16, jnp.float32
    sems = lambda n: pltpu.SemaphoreType.DMA((n,))
    na, nb = GATHERED // CHUNK_A, 1 + len(CUTS_B)
    return pl.pallas_call(
        head_kernel,
        grid=(groups,),
        in_specs=[pl.BlockSpec(memory_space=pltpu.SMEM)] * 2 + [whole(tokens_count, width), whole(*w_qkv_t.shape),
                  whole(columns, width), whole(columns, width), whole(*w_out.shape), whole(*vectors.shape),
                  pl.BlockSpec(memory_space=pl.ANY)],
        out_specs=[col] * 4 + [pl.BlockSpec((1, 4, tokens_count), lambda g: (g, 0, 0)),
                               *[pl.BlockSpec(memory_space=pl.ANY)] * 5, whole(16, width),
                               *[pl.BlockSpec(memory_space=pl.ANY)] * 5],
        out_shape=[shape((tokens_count, width), bf16)] * 4 + [shape((groups, 4, tokens_count), f32)]
        + [shape((tokens_count, width), bf16)] * 2 + [shape((tokens_count, LANES), f32)] * 2
        + [shape((width, 3 * width), bf16), shape((16, width), f32), shape((4, 4, 2, columns, 2 * width), bf16),
           shape((4, 4, 2, columns, OUT_LANES), bf16),
           shape((tokens_count, width), f32), shape((tokens_count, width), bf16), shape((width, tokens_count), bf16)],
        scratch_shapes=[
            pltpu.VMEM((tokens_count, width), f32),
            pltpu.VMEM((tokens_count, width), bf16),
            pltpu.VMEM((width, tokens_count), bf16),
            pltpu.VMEM((tokens_count, width), bf16),
            pltpu.VMEM((tokens_count, width), bf16),
            pltpu.VMEM((tokens_count, width), bf16),
            pltpu.VMEM((tokens_count, LANES), f32),
            pltpu.VMEM((tokens_count, LANES), f32),
            pltpu.VMEM((width, 3 * width), bf16),
            sems(8),
            pltpu.VMEM((4, 4, 2, columns, GATHERED), bf16),
            pltpu.VMEM((4, 2, columns, LANES), f32),
            pltpu.VMEM((tokens_count, width), f32),
            pltpu.VMEM((groups, tokens_count, LANES), bf16),
            pltpu.VMEM((groups, tokens_count, LANES), bf16),
            pltpu.VMEM((groups, tokens_count, LANES), bf16),
            pltpu.VMEM((LANES, tokens_count), f32),
            pltpu.VMEM((LANES, tokens_count), bf16),
            pltpu.VMEM((columns, GATHERED), bf16),
            pltpu.VMEM((columns, 2 * width), bf16),
            pltpu.VMEM((columns, OUT_LANES), bf16),
            sems(8 * na), sems(8 * na), sems(3 * na), sems(3 * na),
            sems(8 * nb), sems(8 * nb), sems(3 * nb), sems(3 * nb), sems(7), sems(7), sems(3),
        ],
        compiler_params=pltpu.CompilerParams(collective_id=2, has_side_effects=True, vmem_limit_bytes=58 << 20),
        name="head",
    )(lengths, counts, tokens, w_qkv_t, w_up_t, w_down_t, w_out, vectors, cotangent)


def middle_kernel(
    len_ref, table_ref, x_hbm, attn_hbm, incoming_hbm, dy_hbm, dyt_hbm, full_o_hbm, full_b,
    out_grad_ref, sums_ref, layer_hbm, after_hbm, attn_grad_hbm, parts_hbm,
    x_ref, attn_ref, cot_ref, full_o_ref, after_grad_ref, parts_s, stores,
    xhat_s, rstd_s, h2_s, h2t_s, dy_s, dyt_s, acc_s, back_s, act_s, pre_s, wt_out_s, w_s, send, recv, local,
):
    step = pl.program_id(0)
    tokens, width = x_ref.shape
    rank, plane, core, chip_x, chip_y = place()
    chip = chip_at(0, chip_x, chip_y)
    late = Gather(lambda m, c, lane: w_s.at[1, :, m, c, :, lane], send, recv, 0, lane_parts(0, 2 * width))
    loads = [pltpu.make_async_copy(full_b.at[pl.ds(2, 2), chip, core], w_s.at[1, :, chip, core], local.at[0]),
             pltpu.make_async_copy(full_o_hbm, full_o_ref, local.at[1]),
             pltpu.make_async_copy(attn_hbm, attn_ref, local.at[2]),
             pltpu.make_async_copy(x_hbm, x_ref, local.at[3]),
             pltpu.make_async_copy(full_b.at[pl.ds(0, 2)], w_s.at[0], local.at[4]),
             pltpu.make_async_copy(dy_hbm, dy_s, local.at[5]),
             pltpu.make_async_copy(dyt_hbm, dyt_s, local.at[6]),
             pltpu.make_async_copy(incoming_hbm, after_grad_ref, local.at[7])]
    ends, offset = row_marks(len_ref)
    chunk = 256
    cuts = [slice(r, r + chunk) for r in range(0, tokens, chunk)]

    @pl.when(step == 0)
    def _():
        for load in loads:
            load.start()
        greet([(2 * chip + 1 - core, plane)]
              + [(2 * chip_at(other, chip_x, chip_y) + core, plane) for other in (1, 2)])
        loads[0].wait()
        late.first()
        for load in loads[1:4]:
            load.wait()
        rows = width // 4
        wt_out_s[...] = jnp.concatenate([full_o_ref[p].reshape(width, OUT_LANES)[:, :rows] for p in range(4)], axis=1)
        sums_ref[...] = jnp.zeros_like(sums_ref)
        gain, shift = table_ref[2:3, :], table_ref[3:4, :]
        for at in cuts:
            after = x_ref[at, :].astype(jnp.float32) + (nn(attn_ref[at, :], wt_out_s[...]) + table_ref[7:8, :])
            acc_s[at, :] = after + table_ref[8:9, :]
            center = after - jnp.mean(after, axis=-1, keepdims=True)
            rstd = lax.rsqrt(jnp.mean(center * center, axis=-1, keepdims=True) + norm_eps)
            xhat = center * rstd
            xhat_s[at, :] = xhat
            rstd_s[at, :] = rstd
            h2_s[at, :] = (xhat * gain + shift).astype(jnp.bfloat16)
        h2t_s[...] = h2_s[...].T
        back_s[...] = jnp.zeros_like(back_s)

    @pl.when(step == 0)
    def _():
        for load in loads[4:]:
            load.wait()
        sums_ref[8:9, :] = jnp.sum(dy_s[...].astype(jnp.float32), axis=0, keepdims=True)

    @pl.when(step == 1)
    def _():
        late.finish()

    def weights(lanes):
        return jnp.concatenate([w_s[step, p, :, :, :, lanes].reshape(width, width) for p in range(2)], axis=1)

    up, down = (weights(slice(part * width, (part + 1) * width)) for part in range(2))
    bias = jnp.concatenate([table_ref[pl.ds(9 + 2 * step + p, 1), :] for p in range(2)], axis=1)

    def products(at):
        return nn(h2_s[at, :], up), nn(dy_s[at, :], down)

    def pointwise(at, pre, act_grad):
        pre = pre + bias
        cdf = 0.5 * (1.0 + lax.erf(pre * (1.0 / math.sqrt(2.0))))
        slope = cdf + pre * (jnp.exp(-0.5 * pre * pre) * (1.0 / math.sqrt(2.0 * math.pi)))
        act_s[at, :] = (pre * cdf).astype(jnp.bfloat16)
        pre_s[at, :] = (act_grad * slope).astype(jnp.bfloat16)

    def collect(at):
        acc_s[at, :] += nt(act_s[at, :], down)
        back_s[at, :] += nt(pre_s[at, :], up)

    held = {}
    for t in range(len(cuts) + 1):
        if t == 2:
            @pl.when(step == 0)
            def _():
                late.second()

        if t < len(cuts):
            held[t] = products(cuts[t])
        if t >= 1:
            pointwise(cuts[t - 1], *held.pop(t - 1))
            collect(cuts[t - 1])

    @pl.when(step == 0)
    def _():
        late.third()

    @pl.when(step == 1)
    def _():
        pltpu.make_async_copy(parts_s, parts_hbm.at[pl.ds(0, 2)], stores.at[0]).wait()

    for part, (left, right) in enumerate(((h2t_s, pre_s), (dyt_s, act_s))):
        grad = nn(left[...], right[...]).astype(jnp.bfloat16)
        for p in range(2):
            parts_s[p, :, part * width : (part + 1) * width] = grad[:, p * width : (p + 1) * width]
    store_parts = pltpu.make_async_copy(parts_s, parts_hbm.at[pl.ds(2 * step, 2)], stores.at[0])
    store_parts.start()
    bias_sum = jnp.sum(pre_s[...].astype(jnp.float32), axis=0, keepdims=True)
    for p in range(2):
        sums_ref[pl.ds(9 + 2 * step + p, 1), :] = bias_sum[:, p * width : (p + 1) * width]

    @pl.when(step == 1)
    def _():
        x_ref[...] = pltpu.roll(acc_s[...], offset, 0).astype(jnp.bfloat16)
        storing = [pltpu.make_async_copy(x_ref, layer_hbm, stores.at[1])]
        storing[0].start()
        gain = table_ref[2:3, :]
        gain_sum = jnp.zeros((1, width), jnp.float32)
        shift_sum = jnp.zeros((1, width), jnp.float32)
        branch_sum = jnp.zeros((1, width), jnp.float32)
        for n, at in enumerate(cuts):
            grad, xhat = back_s[at, :], xhat_s[at, :]
            gain_sum += jnp.sum(grad * xhat, axis=0, keepdims=True)
            shift_sum += jnp.sum(grad, axis=0, keepdims=True)
            scaled = grad * gain
            resid = rstd_s[at, :] * (
                scaled - jnp.mean(scaled, axis=-1, keepdims=True)
                - xhat * jnp.mean(scaled * xhat, axis=-1, keepdims=True))
            after_grad = after_grad_ref[at, :] + resid
            after_grad_ref[at, :] = after_grad
            low = after_grad.astype(jnp.bfloat16)
            dy_s[at, :] = low
            branch_sum += jnp.sum(low.astype(jnp.float32), axis=0, keepdims=True)
            cot_ref[at, :] = nt(low, wt_out_s[...]).astype(jnp.bfloat16)
            rows = pl.ds(at.start, chunk)
            for source, target, slot in ((after_grad_ref, after_hbm, 2), (cot_ref, attn_grad_hbm, 6)):
                copy = pltpu.make_async_copy(source.at[rows], target.at[rows], stores.at[slot + n])
                copy.start()
                storing.append(copy)
        sums_ref[2:3, :] = gain_sum
        sums_ref[3:4, :] = shift_sum
        sums_ref[7:8, :] = branch_sum
        h2t_s[...] = attn_ref[...].T
        out_grad_ref[...] = nn(h2t_s[...], dy_s[...]).astype(jnp.bfloat16)
        store_parts.wait()
        for copy in storing:
            copy.wait()


def middle(lengths, x, attn, incoming, dy, dyt, table, full_o, full_b):
    tokens, width = x.shape
    columns = full_b.shape[3]
    whole = lambda *shape: pl.BlockSpec(shape, lambda j: (0,) * len(shape))
    smem = pl.BlockSpec(memory_space=pltpu.SMEM)
    hbm = pl.BlockSpec(memory_space=pl.ANY)
    shape = jax.ShapeDtypeStruct
    bf16, f32 = jnp.bfloat16, jnp.float32
    flat = pltpu.VMEM((tokens, width), bf16)
    double = pltpu.VMEM((tokens, 2 * width), bf16)
    wide = pltpu.VMEM((tokens, width), f32)
    turned = pltpu.VMEM((width, tokens), bf16)
    sems = lambda n: pltpu.SemaphoreType.DMA((n,))
    return pl.pallas_call(
        middle_kernel,
        grid=(2,),
        in_specs=[smem, whole(16, width)] + [hbm] * 7,
        out_specs=[whole(width, width), whole(16, width)] + [hbm] * 4,
        out_shape=[shape((width, width), bf16), shape((16, width), f32),
                   shape((tokens, width), bf16), shape((tokens, width), f32), shape((tokens, width), bf16),
                   shape((4, width, 2 * width), bf16)],
        scratch_shapes=[flat, flat, flat, pltpu.VMEM(full_o.shape, bf16), wide, pltpu.VMEM((2, width, 2 * width), bf16),
                        sems(10), wide, pltpu.VMEM((tokens, 1), f32), flat, turned, flat, turned, wide, wide, double, double,
                        pltpu.VMEM((width, width), bf16), pltpu.VMEM((2, 2, 4, 2, columns, 2 * width), bf16),
                        sems(8), sems(8), sems(8)],
        compiler_params=pltpu.CompilerParams(collective_id=3, has_side_effects=True, vmem_limit_bytes=62 << 20),
        name="middle",
    )(lengths, table, x, attn, incoming, dy, dyt, full_o, full_b)


def backward_group(between, qr_ref, kr_ref, vr_ref, do_ref, attn_ref, lse_ref, same, qt_s, dot_s, kt_s, delta_s, dqt_s, dk_s, dv_s):
    tokens = qr_ref.shape[0]
    qt_s[...] = qr_ref[...].T
    dot_s[...] = do_ref[...].T
    kt_s[...] = kr_ref[...].T
    prod_t = (do_ref[...].astype(jnp.float32) * attn_ref[...].astype(jnp.float32)).T
    for h in range(4):
        delta_s[h : h + 1, :] = jnp.sum(prod_t[h * HEAD_DIM : (h + 1) * HEAD_DIM, :], axis=0, keepdims=True)
    dk_s[...] = jnp.zeros_like(dk_s)
    dv_s[...] = jnp.zeros_like(dv_s)
    row = lax.broadcasted_iota(jnp.int32, (LANES, tokens), 0)
    lane = lax.broadcasted_iota(jnp.int32, (tokens, LANES), 1)
    zero = jnp.zeros((), jnp.bfloat16)
    jobs = attention_jobs(tokens)
    masked, held = {}, {}

    def products(job):
        h, start, width, key_start, key_count = job
        if h not in masked:
            masked[h] = (
                jnp.where(row // HEAD_DIM == h, qt_s[...], zero), jnp.where(row // HEAD_DIM == h, dot_s[...], zero),
                jnp.where(lane // HEAD_DIM == h, qr_ref[...], zero), jnp.where(lane // HEAD_DIM == h, do_ref[...], zero))
        at, keys = slice(start, start + width), slice(key_start, key_start + key_count)
        scores = nn(kr_ref[keys, :], masked[h][0][:, at])
        if start == LONGEST:
            scores = jnp.where(same, scores, masked_score)
        return scores, nn(vr_ref[keys, :], masked[h][1][:, at])

    def finish(job, scores, weight_grad):
        h, start, width, key_start, key_count = job
        at, keys = slice(start, start + width), slice(key_start, key_start + key_count)
        rows = slice(h * HEAD_DIM, (h + 1) * HEAD_DIM)
        soft = jnp.exp(scores - lse_ref[0, h : h + 1, at])
        score_grad = (soft * (weight_grad - delta_s[h : h + 1, at])).astype(jnp.bfloat16)
        dv_s[keys, :] += nn(soft.astype(jnp.bfloat16), masked[h][3][at, :])
        dk_s[keys, :] += nn(score_grad, masked[h][2][at, :])
        dqt_s[rows, at] = nn(kt_s[rows, keys], score_grad)

    for t in range(len(jobs) + 1):
        if t == len(jobs) // 2:
            between()
        if t < len(jobs):
            held[t] = products(jobs[t])
        if t >= 1:
            finish(jobs[t - 1], *held.pop(t - 1))


def backward_kernel(
    len_ref, qr_ref, kr_ref, vr_ref, do_ref, attn_ref, lse_ref, cos_ref, sin_ref, parts_ref,
    dq_ref, dk_ref, dv_ref, own_ref, total_ref, *scratch,
):
    group = pl.program_id(0)
    lanes = parts_ref.shape[-1] // 2
    halves = [SumStages(parts_ref, scratch[7 + SUM_SCRATCH * n : 7 + SUM_SCRATCH * (n + 1)], pl.ds(n * lanes, lanes))
              for n in range(2)]
    dqt_s, dk_s, dv_s = scratch[4:7]

    @pl.when(group == 0)
    def _():
        greet(all_partners())
        halves[0].core_start()

    @pl.when(group == 1)
    def _():
        halves[1].core_finish()

    def between():
        @pl.when(group == 0)
        def _():
            halves[0].core_finish()
            halves[0].chip_start()
            halves[1].core_start()

        @pl.when(group == 1)
        def _():
            halves[1].chip_start()

        @pl.when(group == 2)
        def _():
            halves[0].chip_turn()

        @pl.when(group == 3)
        def _():
            halves[0].chip_finish()
            halves[0].plane_start()
            halves[1].chip_turn()

        @pl.when(group == 4)
        def _():
            halves[1].chip_finish()
            total_ref[...] = halves[1].total[...]

    ends, offset = row_marks(len_ref)
    backward_group(between, qr_ref, kr_ref, vr_ref, do_ref, attn_ref, lse_ref, same_rest(ends, offset), *scratch[:7])
    first = _half_mask(cos_ref.shape)
    cosine, sine = cos_ref[...], sin_ref[...]

    def pull(values):
        return values * cosine + _turn(values * sine, first)

    dq_ref[...] = (pull(dqt_s[...].T) * (1.0 / math.sqrt(HEAD_DIM))).astype(jnp.bfloat16)
    dk_ref[...] = pull(dk_s[...]).astype(jnp.bfloat16)
    dv_ref[...] = dv_s[...].astype(jnp.bfloat16)

    @pl.when(group == 4)
    def _():
        own_ref[...] = halves[0].plane_finish()


def backward(lengths, qr, kr, vr, attn_grad, attn, lse, cosine, sine, parts):
    tokens, width = qr.shape
    groups = width // LANES
    rows, lanes = parts.shape[-2:]
    col = pl.BlockSpec((tokens, LANES), lambda g: (0, g))
    whole = lambda *shape: pl.BlockSpec(shape, lambda g: (0,) * len(shape))
    shape = jax.ShapeDtypeStruct
    bf16, f32 = jnp.bfloat16, jnp.float32
    return pl.pallas_call(
        backward_kernel,
        grid=(groups,),
        in_specs=[pl.BlockSpec(memory_space=pltpu.SMEM)] + [col] * 5
        + [pl.BlockSpec((1, 4, tokens), lambda g: (g, 0, 0)), whole(tokens, LANES), whole(tokens, LANES),
           pl.BlockSpec(memory_space=pl.ANY)],
        out_specs=[col] * 3 + [whole(rows, lanes // 2), whole(4, rows, lanes // 2)],
        out_shape=[shape((tokens, width), bf16)] * 3 + [shape((rows, lanes // 2), f32), shape((4, rows, lanes // 2), bf16)],
        scratch_shapes=[pltpu.VMEM((LANES, tokens), bf16)] * 3
        + [pltpu.VMEM((8, tokens), f32), pltpu.VMEM((LANES, tokens), f32), pltpu.VMEM((tokens, LANES), f32),
           pltpu.VMEM((tokens, LANES), f32)] + sum_scratch(rows, lanes // 2) * 2,
        compiler_params=pltpu.CompilerParams(collective_id=0, has_side_effects=True, vmem_limit_bytes=58 << 20),
        name="backward",
    )(lengths, qr, kr, vr, attn_grad, attn, lse, cosine, sine, parts)


def row_layout(lengths, counts, row_len):
    lens = lengths[0]
    slots = lens.shape[0]
    order = lax.broadcasted_iota(jnp.int32, (slots, slots), 0)
    upto = lax.broadcasted_iota(jnp.int32, (slots, slots), 1)
    starting = jnp.sum(jnp.where(upto < order, lens[None, :], 0), axis=1)
    slot = lax.broadcasted_iota(jnp.int32, (slots,), 0)
    which = jnp.min(jnp.where(lens == LONGEST, slot, slots))
    offset = jnp.sum(jnp.where(slot == which, starting, 0))
    places = lax.broadcasted_iota(jnp.int32, (row_len,), 0) + offset
    places = jnp.where(places >= row_len, places - row_len, places)
    endings = starting + lens
    segment = jnp.sum((places[:, None] >= endings[None, :]).astype(jnp.int32), axis=1)
    member = segment[:, None] == slot[None, :]
    first_place = jnp.sum(jnp.where(member, starting[None, :], 0), axis=1)
    position = (places - first_place).astype(jnp.float32)
    inverse_count = 1.0 / counts[0].astype(jnp.float32)
    share = jnp.sum(jnp.where(member, inverse_count[None, :], 0.0), axis=1)
    return offset, segment, position, share


def rotary_tables(position):
    lane = lax.broadcasted_iota(jnp.int32, (1, LANES), 1)
    indices = (lane % (HEAD_DIM // 2)).astype(jnp.float32)
    inverse = jnp.exp(indices * (-2.0 * math.log(10000.0) / HEAD_DIM))
    angles = position[:, None] * inverse
    sign = jnp.where((lane % HEAD_DIM) < (HEAD_DIM // 2), -1.0, 1.0)
    return jnp.cos(angles), jnp.sin(angles) * sign


def turn_rows(values, shift):
    twice = jnp.concatenate([values, values], axis=0)
    return lax.dynamic_slice_in_dim(twice, shift, values.shape[0], 0)


def high(left, right):
    return jnp.dot(left, right, precision=lax.Precision.HIGH, preferred_element_type=jnp.float32)


def shards_near(
    tokens, cotangent, lengths, counts,
    w_qkv, w_out, w_up, w_down,
    mom_qkv, mom_out, mom_up, mom_down,
    vectors, vec_first, vec_second,
):
    columns = w_qkv.shape[1]
    weights_t = [w_qkv.T, w_out, w_up.T, w_down.T]
    moments_t = [mom_qkv.T, mom_out, mom_up.T, mom_down.T]
    qr, kr, vr, attn, lse, normed_one, turned, cosine, sine, wt_qkv, table, full_b, full_o, incoming, dy, dyt = head(
        lengths, counts, tokens, cotangent, weights_t[0], weights_t[2], weights_t[3], w_out, vectors)
    out_grad, sums, layer_out, after_grad, attn_grad, parts_b = middle(
        lengths, turned, attn, incoming, dy, dyt, table, full_o, full_b)
    dq, dk, dv, own_up, total_down = backward(
        lengths, qr, kr, vr, attn_grad, attn, lse, cosine, sine, parts_b.reshape(4, 2, 2, 2, columns, -1))
    results = tail(
        normed_one, dq, dk, dv, out_grad, sums, table, own_up, total_down, lengths, moments_t, weights_t,
        (vectors, vec_first, vec_second), wt_qkv, after_grad, turned)
    results = finish([*results, layer_out])
    matrices = [v if x % 4 == 1 else v.T for x, v in enumerate(results[:8])]
    return (results[12], results[11], *matrices, *results[8:11])


def shards_far(
    tokens, cotangent, lengths, counts,
    w_qkv, w_out, w_up, w_down,
    mom_qkv, mom_out, mom_up, mom_down,
    vectors, vec_first, vec_second,
):
    both = ("fsdp", "dp")
    planes = lax.axis_size("fsdp")
    ranks = lax.axis_size("dp")
    row_len, width = tokens.shape
    columns = w_qkv.shape[1]
    old_weights = (w_qkv, w_out, w_up, w_down)
    old_moments = (mom_qkv, mom_out, mom_up, mom_down)
    counts_rows = [w.shape[0] for w in old_weights]
    n_vec = vectors.shape[0]

    slab_a = jnp.concatenate([w_qkv.T, w_out.T, vectors.T], axis=1).astype(jnp.bfloat16)
    slab_b = jnp.concatenate([w_up.T, w_down.T], axis=1).astype(jnp.bfloat16)
    full_a = lax.all_gather(slab_a, both, axis=0, tiled=True).reshape(planes, width, -1)
    full_b = lax.all_gather(slab_b, both, axis=0, tiled=True).reshape(planes, width, -1)
    r0, r1, r2, r3 = counts_rows
    wt_qkv = jnp.concatenate([full_a[j, :, :r0] for j in range(planes)], axis=1)
    wt_out = jnp.concatenate([full_a[j, :, r0 : r0 + r1] for j in range(planes)], axis=1)
    table = full_a[0, :, r0 + r1 :].T.astype(jnp.float32)
    wt_up = jnp.concatenate([full_b[j, :, :r2] for j in range(planes)], axis=1)
    wt_down = jnp.concatenate([full_b[j, :, r2:] for j in range(planes)], axis=1)

    offset, segment, position, share = row_layout(lengths, counts, row_len)
    cosine, sine = rotary_tables(position)
    seg_col, seg_row = segment[:, None], segment[None, :]
    inputs = turn_rows(tokens, offset).astype(jnp.float32)
    incoming = turn_rows(cotangent, offset).astype(jnp.float32) * share[:, None]

    normed_one, pull_one = jax.vjp(layer_norm, inputs, table[0], table[1])
    normed_one = normed_one.astype(jnp.bfloat16)
    project = nn(normed_one, wt_qkv) + table[4:7].reshape(-1)
    qr, kr, vr, attn, lse = attention_forward(project, cosine, sine, seg_col, seg_row)
    after = inputs + (nn(attn, wt_out) + table[7])
    normed_two, pull_two = jax.vjp(layer_norm, after, table[2], table[3])
    normed_two = normed_two.astype(jnp.bfloat16)
    hidden_pre = nn(normed_two, wt_up) + table[9:].reshape(-1)
    hidden, pull_hidden = jax.vjp(gelu_exact, hidden_pre)
    hidden = hidden.astype(jnp.bfloat16)
    layer_out = (after + (nt(hidden, wt_down) + table[8])).astype(jnp.bfloat16)

    grad_low = incoming.astype(jnp.bfloat16)
    grad_t_down = tn(grad_low, hidden)
    pre_grad = pull_hidden(nn(grad_low, wt_down))[0].astype(jnp.bfloat16)
    grad_t_up = tn(normed_two, pre_grad)
    resid_grad, gain_two, shift_two = pull_two(nt(pre_grad, wt_up))
    after_grad = incoming + resid_grad
    branch_low = after_grad.astype(jnp.bfloat16)
    grad_t_out = tn(attn, branch_low)
    attn_grad = nt(branch_low, wt_out).astype(jnp.bfloat16)
    dq, dk, dv = attention_backward(qr, kr, vr, attn_grad, attn, lse, cosine, sine, seg_col, seg_row)
    proj_grad = jnp.concatenate([dq, dk, dv], axis=1)
    grad_t_qkv = tn(normed_one, proj_grad)
    in_grad, gain_one, shift_one = pull_one(nt(proj_grad, wt_qkv))
    input_grad = after_grad + in_grad

    def column_sum(values):
        return jnp.sum(values.astype(jnp.float32), axis=0)

    vector_grad = jnp.concatenate(
        [gain_one[None], shift_one[None], gain_two[None], shift_two[None],
         column_sum(proj_grad).reshape(3, width), column_sum(branch_low)[None], column_sum(grad_low)[None],
         column_sum(pre_grad).reshape(-1, width)],
        axis=0,
    )
    back = jnp.where(offset > 0, row_len - offset, 0)
    layer_out = turn_rows(layer_out, back)
    input_grad = turn_rows(input_grad, back)

    def cut(values, j, rows):
        return values[:, j * rows : (j + 1) * rows]

    parts_b = jnp.stack([jnp.concatenate([cut(grad_t_up, j, r2), cut(grad_t_down, j, r3)], axis=1) for j in range(planes)])
    own_b = lax.psum_scatter(parts_b.reshape(planes * width, -1), both, scatter_dimension=0, tiled=True)
    parts_a = jnp.stack([jnp.concatenate([cut(grad_t_qkv, j, r0), cut(grad_t_out, j, r1), vector_grad.T], axis=1) for j in range(planes)])
    own_a = lax.psum_scatter(parts_a.reshape(planes * width, -1), both, scatter_dimension=0, tiled=True)
    grads_t = (own_a[:, :r0], own_a[:, r0 : r0 + r1], own_b[:, :r2], own_b[:, r2:])
    vector_grad = own_a[:, r0 + r1 :].T
    new_moments_t = [moment_keep * old.T + grad for old, grad in zip(old_moments, grads_t)]

    most = max(counts_rows)
    padded = [jnp.pad(m.astype(jnp.bfloat16), ((0, 0), (0, most - m.shape[1]))) for m in new_moments_t]
    sent = jnp.stack([padded[t % 4] for t in range(planes)])
    mine = lax.all_to_all(sent, "fsdp", 0, 0, tiled=True)
    mine = mine.transpose(1, 0, 2).reshape(columns, planes * most)
    whole = lax.all_gather(mine, "dp", axis=0, tiled=True)
    gram = nt(whole, whole)
    identity = jnp.eye(width, dtype=jnp.float32)
    norm_sq = jnp.trace(gram) + 1e-07
    gram = gram / norm_sq
    factor = None
    for iteration in range(NS_ITERS):
        poly = poly_linear * identity + poly_square * gram + poly_cubic * high(gram, gram)
        factor = poly if factor is None else high(factor, poly)
        if iteration + 1 < NS_ITERS:
            gram = high(high(gram, poly), poly)
    own_rows = lax.dynamic_slice_in_dim(factor, lax.axis_index("dp") * columns, columns, 0) * lax.rsqrt(norm_sq)
    own_orth = high(own_rows, whole.astype(jnp.float32))
    own_orth = own_orth.astype(jnp.bfloat16).reshape(columns, planes, most).transpose(1, 0, 2)
    pieces = lax.all_to_all(own_orth, "fsdp", 0, 0, tiled=True).astype(jnp.float32)

    new_weights = []
    for x, weight_old in enumerate(old_weights):
        rows = weight_old.shape[0]
        scale = muon_rate * math.sqrt(max(1.0, rows * planes / width))
        new_weights.append(weight_old * (1.0 - muon_rate * muon_decay) - scale * pieces[x, :, :rows].T)
    new_first = beta_first * vec_first + (1.0 - beta_first) * vector_grad
    new_second = beta_second * vec_second + (1.0 - beta_second) * vector_grad * vector_grad
    first_fix = 1.0 - beta_first**STEP
    second_fix = 1.0 - beta_second**STEP
    new_vectors = vectors - adam_rate * (new_first / first_fix) / (jnp.sqrt(new_second / second_fix) + adam_eps)
    return (layer_out, input_grad, *[m.T for m in new_moments_t], *new_weights, new_vectors, new_first, new_second)


def solution(mesh):
    rows, cells, table = P(("dp", "fsdp"), None), P("fsdp", "dp"), P(None, "dp")
    near = dict(mesh.shape) == {"dp": 8, "fsdp": 4}
    return jax.shard_map(
        shards_near if near else shards_far,
        mesh=mesh,
        in_specs=(rows,) * 4 + (cells,) * 8 + (table,) * 3,
        out_specs=(rows,) * 2 + (cells,) * 8 + (table,) * 3,
        check_vma=False,
    )
```

```python
import functools
import math

import jax
import jax.numpy as jnp
from jax import lax
from jax.experimental import pallas as pl
from jax.experimental.pallas import tpu as pltpu
from jax.sharding import PartitionSpec as P

HEAD_DIM = 32
NS_ITERS = 5
STEP = 10
LANES = 128
LONGEST = 768

norm_eps = 1e-05
masked_score = -1e30
poly_linear = 3.4445
poly_square = -4.775
poly_cubic = 2.0315
muon_rate = 0.5
muon_decay = 0.01
moment_keep = 0.5
adam_rate = 0.05
beta_first = 0.9
beta_second = 0.999
adam_eps = 1e-08


def layer_norm(values, gain_row, shift_row):
    center = values - jnp.mean(values, axis=-1, keepdims=True)
    spread = jnp.mean(center * center, axis=-1, keepdims=True)
    return center * lax.rsqrt(spread + norm_eps) * gain_row + shift_row


def gelu_exact(values):
    return 0.5 * values * (1.0 + lax.erf(values * (1.0 / math.sqrt(2.0))))


def nn(left, right):
    return jnp.dot(left, right, preferred_element_type=jnp.float32)


def nt(left, right):
    return lax.dot_general(left, right, (((1,), (1,)), ((), ())), preferred_element_type=jnp.float32)


def tn(left, right):
    return lax.dot_general(left, right, (((0,), (0,)), ((), ())), preferred_element_type=jnp.float32)


def _half_mask(shape):
    lane = lax.broadcasted_iota(jnp.int32, shape, 1)
    return (lane % HEAD_DIM) < (HEAD_DIM // 2)


def _turn(values, first):
    half = HEAD_DIM // 2
    left = pltpu.roll(values, LANES - half, 1)
    right = pltpu.roll(values, half, 1)
    return jnp.where(first, left, right)


def attention_forward_kernel(
    q_ref, k_ref, v_ref, cos_ref, sin_ref, segc_ref, segr_ref,
    qr_ref, kr_ref, vr_ref, attn_ref, lse_ref,
    qt_s, vt_s, ot_s,
):
    first = _half_mask(cos_ref.shape)
    cosine, sine = cos_ref[...], sin_ref[...]
    queries = q_ref[...] * (1.0 / math.sqrt(HEAD_DIM))
    qr = (queries * cosine + _turn(queries, first) * sine).astype(jnp.bfloat16)
    keys = k_ref[...]
    kr = (keys * cosine + _turn(keys, first) * sine).astype(jnp.bfloat16)
    vr = v_ref[...].astype(jnp.bfloat16)
    qr_ref[...] = qr
    kr_ref[...] = kr
    vr_ref[...] = vr
    qt_s[...] = qr.T
    vt_s[...] = vr.T
    tokens = qr.shape[0]
    rest = tokens - LONGEST
    row = lax.broadcasted_iota(jnp.int32, (LANES, tokens), 0)
    same = segc_ref[LONGEST:, :] == segr_ref[:, LONGEST:]

    def head(h, carry):
        qth = jnp.where(row // HEAD_DIM == h, qt_s[...], jnp.zeros((), jnp.bfloat16))
        rows = pl.ds(pl.multiple_of(h * HEAD_DIM, HEAD_DIM), HEAD_DIM)

        def block(start, width, key_start, key_count, mask):
            scores = nn(kr_ref[key_start : key_start + key_count, :], qth[:, start : start + width])
            if mask is not None:
                scores = jnp.where(mask, scores, masked_score)
            peak = jnp.max(scores, axis=0, keepdims=True)
            raised = jnp.exp(scores - peak)
            total = jnp.sum(raised, axis=0, keepdims=True)
            out = nn(vt_s[rows, key_start : key_start + key_count], raised.astype(jnp.bfloat16))
            ot_s[rows, start : start + width] = out / total
            lse_ref[0, pl.ds(h, 1), start : start + width] = peak + jnp.log(total)

        for start in range(0, LONGEST, 256):
            block(start, 256, 0, LONGEST, None)
        block(LONGEST, rest, LONGEST, rest, same)
        return carry

    lax.fori_loop(0, LANES // HEAD_DIM, head, 0)
    attn_ref[...] = ot_s[...].T.astype(jnp.bfloat16)


def attention_forward(project, cosine, sine, seg_col, seg_row):
    tokens = project.shape[0]
    width = project.shape[1] // 3
    groups = width // LANES
    col = lambda shift: pl.BlockSpec((tokens, LANES), lambda g, shift=shift: (0, g + shift))
    whole = lambda shape: pl.BlockSpec(shape, lambda g: (0,) * len(shape))
    flops = 4 * (LONGEST**2 + (tokens - LONGEST) ** 2) * 128 * groups * 4
    return pl.pallas_call(
        attention_forward_kernel,
        grid=(groups,),
        in_specs=[col(0), col(groups), col(2 * groups), whole((tokens, LANES)), whole((tokens, LANES)),
                  whole((tokens, 1)), whole((1, tokens))],
        out_specs=[col(0)] * 4 + [pl.BlockSpec((1, 4, tokens), lambda g: (g, 0, 0))],
        out_shape=[jax.ShapeDtypeStruct((tokens, width), jnp.bfloat16)] * 4
        + [jax.ShapeDtypeStruct((groups, 4, tokens), jnp.float32)],
        scratch_shapes=[
            pltpu.VMEM((LANES, tokens), jnp.bfloat16),
            pltpu.VMEM((LANES, tokens), jnp.bfloat16),
            pltpu.VMEM((LANES, tokens), jnp.float32),
        ],
        compiler_params=pltpu.CompilerParams(vmem_limit_bytes=48 << 20),
        cost_estimate=pl.CostEstimate(flops=flops, bytes_accessed=20 << 20, transcendentals=20 << 20),
        name="attention_forward",
    )(project, project, project, cosine, sine, seg_col, seg_row)


def attention_backward_kernel(
    qr_ref, kr_ref, vr_ref, do_ref, attn_ref, lse_ref, cos_ref, sin_ref, segc_ref, segr_ref,
    *rest_refs,
):
    dq_ref, dk_ref, dv_ref = rest_refs[:3]
    qt_s, dot_s, kt_s, delta_s, dqt_s, dk_s, dv_s = rest_refs[3:]
    tokens = qr_ref.shape[0]
    rest = tokens - LONGEST
    qt_s[...] = qr_ref[...].T
    dot_s[...] = do_ref[...].T
    kt_s[...] = kr_ref[...].T
    prod_t = (do_ref[...].astype(jnp.float32) * attn_ref[...].astype(jnp.float32)).T
    for h in range(4):
        delta_s[h : h + 1, :] = jnp.sum(prod_t[h * HEAD_DIM : (h + 1) * HEAD_DIM, :], axis=0, keepdims=True)
    dk_s[...] = jnp.zeros_like(dk_s)
    dv_s[...] = jnp.zeros_like(dv_s)
    row = lax.broadcasted_iota(jnp.int32, (LANES, tokens), 0)
    lane = lax.broadcasted_iota(jnp.int32, (tokens, LANES), 1)
    same = segc_ref[LONGEST:, :] == segr_ref[:, LONGEST:]
    zero = jnp.zeros((), jnp.bfloat16)

    def head(h, carry):
        mine_t = row // HEAD_DIM == h
        mine = lane // HEAD_DIM == h
        qth = jnp.where(mine_t, qt_s[...], zero)
        doth = jnp.where(mine_t, dot_s[...], zero)
        qh = jnp.where(mine, qr_ref[...], zero)
        doh = jnp.where(mine, do_ref[...], zero)
        rows = pl.ds(pl.multiple_of(h * HEAD_DIM, HEAD_DIM), HEAD_DIM)

        def block(start, width, key_start, key_count, mask):
            at = slice(start, start + width)
            keys = slice(key_start, key_start + key_count)
            scores = nn(kr_ref[keys, :], qth[:, at])
            if mask is not None:
                scores = jnp.where(mask, scores, masked_score)
            soft = jnp.exp(scores - lse_ref[0, pl.ds(h, 1), at])
            weight_grad = nn(vr_ref[keys, :], doth[:, at])
            score_grad = (soft * (weight_grad - delta_s[pl.ds(h, 1), at])).astype(jnp.bfloat16)
            dv_s[keys, :] += nn(soft.astype(jnp.bfloat16), doh[at, :])
            dk_s[keys, :] += nn(score_grad, qh[at, :])
            dqt_s[rows, at] = nn(kt_s[rows, keys], score_grad)

        for start in range(0, LONGEST, 256):
            block(start, 256, 0, LONGEST, None)
        block(LONGEST, rest, LONGEST, rest, same)
        return carry

    lax.fori_loop(0, LANES // HEAD_DIM, head, 0)
    first = _half_mask(cos_ref.shape)
    cosine, sine = cos_ref[...], sin_ref[...]

    def pull(values):
        return values * cosine + _turn(values * sine, first)

    dq_ref[...] = (pull(dqt_s[...].T) * (1.0 / math.sqrt(HEAD_DIM))).astype(jnp.bfloat16)
    dk_ref[...] = pull(dk_s[...]).astype(jnp.bfloat16)
    dv_ref[...] = dv_s[...].astype(jnp.bfloat16)


def attention_backward(qr, kr, vr, attn_grad, attn, lse, cosine, sine, seg_col, seg_row):
    tokens, width = qr.shape
    groups = width // LANES
    col = pl.BlockSpec((tokens, LANES), lambda g: (0, g))
    whole = lambda shape: pl.BlockSpec(shape, lambda g: (0,) * len(shape))
    flops = 10 * (LONGEST**2 + (tokens - LONGEST) ** 2) * 128 * groups * 4
    return pl.pallas_call(
        attention_backward_kernel,
        grid=(groups,),
        in_specs=[col] * 5 + [pl.BlockSpec((1, 4, tokens), lambda g: (g, 0, 0)),
                              whole((tokens, LANES)), whole((tokens, LANES)), whole((tokens, 1)), whole((1, tokens))],
        out_specs=[col] * 3,
        out_shape=[jax.ShapeDtypeStruct((tokens, width), jnp.bfloat16)] * 3,
        scratch_shapes=[
            pltpu.VMEM((LANES, tokens), jnp.bfloat16),
            pltpu.VMEM((LANES, tokens), jnp.bfloat16),
            pltpu.VMEM((LANES, tokens), jnp.bfloat16),
            pltpu.VMEM((8, tokens), jnp.float32),
            pltpu.VMEM((LANES, tokens), jnp.float32),
            pltpu.VMEM((tokens, LANES), jnp.float32),
            pltpu.VMEM((tokens, LANES), jnp.float32),
        ],
        compiler_params=pltpu.CompilerParams(vmem_limit_bytes=56 << 20),
        cost_estimate=pl.CostEstimate(flops=flops, bytes_accessed=20 << 20, transcendentals=20 << 20),
        name="attention_backward",
    )(qr, kr, vr, attn_grad, attn, lse, cosine, sine, seg_col, seg_row)


MESH = pl.DeviceIdType.MESH


def place():
    rank, plane = lax.axis_index("dp"), lax.axis_index("fsdp")
    core = rank % 2
    chip_x = (rank // 2) % 2
    chip_y = rank // 4
    return rank, plane, core, chip_x, chip_y


def chip_at(step, chip_x, chip_y):
    other_x = 1 - chip_x if step & 1 else chip_x
    other_y = 1 - chip_y if step & 2 else chip_y
    return 2 * other_y + other_x


def call(partners):
    for partner in partners:
        pl.semaphore_signal(pltpu.get_barrier_semaphore(), inc=1, device_id=partner, device_id_type=MESH)


def hear(partners):
    pl.semaphore_wait(pltpu.get_barrier_semaphore(), len(partners))


def greet(partners):
    call(partners)
    hear(partners)


def all_partners():
    rank, plane, core, chip_x, chip_y = place()
    sibling = 2 * chip_at(0, chip_x, chip_y) + 1 - core
    partners = [(sibling, plane)]
    partners += [(2 * chip_at(step, chip_x, chip_y) + core, plane) for step in (1, 2, 3)]
    partners += [(rank, (plane + step) % 4) for step in (1, 2, 3)]
    return partners


class SumStages:
    def __init__(self, parts, scratch, lanes):
        (self.own, self.from_core, self.from_first, self.middle, self.from_second, self.total, self.from_plane,
         self.send, self.recv, self.local) = scratch
        self.parts, self.lanes = parts, lanes
        self.rank, self.plane, self.core, self.chip_x, self.chip_y = place()

    def remote(self, source, target, slot, device):
        return pltpu.make_async_remote_copy(
            src_ref=source, dst_ref=target, send_sem=self.send.at[slot], recv_sem=self.recv.at[slot],
            device_id=device, device_id_type=MESH)

    def device(self, step):
        return (2 * chip_at(step, self.chip_x, self.chip_y) + self.core, self.plane)

    def add(self, left, right):
        return left.astype(jnp.float32) + right.astype(jnp.float32)

    def give_copy(self, source):
        return self.remote(source, self.from_core, 0, (2 * chip_at(0, self.chip_x, self.chip_y) + 1 - self.core, self.plane))

    def core_add(self, give):
        give.wait()
        for j in range(4):
            self.own[j] = self.add(self.own[j], self.from_core[j]).astype(self.own.dtype)

    def core_copies(self):
        load = pltpu.make_async_copy(self.parts.at[:, :, :, self.core, :, self.lanes], self.own, self.local)
        return load, self.give_copy(self.parts.at[:, :, :, 1 - self.core, :, self.lanes])

    def core_start(self):
        load, give = self.core_copies()
        give.start()
        load.start()

    def core_finish(self):
        load, give = self.core_copies()
        load.wait()
        self.core_add(give)

    def first_copies(self):
        return [
            self.remote(self.own.at[pl.ds(0, 2), :, 1 - self.chip_x], self.from_first.at[0], 1, self.device(1)),
            self.remote(self.own.at[pl.ds(2, 2), 1 - self.chip_y], self.from_first.at[1], 2, self.device(2)),
        ]

    def second_copies(self):
        return [
            self.remote(self.middle.at[0, :, 1 - self.chip_y], self.from_second.at[0], 3, self.device(2)),
            self.remote(self.middle.at[1, :, 1 - self.chip_x], self.from_second.at[1], 4, self.device(1)),
        ]

    def chip_start(self):
        for copy in self.first_copies():
            copy.start()

    def chip_turn(self):
        for copy in self.first_copies():
            copy.wait()
        for j in range(2):
            mine = self.own[j, :, pl.ds(self.chip_x, 1)][:, 0]
            self.middle[0, j] = self.add(mine, self.from_first[0, j]).astype(self.middle.dtype)
            mine = self.own[2 + j, pl.ds(self.chip_y, 1)][0]
            self.middle[1, j] = self.add(mine, self.from_first[1, j]).astype(self.middle.dtype)
        for copy in self.second_copies():
            copy.start()

    def chip_finish(self):
        for copy in self.second_copies():
            copy.wait()
        for half, index in ((0, self.chip_y), (1, self.chip_x)):
            for j in range(2):
                mine = self.middle[half, j, pl.ds(index, 1)][0]
                self.total[2 * half + j] = self.add(mine, self.from_second[half, j]).astype(self.total.dtype)

    def plane_copies(self):
        return [
            self.remote(self.total.at[(self.plane + step) % 4], self.from_plane.at[step - 1], 4 + step,
                        (self.rank, (self.plane + step) % 4))
            for step in (1, 2, 3)
        ]

    def plane_start(self):
        for copy in self.plane_copies():
            copy.start()

    def plane_finish(self):
        for copy in self.plane_copies():
            copy.wait()
        value = self.total[pl.ds(self.plane, 1)][0].astype(jnp.float32)
        for slot in range(3):
            value = value + self.from_plane[slot].astype(jnp.float32)
        return value


def sum_scratch(rows, lanes, dtype=jnp.bfloat16):
    return [
        pltpu.VMEM((4, 2, 2, rows, lanes), dtype),
        pltpu.VMEM((4, 2, 2, rows, lanes), dtype),
        pltpu.VMEM((2, 2, 2, rows, lanes), dtype),
        pltpu.VMEM((2, 2, 2, rows, lanes), dtype),
        pltpu.VMEM((2, 2, rows, lanes), dtype),
        pltpu.VMEM((4, rows, lanes), dtype),
        pltpu.VMEM((3, rows, lanes), dtype),
        pltpu.SemaphoreType.DMA((8,)),
        pltpu.SemaphoreType.DMA((8,)),
        pltpu.SemaphoreType.DMA,
    ]


SUM_SCRATCH = 10


def table_sum(table_ref, table_out, from_core, from_chip, from_plane, held, send, recv):
    rank, plane, core, chip_x, chip_y = place()
    chip = chip_at(0, chip_x, chip_y)

    def remote(source, target, slot, device):
        return pltpu.make_async_remote_copy(
            src_ref=source, dst_ref=target, send_sem=send.at[slot], recv_sem=recv.at[slot],
            device_id=device, device_id_type=MESH)

    give = remote(table_ref.at[:, 1 - core], from_core, 0, (2 * chip + 1 - core, plane))
    give.start()
    yield
    give.wait()
    held[...] = table_ref[:, pl.ds(core, 1)][:, 0] + from_core[...]
    across = [remote(held.at[chip_at(step, chip_x, chip_y)], from_chip.at[step - 1], step,
                     (2 * chip_at(step, chip_x, chip_y) + core, plane)) for step in (1, 2, 3)]
    for copy in across:
        copy.start()
    yield
    for copy in across:
        copy.wait()
    own = held[pl.ds(chip, 1)][0] + from_chip[0] + from_chip[1] + from_chip[2]
    table_out[...] = own
    along = [remote(table_out, from_plane.at[step - 1], 3 + step, (rank, (plane + step) % 4)) for step in (1, 2, 3)]
    for copy in along:
        copy.start()
    yield
    for copy in along:
        copy.wait()
    table_out[...] = own + from_plane[0] + from_plane[1] + from_plane[2]
    yield


class Gather:
    def __init__(self, at, send, recv, base, parts):
        rank, plane, core, chip_x, chip_y = place()
        every, low, high = parts
        chips = [chip_at(step, chip_x, chip_y) for step in range(4)]
        over = [2 * chip + core for chip in chips]

        def copy(chip, lanes, slot, device):
            block = at(chip, core, lanes)
            return pltpu.make_async_remote_copy(
                src_ref=block, dst_ref=block, send_sem=send.at[base + slot], recv_sem=recv.at[base + slot],
                device_id=(device, plane), device_id_type=MESH)

        self.to_x, self.to_y = copy(chips[0], every, 0, over[1]), copy(chips[0], every, 1, over[2])
        self.on_y, self.on_x = copy(chips[1], low, 2, over[2]), copy(chips[2], high, 3, over[1])
        self.beside = [copy(chip, every, 4 + step, 2 * chips[0] + 1 - core) for step, chip in enumerate(chips)]

    def first(self):
        self.to_x.start()
        self.to_y.start()
        self.beside[0].start()

    def second(self):
        self.to_x.wait_recv()
        self.on_y.start()
        self.beside[1].start()
        self.to_y.wait_recv()
        self.on_x.start()
        self.beside[2].start()

    def third(self):
        self.on_y.wait_recv()
        self.on_x.wait_recv()
        self.beside[3].start()

    def finish(self):
        for copy in (self.to_x, self.to_y, self.on_y, self.on_x):
            copy.wait_send()
        for copy in self.beside:
            copy.wait()


def split(values):
    top = values.astype(jnp.bfloat16)
    return top, (values - top.astype(jnp.float32)).astype(jnp.bfloat16)


def put_left(ref, values):
    width = values.shape[1]
    top, low = split(values)
    ref[:, :width] = top
    ref[:, width : 2 * width] = top
    ref[:, 2 * width :] = low


def put_right(ref, values):
    width = values.shape[0]
    top, low = split(values)
    ref[:width, :] = top
    ref[width : 2 * width, :] = low
    ref[2 * width :, :] = top


def tiles_of(width):
    first = width % 256
    edges = ([0] if first else []) + list(range(first, width + 1, 256))
    return list(zip(edges[:-1], edges[1:]))


def symmetric_product(out, left, right, tiles):
    for start, stop in tiles:
        block = nn(left[:stop, :], right[:, start:stop])
        out[:stop, start:stop] = block
        if start:
            out[start:stop, :start] = block[:start, :].T


def orthogonal_rows(whole, mine, gram, poly, temp, rows_s, left_gram, left_temp, right, write):
    width = gram.shape[0]
    tiles = tiles_of(width)
    parts = [whole[j].reshape(width, whole.shape[-1]) for j in range(4)]
    for start, stop in tiles:
        block = sum(nt(part[:stop, :], part[start:stop, :]) for part in parts)
        gram[:stop, start:stop] = block
        if start:
            gram[start:stop, :start] = block[:start, :].T
    diagonal = lax.broadcasted_iota(jnp.int32, (width, width), 0) == lax.broadcasted_iota(jnp.int32, (width, width), 1)
    norm_sq = jnp.sum(jnp.sum(jnp.where(diagonal, gram[...], 0.0), axis=1, keepdims=True), axis=0, keepdims=True) + 1e-07
    gram[...] = gram[...] / norm_sq

    def polynomial():
        put_left(left_gram, gram[...])
        put_right(right, gram[...])
        symmetric_product(temp, left_gram, right, tiles)
        poly[...] = jnp.where(diagonal, poly_linear, 0.0) + poly_square * gram[...] + poly_cubic * temp[...]
        put_right(right, poly[...])

    def next_gram():
        symmetric_product(temp, left_gram, right, tiles)
        put_left(left_temp, temp[...])
        symmetric_product(gram, left_temp, right, tiles)

    def thin(values):
        count = values.shape[0]
        top, low = split(values)
        both = nn(jnp.concatenate([top, low], axis=0), right[:width, :])
        return both[:count, :] + both[count:, :] + nn(top, right[width : 2 * width, :])

    polynomial()
    rows_s[...] = poly[mine, :]

    def iteration(step, carry):
        next_gram()
        polynomial()
        rows_s[...] = thin(rows_s[...])
        return carry

    lax.fori_loop(0, NS_ITERS - 2, iteration, 0)
    next_gram()
    put_right(right, gram[...])
    rows = rows_s[...]
    once = thin(rows)
    twice = thin(once)
    rows = (poly_linear * rows + poly_square * once + poly_cubic * twice) * lax.rsqrt(norm_sq)
    top, low = split(rows)
    for j, part in enumerate(parts):
        write(j, nn(top, part) + nn(low, part))


class PlaneStage:
    def __init__(self, total, from_plane, send, recv):
        rank, self.plane = place()[:2]
        self.total, self.from_plane = total, from_plane
        self.copies = [
            pltpu.make_async_remote_copy(
                src_ref=total.at[(self.plane + step) % 4], dst_ref=from_plane.at[step - 1],
                send_sem=send.at[step - 1], recv_sem=recv.at[step - 1],
                device_id=(rank, (self.plane + step) % 4), device_id_type=MESH)
            for step in (1, 2, 3)
        ]

    def start(self):
        for copy in self.copies:
            copy.start()

    def finish(self):
        for copy in self.copies:
            copy.wait()
        value = self.total[pl.ds(self.plane, 1)][0].astype(jnp.float32)
        for slot in range(3):
            value = value + self.from_plane[slot].astype(jnp.float32)
        return value


MATRIX_OF = (2, 0, 1, 3)
LANES_OF = (640, 512, 256, 640)
FIRST, LAST = (0, 3), (1, 2)
CUTS_A = ((0, 256), (256, 384))


def tail_kernel(
    sums_ref, table_ref, own_up_ref, total_b_ref, len_ref, *refs,
):
    moments, weights, small, large = refs[0:4], refs[4:8], refs[8:11], refs[11:19]
    refs = refs[19:]
    new_moments, new_weights, new_small, input_grad_hbm = refs[0:4], refs[4:8], refs[8:11], refs[11]
    table_out, pieces = refs[12:14]
    refs = refs[14:]
    early, late = (SumStages(None, refs[SUM_SCRATCH * n : SUM_SCRATCH * (n + 1)], None) for n in range(2))
    refs = refs[2 * SUM_SCRATCH :]
    table_scratch, refs = refs[:6], refs[6:]
    blocks, whole, gram, poly, temp, rows_s, left_gram, left_temp, right, from_plane_b = refs[:10]
    plane_send, plane_recv, gather_send, gather_recv, back_send, back_recv, b_send, b_recv, loads = refs[10:19]
    gives_s, (tiles_s, h1t_s, turned_s, stored), held = refs[19:21], refs[21:25], refs[25:]
    h1_ref, dq_ref, dk_ref, dv_ref, out_grad_ref, wt_s, after_s, x_s = held
    rank, plane, core, chip_x, chip_y = place()
    chip = chip_at(0, chip_x, chip_y)
    columns, lanes = blocks.shape[1:]
    tokens, width = h1_ref.shape
    rows_qkv, rows_out = moments[0].shape[1], moments[1].shape[0]
    last_b = PlaneStage(total_b_ref, from_plane_b, b_send, b_recv)
    loading = [pltpu.make_async_copy(source, target, loads.at[n]) for n, (source, target) in enumerate(zip(large, held))]
    for copy in loading:
        copy.start()

    @pl.when((plane == LAST[0]) | (plane == LAST[1]))
    def _():
        whole[...] = jnp.zeros_like(whole)

    call(all_partners())
    loading[0].wait()
    h1t_s[...] = h1_ref[...].T
    hear(all_partners())
    last_b.start()
    for copy in loading[1:5]:
        copy.wait()

    def half(which, targets):
        starts = [pl.multiple_of(columns * (2 * m + which), 16) for m in range(4)]
        left = jnp.concatenate([h1t_s[pl.ds(start, columns), :] for start in starts], axis=0)
        qkv = jnp.concatenate([nn(left, ref[...]).astype(jnp.bfloat16) for ref in (dq_ref, dk_ref, dv_ref)], axis=1)
        out = jnp.concatenate([out_grad_ref[pl.ds(start, columns), :] for start in starts], axis=0)
        for j in range(4):
            both = jnp.concatenate(
                [qkv[:, j * rows_qkv : (j + 1) * rows_qkv], out[:, j * rows_out : (j + 1) * rows_out]], axis=1)
            for target, (start, size) in zip(targets, CUTS_A):
                target[j] = both[:, start : start + size].reshape(2, 2, columns, size)

    half(1 - core, gives_s)
    gives = [stages.give_copy(source) for stages, source in zip((early, late), gives_s)]
    for give in gives:
        give.start()
    half(core, (early.own, late.own))
    early.core_add(gives[0])
    early.chip_start()
    late.core_add(gives[1])

    def momentum(x, gradient):
        rows = gradient.shape[1]
        slot = MATRIX_OF.index(x)
        if x == 1:
            new = moment_keep * moments[x][...].T + gradient
            new_moments[x][...] = new.T
        else:
            new = moment_keep * moments[x][...] + gradient
            new_moments[x][...] = new
        blocks[slot, :, :rows] = new.astype(jnp.bfloat16)
        if rows < lanes:
            blocks[slot, :, rows:] = jnp.zeros((columns, lanes - rows), jnp.bfloat16)

    def out_copy(step, target):
        part = pl.ds(0, LANES_OF[target])
        return pltpu.make_async_remote_copy(
            src_ref=blocks.at[target, :, part], dst_ref=whole.at[plane, chip, core, :, part],
            send_sem=plane_send.at[step - 1], recv_sem=plane_recv.at[step - 1],
            device_id=(rank, (plane + step) % 4), device_id_type=MESH)

    def when_target(targets, act):
        for step in (1, 2, 3):
            for target in targets:
                @pl.when((plane + step) % 4 == target)
                def _():
                    act(out_copy(step, target))

    def place_own(target):
        part = LANES_OF[target]
        whole[target, pl.ds(chip, 1), pl.ds(core, 1), :, :part] = blocks[target, :, :part][None, None]

    def gathers_of(target):
        filled = LANES_OF[target]
        low = (filled // LANES + 1) // 2 * LANES
        parts = pl.ds(0, filled), pl.ds(0, low), pl.ds(low, filled - low)
        ranges = [(target, 1), (0, target), (target + 1, 3 - target)]
        return [
            Gather(lambda m, c, part, cut=pl.ds(*cut): whole.at[cut, m, c, :, part], gather_send, gather_recv, 8 * n, parts)
            for n, cut in enumerate(ranges) if cut[1]
        ]

    def arrived(target):
        for step in (1, 2, 3):
            out_copy(step, target).wait_recv()

    for copy in loading[5:]:
        copy.wait()
    ends, offset = row_marks(len_ref)
    gain = table_ref[0:1, :]
    gain_sum = jnp.zeros((1, width), jnp.float32)
    shift_sum = jnp.zeros((1, width), jnp.float32)
    for r in range(0, tokens, 256):
        at = slice(r, r + 256)
        grad = sum(nt(ref[at, :], wt_s[:, part * width : (part + 1) * width])
                   for part, ref in enumerate((dq_ref, dk_ref, dv_ref)))
        values = x_s[at, :].astype(jnp.float32)
        center = values - jnp.mean(values, axis=-1, keepdims=True)
        rstd = lax.rsqrt(jnp.mean(center * center, axis=-1, keepdims=True) + norm_eps)
        xhat = center * rstd
        gain_sum += jnp.sum(grad * xhat, axis=0, keepdims=True)
        shift_sum += jnp.sum(grad, axis=0, keepdims=True)
        scaled = grad * gain
        after_s[at, :] += rstd * (scaled - jnp.mean(scaled, axis=-1, keepdims=True)
                                  - xhat * jnp.mean(scaled * xhat, axis=-1, keepdims=True))
        if r == 0:
            early.chip_turn()
            late.chip_start()
        if r == 512:
            early.chip_finish()
            early.plane_start()
        if r == 256:
            momentum(2, own_up_ref[...])
            momentum(3, last_b.finish())
            when_target(FIRST, lambda copy: copy.start())
    vector = jnp.concatenate(
        [gain_sum, shift_sum, sums_ref[2:4, :]]
        + [jnp.sum(ref[...].astype(jnp.float32), axis=0, keepdims=True) for ref in (dq_ref, dk_ref, dv_ref)]
        + [sums_ref[7:16, :]], axis=0)
    for block in range(8):
        part = vector[:, block * columns : (block + 1) * columns]
        tiles_s[block // 2, block % 2] = jnp.concatenate(
            [part, jnp.zeros((16, LANES - columns), jnp.float32)], axis=1)
    adding = table_sum(tiles_s, table_out, *table_scratch)
    late.chip_turn()
    next(adding)
    turned_s[...] = pltpu.roll(after_s[...], offset, 0)
    storing = pltpu.make_async_copy(turned_s, input_grad_hbm, stored)
    storing.start()
    late.chip_finish()
    late.plane_start()
    next(adding)
    for target in FIRST:
        @pl.when(plane == target)
        def _():
            place_own(target)
            own, *others = gathers_of(target)
            own.first()
            arrived(target)
            for gather in others:
                gather.first()
    next(adding)
    gradient = jnp.concatenate([early.plane_finish(), late.plane_finish()], axis=1)
    momentum(0, gradient[:, :rows_qkv])
    momentum(1, gradient[:, rows_qkv : rows_qkv + rows_out])
    when_target(LAST, lambda copy: copy.start())
    for target in FIRST:
        @pl.when(plane == target)
        def _():
            gathers = gathers_of(target)
            for gather in gathers:
                gather.second()
            for gather in gathers:
                gather.third()
            for gather in gathers:
                gather.finish()
    next(adding)
    first_fix = 1.0 - beta_first**STEP
    second_fix = 1.0 - beta_second**STEP
    n_vec = small[0].shape[0]
    vector_grad = table_out[:n_vec, :columns]
    vectors, vec_first, vec_second = (ref[...] for ref in small)
    new_first = beta_first * vec_first + (1.0 - beta_first) * vector_grad
    new_second = beta_second * vec_second + (1.0 - beta_second) * vector_grad * vector_grad
    new_small[0][...] = vectors - adam_rate * (new_first / first_fix) / (jnp.sqrt(new_second / second_fix) + adam_eps)
    new_small[1][...] = new_first
    new_small[2][...] = new_second
    for target in LAST:
        @pl.when(plane == target)
        def _():
            place_own(target)
            own, *others = gathers_of(target)
            own.first()
            arrived(target)
            for gather in others:
                gather.first()
            for gather in (own, *others):
                gather.second()
            for gather in (own, *others):
                gather.third()
            for gather in (own, *others):
                gather.finish()
    when_target((0, 1, 2, 3), lambda copy: copy.wait_send())

    def write(j, values):
        blocks[j] = values.astype(jnp.bfloat16)

    orthogonal_rows(whole, pl.ds(pl.multiple_of(rank * columns, 8), columns), gram, poly, temp, rows_s,
                    left_gram, left_temp, right, write)

    def home_copy(step, source):
        part = pl.ds(0, LANES_OF[source])
        return pltpu.make_async_remote_copy(
            src_ref=blocks.at[(plane + step) % 4, :, part], dst_ref=pieces.at[source, :, part],
            send_sem=back_send.at[step - 1], recv_sem=back_recv.at[step - 1],
            device_id=(rank, (plane + step) % 4), device_id_type=MESH)

    for source in range(4):
        @pl.when(plane == source)
        def _():
            for step in (1, 2, 3):
                home_copy(step, source).start()
            pieces[source] = blocks[source]

    def update(x):
        rows = moments[x].shape[0 if x == 1 else 1]
        scale = muon_rate * math.sqrt(max(1.0, rows * 4 / width))
        change = pieces[MATRIX_OF.index(x), :, :rows].astype(jnp.float32)
        new_weights[x][...] = (weights[x][...] * (1.0 - muon_rate * muon_decay)
                               - scale * (change.T if x == 1 else change))

    for source in (*FIRST, *reversed(LAST)):
        for step in (1, 2, 3):
            @pl.when((plane + 4 - source) % 4 == step)
            def _():
                home_copy(step, source).wait_recv()
        update(MATRIX_OF[source])
    for source in range(4):
        @pl.when(plane == source)
        def _():
            for step in (1, 2, 3):
                home_copy(step, source).wait_send()
    storing.wait()


def tail(h1, dq, dk, dv, out_grad, sums, table, own_up, total_b, lengths, moments, weights, small, wt_qkv, after_grad, x):
    tokens, width = h1.shape
    rows = width // 8
    large = (h1, dq, dk, dv, out_grad, wt_qkv, after_grad, x)
    vmem = pl.BlockSpec(memory_space=pltpu.VMEM)
    hbm = pl.BlockSpec(memory_space=pl.ANY)
    tile = (16, LANES)
    most = max(moments[n].shape[1] for n in (0, 2, 3))
    shape = jax.ShapeDtypeStruct
    f32, bf16 = jnp.float32, jnp.bfloat16
    square = pltpu.VMEM((width, width), f32)
    sems = lambda n: pltpu.SemaphoreType.DMA((n,))
    lanes_b = total_b.shape[-1]
    return pl.pallas_call(
        tail_kernel,
        in_specs=[vmem] * 4 + [pl.BlockSpec(memory_space=pltpu.SMEM)] + [vmem] * 11 + [hbm] * 8,
        out_specs=[vmem] * 11 + [hbm],
        out_shape=[shape(v.shape, f32) for v in (*moments, *weights, *small)] + [shape((tokens, width), f32)],
        scratch_shapes=[pltpu.VMEM(tile, f32), pltpu.VMEM((4, rows, most), bf16)]
        + [scratch for _, size in CUTS_A for scratch in sum_scratch(rows, size)]
        + [pltpu.VMEM((4, *tile), f32), pltpu.VMEM((3, *tile), f32),
           pltpu.VMEM((3, *tile), f32), pltpu.VMEM((4, *tile), f32), sems(7), sems(7)]
        + [pltpu.VMEM((4, rows, most), bf16), pltpu.VMEM((4, 4, 2, rows, most), bf16),
           square, square, square, pltpu.VMEM((rows, width), f32),
           pltpu.VMEM((width, 3 * width), bf16), pltpu.VMEM((width, 3 * width), bf16),
           pltpu.VMEM((3 * width, width), bf16), pltpu.VMEM((3, rows, lanes_b), bf16)]
        + [sems(3), sems(3), sems(24), sems(24), sems(3), sems(3), sems(3), sems(3), sems(8)]
        + [pltpu.VMEM((4, 2, 2, rows, size), bf16) for _, size in CUTS_A]
        + [pltpu.VMEM((4, 2, *tile), f32), pltpu.VMEM((width, tokens), bf16),
           pltpu.VMEM((tokens, width), f32), pltpu.SemaphoreType.DMA]
        + [pltpu.VMEM(v.shape, v.dtype) for v in large],
        compiler_params=pltpu.CompilerParams(collective_id=1, has_side_effects=True, vmem_limit_bytes=60 << 20),
        name="tail",
    )(sums, table, own_up, total_b, lengths, *moments, *weights, *small, *large)


def finish_kernel(*refs):
    count = len(refs) // 3
    sources, targets, held, loads, stores = refs[:count], refs[count : 2 * count], refs[2 * count : -2], refs[-2], refs[-1]
    loading, storing = [], []
    for n in range(count):
        rows = sources[n].shape[0]
        parts = 4 if rows >= ROW_LEN else 1
        for p in range(parts):
            at = pl.ds(p * (rows // parts), rows // parts)
            slot = len(loading)
            loading.append(pltpu.make_async_copy(sources[n].at[at], held[n].at[at], loads.at[slot]))
            storing.append(pltpu.make_async_copy(held[n].at[at], targets[n].at[at], stores.at[slot]))
    for copy in loading:
        copy.start()
    for load, store in zip(loading, storing):
        load.wait()
        store.start()
    for copy in storing:
        copy.wait()


def finish(values):
    hbm = pl.BlockSpec(memory_space=pl.ANY)
    count = len(values)
    copies = sum(4 if x.shape[0] >= ROW_LEN else 1 for x in values)
    return pl.pallas_call(
        finish_kernel,
        in_specs=[hbm] * count,
        out_specs=[hbm] * count,
        out_shape=[jax.ShapeDtypeStruct(x.shape, x.dtype) for x in values],
        scratch_shapes=[pltpu.VMEM(x.shape, x.dtype) for x in values]
        + [pltpu.SemaphoreType.DMA((copies,)), pltpu.SemaphoreType.DMA((copies,))],
        compiler_params=pltpu.CompilerParams(vmem_limit_bytes=62 << 20),
        name="finish",
    )(*values)


def lane_parts(start, size):
    half = size // 2
    return pl.ds(start, size), pl.ds(start, half), pl.ds(start + half, half)


ROW_LEN = 1024
GATHERED = 512
CHUNK_A = 256
OUT_LANES = 256
CUTS_B = ((0, 512), (512, 768))


def row_marks(len_ref):
    ends = [len_ref[0, 0]]
    for slot in (1, 2):
        ends.append(ends[-1] + len_ref[0, slot])
    starts = [0, *ends]
    offset = starts[3]
    for slot in (2, 1, 0):
        offset = jnp.where(len_ref[0, slot] == LONGEST, starts[slot], offset)
    return ends, offset


def segment_of(index, ends, offset):
    where = index + offset
    where = jnp.where(where >= ROW_LEN, where - ROW_LEN, where)
    segment = sum((where >= end).astype(jnp.int32) for end in ends)
    return where, segment


def turned_rows(values, offset):
    return pltpu.roll(values.astype(jnp.float32), jnp.where(offset > 0, ROW_LEN - offset, 0), 0)


def same_rest(ends, offset):
    rest = ROW_LEN - LONGEST
    columns = lax.broadcasted_iota(jnp.int32, (rest, rest), 0) + LONGEST
    rows = lax.broadcasted_iota(jnp.int32, (rest, rest), 1) + LONGEST
    return segment_of(columns, ends, offset)[1] == segment_of(rows, ends, offset)[1]


def attention_jobs(tokens):
    blocks = [(start, 256, 0, LONGEST) for start in range(0, LONGEST, 256)] + [(LONGEST, tokens - LONGEST, LONGEST, tokens - LONGEST)]
    return [(h, *block) for h in range(LANES // HEAD_DIM) for block in blocks]


def attention_group(q, k_ref, v, same, ot_s, vt_s, lse_ref):
    tokens = q.shape[0]
    qt = q.T
    vt_s[...] = v.T
    row = lax.broadcasted_iota(jnp.int32, qt.shape, 0)
    jobs = attention_jobs(tokens)
    queries, scores, soft = {}, {}, {}

    def score(job):
        h, start, width, key_start, key_count = job
        if h not in queries:
            queries[h] = jnp.where(row // HEAD_DIM == h, qt, jnp.zeros((), jnp.bfloat16))
        out = nn(k_ref[key_start : key_start + key_count, :], queries[h][:, start : start + width])
        return jnp.where(same, out, masked_score) if start == LONGEST else out

    def soften(values):
        peak = jnp.max(values, axis=0, keepdims=True)
        raised = jnp.exp(values - peak)
        return raised.astype(jnp.bfloat16), peak, jnp.sum(raised, axis=0, keepdims=True)

    def collect(job, raised, peak, total):
        h, start, width, key_start, key_count = job
        rows = slice(h * HEAD_DIM, (h + 1) * HEAD_DIM)
        out = nn(vt_s[rows, key_start : key_start + key_count], raised)
        ot_s[rows, start : start + width] = out / total
        lse_ref[0, h : h + 1, start : start + width] = peak + jnp.log(total)

    count = len(jobs)
    for t in range(count + 2):
        if t < count:
            scores[t] = score(jobs[t])
        if 0 <= t - 1 < count:
            soft[t - 1] = soften(scores.pop(t - 1))
        if 0 <= t - 2:
            collect(jobs[t - 2], *soft.pop(t - 2))
    return ot_s[...].T.astype(jnp.bfloat16)


def head_kernel(
    len_ref, count_ref, tokens_ref, w_qkv_ref, w_up_ref, w_down_ref, w_out_ref, vectors_ref, cot_hbm,
    qr_ref, kr_ref, vr_ref, attn_ref, lse_ref, h1_hbm, x_hbm, cos_hbm, sin_hbm, wt_hbm, table_ref, full_b, full_o,
    incoming_hbm, dy_hbm, dyt_hbm, incoming_s, dy_s, dyt_s, cot_s,
    h1_ref, x_ref, cos_ref, sin_ref, wt_ref, stores, full_a, full_v, twice_s, q_s, k_s, v_s, ot_s, vt_s, slab_a, slab_b, slab_o,
    a_send, a_recv, az_send, az_recv, b_send, b_recv, bz_send, bz_recv, v_send, v_recv, local,
):
    group = pl.program_id(0)
    rank, plane, core, chip_x, chip_y = place()
    chip = chip_at(0, chip_x, chip_y)
    columns = slab_a.shape[0]
    chunks_a = GATHERED // CHUNK_A
    gather_a = [Gather(lambda m, c, lane: full_a.at[:, m, c, :, lane], a_send, a_recv, 8 * n,
                       lane_parts(CHUNK_A * n, CHUNK_A))
                for n in range(chunks_a)]
    gather_o = Gather(lambda m, c, lane: full_o.at[:, m, c, :, lane], b_send, b_recv, 0, lane_parts(0, OUT_LANES))
    gather_b = [Gather(lambda m, c, lane: full_b.at[pl.ds(0, 2), m, c, :, lane], b_send, b_recv, 8 + 8 * n,
                       lane_parts(*cut))
                for n, cut in enumerate(CUTS_B)]

    def along(slab, full, send, recv, n, start, size):
        lanes = pl.ds(start, size)
        return [
            pltpu.make_async_remote_copy(
                src_ref=slab.at[:, lanes], dst_ref=full.at[plane, chip, core, :, lanes],
                send_sem=send.at[3 * n + step - 1], recv_sem=recv.at[3 * n + step - 1],
                device_id=(rank, (plane + step) % 4), device_id_type=MESH)
            for step in (1, 2, 3)
        ]

    along_a = [along(slab_a, full_a, az_send, az_recv, n, CHUNK_A * n, CHUNK_A) for n in range(chunks_a)]
    along_o = along(slab_o, full_o, bz_send, bz_recv, 0, 0, OUT_LANES)
    along_b = [along(slab_b, full_b, bz_send, bz_recv, 1 + n, *cut) for n, cut in enumerate(CUTS_B)]
    own_b = [pltpu.make_async_copy(slab_b, full_b.at[plane, chip, core], local.at[0]),
             pltpu.make_async_copy(slab_o, full_o.at[plane, chip, core], local.at[1])]
    storing = [pltpu.make_async_copy(source, target, stores.at[n]) for n, (source, target) in enumerate(
        ((h1_ref, h1_hbm), (x_ref, x_hbm), (cos_ref, cos_hbm), (sin_ref, sin_hbm), (wt_ref, wt_hbm),
         (incoming_s, incoming_hbm), (dy_s, dy_hbm), (dyt_s, dyt_hbm)))]
    load_cot = pltpu.make_async_copy(cot_hbm, cot_s, local.at[2])
    ends, offset = row_marks(len_ref)

    def widen(values, lanes):
        return jnp.concatenate([values, jnp.zeros((values.shape[0], lanes - values.shape[1]), values.dtype)], axis=1)

    @pl.when(group == 0)
    def _():
        call(all_partners())
        load_cot.start()
        slab_a[...] = widen(w_qkv_ref[...].astype(jnp.bfloat16), GATHERED)
        n_vec, width = vectors_ref.shape[0], tokens_ref.shape[1]
        vectors = jnp.concatenate([vectors_ref[...], jnp.zeros((LANES - n_vec, columns), jnp.float32)], axis=0)
        vectors = vectors.astype(jnp.bfloat16).astype(jnp.float32)
        full_v[pl.ds(chip, 1), pl.ds(core, 1)] = widen(vectors, LANES).T[:columns, :][None, None]
        full_a[pl.ds(plane, 1), pl.ds(chip, 1), pl.ds(core, 1)] = slab_a[...][None, None, None]
        hear(all_partners())
        for copy in along_a[0]:
            copy.start()
        slab_b[:, :width] = w_up_ref[...].astype(jnp.bfloat16)
        slab_b[:, width:] = w_down_ref[...].astype(jnp.bfloat16)
        slab_o[...] = widen(w_out_ref[...].T.astype(jnp.bfloat16), OUT_LANES)
        for copy in own_b:
            copy.start()

        def vec_copy(m, slot, device):
            block = full_v.at[m, core]
            return pltpu.make_async_remote_copy(
                src_ref=block, dst_ref=block, send_sem=v_send.at[slot], recv_sem=v_recv.at[slot],
                device_id=(device, plane), device_id_type=MESH)

        chips = [chip_at(step, chip_x, chip_y) for step in range(4)]
        vec_over = [vec_copy(chip, step - 1, 2 * chips[step] + core) for step in (1, 2, 3)]
        vec_beside = [vec_copy(m, 3 + step, 2 * chip + 1 - core) for step, m in enumerate(chips)]
        for copy in (*vec_over, vec_beside[0]):
            copy.start()
        twice_s[...] = turned_rows(tokens_ref[...], offset)
        for copy in along_a[0]:
            copy.wait()
        for copy in along_a[1]:
            copy.start()
        gather_a[0].first()
        index = lax.broadcasted_iota(jnp.int32, (ROW_LEN, LANES), 0)
        where, segment = segment_of(index, ends, offset)
        start = jnp.where(segment == 0, 0, jnp.where(segment == 1, ends[0], jnp.where(segment == 2, ends[1], ends[2])))
        position = (where - start).astype(jnp.float32)
        lane = lax.broadcasted_iota(jnp.int32, (1, LANES), 1)
        inverse = jnp.exp((lane % (HEAD_DIM // 2)).astype(jnp.float32) * (-2.0 * math.log(10000.0) / HEAD_DIM))
        sign = jnp.where((lane % HEAD_DIM) < (HEAD_DIM // 2), -1.0, 1.0)
        angles = position * inverse
        for copy in along_a[1]:
            copy.wait()
        gather_a[1].first()
        for copies in (along_o, *along_b):
            for copy in copies:
                copy.start()
        cos_ref[...] = jnp.cos(angles)
        for step in range(3):
            vec_over[step].wait()
            vec_beside[step + 1].start()
        gather_a[0].second()
        sin_ref[...] = jnp.sin(angles) * sign
        for copy in vec_beside:
            copy.wait()
        table_t = jnp.concatenate([full_v[m, c] for m in range(4) for c in range(2)], axis=0)
        table_ref[...] = table_t.T[: table_ref.shape[0], :]
        gather_a[1].second()
        load_cot.wait()
        _, segment = segment_of(lax.broadcasted_iota(jnp.int32, (ROW_LEN, 1), 0), ends, offset)
        number = jnp.where(segment == 0, count_ref[0, 0], jnp.where(
            segment == 1, count_ref[0, 1], jnp.where(segment == 2, count_ref[0, 2], count_ref[0, 3])))
        incoming_s[...] = turned_rows(cot_s[...], offset) * (1.0 / number.astype(jnp.float32))
        dy_s[...] = incoming_s[...].astype(jnp.bfloat16)
        dyt_s[...] = dy_s[...].T
        gather_a[0].third()
        gather_a[1].third()
        gain, shift = table_ref[0:1, :], table_ref[1:2, :]
        for r in range(0, ROW_LEN, 256):
            values = twice_s[r : r + 256, :]
            x_ref[r : r + 256, :] = values.astype(jnp.bfloat16)
            h1_ref[r : r + 256, :] = layer_norm(values, gain, shift).astype(jnp.bfloat16)
        for gather in gather_a:
            gather.finish()
        for copy in (*own_b, *along_o):
            copy.wait()
        gather_o.first()
        rows = wt_ref.shape[1] // 4
        wt_ref[...] = jnp.concatenate(
            [full_a[j].reshape(width, GATHERED)[:, :rows] for j in range(4)], axis=1)
        first = _half_mask((256, LANES))
        bias = [table_ref[4 + part : 5 + part, :] for part in range(3)]
        for r in range(0, ROW_LEN, 256):
            at = slice(r, r + 256)
            project = nn(h1_ref[at, :], wt_ref[...])
            cosine, sine = cos_ref[at, :], sin_ref[at, :]
            for g in range(width // LANES):
                lanes = slice(g * LANES, (g + 1) * LANES)
                queries = (project[:, lanes] + bias[0][:, lanes]) * (1.0 / math.sqrt(HEAD_DIM))
                keys = project[:, width + g * LANES : width + (g + 1) * LANES] + bias[1][:, lanes]
                q_s[g, at, :] = (queries * cosine + _turn(queries, first) * sine).astype(jnp.bfloat16)
                k_s[g, at, :] = (keys * cosine + _turn(keys, first) * sine).astype(jnp.bfloat16)
                v_s[g, at, :] = (project[:, 2 * width + g * LANES : 2 * width + (g + 1) * LANES]
                                 + bias[2][:, lanes]).astype(jnp.bfloat16)
        for copy in storing:
            copy.start()
        for copy in along_b[0]:
            copy.wait()
        gather_b[0].first()
        gather_o.second()

    @pl.when(group == 1)
    def _():
        for copy in along_b[1]:
            copy.wait()
        gather_b[1].first()
        gather_o.third()

    @pl.when(group == 2)
    def _():
        gather_b[0].second()

    @pl.when(group == 4)
    def _():
        gather_b[1].second()
        gather_b[0].third()

    qr_ref[...] = q_s[group]
    kr_ref[...] = k_s[group]
    vr_ref[...] = v_s[group]
    attn_ref[...] = attention_group(q_s[group], kr_ref, v_s[group], same_rest(ends, offset), ot_s, vt_s, lse_ref)

    @pl.when(group == 4)
    def _():
        gather_b[1].third()
        for gather in (gather_o, *gather_b):
            gather.finish()
        for copy in storing:
            copy.wait()


def head(lengths, counts, tokens, cotangent, w_qkv_t, w_up_t, w_down_t, w_out, vectors):
    tokens_count, width = tokens.shape
    groups = width // LANES
    columns = w_qkv_t.shape[0]
    col = pl.BlockSpec((tokens_count, LANES), lambda g: (0, g))
    whole = lambda *shape: pl.BlockSpec(shape, lambda g: (0,) * len(shape))
    shape = jax.ShapeDtypeStruct
    bf16, f32 = jnp.bfloat16, jnp.float32
    sems = lambda n: pltpu.SemaphoreType.DMA((n,))
    na, nb = GATHERED // CHUNK_A, 1 + len(CUTS_B)
    return pl.pallas_call(
        head_kernel,
        grid=(groups,),
        in_specs=[pl.BlockSpec(memory_space=pltpu.SMEM)] * 2 + [whole(tokens_count, width), whole(*w_qkv_t.shape),
                  whole(columns, width), whole(columns, width), whole(*w_out.shape), whole(*vectors.shape),
                  pl.BlockSpec(memory_space=pl.ANY)],
        out_specs=[col] * 4 + [pl.BlockSpec((1, 4, tokens_count), lambda g: (g, 0, 0)),
                               *[pl.BlockSpec(memory_space=pl.ANY)] * 5, whole(16, width),
                               *[pl.BlockSpec(memory_space=pl.ANY)] * 5],
        out_shape=[shape((tokens_count, width), bf16)] * 4 + [shape((groups, 4, tokens_count), f32)]
        + [shape((tokens_count, width), bf16)] * 2 + [shape((tokens_count, LANES), f32)] * 2
        + [shape((width, 3 * width), bf16), shape((16, width), f32), shape((4, 4, 2, columns, 2 * width), bf16),
           shape((4, 4, 2, columns, OUT_LANES), bf16),
           shape((tokens_count, width), f32), shape((tokens_count, width), bf16), shape((width, tokens_count), bf16)],
        scratch_shapes=[
            pltpu.VMEM((tokens_count, width), f32),
            pltpu.VMEM((tokens_count, width), bf16),
            pltpu.VMEM((width, tokens_count), bf16),
            pltpu.VMEM((tokens_count, width), bf16),
            pltpu.VMEM((tokens_count, width), bf16),
            pltpu.VMEM((tokens_count, width), bf16),
            pltpu.VMEM((tokens_count, LANES), f32),
            pltpu.VMEM((tokens_count, LANES), f32),
            pltpu.VMEM((width, 3 * width), bf16),
            sems(8),
            pltpu.VMEM((4, 4, 2, columns, GATHERED), bf16),
            pltpu.VMEM((4, 2, columns, LANES), f32),
            pltpu.VMEM((tokens_count, width), f32),
            pltpu.VMEM((groups, tokens_count, LANES), bf16),
            pltpu.VMEM((groups, tokens_count, LANES), bf16),
            pltpu.VMEM((groups, tokens_count, LANES), bf16),
            pltpu.VMEM((LANES, tokens_count), f32),
            pltpu.VMEM((LANES, tokens_count), bf16),
            pltpu.VMEM((columns, GATHERED), bf16),
            pltpu.VMEM((columns, 2 * width), bf16),
            pltpu.VMEM((columns, OUT_LANES), bf16),
            sems(8 * na), sems(8 * na), sems(3 * na), sems(3 * na),
            sems(8 * nb), sems(8 * nb), sems(3 * nb), sems(3 * nb), sems(7), sems(7), sems(3),
        ],
        compiler_params=pltpu.CompilerParams(collective_id=2, has_side_effects=True, vmem_limit_bytes=58 << 20),
        name="head",
    )(lengths, counts, tokens, w_qkv_t, w_up_t, w_down_t, w_out, vectors, cotangent)


def middle_kernel(
    len_ref, table_ref, x_hbm, attn_hbm, incoming_hbm, dy_hbm, dyt_hbm, full_o_hbm, full_b,
    out_grad_ref, sums_ref, layer_hbm, after_hbm, attn_grad_hbm, parts_hbm,
    x_ref, attn_ref, cot_ref, full_o_ref, after_grad_ref, parts_s, stores,
    xhat_s, rstd_s, h2_s, h2t_s, dy_s, dyt_s, acc_s, back_s, act_s, pre_s, wt_out_s, w_s, send, recv, local,
):
    step = pl.program_id(0)
    tokens, width = x_ref.shape
    rank, plane, core, chip_x, chip_y = place()
    chip = chip_at(0, chip_x, chip_y)
    late = Gather(lambda m, c, lane: w_s.at[1, :, m, c, :, lane], send, recv, 0, lane_parts(0, 2 * width))
    loads = [pltpu.make_async_copy(full_b.at[pl.ds(2, 2), chip, core], w_s.at[1, :, chip, core], local.at[0]),
             pltpu.make_async_copy(full_o_hbm, full_o_ref, local.at[1]),
             pltpu.make_async_copy(attn_hbm, attn_ref, local.at[2]),
             pltpu.make_async_copy(x_hbm, x_ref, local.at[3]),
             pltpu.make_async_copy(full_b.at[pl.ds(0, 2)], w_s.at[0], local.at[4]),
             pltpu.make_async_copy(dy_hbm, dy_s, local.at[5]),
             pltpu.make_async_copy(dyt_hbm, dyt_s, local.at[6]),
             pltpu.make_async_copy(incoming_hbm, after_grad_ref, local.at[7])]
    ends, offset = row_marks(len_ref)
    chunk = 256
    cuts = [slice(r, r + chunk) for r in range(0, tokens, chunk)]

    @pl.when(step == 0)
    def _():
        beside = ([(2 * chip + 1 - core, plane)]
                  + [(2 * chip_at(other, chip_x, chip_y) + core, plane) for other in (1, 2)])
        call(beside)
        for load in loads[:6]:
            load.start()
        loads[0].wait()
        hear(beside)
        late.first()
        for load in loads[1:4]:
            load.wait()
        rows = width // 4
        wt_out_s[...] = jnp.concatenate([full_o_ref[p].reshape(width, OUT_LANES)[:, :rows] for p in range(4)], axis=1)
        sums_ref[...] = jnp.zeros_like(sums_ref)
        gain, shift = table_ref[2:3, :], table_ref[3:4, :]
        branch = {}
        for t in range(len(cuts) + 1):
            if t < len(cuts):
                branch[t] = nn(attn_ref[cuts[t], :], wt_out_s[...])
            if t == 0:
                continue
            at = cuts[t - 1]
            after = x_ref[at, :].astype(jnp.float32) + (branch.pop(t - 1) + table_ref[7:8, :])
            acc_s[at, :] = after + table_ref[8:9, :]
            center = after - jnp.mean(after, axis=-1, keepdims=True)
            rstd = lax.rsqrt(jnp.mean(center * center, axis=-1, keepdims=True) + norm_eps)
            xhat = center * rstd
            xhat_s[at, :] = xhat
            rstd_s[at, :] = rstd
            h2_s[at, :] = (xhat * gain + shift).astype(jnp.bfloat16)
        h2t_s[...] = h2_s[...].T
        back_s[...] = jnp.zeros_like(back_s)

    @pl.when(step == 0)
    def _():
        for load in loads[6:]:
            load.start()
        for load in loads[4:6]:
            load.wait()
        sums_ref[8:9, :] = jnp.sum(dy_s[...].astype(jnp.float32), axis=0, keepdims=True)

    @pl.when(step == 1)
    def _():
        late.finish()

    def weights(lanes):
        return jnp.concatenate([w_s[step, p, :, :, :, lanes].reshape(width, width) for p in range(2)], axis=1)

    up, down = (weights(slice(part * width, (part + 1) * width)) for part in range(2))
    bias = jnp.concatenate([table_ref[pl.ds(9 + 2 * step + p, 1), :] for p in range(2)], axis=1)

    def products(at):
        return nn(h2_s[at, :], up), nn(dy_s[at, :], down)

    def pointwise(at, pre, act_grad):
        pre = pre + bias
        cdf = 0.5 * (1.0 + lax.erf(pre * (1.0 / math.sqrt(2.0))))
        slope = cdf + pre * (jnp.exp(-0.5 * pre * pre) * (1.0 / math.sqrt(2.0 * math.pi)))
        act_s[at, :] = (pre * cdf).astype(jnp.bfloat16)
        pre_s[at, :] = (act_grad * slope).astype(jnp.bfloat16)

    def collect(at):
        acc_s[at, :] += nt(act_s[at, :], down)
        back_s[at, :] += nt(pre_s[at, :], up)

    held = {}
    for t in range(len(cuts) + 1):
        if t == 2:
            @pl.when(step == 0)
            def _():
                late.second()
                for load in loads[6:]:
                    load.wait()

        if t < len(cuts):
            held[t] = products(cuts[t])
        if t >= 1:
            pointwise(cuts[t - 1], *held.pop(t - 1))
            collect(cuts[t - 1])

    @pl.when(step == 0)
    def _():
        late.third()

    @pl.when(step == 1)
    def _():
        for part in range(2):
            lanes = pl.ds(part * width, width)
            pltpu.make_async_copy(parts_s.at[:, :, lanes], parts_hbm.at[pl.ds(0, 2), :, lanes],
                                  stores.at[0 if part == 0 else 10]).wait()

    store_parts = []
    for part, (left, right) in enumerate(((h2t_s, pre_s), (dyt_s, act_s))):
        grad = nn(left[...], right[...]).astype(jnp.bfloat16)
        for p in range(2):
            parts_s[p, :, part * width : (part + 1) * width] = grad[:, p * width : (p + 1) * width]
        lanes = pl.ds(part * width, width)
        store_parts.append(pltpu.make_async_copy(
            parts_s.at[:, :, lanes], parts_hbm.at[pl.ds(2 * step, 2), :, lanes], stores.at[0 if part == 0 else 10]))
        store_parts[part].start()
    bias_sum = jnp.sum(pre_s[...].astype(jnp.float32), axis=0, keepdims=True)
    for p in range(2):
        sums_ref[pl.ds(9 + 2 * step + p, 1), :] = bias_sum[:, p * width : (p + 1) * width]

    @pl.when(step == 1)
    def _():
        x_ref[...] = pltpu.roll(acc_s[...], offset, 0).astype(jnp.bfloat16)
        storing = [pltpu.make_async_copy(x_ref, layer_hbm, stores.at[1])]
        storing[0].start()
        gain = table_ref[2:3, :]
        gain_sum = jnp.zeros((1, width), jnp.float32)
        shift_sum = jnp.zeros((1, width), jnp.float32)
        branch_sum = jnp.zeros((1, width), jnp.float32)
        for n in range(len(cuts) + 1):
            if n >= 1:
                at = cuts[n - 1]
                cot_ref[at, :] = nt(dy_s[at, :], wt_out_s[...]).astype(jnp.bfloat16)
                rows = pl.ds(at.start, chunk)
                for source, target, slot in ((after_grad_ref, after_hbm, 1), (cot_ref, attn_grad_hbm, 5)):
                    copy = pltpu.make_async_copy(source.at[rows], target.at[rows], stores.at[slot + n])
                    copy.start()
                    storing.append(copy)
            if n == len(cuts):
                break
            at = cuts[n]
            grad, xhat = back_s[at, :], xhat_s[at, :]
            gain_sum += jnp.sum(grad * xhat, axis=0, keepdims=True)
            shift_sum += jnp.sum(grad, axis=0, keepdims=True)
            scaled = grad * gain
            resid = rstd_s[at, :] * (
                scaled - jnp.mean(scaled, axis=-1, keepdims=True)
                - xhat * jnp.mean(scaled * xhat, axis=-1, keepdims=True))
            after_grad = after_grad_ref[at, :] + resid
            after_grad_ref[at, :] = after_grad
            low = after_grad.astype(jnp.bfloat16)
            dy_s[at, :] = low
            branch_sum += jnp.sum(low.astype(jnp.float32), axis=0, keepdims=True)
        sums_ref[2:3, :] = gain_sum
        sums_ref[3:4, :] = shift_sum
        sums_ref[7:8, :] = branch_sum
        h2t_s[...] = attn_ref[...].T
        out_grad_ref[...] = nn(h2t_s[...], dy_s[...]).astype(jnp.bfloat16)
        for copy in (*store_parts, *storing):
            copy.wait()


def middle(lengths, x, attn, incoming, dy, dyt, table, full_o, full_b):
    tokens, width = x.shape
    columns = full_b.shape[3]
    whole = lambda *shape: pl.BlockSpec(shape, lambda j: (0,) * len(shape))
    smem = pl.BlockSpec(memory_space=pltpu.SMEM)
    hbm = pl.BlockSpec(memory_space=pl.ANY)
    shape = jax.ShapeDtypeStruct
    bf16, f32 = jnp.bfloat16, jnp.float32
    flat = pltpu.VMEM((tokens, width), bf16)
    double = pltpu.VMEM((tokens, 2 * width), bf16)
    wide = pltpu.VMEM((tokens, width), f32)
    turned = pltpu.VMEM((width, tokens), bf16)
    sems = lambda n: pltpu.SemaphoreType.DMA((n,))
    return pl.pallas_call(
        middle_kernel,
        grid=(2,),
        in_specs=[smem, whole(16, width)] + [hbm] * 7,
        out_specs=[whole(width, width), whole(16, width)] + [hbm] * 4,
        out_shape=[shape((width, width), bf16), shape((16, width), f32),
                   shape((tokens, width), bf16), shape((tokens, width), f32), shape((tokens, width), bf16),
                   shape((4, width, 2 * width), bf16)],
        scratch_shapes=[flat, flat, flat, pltpu.VMEM(full_o.shape, bf16), wide, pltpu.VMEM((2, width, 2 * width), bf16),
                        sems(11), wide, pltpu.VMEM((tokens, 1), f32), flat, turned, flat, turned, wide, wide, double, double,
                        pltpu.VMEM((width, width), bf16), pltpu.VMEM((2, 2, 4, 2, columns, 2 * width), bf16),
                        sems(8), sems(8), sems(8)],
        compiler_params=pltpu.CompilerParams(collective_id=3, has_side_effects=True, vmem_limit_bytes=62 << 20),
        name="middle",
    )(lengths, table, x, attn, incoming, dy, dyt, full_o, full_b)


def backward_group(between, qr_ref, kr_ref, vr_ref, do_ref, attn_ref, lse_ref, same, qt_s, dot_s, kt_s, delta_s, dqt_s, dk_s, dv_s):
    tokens = qr_ref.shape[0]
    qt_s[...] = qr_ref[...].T
    dot_s[...] = do_ref[...].T
    kt_s[...] = kr_ref[...].T
    prod_t = (do_ref[...].astype(jnp.float32) * attn_ref[...].astype(jnp.float32)).T
    for h in range(4):
        delta_s[h : h + 1, :] = jnp.sum(prod_t[h * HEAD_DIM : (h + 1) * HEAD_DIM, :], axis=0, keepdims=True)
    dk_s[...] = jnp.zeros_like(dk_s)
    dv_s[...] = jnp.zeros_like(dv_s)
    row = lax.broadcasted_iota(jnp.int32, (LANES, tokens), 0)
    lane = lax.broadcasted_iota(jnp.int32, (tokens, LANES), 1)
    zero = jnp.zeros((), jnp.bfloat16)
    jobs = attention_jobs(tokens)
    masked, held = {}, {}

    def products(job):
        h, start, width, key_start, key_count = job
        if h not in masked:
            masked[h] = (
                jnp.where(row // HEAD_DIM == h, qt_s[...], zero), jnp.where(row // HEAD_DIM == h, dot_s[...], zero),
                jnp.where(lane // HEAD_DIM == h, qr_ref[...], zero), jnp.where(lane // HEAD_DIM == h, do_ref[...], zero))
        at, keys = slice(start, start + width), slice(key_start, key_start + key_count)
        scores = nn(kr_ref[keys, :], masked[h][0][:, at])
        if start == LONGEST:
            scores = jnp.where(same, scores, masked_score)
        return scores, nn(vr_ref[keys, :], masked[h][1][:, at])

    def finish(job, scores, weight_grad):
        h, start, width, key_start, key_count = job
        at, keys = slice(start, start + width), slice(key_start, key_start + key_count)
        rows = slice(h * HEAD_DIM, (h + 1) * HEAD_DIM)
        soft = jnp.exp(scores - lse_ref[0, h : h + 1, at])
        score_grad = (soft * (weight_grad - delta_s[h : h + 1, at])).astype(jnp.bfloat16)
        dv_s[keys, :] += nn(soft.astype(jnp.bfloat16), masked[h][3][at, :])
        dk_s[keys, :] += nn(score_grad, masked[h][2][at, :])
        dqt_s[rows, at] = nn(kt_s[rows, keys], score_grad)

    for t in range(len(jobs) + 1):
        if t == len(jobs) // 2:
            between()
        if t < len(jobs):
            held[t] = products(jobs[t])
        if t >= 1:
            finish(jobs[t - 1], *held.pop(t - 1))


def backward_kernel(
    len_ref, qr_ref, kr_ref, vr_ref, do_ref, attn_ref, lse_ref, cos_ref, sin_ref, parts_ref,
    dq_ref, dk_ref, dv_ref, own_ref, total_ref, *scratch,
):
    group = pl.program_id(0)
    lanes = parts_ref.shape[-1] // 2
    halves = [SumStages(parts_ref, scratch[7 + SUM_SCRATCH * n : 7 + SUM_SCRATCH * (n + 1)], pl.ds(n * lanes, lanes))
              for n in range(2)]
    dqt_s, dk_s, dv_s = scratch[4:7]

    @pl.when(group == 0)
    def _():
        greet(all_partners())
        halves[0].core_start()

    @pl.when(group == 1)
    def _():
        halves[1].core_finish()

    def between():
        @pl.when(group == 0)
        def _():
            halves[0].core_finish()
            halves[0].chip_start()
            halves[1].core_start()

        @pl.when(group == 1)
        def _():
            halves[1].chip_start()

        @pl.when(group == 2)
        def _():
            halves[0].chip_turn()

        @pl.when(group == 3)
        def _():
            halves[0].chip_finish()
            halves[0].plane_start()
            halves[1].chip_turn()

        @pl.when(group == 4)
        def _():
            halves[1].chip_finish()
            total_ref[...] = halves[1].total[...]

    ends, offset = row_marks(len_ref)
    backward_group(between, qr_ref, kr_ref, vr_ref, do_ref, attn_ref, lse_ref, same_rest(ends, offset), *scratch[:7])
    first = _half_mask(cos_ref.shape)
    cosine, sine = cos_ref[...], sin_ref[...]

    def pull(values):
        return values * cosine + _turn(values * sine, first)

    dq_ref[...] = (pull(dqt_s[...].T) * (1.0 / math.sqrt(HEAD_DIM))).astype(jnp.bfloat16)
    dk_ref[...] = pull(dk_s[...]).astype(jnp.bfloat16)
    dv_ref[...] = dv_s[...].astype(jnp.bfloat16)

    @pl.when(group == 4)
    def _():
        own_ref[...] = halves[0].plane_finish()


def backward(lengths, qr, kr, vr, attn_grad, attn, lse, cosine, sine, parts):
    tokens, width = qr.shape
    groups = width // LANES
    rows, lanes = parts.shape[-2:]
    col = pl.BlockSpec((tokens, LANES), lambda g: (0, g))
    whole = lambda *shape: pl.BlockSpec(shape, lambda g: (0,) * len(shape))
    shape = jax.ShapeDtypeStruct
    bf16, f32 = jnp.bfloat16, jnp.float32
    return pl.pallas_call(
        backward_kernel,
        grid=(groups,),
        in_specs=[pl.BlockSpec(memory_space=pltpu.SMEM)] + [col] * 5
        + [pl.BlockSpec((1, 4, tokens), lambda g: (g, 0, 0)), whole(tokens, LANES), whole(tokens, LANES),
           pl.BlockSpec(memory_space=pl.ANY)],
        out_specs=[col] * 3 + [whole(rows, lanes // 2), whole(4, rows, lanes // 2)],
        out_shape=[shape((tokens, width), bf16)] * 3 + [shape((rows, lanes // 2), f32), shape((4, rows, lanes // 2), bf16)],
        scratch_shapes=[pltpu.VMEM((LANES, tokens), bf16)] * 3
        + [pltpu.VMEM((8, tokens), f32), pltpu.VMEM((LANES, tokens), f32), pltpu.VMEM((tokens, LANES), f32),
           pltpu.VMEM((tokens, LANES), f32)] + sum_scratch(rows, lanes // 2) * 2,
        compiler_params=pltpu.CompilerParams(collective_id=0, has_side_effects=True, vmem_limit_bytes=58 << 20),
        name="backward",
    )(lengths, qr, kr, vr, attn_grad, attn, lse, cosine, sine, parts)


def row_layout(lengths, counts, row_len):
    lens = lengths[0]
    slots = lens.shape[0]
    order = lax.broadcasted_iota(jnp.int32, (slots, slots), 0)
    upto = lax.broadcasted_iota(jnp.int32, (slots, slots), 1)
    starting = jnp.sum(jnp.where(upto < order, lens[None, :], 0), axis=1)
    slot = lax.broadcasted_iota(jnp.int32, (slots,), 0)
    which = jnp.min(jnp.where(lens == LONGEST, slot, slots))
    offset = jnp.sum(jnp.where(slot == which, starting, 0))
    places = lax.broadcasted_iota(jnp.int32, (row_len,), 0) + offset
    places = jnp.where(places >= row_len, places - row_len, places)
    endings = starting + lens
    segment = jnp.sum((places[:, None] >= endings[None, :]).astype(jnp.int32), axis=1)
    member = segment[:, None] == slot[None, :]
    first_place = jnp.sum(jnp.where(member, starting[None, :], 0), axis=1)
    position = (places - first_place).astype(jnp.float32)
    inverse_count = 1.0 / counts[0].astype(jnp.float32)
    share = jnp.sum(jnp.where(member, inverse_count[None, :], 0.0), axis=1)
    return offset, segment, position, share


def rotary_tables(position):
    lane = lax.broadcasted_iota(jnp.int32, (1, LANES), 1)
    indices = (lane % (HEAD_DIM // 2)).astype(jnp.float32)
    inverse = jnp.exp(indices * (-2.0 * math.log(10000.0) / HEAD_DIM))
    angles = position[:, None] * inverse
    sign = jnp.where((lane % HEAD_DIM) < (HEAD_DIM // 2), -1.0, 1.0)
    return jnp.cos(angles), jnp.sin(angles) * sign


def turn_rows(values, shift):
    twice = jnp.concatenate([values, values], axis=0)
    return lax.dynamic_slice_in_dim(twice, shift, values.shape[0], 0)


def high(left, right):
    return jnp.dot(left, right, precision=lax.Precision.HIGH, preferred_element_type=jnp.float32)


def shards_near(
    tokens, cotangent, lengths, counts,
    w_qkv, w_out, w_up, w_down,
    mom_qkv, mom_out, mom_up, mom_down,
    vectors, vec_first, vec_second,
):
    columns = w_qkv.shape[1]
    weights_t = [w_qkv.T, w_out, w_up.T, w_down.T]
    moments_t = [mom_qkv.T, mom_out, mom_up.T, mom_down.T]
    qr, kr, vr, attn, lse, normed_one, turned, cosine, sine, wt_qkv, table, full_b, full_o, incoming, dy, dyt = head(
        lengths, counts, tokens, cotangent, weights_t[0], weights_t[2], weights_t[3], w_out, vectors)
    out_grad, sums, layer_out, after_grad, attn_grad, parts_b = middle(
        lengths, turned, attn, incoming, dy, dyt, table, full_o, full_b)
    dq, dk, dv, own_up, total_down = backward(
        lengths, qr, kr, vr, attn_grad, attn, lse, cosine, sine, parts_b.reshape(4, 2, 2, 2, columns, -1))
    results = tail(
        normed_one, dq, dk, dv, out_grad, sums, table, own_up, total_down, lengths, moments_t, weights_t,
        (vectors, vec_first, vec_second), wt_qkv, after_grad, turned)
    results = finish([*results, layer_out])
    matrices = [v if x % 4 == 1 else v.T for x, v in enumerate(results[:8])]
    return (results[12], results[11], *matrices, *results[8:11])


def shards_far(
    tokens, cotangent, lengths, counts,
    w_qkv, w_out, w_up, w_down,
    mom_qkv, mom_out, mom_up, mom_down,
    vectors, vec_first, vec_second,
):
    both = ("fsdp", "dp")
    planes = lax.axis_size("fsdp")
    ranks = lax.axis_size("dp")
    row_len, width = tokens.shape
    columns = w_qkv.shape[1]
    old_weights = (w_qkv, w_out, w_up, w_down)
    old_moments = (mom_qkv, mom_out, mom_up, mom_down)
    counts_rows = [w.shape[0] for w in old_weights]
    n_vec = vectors.shape[0]

    slab_a = jnp.concatenate([w_qkv.T, w_out.T, vectors.T], axis=1).astype(jnp.bfloat16)
    slab_b = jnp.concatenate([w_up.T, w_down.T], axis=1).astype(jnp.bfloat16)
    full_a = lax.all_gather(slab_a, both, axis=0, tiled=True).reshape(planes, width, -1)
    full_b = lax.all_gather(slab_b, both, axis=0, tiled=True).reshape(planes, width, -1)
    r0, r1, r2, r3 = counts_rows
    wt_qkv = jnp.concatenate([full_a[j, :, :r0] for j in range(planes)], axis=1)
    wt_out = jnp.concatenate([full_a[j, :, r0 : r0 + r1] for j in range(planes)], axis=1)
    table = full_a[0, :, r0 + r1 :].T.astype(jnp.float32)
    wt_up = jnp.concatenate([full_b[j, :, :r2] for j in range(planes)], axis=1)
    wt_down = jnp.concatenate([full_b[j, :, r2:] for j in range(planes)], axis=1)

    offset, segment, position, share = row_layout(lengths, counts, row_len)
    cosine, sine = rotary_tables(position)
    seg_col, seg_row = segment[:, None], segment[None, :]
    inputs = turn_rows(tokens, offset).astype(jnp.float32)
    incoming = turn_rows(cotangent, offset).astype(jnp.float32) * share[:, None]

    normed_one, pull_one = jax.vjp(layer_norm, inputs, table[0], table[1])
    normed_one = normed_one.astype(jnp.bfloat16)
    project = nn(normed_one, wt_qkv) + table[4:7].reshape(-1)
    qr, kr, vr, attn, lse = attention_forward(project, cosine, sine, seg_col, seg_row)
    after = inputs + (nn(attn, wt_out) + table[7])
    normed_two, pull_two = jax.vjp(layer_norm, after, table[2], table[3])
    normed_two = normed_two.astype(jnp.bfloat16)
    hidden_pre = nn(normed_two, wt_up) + table[9:].reshape(-1)
    hidden, pull_hidden = jax.vjp(gelu_exact, hidden_pre)
    hidden = hidden.astype(jnp.bfloat16)
    layer_out = (after + (nt(hidden, wt_down) + table[8])).astype(jnp.bfloat16)

    grad_low = incoming.astype(jnp.bfloat16)
    grad_t_down = tn(grad_low, hidden)
    pre_grad = pull_hidden(nn(grad_low, wt_down))[0].astype(jnp.bfloat16)
    grad_t_up = tn(normed_two, pre_grad)
    resid_grad, gain_two, shift_two = pull_two(nt(pre_grad, wt_up))
    after_grad = incoming + resid_grad
    branch_low = after_grad.astype(jnp.bfloat16)
    grad_t_out = tn(attn, branch_low)
    attn_grad = nt(branch_low, wt_out).astype(jnp.bfloat16)
    dq, dk, dv = attention_backward(qr, kr, vr, attn_grad, attn, lse, cosine, sine, seg_col, seg_row)
    proj_grad = jnp.concatenate([dq, dk, dv], axis=1)
    grad_t_qkv = tn(normed_one, proj_grad)
    in_grad, gain_one, shift_one = pull_one(nt(proj_grad, wt_qkv))
    input_grad = after_grad + in_grad

    def column_sum(values):
        return jnp.sum(values.astype(jnp.float32), axis=0)

    vector_grad = jnp.concatenate(
        [gain_one[None], shift_one[None], gain_two[None], shift_two[None],
         column_sum(proj_grad).reshape(3, width), column_sum(branch_low)[None], column_sum(grad_low)[None],
         column_sum(pre_grad).reshape(-1, width)],
        axis=0,
    )
    back = jnp.where(offset > 0, row_len - offset, 0)
    layer_out = turn_rows(layer_out, back)
    input_grad = turn_rows(input_grad, back)

    def cut(values, j, rows):
        return values[:, j * rows : (j + 1) * rows]

    parts_b = jnp.stack([jnp.concatenate([cut(grad_t_up, j, r2), cut(grad_t_down, j, r3)], axis=1) for j in range(planes)])
    own_b = lax.psum_scatter(parts_b.reshape(planes * width, -1), both, scatter_dimension=0, tiled=True)
    parts_a = jnp.stack([jnp.concatenate([cut(grad_t_qkv, j, r0), cut(grad_t_out, j, r1), vector_grad.T], axis=1) for j in range(planes)])
    own_a = lax.psum_scatter(parts_a.reshape(planes * width, -1), both, scatter_dimension=0, tiled=True)
    grads_t = (own_a[:, :r0], own_a[:, r0 : r0 + r1], own_b[:, :r2], own_b[:, r2:])
    vector_grad = own_a[:, r0 + r1 :].T
    new_moments_t = [moment_keep * old.T + grad for old, grad in zip(old_moments, grads_t)]

    most = max(counts_rows)
    padded = [jnp.pad(m.astype(jnp.bfloat16), ((0, 0), (0, most - m.shape[1]))) for m in new_moments_t]
    sent = jnp.stack([padded[t % 4] for t in range(planes)])
    mine = lax.all_to_all(sent, "fsdp", 0, 0, tiled=True)
    mine = mine.transpose(1, 0, 2).reshape(columns, planes * most)
    whole = lax.all_gather(mine, "dp", axis=0, tiled=True)
    gram = nt(whole, whole)
    identity = jnp.eye(width, dtype=jnp.float32)
    norm_sq = jnp.trace(gram) + 1e-07
    gram = gram / norm_sq
    factor = None
    for iteration in range(NS_ITERS):
        poly = poly_linear * identity + poly_square * gram + poly_cubic * high(gram, gram)
        factor = poly if factor is None else high(factor, poly)
        if iteration + 1 < NS_ITERS:
            gram = high(high(gram, poly), poly)
    own_rows = lax.dynamic_slice_in_dim(factor, lax.axis_index("dp") * columns, columns, 0) * lax.rsqrt(norm_sq)
    own_orth = high(own_rows, whole.astype(jnp.float32))
    own_orth = own_orth.astype(jnp.bfloat16).reshape(columns, planes, most).transpose(1, 0, 2)
    pieces = lax.all_to_all(own_orth, "fsdp", 0, 0, tiled=True).astype(jnp.float32)

    new_weights = []
    for x, weight_old in enumerate(old_weights):
        rows = weight_old.shape[0]
        scale = muon_rate * math.sqrt(max(1.0, rows * planes / width))
        new_weights.append(weight_old * (1.0 - muon_rate * muon_decay) - scale * pieces[x, :, :rows].T)
    new_first = beta_first * vec_first + (1.0 - beta_first) * vector_grad
    new_second = beta_second * vec_second + (1.0 - beta_second) * vector_grad * vector_grad
    first_fix = 1.0 - beta_first**STEP
    second_fix = 1.0 - beta_second**STEP
    new_vectors = vectors - adam_rate * (new_first / first_fix) / (jnp.sqrt(new_second / second_fix) + adam_eps)
    return (layer_out, input_grad, *[m.T for m in new_moments_t], *new_weights, new_vectors, new_first, new_second)


def solution(mesh):
    rows, cells, table = P(("dp", "fsdp"), None), P("fsdp", "dp"), P(None, "dp")
    near = dict(mesh.shape) == {"dp": 8, "fsdp": 4}
    return jax.shard_map(
        shards_near if near else shards_far,
        mesh=mesh,
        in_specs=(rows,) * 4 + (cells,) * 8 + (table,) * 3,
        out_specs=(rows,) * 2 + (cells,) * 8 + (table,) * 3,
        check_vma=False,
    )
```

```python
import functools
import math

import jax
import jax.numpy as jnp
from jax import lax
from jax.experimental import pallas as pl
from jax.experimental.pallas import tpu as pltpu
from jax.sharding import PartitionSpec as P

HEAD_DIM = 32
NS_ITERS = 5
STEP = 10
LANES = 128
LONGEST = 768

norm_eps = 1e-05
masked_score = -1e30
poly_linear = 3.4445
poly_square = -4.775
poly_cubic = 2.0315
muon_rate = 0.5
muon_decay = 0.01
moment_keep = 0.5
adam_rate = 0.05
beta_first = 0.9
beta_second = 0.999
adam_eps = 1e-08


def layer_norm(values, gain_row, shift_row):
    center = values - jnp.mean(values, axis=-1, keepdims=True)
    spread = jnp.mean(center * center, axis=-1, keepdims=True)
    return center * lax.rsqrt(spread + norm_eps) * gain_row + shift_row


def gelu_exact(values):
    return 0.5 * values * (1.0 + lax.erf(values * (1.0 / math.sqrt(2.0))))


def nn(left, right):
    return jnp.dot(left, right, preferred_element_type=jnp.float32)


def nt(left, right):
    return lax.dot_general(left, right, (((1,), (1,)), ((), ())), preferred_element_type=jnp.float32)


def tn(left, right):
    return lax.dot_general(left, right, (((0,), (0,)), ((), ())), preferred_element_type=jnp.float32)


def _half_mask(shape):
    lane = lax.broadcasted_iota(jnp.int32, shape, 1)
    return (lane % HEAD_DIM) < (HEAD_DIM // 2)


def _turn(values, first):
    half = HEAD_DIM // 2
    left = pltpu.roll(values, LANES - half, 1)
    right = pltpu.roll(values, half, 1)
    return jnp.where(first, left, right)


def attention_forward_kernel(
    q_ref, k_ref, v_ref, cos_ref, sin_ref, segc_ref, segr_ref,
    qr_ref, kr_ref, vr_ref, attn_ref, lse_ref,
    qt_s, vt_s, ot_s,
):
    first = _half_mask(cos_ref.shape)
    cosine, sine = cos_ref[...], sin_ref[...]
    queries = q_ref[...] * (1.0 / math.sqrt(HEAD_DIM))
    qr = (queries * cosine + _turn(queries, first) * sine).astype(jnp.bfloat16)
    keys = k_ref[...]
    kr = (keys * cosine + _turn(keys, first) * sine).astype(jnp.bfloat16)
    vr = v_ref[...].astype(jnp.bfloat16)
    qr_ref[...] = qr
    kr_ref[...] = kr
    vr_ref[...] = vr
    qt_s[...] = qr.T
    vt_s[...] = vr.T
    tokens = qr.shape[0]
    rest = tokens - LONGEST
    row = lax.broadcasted_iota(jnp.int32, (LANES, tokens), 0)
    same = segc_ref[LONGEST:, :] == segr_ref[:, LONGEST:]

    def head(h, carry):
        qth = jnp.where(row // HEAD_DIM == h, qt_s[...], jnp.zeros((), jnp.bfloat16))
        rows = pl.ds(pl.multiple_of(h * HEAD_DIM, HEAD_DIM), HEAD_DIM)

        def block(start, width, key_start, key_count, mask):
            scores = nn(kr_ref[key_start : key_start + key_count, :], qth[:, start : start + width])
            if mask is not None:
                scores = jnp.where(mask, scores, masked_score)
            peak = jnp.max(scores, axis=0, keepdims=True)
            raised = jnp.exp(scores - peak)
            total = jnp.sum(raised, axis=0, keepdims=True)
            out = nn(vt_s[rows, key_start : key_start + key_count], raised.astype(jnp.bfloat16))
            ot_s[rows, start : start + width] = out / total
            lse_ref[0, pl.ds(h, 1), start : start + width] = peak + jnp.log(total)

        for start in range(0, LONGEST, 256):
            block(start, 256, 0, LONGEST, None)
        block(LONGEST, rest, LONGEST, rest, same)
        return carry

    lax.fori_loop(0, LANES // HEAD_DIM, head, 0)
    attn_ref[...] = ot_s[...].T.astype(jnp.bfloat16)


def attention_forward(project, cosine, sine, seg_col, seg_row):
    tokens = project.shape[0]
    width = project.shape[1] // 3
    groups = width // LANES
    col = lambda shift: pl.BlockSpec((tokens, LANES), lambda g, shift=shift: (0, g + shift))
    whole = lambda shape: pl.BlockSpec(shape, lambda g: (0,) * len(shape))
    flops = 4 * (LONGEST**2 + (tokens - LONGEST) ** 2) * 128 * groups * 4
    return pl.pallas_call(
        attention_forward_kernel,
        grid=(groups,),
        in_specs=[col(0), col(groups), col(2 * groups), whole((tokens, LANES)), whole((tokens, LANES)),
                  whole((tokens, 1)), whole((1, tokens))],
        out_specs=[col(0)] * 4 + [pl.BlockSpec((1, 4, tokens), lambda g: (g, 0, 0))],
        out_shape=[jax.ShapeDtypeStruct((tokens, width), jnp.bfloat16)] * 4
        + [jax.ShapeDtypeStruct((groups, 4, tokens), jnp.float32)],
        scratch_shapes=[
            pltpu.VMEM((LANES, tokens), jnp.bfloat16),
            pltpu.VMEM((LANES, tokens), jnp.bfloat16),
            pltpu.VMEM((LANES, tokens), jnp.float32),
        ],
        compiler_params=pltpu.CompilerParams(vmem_limit_bytes=48 << 20),
        cost_estimate=pl.CostEstimate(flops=flops, bytes_accessed=20 << 20, transcendentals=20 << 20),
        name="attention_forward",
    )(project, project, project, cosine, sine, seg_col, seg_row)


def attention_backward_kernel(
    qr_ref, kr_ref, vr_ref, do_ref, attn_ref, lse_ref, cos_ref, sin_ref, segc_ref, segr_ref,
    *rest_refs,
):
    dq_ref, dk_ref, dv_ref = rest_refs[:3]
    qt_s, dot_s, kt_s, delta_s, dqt_s, dk_s, dv_s = rest_refs[3:]
    tokens = qr_ref.shape[0]
    rest = tokens - LONGEST
    qt_s[...] = qr_ref[...].T
    dot_s[...] = do_ref[...].T
    kt_s[...] = kr_ref[...].T
    prod_t = (do_ref[...].astype(jnp.float32) * attn_ref[...].astype(jnp.float32)).T
    for h in range(4):
        delta_s[h : h + 1, :] = jnp.sum(prod_t[h * HEAD_DIM : (h + 1) * HEAD_DIM, :], axis=0, keepdims=True)
    dk_s[...] = jnp.zeros_like(dk_s)
    dv_s[...] = jnp.zeros_like(dv_s)
    row = lax.broadcasted_iota(jnp.int32, (LANES, tokens), 0)
    lane = lax.broadcasted_iota(jnp.int32, (tokens, LANES), 1)
    same = segc_ref[LONGEST:, :] == segr_ref[:, LONGEST:]
    zero = jnp.zeros((), jnp.bfloat16)

    def head(h, carry):
        mine_t = row // HEAD_DIM == h
        mine = lane // HEAD_DIM == h
        qth = jnp.where(mine_t, qt_s[...], zero)
        doth = jnp.where(mine_t, dot_s[...], zero)
        qh = jnp.where(mine, qr_ref[...], zero)
        doh = jnp.where(mine, do_ref[...], zero)
        rows = pl.ds(pl.multiple_of(h * HEAD_DIM, HEAD_DIM), HEAD_DIM)

        def block(start, width, key_start, key_count, mask):
            at = slice(start, start + width)
            keys = slice(key_start, key_start + key_count)
            scores = nn(kr_ref[keys, :], qth[:, at])
            if mask is not None:
                scores = jnp.where(mask, scores, masked_score)
            soft = jnp.exp(scores - lse_ref[0, pl.ds(h, 1), at])
            weight_grad = nn(vr_ref[keys, :], doth[:, at])
            score_grad = (soft * (weight_grad - delta_s[pl.ds(h, 1), at])).astype(jnp.bfloat16)
            dv_s[keys, :] += nn(soft.astype(jnp.bfloat16), doh[at, :])
            dk_s[keys, :] += nn(score_grad, qh[at, :])
            dqt_s[rows, at] = nn(kt_s[rows, keys], score_grad)

        for start in range(0, LONGEST, 256):
            block(start, 256, 0, LONGEST, None)
        block(LONGEST, rest, LONGEST, rest, same)
        return carry

    lax.fori_loop(0, LANES // HEAD_DIM, head, 0)
    first = _half_mask(cos_ref.shape)
    cosine, sine = cos_ref[...], sin_ref[...]

    def pull(values):
        return values * cosine + _turn(values * sine, first)

    dq_ref[...] = (pull(dqt_s[...].T) * (1.0 / math.sqrt(HEAD_DIM))).astype(jnp.bfloat16)
    dk_ref[...] = pull(dk_s[...]).astype(jnp.bfloat16)
    dv_ref[...] = dv_s[...].astype(jnp.bfloat16)


def attention_backward(qr, kr, vr, attn_grad, attn, lse, cosine, sine, seg_col, seg_row):
    tokens, width = qr.shape
    groups = width // LANES
    col = pl.BlockSpec((tokens, LANES), lambda g: (0, g))
    whole = lambda shape: pl.BlockSpec(shape, lambda g: (0,) * len(shape))
    flops = 10 * (LONGEST**2 + (tokens - LONGEST) ** 2) * 128 * groups * 4
    return pl.pallas_call(
        attention_backward_kernel,
        grid=(groups,),
        in_specs=[col] * 5 + [pl.BlockSpec((1, 4, tokens), lambda g: (g, 0, 0)),
                              whole((tokens, LANES)), whole((tokens, LANES)), whole((tokens, 1)), whole((1, tokens))],
        out_specs=[col] * 3,
        out_shape=[jax.ShapeDtypeStruct((tokens, width), jnp.bfloat16)] * 3,
        scratch_shapes=[
            pltpu.VMEM((LANES, tokens), jnp.bfloat16),
            pltpu.VMEM((LANES, tokens), jnp.bfloat16),
            pltpu.VMEM((LANES, tokens), jnp.bfloat16),
            pltpu.VMEM((8, tokens), jnp.float32),
            pltpu.VMEM((LANES, tokens), jnp.float32),
            pltpu.VMEM((tokens, LANES), jnp.float32),
            pltpu.VMEM((tokens, LANES), jnp.float32),
        ],
        compiler_params=pltpu.CompilerParams(vmem_limit_bytes=56 << 20),
        cost_estimate=pl.CostEstimate(flops=flops, bytes_accessed=20 << 20, transcendentals=20 << 20),
        name="attention_backward",
    )(qr, kr, vr, attn_grad, attn, lse, cosine, sine, seg_col, seg_row)


MESH = pl.DeviceIdType.MESH


def place():
    rank, plane = lax.axis_index("dp"), lax.axis_index("fsdp")
    core = rank % 2
    chip_x = (rank // 2) % 2
    chip_y = rank // 4
    return rank, plane, core, chip_x, chip_y


def chip_at(step, chip_x, chip_y):
    other_x = 1 - chip_x if step & 1 else chip_x
    other_y = 1 - chip_y if step & 2 else chip_y
    return 2 * other_y + other_x


def call(partners):
    for partner in partners:
        pl.semaphore_signal(pltpu.get_barrier_semaphore(), inc=1, device_id=partner, device_id_type=MESH)


def hear(partners):
    pl.semaphore_wait(pltpu.get_barrier_semaphore(), len(partners))


def greet(partners):
    call(partners)
    hear(partners)


def all_partners():
    rank, plane, core, chip_x, chip_y = place()
    sibling = 2 * chip_at(0, chip_x, chip_y) + 1 - core
    partners = [(sibling, plane)]
    partners += [(2 * chip_at(step, chip_x, chip_y) + core, plane) for step in (1, 2, 3)]
    partners += [(rank, (plane + step) % 4) for step in (1, 2, 3)]
    return partners


class SumStages:
    def __init__(self, parts, scratch, lanes):
        (self.own, self.from_core, self.from_first, self.middle, self.from_second, self.total, self.from_plane,
         self.send, self.recv, self.local) = scratch
        self.parts, self.lanes = parts, lanes
        self.rank, self.plane, self.core, self.chip_x, self.chip_y = place()

    def remote(self, source, target, slot, device):
        return pltpu.make_async_remote_copy(
            src_ref=source, dst_ref=target, send_sem=self.send.at[slot], recv_sem=self.recv.at[slot],
            device_id=device, device_id_type=MESH)

    def device(self, step):
        return (2 * chip_at(step, self.chip_x, self.chip_y) + self.core, self.plane)

    def add(self, left, right):
        return left.astype(jnp.float32) + right.astype(jnp.float32)

    def give_copy(self, source):
        return self.remote(source, self.from_core, 0, (2 * chip_at(0, self.chip_x, self.chip_y) + 1 - self.core, self.plane))

    def core_add(self, give):
        give.wait()
        for j in range(4):
            self.own[j] = self.add(self.own[j], self.from_core[j]).astype(self.own.dtype)

    def core_copies(self):
        load = pltpu.make_async_copy(self.parts.at[:, :, :, self.core, :, self.lanes], self.own, self.local)
        return load, self.give_copy(self.parts.at[:, :, :, 1 - self.core, :, self.lanes])

    def core_start(self):
        load, give = self.core_copies()
        give.start()
        load.start()

    def core_finish(self):
        load, give = self.core_copies()
        load.wait()
        self.core_add(give)

    def first_copies(self):
        return [
            self.remote(self.own.at[pl.ds(0, 2), :, 1 - self.chip_x], self.from_first.at[0], 1, self.device(1)),
            self.remote(self.own.at[pl.ds(2, 2), 1 - self.chip_y], self.from_first.at[1], 2, self.device(2)),
        ]

    def second_copies(self):
        return [
            self.remote(self.middle.at[0, :, 1 - self.chip_y], self.from_second.at[0], 3, self.device(2)),
            self.remote(self.middle.at[1, :, 1 - self.chip_x], self.from_second.at[1], 4, self.device(1)),
        ]

    def chip_start(self):
        for copy in self.first_copies():
            copy.start()

    def chip_turn(self):
        for copy in self.first_copies():
            copy.wait()
        for j in range(2):
            mine = self.own[j, :, pl.ds(self.chip_x, 1)][:, 0]
            self.middle[0, j] = self.add(mine, self.from_first[0, j]).astype(self.middle.dtype)
            mine = self.own[2 + j, pl.ds(self.chip_y, 1)][0]
            self.middle[1, j] = self.add(mine, self.from_first[1, j]).astype(self.middle.dtype)
        for copy in self.second_copies():
            copy.start()

    def chip_finish(self):
        for copy in self.second_copies():
            copy.wait()
        for half, index in ((0, self.chip_y), (1, self.chip_x)):
            for j in range(2):
                mine = self.middle[half, j, pl.ds(index, 1)][0]
                self.total[2 * half + j] = self.add(mine, self.from_second[half, j]).astype(self.total.dtype)

    def plane_copies(self):
        return [
            self.remote(self.total.at[(self.plane + step) % 4], self.from_plane.at[step - 1], 4 + step,
                        (self.rank, (self.plane + step) % 4))
            for step in (1, 2, 3)
        ]

    def plane_start(self):
        for copy in self.plane_copies():
            copy.start()

    def plane_finish(self):
        for copy in self.plane_copies():
            copy.wait()
        value = self.total[pl.ds(self.plane, 1)][0].astype(jnp.float32)
        for slot in range(3):
            value = value + self.from_plane[slot].astype(jnp.float32)
        return value


def sum_scratch(rows, lanes, dtype=jnp.bfloat16):
    return [
        pltpu.VMEM((4, 2, 2, rows, lanes), dtype),
        pltpu.VMEM((4, 2, 2, rows, lanes), dtype),
        pltpu.VMEM((2, 2, 2, rows, lanes), dtype),
        pltpu.VMEM((2, 2, 2, rows, lanes), dtype),
        pltpu.VMEM((2, 2, rows, lanes), dtype),
        pltpu.VMEM((4, rows, lanes), dtype),
        pltpu.VMEM((3, rows, lanes), dtype),
        pltpu.SemaphoreType.DMA((8,)),
        pltpu.SemaphoreType.DMA((8,)),
        pltpu.SemaphoreType.DMA,
    ]


SUM_SCRATCH = 10


def table_sum(table_ref, table_out, from_core, from_chip, from_plane, held, send, recv):
    rank, plane, core, chip_x, chip_y = place()
    chip = chip_at(0, chip_x, chip_y)

    def remote(source, target, slot, device):
        return pltpu.make_async_remote_copy(
            src_ref=source, dst_ref=target, send_sem=send.at[slot], recv_sem=recv.at[slot],
            device_id=device, device_id_type=MESH)

    give = remote(table_ref.at[:, 1 - core], from_core, 0, (2 * chip + 1 - core, plane))
    give.start()
    yield
    give.wait()
    held[...] = table_ref[:, pl.ds(core, 1)][:, 0] + from_core[...]
    across = [remote(held.at[chip_at(step, chip_x, chip_y)], from_chip.at[step - 1], step,
                     (2 * chip_at(step, chip_x, chip_y) + core, plane)) for step in (1, 2, 3)]
    for copy in across:
        copy.start()
    yield
    for copy in across:
        copy.wait()
    own = held[pl.ds(chip, 1)][0] + from_chip[0] + from_chip[1] + from_chip[2]
    table_out[...] = own
    along = [remote(table_out, from_plane.at[step - 1], 3 + step, (rank, (plane + step) % 4)) for step in (1, 2, 3)]
    for copy in along:
        copy.start()
    yield
    for copy in along:
        copy.wait()
    table_out[...] = own + from_plane[0] + from_plane[1] + from_plane[2]
    yield


class Gather:
    def __init__(self, at, send, recv, base, parts):
        rank, plane, core, chip_x, chip_y = place()
        every, low, high = parts
        chips = [chip_at(step, chip_x, chip_y) for step in range(4)]
        over = [2 * chip + core for chip in chips]

        def copy(chip, lanes, slot, device):
            block = at(chip, core, lanes)
            return pltpu.make_async_remote_copy(
                src_ref=block, dst_ref=block, send_sem=send.at[base + slot], recv_sem=recv.at[base + slot],
                device_id=(device, plane), device_id_type=MESH)

        self.to_x, self.to_y = copy(chips[0], every, 0, over[1]), copy(chips[0], every, 1, over[2])
        self.on_y, self.on_x = copy(chips[1], low, 2, over[2]), copy(chips[2], high, 3, over[1])
        self.beside = [copy(chip, every, 4 + step, 2 * chips[0] + 1 - core) for step, chip in enumerate(chips)]

    def first(self):
        self.to_x.start()
        self.to_y.start()
        self.beside[0].start()

    def second(self):
        self.to_x.wait_recv()
        self.on_y.start()
        self.beside[1].start()
        self.to_y.wait_recv()
        self.on_x.start()
        self.beside[2].start()

    def third(self):
        self.on_y.wait_recv()
        self.on_x.wait_recv()
        self.beside[3].start()

    def landed(self):
        for copy in self.beside:
            copy.wait_recv()

    def sent(self):
        for copy in (self.to_x, self.to_y, self.on_y, self.on_x, *self.beside):
            copy.wait_send()

    def finish(self):
        self.landed()
        self.sent()


def split(values):
    top = values.astype(jnp.bfloat16)
    return top, (values - top.astype(jnp.float32)).astype(jnp.bfloat16)


def put_left(ref, values):
    width = values.shape[1]
    top, low = split(values)
    ref[:, :width] = top
    ref[:, width : 2 * width] = top
    ref[:, 2 * width :] = low


def put_right(ref, values):
    width = values.shape[0]
    top, low = split(values)
    ref[:width, :] = top
    ref[width : 2 * width, :] = low
    ref[2 * width :, :] = top


def tiles_of(width):
    first = width % 256
    edges = ([0] if first else []) + list(range(first, width + 1, 256))
    return list(zip(edges[:-1], edges[1:]))


def symmetric_product(out, left, right, tiles):
    for start, stop in tiles:
        block = nn(left[:stop, :], right[:, start:stop])
        out[:stop, start:stop] = block
        if start:
            out[start:stop, :start] = block[:start, :].T


def orthogonal_rows(whole, mine, gram, poly, temp, rows_s, left_gram, left_temp, right, write):
    width = gram.shape[0]
    tiles = tiles_of(width)
    parts = [whole[j].reshape(width, whole.shape[-1]) for j in range(4)]
    for start, stop in tiles:
        block = sum(nt(part[:stop, :], part[start:stop, :]) for part in parts)
        gram[:stop, start:stop] = block
        if start:
            gram[start:stop, :start] = block[:start, :].T
    diagonal = lax.broadcasted_iota(jnp.int32, (width, width), 0) == lax.broadcasted_iota(jnp.int32, (width, width), 1)
    norm_sq = jnp.sum(jnp.sum(jnp.where(diagonal, gram[...], 0.0), axis=1, keepdims=True), axis=0, keepdims=True) + 1e-07
    gram[...] = gram[...] / norm_sq

    def polynomial():
        put_left(left_gram, gram[...])
        put_right(right, gram[...])
        symmetric_product(temp, left_gram, right, tiles)
        poly[...] = jnp.where(diagonal, poly_linear, 0.0) + poly_square * gram[...] + poly_cubic * temp[...]
        put_right(right, poly[...])

    def next_gram():
        symmetric_product(temp, left_gram, right, tiles)
        put_left(left_temp, temp[...])
        symmetric_product(gram, left_temp, right, tiles)

    def thin(values):
        count = values.shape[0]
        top, low = split(values)
        both = nn(jnp.concatenate([top, low], axis=0), right[:width, :])
        return both[:count, :] + both[count:, :] + nn(top, right[width : 2 * width, :])

    polynomial()
    rows_s[...] = poly[mine, :]

    def iteration(step, carry):
        next_gram()
        polynomial()
        rows_s[...] = thin(rows_s[...])
        return carry

    lax.fori_loop(0, NS_ITERS - 2, iteration, 0)
    next_gram()
    put_right(right, gram[...])
    rows = rows_s[...]
    once = thin(rows)
    twice = thin(once)
    rows = (poly_linear * rows + poly_square * once + poly_cubic * twice) * lax.rsqrt(norm_sq)
    top, low = split(rows)
    for j, part in enumerate(parts):
        write(j, nn(top, part) + nn(low, part))


class PlaneStage:
    def __init__(self, total, from_plane, send, recv):
        rank, self.plane = place()[:2]
        self.total, self.from_plane = total, from_plane
        self.copies = [
            pltpu.make_async_remote_copy(
                src_ref=total.at[(self.plane + step) % 4], dst_ref=from_plane.at[step - 1],
                send_sem=send.at[step - 1], recv_sem=recv.at[step - 1],
                device_id=(rank, (self.plane + step) % 4), device_id_type=MESH)
            for step in (1, 2, 3)
        ]

    def start(self):
        for copy in self.copies:
            copy.start()

    def finish(self):
        for copy in self.copies:
            copy.wait()
        value = self.total[pl.ds(self.plane, 1)][0].astype(jnp.float32)
        for slot in range(3):
            value = value + self.from_plane[slot].astype(jnp.float32)
        return value


MATRIX_OF = (2, 0, 1, 3)
LANES_OF = (640, 512, 256, 640)
FIRST, LAST = (0, 3), (1, 2)
CUTS_A = ((0, 256), (256, 384))


def tail_kernel(
    sums_ref, table_ref, own_up_ref, total_b_ref, len_ref, *refs,
):
    moments, weights, small, large = refs[0:4], refs[4:8], refs[8:11], refs[11:19]
    refs = refs[19:]
    new_moments, new_weights, new_small, input_grad_hbm = refs[0:4], refs[4:8], refs[8:11], refs[11]
    table_out, pieces = refs[12:14]
    refs = refs[14:]
    early, late = (SumStages(None, refs[SUM_SCRATCH * n : SUM_SCRATCH * (n + 1)], None) for n in range(2))
    refs = refs[2 * SUM_SCRATCH :]
    table_scratch, refs = refs[:6], refs[6:]
    blocks, whole, gram, poly, temp, rows_s, left_gram, left_temp, right, from_plane_b = refs[:10]
    plane_send, plane_recv, gather_send, gather_recv, back_send, back_recv, b_send, b_recv, loads = refs[10:19]
    gives_s, (tiles_s, h1t_s, turned_s, stored), held = refs[19:21], refs[21:25], refs[25:]
    h1_ref, dq_ref, dk_ref, dv_ref, out_grad_ref, wt_s, after_s, x_s = held
    rank, plane, core, chip_x, chip_y = place()
    chip = chip_at(0, chip_x, chip_y)
    columns, lanes = blocks.shape[1:]
    tokens, width = h1_ref.shape
    rows_qkv, rows_out = moments[0].shape[1], moments[1].shape[0]
    last_b = PlaneStage(total_b_ref, from_plane_b, b_send, b_recv)
    loading = [pltpu.make_async_copy(source, target, loads.at[n]) for n, (source, target) in enumerate(zip(large, held))]
    for copy in loading:
        copy.start()

    @pl.when((plane == LAST[0]) | (plane == LAST[1]))
    def _():
        whole[...] = jnp.zeros_like(whole)

    call(all_partners())
    loading[0].wait()
    h1t_s[...] = h1_ref[...].T
    hear(all_partners())
    last_b.start()
    for copy in loading[1:5]:
        copy.wait()

    def half(which, targets):
        starts = [pl.multiple_of(columns * (2 * m + which), 16) for m in range(4)]
        left = jnp.concatenate([h1t_s[pl.ds(start, columns), :] for start in starts], axis=0)
        qkv = jnp.concatenate([nn(left, ref[...]).astype(jnp.bfloat16) for ref in (dq_ref, dk_ref, dv_ref)], axis=1)
        out = jnp.concatenate([out_grad_ref[pl.ds(start, columns), :] for start in starts], axis=0)
        for j in range(4):
            both = jnp.concatenate(
                [qkv[:, j * rows_qkv : (j + 1) * rows_qkv], out[:, j * rows_out : (j + 1) * rows_out]], axis=1)
            for target, (start, size) in zip(targets, CUTS_A):
                target[j] = both[:, start : start + size].reshape(2, 2, columns, size)

    half(1 - core, gives_s)
    gives = [stages.give_copy(source) for stages, source in zip((early, late), gives_s)]
    for give in gives:
        give.start()
    half(core, (early.own, late.own))
    early.core_add(gives[0])
    early.chip_start()
    late.core_add(gives[1])

    def momentum(x, gradient):
        rows = gradient.shape[1]
        slot = MATRIX_OF.index(x)
        if x == 1:
            new = moment_keep * moments[x][...].T + gradient
            new_moments[x][...] = new.T
        else:
            new = moment_keep * moments[x][...] + gradient
            new_moments[x][...] = new
        blocks[slot, :, :rows] = new.astype(jnp.bfloat16)
        if rows < lanes:
            blocks[slot, :, rows:] = jnp.zeros((columns, lanes - rows), jnp.bfloat16)

    def out_copy(step, target):
        part = pl.ds(0, LANES_OF[target])
        return pltpu.make_async_remote_copy(
            src_ref=blocks.at[target, :, part], dst_ref=whole.at[plane, chip, core, :, part],
            send_sem=plane_send.at[step - 1], recv_sem=plane_recv.at[step - 1],
            device_id=(rank, (plane + step) % 4), device_id_type=MESH)

    def when_target(targets, act):
        for step in (1, 2, 3):
            for target in targets:
                @pl.when((plane + step) % 4 == target)
                def _():
                    act(out_copy(step, target))

    def place_own(target):
        part = LANES_OF[target]
        whole[target, pl.ds(chip, 1), pl.ds(core, 1), :, :part] = blocks[target, :, :part][None, None]

    def gathers_of(target):
        filled = LANES_OF[target]
        low = (filled // LANES + 1) // 2 * LANES
        parts = pl.ds(0, filled), pl.ds(0, low), pl.ds(low, filled - low)
        ranges = [(target, 1), (0, target), (target + 1, 3 - target)]
        return [
            Gather(lambda m, c, part, cut=pl.ds(*cut): whole.at[cut, m, c, :, part], gather_send, gather_recv, 8 * n, parts)
            for n, cut in enumerate(ranges) if cut[1]
        ]

    def arrived(target):
        for step in (1, 2, 3):
            out_copy(step, target).wait_recv()

    for copy in loading[5:]:
        copy.wait()
    ends, offset = row_marks(len_ref)
    gain = table_ref[0:1, :]
    gain_sum = jnp.zeros((1, width), jnp.float32)
    shift_sum = jnp.zeros((1, width), jnp.float32)
    for r in range(0, tokens, 256):
        at = slice(r, r + 256)
        grad = sum(nt(ref[at, :], wt_s[:, part * width : (part + 1) * width])
                   for part, ref in enumerate((dq_ref, dk_ref, dv_ref)))
        values = x_s[at, :].astype(jnp.float32)
        center = values - jnp.mean(values, axis=-1, keepdims=True)
        rstd = lax.rsqrt(jnp.mean(center * center, axis=-1, keepdims=True) + norm_eps)
        xhat = center * rstd
        gain_sum += jnp.sum(grad * xhat, axis=0, keepdims=True)
        shift_sum += jnp.sum(grad, axis=0, keepdims=True)
        scaled = grad * gain
        after_s[at, :] += rstd * (scaled - jnp.mean(scaled, axis=-1, keepdims=True)
                                  - xhat * jnp.mean(scaled * xhat, axis=-1, keepdims=True))
        if r == 0:
            early.chip_turn()
            late.chip_start()
        if r == 512:
            early.chip_finish()
            early.plane_start()
        if r == 256:
            momentum(2, own_up_ref[...])
            momentum(3, last_b.finish())
            when_target(FIRST, lambda copy: copy.start())
    vector = jnp.concatenate(
        [gain_sum, shift_sum, sums_ref[2:4, :]]
        + [jnp.sum(ref[...].astype(jnp.float32), axis=0, keepdims=True) for ref in (dq_ref, dk_ref, dv_ref)]
        + [sums_ref[7:16, :]], axis=0)
    for block in range(8):
        part = vector[:, block * columns : (block + 1) * columns]
        tiles_s[block // 2, block % 2] = jnp.concatenate(
            [part, jnp.zeros((16, LANES - columns), jnp.float32)], axis=1)
    adding = table_sum(tiles_s, table_out, *table_scratch)
    late.chip_turn()
    next(adding)
    turned_s[...] = pltpu.roll(after_s[...], offset, 0)
    storing = pltpu.make_async_copy(turned_s, input_grad_hbm, stored)
    storing.start()
    late.chip_finish()
    late.plane_start()
    next(adding)
    for target in FIRST:
        @pl.when(plane == target)
        def _():
            place_own(target)
            own, *others = gathers_of(target)
            own.first()
            arrived(target)
            for gather in others:
                gather.first()
    next(adding)
    gradient = jnp.concatenate([early.plane_finish(), late.plane_finish()], axis=1)
    momentum(0, gradient[:, :rows_qkv])
    momentum(1, gradient[:, rows_qkv : rows_qkv + rows_out])
    when_target(LAST, lambda copy: copy.start())
    for target in FIRST:
        @pl.when(plane == target)
        def _():
            gathers = gathers_of(target)
            for gather in gathers:
                gather.second()
            for gather in gathers:
                gather.third()
            for gather in gathers:
                gather.landed()
    next(adding)
    first_fix = 1.0 - beta_first**STEP
    second_fix = 1.0 - beta_second**STEP
    n_vec = small[0].shape[0]
    vector_grad = table_out[:n_vec, :columns]
    vectors, vec_first, vec_second = (ref[...] for ref in small)
    new_first = beta_first * vec_first + (1.0 - beta_first) * vector_grad
    new_second = beta_second * vec_second + (1.0 - beta_second) * vector_grad * vector_grad
    new_small[0][...] = vectors - adam_rate * (new_first / first_fix) / (jnp.sqrt(new_second / second_fix) + adam_eps)
    new_small[1][...] = new_first
    new_small[2][...] = new_second
    for target in LAST:
        @pl.when(plane == target)
        def _():
            place_own(target)
            own, *others = gathers_of(target)
            own.first()
            arrived(target)
            for gather in others:
                gather.first()
            for gather in (own, *others):
                gather.second()
            for gather in (own, *others):
                gather.third()
            for gather in (own, *others):
                gather.landed()
    when_target((0, 1, 2, 3), lambda copy: copy.wait_send())

    def write(j, values):
        blocks[j] = values.astype(jnp.bfloat16)

    orthogonal_rows(whole, pl.ds(pl.multiple_of(rank * columns, 8), columns), gram, poly, temp, rows_s,
                    left_gram, left_temp, right, write)

    def home_copy(step, source):
        part = pl.ds(0, LANES_OF[source])
        return pltpu.make_async_remote_copy(
            src_ref=blocks.at[(plane + step) % 4, :, part], dst_ref=pieces.at[source, :, part],
            send_sem=back_send.at[step - 1], recv_sem=back_recv.at[step - 1],
            device_id=(rank, (plane + step) % 4), device_id_type=MESH)

    for source in range(4):
        @pl.when(plane == source)
        def _():
            for step in (1, 2, 3):
                home_copy(step, source).start()
            pieces[source] = blocks[source]

    def update(x):
        rows = moments[x].shape[0 if x == 1 else 1]
        scale = muon_rate * math.sqrt(max(1.0, rows * 4 / width))
        change = pieces[MATRIX_OF.index(x), :, :rows].astype(jnp.float32)
        new_weights[x][...] = (weights[x][...] * (1.0 - muon_rate * muon_decay)
                               - scale * (change.T if x == 1 else change))

    for source in (*FIRST, *reversed(LAST)):
        for step in (1, 2, 3):
            @pl.when((plane + 4 - source) % 4 == step)
            def _():
                home_copy(step, source).wait_recv()
        update(MATRIX_OF[source])
    for source in range(4):
        @pl.when(plane == source)
        def _():
            for step in (1, 2, 3):
                home_copy(step, source).wait_send()
            for gather in gathers_of(source):
                gather.sent()
    storing.wait()


def tail(h1, dq, dk, dv, out_grad, sums, table, own_up, total_b, lengths, moments, weights, small, wt_qkv, after_grad, x):
    tokens, width = h1.shape
    rows = width // 8
    large = (h1, dq, dk, dv, out_grad, wt_qkv, after_grad, x)
    vmem = pl.BlockSpec(memory_space=pltpu.VMEM)
    hbm = pl.BlockSpec(memory_space=pl.ANY)
    tile = (16, LANES)
    most = max(moments[n].shape[1] for n in (0, 2, 3))
    shape = jax.ShapeDtypeStruct
    f32, bf16 = jnp.float32, jnp.bfloat16
    square = pltpu.VMEM((width, width), f32)
    sems = lambda n: pltpu.SemaphoreType.DMA((n,))
    lanes_b = total_b.shape[-1]
    return pl.pallas_call(
        tail_kernel,
        in_specs=[vmem] * 4 + [pl.BlockSpec(memory_space=pltpu.SMEM)] + [vmem] * 11 + [hbm] * 8,
        out_specs=[vmem] * 11 + [hbm],
        out_shape=[shape(v.shape, f32) for v in (*moments, *weights, *small)] + [shape((tokens, width), f32)],
        scratch_shapes=[pltpu.VMEM(tile, f32), pltpu.VMEM((4, rows, most), bf16)]
        + [scratch for _, size in CUTS_A for scratch in sum_scratch(rows, size)]
        + [pltpu.VMEM((4, *tile), f32), pltpu.VMEM((3, *tile), f32),
           pltpu.VMEM((3, *tile), f32), pltpu.VMEM((4, *tile), f32), sems(7), sems(7)]
        + [pltpu.VMEM((4, rows, most), bf16), pltpu.VMEM((4, 4, 2, rows, most), bf16),
           square, square, square, pltpu.VMEM((rows, width), f32),
           pltpu.VMEM((width, 3 * width), bf16), pltpu.VMEM((width, 3 * width), bf16),
           pltpu.VMEM((3 * width, width), bf16), pltpu.VMEM((3, rows, lanes_b), bf16)]
        + [sems(3), sems(3), sems(24), sems(24), sems(3), sems(3), sems(3), sems(3), sems(8)]
        + [pltpu.VMEM((4, 2, 2, rows, size), bf16) for _, size in CUTS_A]
        + [pltpu.VMEM((4, 2, *tile), f32), pltpu.VMEM((width, tokens), bf16),
           pltpu.VMEM((tokens, width), f32), pltpu.SemaphoreType.DMA]
        + [pltpu.VMEM(v.shape, v.dtype) for v in large],
        compiler_params=pltpu.CompilerParams(collective_id=1, has_side_effects=True, vmem_limit_bytes=60 << 20),
        name="tail",
    )(sums, table, own_up, total_b, lengths, *moments, *weights, *small, *large)


def finish_kernel(*refs):
    count = len(refs) // 3
    sources, targets, held, loads, stores = refs[:count], refs[count : 2 * count], refs[2 * count : -2], refs[-2], refs[-1]
    loading, storing = [], []
    for n in sorted(range(count), key=lambda n: -sources[n].shape[0]):
        rows = sources[n].shape[0]
        parts = 8 if rows >= ROW_LEN else 1
        for p in range(parts):
            at = pl.ds(p * (rows // parts), rows // parts)
            slot = len(loading)
            loading.append(pltpu.make_async_copy(sources[n].at[at], held[n].at[at], loads.at[slot]))
            storing.append(pltpu.make_async_copy(held[n].at[at], targets[n].at[at], stores.at[slot]))
    for copy in loading:
        copy.start()
    for load, store in zip(loading, storing):
        load.wait()
        store.start()
    for copy in storing:
        copy.wait()


def finish(values):
    hbm = pl.BlockSpec(memory_space=pl.ANY)
    count = len(values)
    copies = sum(8 if x.shape[0] >= ROW_LEN else 1 for x in values)
    return pl.pallas_call(
        finish_kernel,
        in_specs=[hbm] * count,
        out_specs=[hbm] * count,
        out_shape=[jax.ShapeDtypeStruct(x.shape, x.dtype) for x in values],
        scratch_shapes=[pltpu.VMEM(x.shape, x.dtype) for x in values]
        + [pltpu.SemaphoreType.DMA((copies,)), pltpu.SemaphoreType.DMA((copies,))],
        compiler_params=pltpu.CompilerParams(vmem_limit_bytes=62 << 20),
        name="finish",
    )(*values)


def lane_parts(start, size):
    half = size // 2
    return pl.ds(start, size), pl.ds(start, half), pl.ds(start + half, half)


ROW_LEN = 1024
GATHERED = 512
CHUNK_A = 256
OUT_LANES = 256
CUTS_B = ((0, 512), (512, 768))


def row_marks(len_ref):
    ends = [len_ref[0, 0]]
    for slot in (1, 2):
        ends.append(ends[-1] + len_ref[0, slot])
    starts = [0, *ends]
    offset = starts[3]
    for slot in (2, 1, 0):
        offset = jnp.where(len_ref[0, slot] == LONGEST, starts[slot], offset)
    return ends, offset


def segment_of(index, ends, offset):
    where = index + offset
    where = jnp.where(where >= ROW_LEN, where - ROW_LEN, where)
    segment = sum((where >= end).astype(jnp.int32) for end in ends)
    return where, segment


def turned_rows(values, offset):
    return pltpu.roll(values.astype(jnp.float32), jnp.where(offset > 0, ROW_LEN - offset, 0), 0)


def same_rest(ends, offset):
    rest = ROW_LEN - LONGEST
    columns = lax.broadcasted_iota(jnp.int32, (rest, rest), 0) + LONGEST
    rows = lax.broadcasted_iota(jnp.int32, (rest, rest), 1) + LONGEST
    return segment_of(columns, ends, offset)[1] == segment_of(rows, ends, offset)[1]


def attention_jobs(tokens):
    blocks = [(start, 256, 0, LONGEST) for start in range(0, LONGEST, 256)] + [(LONGEST, tokens - LONGEST, LONGEST, tokens - LONGEST)]
    return [(h, *block) for h in range(LANES // HEAD_DIM) for block in blocks]


def attention_group(q, k_ref, v, same, ot_s, vt_s, lse_ref):
    tokens = q.shape[0]
    qt = q.T
    vt_s[...] = v.T
    row = lax.broadcasted_iota(jnp.int32, qt.shape, 0)
    jobs = attention_jobs(tokens)
    queries, scores, soft = {}, {}, {}

    def score(job):
        h, start, width, key_start, key_count = job
        if h not in queries:
            queries[h] = jnp.where(row // HEAD_DIM == h, qt, jnp.zeros((), jnp.bfloat16))
        out = nn(k_ref[key_start : key_start + key_count, :], queries[h][:, start : start + width])
        return jnp.where(same, out, masked_score) if start == LONGEST else out

    def soften(values):
        peak = jnp.max(values, axis=0, keepdims=True)
        raised = jnp.exp(values - peak)
        return raised.astype(jnp.bfloat16), peak, jnp.sum(raised, axis=0, keepdims=True)

    def collect(job, raised, peak, total):
        h, start, width, key_start, key_count = job
        rows = slice(h * HEAD_DIM, (h + 1) * HEAD_DIM)
        out = nn(vt_s[rows, key_start : key_start + key_count], raised)
        ot_s[rows, start : start + width] = out / total
        lse_ref[0, h : h + 1, start : start + width] = peak + jnp.log(total)

    count = len(jobs)
    for t in range(count + 2):
        if t < count:
            scores[t] = score(jobs[t])
        if 0 <= t - 1 < count:
            soft[t - 1] = soften(scores.pop(t - 1))
        if 0 <= t - 2:
            collect(jobs[t - 2], *soft.pop(t - 2))
    return ot_s[...].T.astype(jnp.bfloat16)


def head_kernel(
    len_ref, count_ref, tokens_ref, w_qkv_ref, w_up_ref, w_down_ref, w_out_ref, vectors_ref, cot_hbm,
    qr_ref, kr_ref, vr_ref, attn_ref, lse_ref, h1_hbm, x_hbm, cos_hbm, sin_hbm, wt_hbm, table_ref, full_b, full_o,
    incoming_hbm, dy_hbm, dyt_hbm, incoming_s, dy_s, dyt_s, cot_s,
    h1_ref, x_ref, cos_ref, sin_ref, wt_ref, stores, full_a, full_v, twice_s, q_s, k_s, v_s, ot_s, vt_s, slab_a, slab_b, slab_o,
    a_send, a_recv, az_send, az_recv, b_send, b_recv, bz_send, bz_recv, v_send, v_recv, local,
):
    group = pl.program_id(0)
    rank, plane, core, chip_x, chip_y = place()
    chip = chip_at(0, chip_x, chip_y)
    columns = slab_a.shape[0]
    chunks_a = GATHERED // CHUNK_A
    gather_a = [Gather(lambda m, c, lane: full_a.at[:, m, c, :, lane], a_send, a_recv, 8 * n,
                       lane_parts(CHUNK_A * n, CHUNK_A))
                for n in range(chunks_a)]
    gather_o = Gather(lambda m, c, lane: full_o.at[:, m, c, :, lane], b_send, b_recv, 0, lane_parts(0, OUT_LANES))
    gather_b = [Gather(lambda m, c, lane: full_b.at[pl.ds(0, 2), m, c, :, lane], b_send, b_recv, 8 + 8 * n,
                       lane_parts(*cut))
                for n, cut in enumerate(CUTS_B)]

    def along(slab, full, send, recv, n, start, size):
        lanes = pl.ds(start, size)
        return [
            pltpu.make_async_remote_copy(
                src_ref=slab.at[:, lanes], dst_ref=full.at[plane, chip, core, :, lanes],
                send_sem=send.at[3 * n + step - 1], recv_sem=recv.at[3 * n + step - 1],
                device_id=(rank, (plane + step) % 4), device_id_type=MESH)
            for step in (1, 2, 3)
        ]

    along_a = [along(slab_a, full_a, az_send, az_recv, n, CHUNK_A * n, CHUNK_A) for n in range(chunks_a)]
    along_o = along(slab_o, full_o, bz_send, bz_recv, 0, 0, OUT_LANES)
    along_b = [along(slab_b, full_b, bz_send, bz_recv, 1 + n, *cut) for n, cut in enumerate(CUTS_B)]
    own_b = [pltpu.make_async_copy(slab_b, full_b.at[plane, chip, core], local.at[0]),
             pltpu.make_async_copy(slab_o, full_o.at[plane, chip, core], local.at[1])]
    storing = [pltpu.make_async_copy(source, target, stores.at[n]) for n, (source, target) in enumerate(
        ((h1_ref, h1_hbm), (x_ref, x_hbm), (cos_ref, cos_hbm), (sin_ref, sin_hbm), (wt_ref, wt_hbm),
         (incoming_s, incoming_hbm), (dy_s, dy_hbm), (dyt_s, dyt_hbm)))]
    load_cot = pltpu.make_async_copy(cot_hbm, cot_s, local.at[2])
    ends, offset = row_marks(len_ref)

    def widen(values, lanes):
        return jnp.concatenate([values, jnp.zeros((values.shape[0], lanes - values.shape[1]), values.dtype)], axis=1)

    @pl.when(group == 0)
    def _():
        call(all_partners())
        load_cot.start()
        slab_a[...] = widen(w_qkv_ref[...].astype(jnp.bfloat16), GATHERED)
        n_vec, width = vectors_ref.shape[0], tokens_ref.shape[1]
        vectors = jnp.concatenate([vectors_ref[...], jnp.zeros((LANES - n_vec, columns), jnp.float32)], axis=0)
        vectors = vectors.astype(jnp.bfloat16).astype(jnp.float32)
        full_v[pl.ds(chip, 1), pl.ds(core, 1)] = widen(vectors, LANES).T[:columns, :][None, None]
        full_a[pl.ds(plane, 1), pl.ds(chip, 1), pl.ds(core, 1)] = slab_a[...][None, None, None]
        hear(all_partners())
        for copy in along_a[0]:
            copy.start()
        slab_b[:, :width] = w_up_ref[...].astype(jnp.bfloat16)
        slab_b[:, width:] = w_down_ref[...].astype(jnp.bfloat16)
        slab_o[...] = widen(w_out_ref[...].T.astype(jnp.bfloat16), OUT_LANES)
        for copy in own_b:
            copy.start()

        def vec_copy(m, slot, device):
            block = full_v.at[m, core]
            return pltpu.make_async_remote_copy(
                src_ref=block, dst_ref=block, send_sem=v_send.at[slot], recv_sem=v_recv.at[slot],
                device_id=(device, plane), device_id_type=MESH)

        chips = [chip_at(step, chip_x, chip_y) for step in range(4)]
        vec_over = [vec_copy(chip, step - 1, 2 * chips[step] + core) for step in (1, 2, 3)]
        vec_beside = [vec_copy(m, 3 + step, 2 * chip + 1 - core) for step, m in enumerate(chips)]
        for copy in (*vec_over, vec_beside[0]):
            copy.start()
        twice_s[...] = turned_rows(tokens_ref[...], offset)
        for copy in along_a[0]:
            copy.wait()
        for copy in along_a[1]:
            copy.start()
        gather_a[0].first()
        index = lax.broadcasted_iota(jnp.int32, (ROW_LEN, LANES), 0)
        where, segment = segment_of(index, ends, offset)
        start = jnp.where(segment == 0, 0, jnp.where(segment == 1, ends[0], jnp.where(segment == 2, ends[1], ends[2])))
        position = (where - start).astype(jnp.float32)
        lane = lax.broadcasted_iota(jnp.int32, (1, LANES), 1)
        inverse = jnp.exp((lane % (HEAD_DIM // 2)).astype(jnp.float32) * (-2.0 * math.log(10000.0) / HEAD_DIM))
        sign = jnp.where((lane % HEAD_DIM) < (HEAD_DIM // 2), -1.0, 1.0)
        angles = position * inverse
        for copy in along_a[1]:
            copy.wait()
        gather_a[1].first()
        for copies in (along_o, *along_b):
            for copy in copies:
                copy.start()
        cos_ref[...] = jnp.cos(angles)
        for step in range(3):
            vec_over[step].wait()
            vec_beside[step + 1].start()
        gather_a[0].second()
        sin_ref[...] = jnp.sin(angles) * sign
        for copy in vec_beside:
            copy.wait()
        table_t = jnp.concatenate([full_v[m, c] for m in range(4) for c in range(2)], axis=0)
        table_ref[...] = table_t.T[: table_ref.shape[0], :]
        gather_a[1].second()
        load_cot.wait()
        _, segment = segment_of(lax.broadcasted_iota(jnp.int32, (ROW_LEN, 1), 0), ends, offset)
        number = jnp.where(segment == 0, count_ref[0, 0], jnp.where(
            segment == 1, count_ref[0, 1], jnp.where(segment == 2, count_ref[0, 2], count_ref[0, 3])))
        incoming_s[...] = turned_rows(cot_s[...], offset) * (1.0 / number.astype(jnp.float32))
        dy_s[...] = incoming_s[...].astype(jnp.bfloat16)
        dyt_s[...] = dy_s[...].T
        gather_a[0].third()
        gather_a[1].third()
        gain, shift = table_ref[0:1, :], table_ref[1:2, :]
        for r in range(0, ROW_LEN, 256):
            values = twice_s[r : r + 256, :]
            x_ref[r : r + 256, :] = values.astype(jnp.bfloat16)
            h1_ref[r : r + 256, :] = layer_norm(values, gain, shift).astype(jnp.bfloat16)
        for gather in gather_a:
            gather.finish()
        for copy in (*own_b, *along_o):
            copy.wait()
        gather_o.first()
        rows = wt_ref.shape[1] // 4
        wt_ref[...] = jnp.concatenate(
            [full_a[j].reshape(width, GATHERED)[:, :rows] for j in range(4)], axis=1)
        first = _half_mask((256, LANES))
        bias = [table_ref[4 + part : 5 + part, :] for part in range(3)]
        for r in range(0, ROW_LEN, 256):
            at = slice(r, r + 256)
            project = nn(h1_ref[at, :], wt_ref[...])
            cosine, sine = cos_ref[at, :], sin_ref[at, :]
            for g in range(width // LANES):
                lanes = slice(g * LANES, (g + 1) * LANES)
                queries = (project[:, lanes] + bias[0][:, lanes]) * (1.0 / math.sqrt(HEAD_DIM))
                keys = project[:, width + g * LANES : width + (g + 1) * LANES] + bias[1][:, lanes]
                q_s[g, at, :] = (queries * cosine + _turn(queries, first) * sine).astype(jnp.bfloat16)
                k_s[g, at, :] = (keys * cosine + _turn(keys, first) * sine).astype(jnp.bfloat16)
                v_s[g, at, :] = (project[:, 2 * width + g * LANES : 2 * width + (g + 1) * LANES]
                                 + bias[2][:, lanes]).astype(jnp.bfloat16)
        for copy in storing:
            copy.start()
        for copy in along_b[0]:
            copy.wait()
        gather_b[0].first()
        gather_o.second()

    @pl.when(group == 1)
    def _():
        for copy in along_b[1]:
            copy.wait()
        gather_b[1].first()
        gather_o.third()

    @pl.when(group == 2)
    def _():
        gather_b[0].second()

    @pl.when(group == 4)
    def _():
        gather_b[1].second()
        gather_b[0].third()

    qr_ref[...] = q_s[group]
    kr_ref[...] = k_s[group]
    vr_ref[...] = v_s[group]
    attn_ref[...] = attention_group(q_s[group], kr_ref, v_s[group], same_rest(ends, offset), ot_s, vt_s, lse_ref)

    @pl.when(group == 4)
    def _():
        gather_b[1].third()
        for gather in (gather_o, *gather_b):
            gather.finish()
        for copy in storing:
            copy.wait()


def head(lengths, counts, tokens, cotangent, w_qkv_t, w_up_t, w_down_t, w_out, vectors):
    tokens_count, width = tokens.shape
    groups = width // LANES
    columns = w_qkv_t.shape[0]
    col = pl.BlockSpec((tokens_count, LANES), lambda g: (0, g))
    whole = lambda *shape: pl.BlockSpec(shape, lambda g: (0,) * len(shape))
    shape = jax.ShapeDtypeStruct
    bf16, f32 = jnp.bfloat16, jnp.float32
    sems = lambda n: pltpu.SemaphoreType.DMA((n,))
    na, nb = GATHERED // CHUNK_A, 1 + len(CUTS_B)
    return pl.pallas_call(
        head_kernel,
        grid=(groups,),
        in_specs=[pl.BlockSpec(memory_space=pltpu.SMEM)] * 2 + [whole(tokens_count, width), whole(*w_qkv_t.shape),
                  whole(columns, width), whole(columns, width), whole(*w_out.shape), whole(*vectors.shape),
                  pl.BlockSpec(memory_space=pl.ANY)],
        out_specs=[col] * 4 + [pl.BlockSpec((1, 4, tokens_count), lambda g: (g, 0, 0)),
                               *[pl.BlockSpec(memory_space=pl.ANY)] * 5, whole(16, width),
                               *[pl.BlockSpec(memory_space=pl.ANY)] * 5],
        out_shape=[shape((tokens_count, width), bf16)] * 4 + [shape((groups, 4, tokens_count), f32)]
        + [shape((tokens_count, width), bf16)] * 2 + [shape((tokens_count, LANES), f32)] * 2
        + [shape((width, 3 * width), bf16), shape((16, width), f32), shape((4, 4, 2, columns, 2 * width), bf16),
           shape((4, 4, 2, columns, OUT_LANES), bf16),
           shape((tokens_count, width), f32), shape((tokens_count, width), bf16), shape((width, tokens_count), bf16)],
        scratch_shapes=[
            pltpu.VMEM((tokens_count, width), f32),
            pltpu.VMEM((tokens_count, width), bf16),
            pltpu.VMEM((width, tokens_count), bf16),
            pltpu.VMEM((tokens_count, width), bf16),
            pltpu.VMEM((tokens_count, width), bf16),
            pltpu.VMEM((tokens_count, width), bf16),
            pltpu.VMEM((tokens_count, LANES), f32),
            pltpu.VMEM((tokens_count, LANES), f32),
            pltpu.VMEM((width, 3 * width), bf16),
            sems(8),
            pltpu.VMEM((4, 4, 2, columns, GATHERED), bf16),
            pltpu.VMEM((4, 2, columns, LANES), f32),
            pltpu.VMEM((tokens_count, width), f32),
            pltpu.VMEM((groups, tokens_count, LANES), bf16),
            pltpu.VMEM((groups, tokens_count, LANES), bf16),
            pltpu.VMEM((groups, tokens_count, LANES), bf16),
            pltpu.VMEM((LANES, tokens_count), f32),
            pltpu.VMEM((LANES, tokens_count), bf16),
            pltpu.VMEM((columns, GATHERED), bf16),
            pltpu.VMEM((columns, 2 * width), bf16),
            pltpu.VMEM((columns, OUT_LANES), bf16),
            sems(8 * na), sems(8 * na), sems(3 * na), sems(3 * na),
            sems(8 * nb), sems(8 * nb), sems(3 * nb), sems(3 * nb), sems(7), sems(7), sems(3),
        ],
        compiler_params=pltpu.CompilerParams(collective_id=2, has_side_effects=True, vmem_limit_bytes=58 << 20),
        name="head",
    )(lengths, counts, tokens, w_qkv_t, w_up_t, w_down_t, w_out, vectors, cotangent)


def middle_kernel(
    len_ref, table_ref, x_hbm, attn_hbm, incoming_hbm, dy_hbm, dyt_hbm, full_o_hbm, full_b,
    out_grad_ref, sums_ref, layer_hbm, after_hbm, attn_grad_hbm, parts_hbm,
    x_ref, attn_ref, cot_ref, full_o_ref, after_grad_ref, parts_s, stores,
    xhat_s, rstd_s, h2_s, h2t_s, dy_s, dyt_s, acc_s, back_s, act_s, pre_s, wt_out_s, w_s, send, recv, local,
):
    step = pl.program_id(0)
    tokens, width = x_ref.shape
    rank, plane, core, chip_x, chip_y = place()
    chip = chip_at(0, chip_x, chip_y)
    late = Gather(lambda m, c, lane: w_s.at[1, :, m, c, :, lane], send, recv, 0, lane_parts(0, 2 * width))
    loads = [pltpu.make_async_copy(full_b.at[pl.ds(2, 2), chip, core], w_s.at[1, :, chip, core], local.at[0]),
             pltpu.make_async_copy(full_o_hbm, full_o_ref, local.at[1]),
             pltpu.make_async_copy(attn_hbm, attn_ref, local.at[2]),
             pltpu.make_async_copy(x_hbm, x_ref, local.at[3]),
             pltpu.make_async_copy(full_b.at[pl.ds(0, 2)], w_s.at[0], local.at[4]),
             pltpu.make_async_copy(dy_hbm, dy_s, local.at[5]),
             pltpu.make_async_copy(dyt_hbm, dyt_s, local.at[6]),
             pltpu.make_async_copy(incoming_hbm, after_grad_ref, local.at[7])]
    ends, offset = row_marks(len_ref)
    chunk = 256
    cuts = [slice(r, r + chunk) for r in range(0, tokens, chunk)]

    @pl.when(step == 0)
    def _():
        beside = ([(2 * chip + 1 - core, plane)]
                  + [(2 * chip_at(other, chip_x, chip_y) + core, plane) for other in (1, 2)])
        call(beside)
        for load in loads[:6]:
            load.start()
        loads[0].wait()
        hear(beside)
        late.first()
        for load in loads[1:4]:
            load.wait()
        rows = width // 4
        wt_out_s[...] = jnp.concatenate([full_o_ref[p].reshape(width, OUT_LANES)[:, :rows] for p in range(4)], axis=1)
        sums_ref[...] = jnp.zeros_like(sums_ref)
        gain, shift = table_ref[2:3, :], table_ref[3:4, :]
        branch = {}
        for t in range(len(cuts) + 1):
            if t < len(cuts):
                branch[t] = nn(attn_ref[cuts[t], :], wt_out_s[...])
            if t == 0:
                continue
            at = cuts[t - 1]
            after = x_ref[at, :].astype(jnp.float32) + (branch.pop(t - 1) + table_ref[7:8, :])
            acc_s[at, :] = after + table_ref[8:9, :]
            center = after - jnp.mean(after, axis=-1, keepdims=True)
            rstd = lax.rsqrt(jnp.mean(center * center, axis=-1, keepdims=True) + norm_eps)
            xhat = center * rstd
            xhat_s[at, :] = xhat
            rstd_s[at, :] = rstd
            h2_s[at, :] = (xhat * gain + shift).astype(jnp.bfloat16)
        h2t_s[...] = h2_s[...].T
        back_s[...] = jnp.zeros_like(back_s)

    @pl.when(step == 0)
    def _():
        for load in loads[6:]:
            load.start()
        for load in loads[4:6]:
            load.wait()
        sums_ref[8:9, :] = jnp.sum(dy_s[...].astype(jnp.float32), axis=0, keepdims=True)

    @pl.when(step == 1)
    def _():
        late.finish()

    def weights(lanes):
        return jnp.concatenate([w_s[step, p, :, :, :, lanes].reshape(width, width) for p in range(2)], axis=1)

    up, down = (weights(slice(part * width, (part + 1) * width)) for part in range(2))
    bias = jnp.concatenate([table_ref[pl.ds(9 + 2 * step + p, 1), :] for p in range(2)], axis=1)

    def products(at):
        return nn(h2_s[at, :], up), nn(dy_s[at, :], down)

    def pointwise(at, pre, act_grad):
        pre = pre + bias
        cdf = 0.5 * (1.0 + lax.erf(pre * (1.0 / math.sqrt(2.0))))
        slope = cdf + pre * (jnp.exp(-0.5 * pre * pre) * (1.0 / math.sqrt(2.0 * math.pi)))
        act_s[at, :] = (pre * cdf).astype(jnp.bfloat16)
        pre_s[at, :] = (act_grad * slope).astype(jnp.bfloat16)

    def collect(at):
        acc_s[at, :] += nt(act_s[at, :], down)
        back_s[at, :] += nt(pre_s[at, :], up)

    held = {}
    for t in range(len(cuts) + 1):
        if t == 2:
            @pl.when(step == 0)
            def _():
                late.second()
                for load in loads[6:]:
                    load.wait()

        if t < len(cuts):
            held[t] = products(cuts[t])
        if t >= 1:
            pointwise(cuts[t - 1], *held.pop(t - 1))
            collect(cuts[t - 1])

    @pl.when(step == 0)
    def _():
        late.third()

    @pl.when(step == 1)
    def _():
        for part in range(2):
            lanes = pl.ds(part * width, width)
            pltpu.make_async_copy(parts_s.at[:, :, lanes], parts_hbm.at[pl.ds(0, 2), :, lanes],
                                  stores.at[0 if part == 0 else 10]).wait()

    store_parts = []
    for part, (left, right) in enumerate(((h2t_s, pre_s), (dyt_s, act_s))):
        grad = nn(left[...], right[...]).astype(jnp.bfloat16)
        for p in range(2):
            parts_s[p, :, part * width : (part + 1) * width] = grad[:, p * width : (p + 1) * width]
        lanes = pl.ds(part * width, width)
        store_parts.append(pltpu.make_async_copy(
            parts_s.at[:, :, lanes], parts_hbm.at[pl.ds(2 * step, 2), :, lanes], stores.at[0 if part == 0 else 10]))
        store_parts[part].start()
    bias_sum = jnp.sum(pre_s[...].astype(jnp.float32), axis=0, keepdims=True)
    for p in range(2):
        sums_ref[pl.ds(9 + 2 * step + p, 1), :] = bias_sum[:, p * width : (p + 1) * width]

    @pl.when(step == 1)
    def _():
        x_ref[...] = pltpu.roll(acc_s[...], offset, 0).astype(jnp.bfloat16)
        storing = [pltpu.make_async_copy(x_ref, layer_hbm, stores.at[1])]
        storing[0].start()
        gain = table_ref[2:3, :]
        gain_sum = jnp.zeros((1, width), jnp.float32)
        shift_sum = jnp.zeros((1, width), jnp.float32)
        branch_sum = jnp.zeros((1, width), jnp.float32)
        for n in range(len(cuts) + 1):
            if n >= 1:
                at = cuts[n - 1]
                cot_ref[at, :] = nt(dy_s[at, :], wt_out_s[...]).astype(jnp.bfloat16)
                rows = pl.ds(at.start, chunk)
                for source, target, slot in ((after_grad_ref, after_hbm, 1), (cot_ref, attn_grad_hbm, 5)):
                    copy = pltpu.make_async_copy(source.at[rows], target.at[rows], stores.at[slot + n])
                    copy.start()
                    storing.append(copy)
            if n == len(cuts):
                break
            at = cuts[n]
            grad, xhat = back_s[at, :], xhat_s[at, :]
            gain_sum += jnp.sum(grad * xhat, axis=0, keepdims=True)
            shift_sum += jnp.sum(grad, axis=0, keepdims=True)
            scaled = grad * gain
            resid = rstd_s[at, :] * (
                scaled - jnp.mean(scaled, axis=-1, keepdims=True)
                - xhat * jnp.mean(scaled * xhat, axis=-1, keepdims=True))
            after_grad = after_grad_ref[at, :] + resid
            after_grad_ref[at, :] = after_grad
            low = after_grad.astype(jnp.bfloat16)
            dy_s[at, :] = low
            branch_sum += jnp.sum(low.astype(jnp.float32), axis=0, keepdims=True)
        sums_ref[2:3, :] = gain_sum
        sums_ref[3:4, :] = shift_sum
        sums_ref[7:8, :] = branch_sum
        h2t_s[...] = attn_ref[...].T
        out_grad_ref[...] = nn(h2t_s[...], dy_s[...]).astype(jnp.bfloat16)
        for copy in (*store_parts, *storing):
            copy.wait()


def middle(lengths, x, attn, incoming, dy, dyt, table, full_o, full_b):
    tokens, width = x.shape
    columns = full_b.shape[3]
    whole = lambda *shape: pl.BlockSpec(shape, lambda j: (0,) * len(shape))
    smem = pl.BlockSpec(memory_space=pltpu.SMEM)
    hbm = pl.BlockSpec(memory_space=pl.ANY)
    shape = jax.ShapeDtypeStruct
    bf16, f32 = jnp.bfloat16, jnp.float32
    flat = pltpu.VMEM((tokens, width), bf16)
    double = pltpu.VMEM((tokens, 2 * width), bf16)
    wide = pltpu.VMEM((tokens, width), f32)
    turned = pltpu.VMEM((width, tokens), bf16)
    sems = lambda n: pltpu.SemaphoreType.DMA((n,))
    return pl.pallas_call(
        middle_kernel,
        grid=(2,),
        in_specs=[smem, whole(16, width)] + [hbm] * 7,
        out_specs=[whole(width, width), whole(16, width)] + [hbm] * 4,
        out_shape=[shape((width, width), bf16), shape((16, width), f32),
                   shape((tokens, width), bf16), shape((tokens, width), f32), shape((tokens, width), bf16),
                   shape((4, width, 2 * width), bf16)],
        scratch_shapes=[flat, flat, flat, pltpu.VMEM(full_o.shape, bf16), wide, pltpu.VMEM((2, width, 2 * width), bf16),
                        sems(11), wide, pltpu.VMEM((tokens, 1), f32), flat, turned, flat, turned, wide, wide, double, double,
                        pltpu.VMEM((width, width), bf16), pltpu.VMEM((2, 2, 4, 2, columns, 2 * width), bf16),
                        sems(8), sems(8), sems(8)],
        compiler_params=pltpu.CompilerParams(collective_id=3, has_side_effects=True, vmem_limit_bytes=62 << 20),
        name="middle",
    )(lengths, table, x, attn, incoming, dy, dyt, full_o, full_b)


def backward_group(between, qr_ref, kr_ref, vr_ref, do_ref, attn_ref, lse_ref, same, qt_s, dot_s, kt_s, delta_s, dqt_s, dk_s, dv_s):
    tokens = qr_ref.shape[0]
    qt_s[...] = qr_ref[...].T
    dot_s[...] = do_ref[...].T
    kt_s[...] = kr_ref[...].T
    heads = (lax.broadcasted_iota(jnp.int32, (8, LANES), 0)
             == lax.broadcasted_iota(jnp.int32, (8, LANES), 1) // HEAD_DIM).astype(jnp.float32).astype(jnp.bfloat16)
    top, low = split(do_ref[...].astype(jnp.float32) * attn_ref[...].astype(jnp.float32))
    delta_s[...] = nt(heads, top) + nt(heads, low)
    dk_s[...] = jnp.zeros_like(dk_s)
    dv_s[...] = jnp.zeros_like(dv_s)
    row = lax.broadcasted_iota(jnp.int32, (LANES, tokens), 0)
    lane = lax.broadcasted_iota(jnp.int32, (tokens, LANES), 1)
    zero = jnp.zeros((), jnp.bfloat16)
    jobs = attention_jobs(tokens)
    masked, held = {}, {}

    def products(job):
        h, start, width, key_start, key_count = job
        if h not in masked:
            masked[h] = (
                jnp.where(row // HEAD_DIM == h, qt_s[...], zero), jnp.where(row // HEAD_DIM == h, dot_s[...], zero),
                jnp.where(lane // HEAD_DIM == h, qr_ref[...], zero), jnp.where(lane // HEAD_DIM == h, do_ref[...], zero))
        at, keys = slice(start, start + width), slice(key_start, key_start + key_count)
        scores = nn(kr_ref[keys, :], masked[h][0][:, at])
        if start == LONGEST:
            scores = jnp.where(same, scores, masked_score)
        return scores, nn(vr_ref[keys, :], masked[h][1][:, at])

    def finish(job, scores, weight_grad):
        h, start, width, key_start, key_count = job
        at, keys = slice(start, start + width), slice(key_start, key_start + key_count)
        rows = slice(h * HEAD_DIM, (h + 1) * HEAD_DIM)
        soft = jnp.exp(scores - lse_ref[0, h : h + 1, at])
        score_grad = (soft * (weight_grad - delta_s[h : h + 1, at])).astype(jnp.bfloat16)
        dv_s[keys, :] += nn(soft.astype(jnp.bfloat16), masked[h][3][at, :])
        dk_s[keys, :] += nn(score_grad, masked[h][2][at, :])
        dqt_s[rows, at] = nn(kt_s[rows, keys], score_grad)

    for t in range(len(jobs) + 1):
        if t == len(jobs) // 2:
            between()
        if t < len(jobs):
            held[t] = products(jobs[t])
        if t >= 1:
            finish(jobs[t - 1], *held.pop(t - 1))


def backward_kernel(
    len_ref, qr_ref, kr_ref, vr_ref, do_ref, attn_ref, lse_ref, cos_ref, sin_ref, parts_ref,
    dq_ref, dk_ref, dv_ref, own_ref, total_ref, *scratch,
):
    group = pl.program_id(0)
    lanes = parts_ref.shape[-1] // 2
    halves = [SumStages(parts_ref, scratch[7 + SUM_SCRATCH * n : 7 + SUM_SCRATCH * (n + 1)], pl.ds(n * lanes, lanes))
              for n in range(2)]
    dqt_s, dk_s, dv_s = scratch[4:7]

    @pl.when(group == 0)
    def _():
        greet(all_partners())
        halves[0].core_start()

    @pl.when(group == 1)
    def _():
        halves[1].core_finish()

    def between():
        @pl.when(group == 0)
        def _():
            halves[0].core_finish()
            halves[0].chip_start()
            halves[1].core_start()

        @pl.when(group == 1)
        def _():
            halves[1].chip_start()

        @pl.when(group == 2)
        def _():
            halves[0].chip_turn()

        @pl.when(group == 3)
        def _():
            halves[0].chip_finish()
            halves[0].plane_start()
            halves[1].chip_turn()

        @pl.when(group == 4)
        def _():
            halves[1].chip_finish()
            total_ref[...] = halves[1].total[...]

    ends, offset = row_marks(len_ref)
    backward_group(between, qr_ref, kr_ref, vr_ref, do_ref, attn_ref, lse_ref, same_rest(ends, offset), *scratch[:7])
    first = _half_mask(cos_ref.shape)
    cosine, sine = cos_ref[...], sin_ref[...]

    def pull(values):
        return values * cosine + _turn(values * sine, first)

    dq_ref[...] = (pull(dqt_s[...].T) * (1.0 / math.sqrt(HEAD_DIM))).astype(jnp.bfloat16)
    dk_ref[...] = pull(dk_s[...]).astype(jnp.bfloat16)
    dv_ref[...] = dv_s[...].astype(jnp.bfloat16)

    @pl.when(group == 4)
    def _():
        own_ref[...] = halves[0].plane_finish()


def backward(lengths, qr, kr, vr, attn_grad, attn, lse, cosine, sine, parts):
    tokens, width = qr.shape
    groups = width // LANES
    rows, lanes = parts.shape[-2:]
    col = pl.BlockSpec((tokens, LANES), lambda g: (0, g))
    whole = lambda *shape: pl.BlockSpec(shape, lambda g: (0,) * len(shape))
    shape = jax.ShapeDtypeStruct
    bf16, f32 = jnp.bfloat16, jnp.float32
    return pl.pallas_call(
        backward_kernel,
        grid=(groups,),
        in_specs=[pl.BlockSpec(memory_space=pltpu.SMEM)] + [col] * 5
        + [pl.BlockSpec((1, 4, tokens), lambda g: (g, 0, 0)), whole(tokens, LANES), whole(tokens, LANES),
           pl.BlockSpec(memory_space=pl.ANY)],
        out_specs=[col] * 3 + [whole(rows, lanes // 2), whole(4, rows, lanes // 2)],
        out_shape=[shape((tokens, width), bf16)] * 3 + [shape((rows, lanes // 2), f32), shape((4, rows, lanes // 2), bf16)],
        scratch_shapes=[pltpu.VMEM((LANES, tokens), bf16)] * 3
        + [pltpu.VMEM((8, tokens), f32), pltpu.VMEM((LANES, tokens), f32), pltpu.VMEM((tokens, LANES), f32),
           pltpu.VMEM((tokens, LANES), f32)] + sum_scratch(rows, lanes // 2) * 2,
        compiler_params=pltpu.CompilerParams(collective_id=0, has_side_effects=True, vmem_limit_bytes=58 << 20),
        name="backward",
    )(lengths, qr, kr, vr, attn_grad, attn, lse, cosine, sine, parts)


def row_layout(lengths, counts, row_len):
    lens = lengths[0]
    slots = lens.shape[0]
    order = lax.broadcasted_iota(jnp.int32, (slots, slots), 0)
    upto = lax.broadcasted_iota(jnp.int32, (slots, slots), 1)
    starting = jnp.sum(jnp.where(upto < order, lens[None, :], 0), axis=1)
    slot = lax.broadcasted_iota(jnp.int32, (slots,), 0)
    which = jnp.min(jnp.where(lens == LONGEST, slot, slots))
    offset = jnp.sum(jnp.where(slot == which, starting, 0))
    places = lax.broadcasted_iota(jnp.int32, (row_len,), 0) + offset
    places = jnp.where(places >= row_len, places - row_len, places)
    endings = starting + lens
    segment = jnp.sum((places[:, None] >= endings[None, :]).astype(jnp.int32), axis=1)
    member = segment[:, None] == slot[None, :]
    first_place = jnp.sum(jnp.where(member, starting[None, :], 0), axis=1)
    position = (places - first_place).astype(jnp.float32)
    inverse_count = 1.0 / counts[0].astype(jnp.float32)
    share = jnp.sum(jnp.where(member, inverse_count[None, :], 0.0), axis=1)
    return offset, segment, position, share


def rotary_tables(position):
    lane = lax.broadcasted_iota(jnp.int32, (1, LANES), 1)
    indices = (lane % (HEAD_DIM // 2)).astype(jnp.float32)
    inverse = jnp.exp(indices * (-2.0 * math.log(10000.0) / HEAD_DIM))
    angles = position[:, None] * inverse
    sign = jnp.where((lane % HEAD_DIM) < (HEAD_DIM // 2), -1.0, 1.0)
    return jnp.cos(angles), jnp.sin(angles) * sign


def turn_rows(values, shift):
    twice = jnp.concatenate([values, values], axis=0)
    return lax.dynamic_slice_in_dim(twice, shift, values.shape[0], 0)


def high(left, right):
    return jnp.dot(left, right, precision=lax.Precision.HIGH, preferred_element_type=jnp.float32)


def shards_near(
    tokens, cotangent, lengths, counts,
    w_qkv, w_out, w_up, w_down,
    mom_qkv, mom_out, mom_up, mom_down,
    vectors, vec_first, vec_second,
):
    columns = w_qkv.shape[1]
    weights_t = [w_qkv.T, w_out, w_up.T, w_down.T]
    moments_t = [mom_qkv.T, mom_out, mom_up.T, mom_down.T]
    qr, kr, vr, attn, lse, normed_one, turned, cosine, sine, wt_qkv, table, full_b, full_o, incoming, dy, dyt = head(
        lengths, counts, tokens, cotangent, weights_t[0], weights_t[2], weights_t[3], w_out, vectors)
    out_grad, sums, layer_out, after_grad, attn_grad, parts_b = middle(
        lengths, turned, attn, incoming, dy, dyt, table, full_o, full_b)
    dq, dk, dv, own_up, total_down = backward(
        lengths, qr, kr, vr, attn_grad, attn, lse, cosine, sine, parts_b.reshape(4, 2, 2, 2, columns, -1))
    results = tail(
        normed_one, dq, dk, dv, out_grad, sums, table, own_up, total_down, lengths, moments_t, weights_t,
        (vectors, vec_first, vec_second), wt_qkv, after_grad, turned)
    results = finish([*results, layer_out])
    matrices = [v if x % 4 == 1 else v.T for x, v in enumerate(results[:8])]
    return (results[12], results[11], *matrices, *results[8:11])


def shards_far(
    tokens, cotangent, lengths, counts,
    w_qkv, w_out, w_up, w_down,
    mom_qkv, mom_out, mom_up, mom_down,
    vectors, vec_first, vec_second,
):
    both = ("fsdp", "dp")
    planes = lax.axis_size("fsdp")
    ranks = lax.axis_size("dp")
    row_len, width = tokens.shape
    columns = w_qkv.shape[1]
    old_weights = (w_qkv, w_out, w_up, w_down)
    old_moments = (mom_qkv, mom_out, mom_up, mom_down)
    counts_rows = [w.shape[0] for w in old_weights]
    n_vec = vectors.shape[0]

    slab_a = jnp.concatenate([w_qkv.T, w_out.T, vectors.T], axis=1).astype(jnp.bfloat16)
    slab_b = jnp.concatenate([w_up.T, w_down.T], axis=1).astype(jnp.bfloat16)
    full_a = lax.all_gather(slab_a, both, axis=0, tiled=True).reshape(planes, width, -1)
    full_b = lax.all_gather(slab_b, both, axis=0, tiled=True).reshape(planes, width, -1)
    r0, r1, r2, r3 = counts_rows
    wt_qkv = jnp.concatenate([full_a[j, :, :r0] for j in range(planes)], axis=1)
    wt_out = jnp.concatenate([full_a[j, :, r0 : r0 + r1] for j in range(planes)], axis=1)
    table = full_a[0, :, r0 + r1 :].T.astype(jnp.float32)
    wt_up = jnp.concatenate([full_b[j, :, :r2] for j in range(planes)], axis=1)
    wt_down = jnp.concatenate([full_b[j, :, r2:] for j in range(planes)], axis=1)

    offset, segment, position, share = row_layout(lengths, counts, row_len)
    cosine, sine = rotary_tables(position)
    seg_col, seg_row = segment[:, None], segment[None, :]
    inputs = turn_rows(tokens, offset).astype(jnp.float32)
    incoming = turn_rows(cotangent, offset).astype(jnp.float32) * share[:, None]

    normed_one, pull_one = jax.vjp(layer_norm, inputs, table[0], table[1])
    normed_one = normed_one.astype(jnp.bfloat16)
    project = nn(normed_one, wt_qkv) + table[4:7].reshape(-1)
    qr, kr, vr, attn, lse = attention_forward(project, cosine, sine, seg_col, seg_row)
    after = inputs + (nn(attn, wt_out) + table[7])
    normed_two, pull_two = jax.vjp(layer_norm, after, table[2], table[3])
    normed_two = normed_two.astype(jnp.bfloat16)
    hidden_pre = nn(normed_two, wt_up) + table[9:].reshape(-1)
    hidden, pull_hidden = jax.vjp(gelu_exact, hidden_pre)
    hidden = hidden.astype(jnp.bfloat16)
    layer_out = (after + (nt(hidden, wt_down) + table[8])).astype(jnp.bfloat16)

    grad_low = incoming.astype(jnp.bfloat16)
    grad_t_down = tn(grad_low, hidden)
    pre_grad = pull_hidden(nn(grad_low, wt_down))[0].astype(jnp.bfloat16)
    grad_t_up = tn(normed_two, pre_grad)
    resid_grad, gain_two, shift_two = pull_two(nt(pre_grad, wt_up))
    after_grad = incoming + resid_grad
    branch_low = after_grad.astype(jnp.bfloat16)
    grad_t_out = tn(attn, branch_low)
    attn_grad = nt(branch_low, wt_out).astype(jnp.bfloat16)
    dq, dk, dv = attention_backward(qr, kr, vr, attn_grad, attn, lse, cosine, sine, seg_col, seg_row)
    proj_grad = jnp.concatenate([dq, dk, dv], axis=1)
    grad_t_qkv = tn(normed_one, proj_grad)
    in_grad, gain_one, shift_one = pull_one(nt(proj_grad, wt_qkv))
    input_grad = after_grad + in_grad

    def column_sum(values):
        return jnp.sum(values.astype(jnp.float32), axis=0)

    vector_grad = jnp.concatenate(
        [gain_one[None], shift_one[None], gain_two[None], shift_two[None],
         column_sum(proj_grad).reshape(3, width), column_sum(branch_low)[None], column_sum(grad_low)[None],
         column_sum(pre_grad).reshape(-1, width)],
        axis=0,
    )
    back = jnp.where(offset > 0, row_len - offset, 0)
    layer_out = turn_rows(layer_out, back)
    input_grad = turn_rows(input_grad, back)

    def cut(values, j, rows):
        return values[:, j * rows : (j + 1) * rows]

    parts_b = jnp.stack([jnp.concatenate([cut(grad_t_up, j, r2), cut(grad_t_down, j, r3)], axis=1) for j in range(planes)])
    own_b = lax.psum_scatter(parts_b.reshape(planes * width, -1), both, scatter_dimension=0, tiled=True)
    parts_a = jnp.stack([jnp.concatenate([cut(grad_t_qkv, j, r0), cut(grad_t_out, j, r1), vector_grad.T], axis=1) for j in range(planes)])
    own_a = lax.psum_scatter(parts_a.reshape(planes * width, -1), both, scatter_dimension=0, tiled=True)
    grads_t = (own_a[:, :r0], own_a[:, r0 : r0 + r1], own_b[:, :r2], own_b[:, r2:])
    vector_grad = own_a[:, r0 + r1 :].T
    new_moments_t = [moment_keep * old.T + grad for old, grad in zip(old_moments, grads_t)]

    most = max(counts_rows)
    padded = [jnp.pad(m.astype(jnp.bfloat16), ((0, 0), (0, most - m.shape[1]))) for m in new_moments_t]
    sent = jnp.stack([padded[t % 4] for t in range(planes)])
    mine = lax.all_to_all(sent, "fsdp", 0, 0, tiled=True)
    mine = mine.transpose(1, 0, 2).reshape(columns, planes * most)
    whole = lax.all_gather(mine, "dp", axis=0, tiled=True)
    gram = nt(whole, whole)
    identity = jnp.eye(width, dtype=jnp.float32)
    norm_sq = jnp.trace(gram) + 1e-07
    gram = gram / norm_sq
    factor = None
    for iteration in range(NS_ITERS):
        poly = poly_linear * identity + poly_square * gram + poly_cubic * high(gram, gram)
        factor = poly if factor is None else high(factor, poly)
        if iteration + 1 < NS_ITERS:
            gram = high(high(gram, poly), poly)
    own_rows = lax.dynamic_slice_in_dim(factor, lax.axis_index("dp") * columns, columns, 0) * lax.rsqrt(norm_sq)
    own_orth = high(own_rows, whole.astype(jnp.float32))
    own_orth = own_orth.astype(jnp.bfloat16).reshape(columns, planes, most).transpose(1, 0, 2)
    pieces = lax.all_to_all(own_orth, "fsdp", 0, 0, tiled=True).astype(jnp.float32)

    new_weights = []
    for x, weight_old in enumerate(old_weights):
        rows = weight_old.shape[0]
        scale = muon_rate * math.sqrt(max(1.0, rows * planes / width))
        new_weights.append(weight_old * (1.0 - muon_rate * muon_decay) - scale * pieces[x, :, :rows].T)
    new_first = beta_first * vec_first + (1.0 - beta_first) * vector_grad
    new_second = beta_second * vec_second + (1.0 - beta_second) * vector_grad * vector_grad
    first_fix = 1.0 - beta_first**STEP
    second_fix = 1.0 - beta_second**STEP
    new_vectors = vectors - adam_rate * (new_first / first_fix) / (jnp.sqrt(new_second / second_fix) + adam_eps)
    return (layer_out, input_grad, *[m.T for m in new_moments_t], *new_weights, new_vectors, new_first, new_second)


def solution(mesh):
    rows, cells, table = P(("dp", "fsdp"), None), P("fsdp", "dp"), P(None, "dp")
    near = dict(mesh.shape) == {"dp": 8, "fsdp": 4}
    return jax.shard_map(
        shards_near if near else shards_far,
        mesh=mesh,
        in_specs=(rows,) * 4 + (cells,) * 8 + (table,) * 3,
        out_specs=(rows,) * 2 + (cells,) * 8 + (table,) * 3,
        check_vma=False,
    )
```

```python
import functools
import math

import jax
import jax.numpy as jnp
from jax import lax
from jax.experimental import pallas as pl
from jax.experimental.pallas import tpu as pltpu
from jax.sharding import PartitionSpec as P

HEAD_DIM = 32
NS_ITERS = 5
STEP = 10
LANES = 128
LONGEST = 768

norm_eps = 1e-05
masked_score = -1e30
poly_linear = 3.4445
poly_square = -4.775
poly_cubic = 2.0315
muon_rate = 0.5
muon_decay = 0.01
moment_keep = 0.5
adam_rate = 0.05
beta_first = 0.9
beta_second = 0.999
adam_eps = 1e-08


def layer_norm(values, gain_row, shift_row):
    center = values - jnp.mean(values, axis=-1, keepdims=True)
    spread = jnp.mean(center * center, axis=-1, keepdims=True)
    return center * lax.rsqrt(spread + norm_eps) * gain_row + shift_row


def gelu_exact(values):
    return 0.5 * values * (1.0 + lax.erf(values * (1.0 / math.sqrt(2.0))))


def nn(left, right):
    return jnp.dot(left, right, preferred_element_type=jnp.float32)


def nt(left, right):
    return lax.dot_general(left, right, (((1,), (1,)), ((), ())), preferred_element_type=jnp.float32)


def tn(left, right):
    return lax.dot_general(left, right, (((0,), (0,)), ((), ())), preferred_element_type=jnp.float32)


def _half_mask(shape):
    lane = lax.broadcasted_iota(jnp.int32, shape, 1)
    return (lane % HEAD_DIM) < (HEAD_DIM // 2)


def _turn(values, first):
    half = HEAD_DIM // 2
    left = pltpu.roll(values, LANES - half, 1)
    right = pltpu.roll(values, half, 1)
    return jnp.where(first, left, right)


def attention_forward_kernel(
    q_ref, k_ref, v_ref, cos_ref, sin_ref, segc_ref, segr_ref,
    qr_ref, kr_ref, vr_ref, attn_ref, lse_ref,
    qt_s, vt_s, ot_s,
):
    first = _half_mask(cos_ref.shape)
    cosine, sine = cos_ref[...], sin_ref[...]
    queries = q_ref[...] * (1.0 / math.sqrt(HEAD_DIM))
    qr = (queries * cosine + _turn(queries, first) * sine).astype(jnp.bfloat16)
    keys = k_ref[...]
    kr = (keys * cosine + _turn(keys, first) * sine).astype(jnp.bfloat16)
    vr = v_ref[...].astype(jnp.bfloat16)
    qr_ref[...] = qr
    kr_ref[...] = kr
    vr_ref[...] = vr
    qt_s[...] = qr.T
    vt_s[...] = vr.T
    tokens = qr.shape[0]
    rest = tokens - LONGEST
    row = lax.broadcasted_iota(jnp.int32, (LANES, tokens), 0)
    same = segc_ref[LONGEST:, :] == segr_ref[:, LONGEST:]

    def head(h, carry):
        qth = jnp.where(row // HEAD_DIM == h, qt_s[...], jnp.zeros((), jnp.bfloat16))
        rows = pl.ds(pl.multiple_of(h * HEAD_DIM, HEAD_DIM), HEAD_DIM)

        def block(start, width, key_start, key_count, mask):
            scores = nn(kr_ref[key_start : key_start + key_count, :], qth[:, start : start + width])
            if mask is not None:
                scores = jnp.where(mask, scores, masked_score)
            peak = jnp.max(scores, axis=0, keepdims=True)
            raised = jnp.exp(scores - peak)
            total = jnp.sum(raised, axis=0, keepdims=True)
            out = nn(vt_s[rows, key_start : key_start + key_count], raised.astype(jnp.bfloat16))
            ot_s[rows, start : start + width] = out / total
            lse_ref[0, pl.ds(h, 1), start : start + width] = peak + jnp.log(total)

        for start in range(0, LONGEST, 256):
            block(start, 256, 0, LONGEST, None)
        block(LONGEST, rest, LONGEST, rest, same)
        return carry

    lax.fori_loop(0, LANES // HEAD_DIM, head, 0)
    attn_ref[...] = ot_s[...].T.astype(jnp.bfloat16)


def attention_forward(project, cosine, sine, seg_col, seg_row):
    tokens = project.shape[0]
    width = project.shape[1] // 3
    groups = width // LANES
    col = lambda shift: pl.BlockSpec((tokens, LANES), lambda g, shift=shift: (0, g + shift))
    whole = lambda shape: pl.BlockSpec(shape, lambda g: (0,) * len(shape))
    flops = 4 * (LONGEST**2 + (tokens - LONGEST) ** 2) * 128 * groups * 4
    return pl.pallas_call(
        attention_forward_kernel,
        grid=(groups,),
        in_specs=[col(0), col(groups), col(2 * groups), whole((tokens, LANES)), whole((tokens, LANES)),
                  whole((tokens, 1)), whole((1, tokens))],
        out_specs=[col(0)] * 4 + [pl.BlockSpec((1, 4, tokens), lambda g: (g, 0, 0))],
        out_shape=[jax.ShapeDtypeStruct((tokens, width), jnp.bfloat16)] * 4
        + [jax.ShapeDtypeStruct((groups, 4, tokens), jnp.float32)],
        scratch_shapes=[
            pltpu.VMEM((LANES, tokens), jnp.bfloat16),
            pltpu.VMEM((LANES, tokens), jnp.bfloat16),
            pltpu.VMEM((LANES, tokens), jnp.float32),
        ],
        compiler_params=pltpu.CompilerParams(vmem_limit_bytes=48 << 20),
        cost_estimate=pl.CostEstimate(flops=flops, bytes_accessed=20 << 20, transcendentals=20 << 20),
        name="attention_forward",
    )(project, project, project, cosine, sine, seg_col, seg_row)


def attention_backward_kernel(
    qr_ref, kr_ref, vr_ref, do_ref, attn_ref, lse_ref, cos_ref, sin_ref, segc_ref, segr_ref,
    *rest_refs,
):
    dq_ref, dk_ref, dv_ref = rest_refs[:3]
    qt_s, dot_s, kt_s, delta_s, dqt_s, dk_s, dv_s = rest_refs[3:]
    tokens = qr_ref.shape[0]
    rest = tokens - LONGEST
    qt_s[...] = qr_ref[...].T
    dot_s[...] = do_ref[...].T
    kt_s[...] = kr_ref[...].T
    prod_t = (do_ref[...].astype(jnp.float32) * attn_ref[...].astype(jnp.float32)).T
    for h in range(4):
        delta_s[h : h + 1, :] = jnp.sum(prod_t[h * HEAD_DIM : (h + 1) * HEAD_DIM, :], axis=0, keepdims=True)
    dk_s[...] = jnp.zeros_like(dk_s)
    dv_s[...] = jnp.zeros_like(dv_s)
    row = lax.broadcasted_iota(jnp.int32, (LANES, tokens), 0)
    lane = lax.broadcasted_iota(jnp.int32, (tokens, LANES), 1)
    same = segc_ref[LONGEST:, :] == segr_ref[:, LONGEST:]
    zero = jnp.zeros((), jnp.bfloat16)

    def head(h, carry):
        mine_t = row // HEAD_DIM == h
        mine = lane // HEAD_DIM == h
        qth = jnp.where(mine_t, qt_s[...], zero)
        doth = jnp.where(mine_t, dot_s[...], zero)
        qh = jnp.where(mine, qr_ref[...], zero)
        doh = jnp.where(mine, do_ref[...], zero)
        rows = pl.ds(pl.multiple_of(h * HEAD_DIM, HEAD_DIM), HEAD_DIM)

        def block(start, width, key_start, key_count, mask):
            at = slice(start, start + width)
            keys = slice(key_start, key_start + key_count)
            scores = nn(kr_ref[keys, :], qth[:, at])
            if mask is not None:
                scores = jnp.where(mask, scores, masked_score)
            soft = jnp.exp(scores - lse_ref[0, pl.ds(h, 1), at])
            weight_grad = nn(vr_ref[keys, :], doth[:, at])
            score_grad = (soft * (weight_grad - delta_s[pl.ds(h, 1), at])).astype(jnp.bfloat16)
            dv_s[keys, :] += nn(soft.astype(jnp.bfloat16), doh[at, :])
            dk_s[keys, :] += nn(score_grad, qh[at, :])
            dqt_s[rows, at] = nn(kt_s[rows, keys], score_grad)

        for start in range(0, LONGEST, 256):
            block(start, 256, 0, LONGEST, None)
        block(LONGEST, rest, LONGEST, rest, same)
        return carry

    lax.fori_loop(0, LANES // HEAD_DIM, head, 0)
    first = _half_mask(cos_ref.shape)
    cosine, sine = cos_ref[...], sin_ref[...]

    def pull(values):
        return values * cosine + _turn(values * sine, first)

    dq_ref[...] = (pull(dqt_s[...].T) * (1.0 / math.sqrt(HEAD_DIM))).astype(jnp.bfloat16)
    dk_ref[...] = pull(dk_s[...]).astype(jnp.bfloat16)
    dv_ref[...] = dv_s[...].astype(jnp.bfloat16)


def attention_backward(qr, kr, vr, attn_grad, attn, lse, cosine, sine, seg_col, seg_row):
    tokens, width = qr.shape
    groups = width // LANES
    col = pl.BlockSpec((tokens, LANES), lambda g: (0, g))
    whole = lambda shape: pl.BlockSpec(shape, lambda g: (0,) * len(shape))
    flops = 10 * (LONGEST**2 + (tokens - LONGEST) ** 2) * 128 * groups * 4
    return pl.pallas_call(
        attention_backward_kernel,
        grid=(groups,),
        in_specs=[col] * 5 + [pl.BlockSpec((1, 4, tokens), lambda g: (g, 0, 0)),
                              whole((tokens, LANES)), whole((tokens, LANES)), whole((tokens, 1)), whole((1, tokens))],
        out_specs=[col] * 3,
        out_shape=[jax.ShapeDtypeStruct((tokens, width), jnp.bfloat16)] * 3,
        scratch_shapes=[
            pltpu.VMEM((LANES, tokens), jnp.bfloat16),
            pltpu.VMEM((LANES, tokens), jnp.bfloat16),
            pltpu.VMEM((LANES, tokens), jnp.bfloat16),
            pltpu.VMEM((8, tokens), jnp.float32),
            pltpu.VMEM((LANES, tokens), jnp.float32),
            pltpu.VMEM((tokens, LANES), jnp.float32),
            pltpu.VMEM((tokens, LANES), jnp.float32),
        ],
        compiler_params=pltpu.CompilerParams(vmem_limit_bytes=56 << 20),
        cost_estimate=pl.CostEstimate(flops=flops, bytes_accessed=20 << 20, transcendentals=20 << 20),
        name="attention_backward",
    )(qr, kr, vr, attn_grad, attn, lse, cosine, sine, seg_col, seg_row)


MESH = pl.DeviceIdType.MESH


def place():
    rank, plane = lax.axis_index("dp"), lax.axis_index("fsdp")
    core = rank % 2
    chip_x = (rank // 2) % 2
    chip_y = rank // 4
    return rank, plane, core, chip_x, chip_y


def chip_at(step, chip_x, chip_y):
    other_x = 1 - chip_x if step & 1 else chip_x
    other_y = 1 - chip_y if step & 2 else chip_y
    return 2 * other_y + other_x


def call(partners):
    for partner in partners:
        pl.semaphore_signal(pltpu.get_barrier_semaphore(), inc=1, device_id=partner, device_id_type=MESH)


def hear(partners):
    pl.semaphore_wait(pltpu.get_barrier_semaphore(), len(partners))


def greet(partners):
    call(partners)
    hear(partners)


def all_partners():
    rank, plane, core, chip_x, chip_y = place()
    sibling = 2 * chip_at(0, chip_x, chip_y) + 1 - core
    partners = [(sibling, plane)]
    partners += [(2 * chip_at(step, chip_x, chip_y) + core, plane) for step in (1, 2, 3)]
    partners += [(rank, (plane + step) % 4) for step in (1, 2, 3)]
    return partners


class SumStages:
    def __init__(self, parts, scratch, lanes):
        (self.own, self.from_core, self.from_first, self.middle, self.from_second, self.total, self.from_plane,
         self.send, self.recv, self.local) = scratch
        self.parts, self.lanes = parts, lanes
        self.rank, self.plane, self.core, self.chip_x, self.chip_y = place()

    def remote(self, source, target, slot, device):
        return pltpu.make_async_remote_copy(
            src_ref=source, dst_ref=target, send_sem=self.send.at[slot], recv_sem=self.recv.at[slot],
            device_id=device, device_id_type=MESH)

    def device(self, step):
        return (2 * chip_at(step, self.chip_x, self.chip_y) + self.core, self.plane)

    def add(self, left, right):
        return left.astype(jnp.float32) + right.astype(jnp.float32)

    def give_copy(self, source):
        return self.remote(source, self.from_core, 0, (2 * chip_at(0, self.chip_x, self.chip_y) + 1 - self.core, self.plane))

    def core_add(self, give):
        give.wait()
        for j in range(4):
            self.own[j] = self.add(self.own[j], self.from_core[j]).astype(self.own.dtype)

    def core_copies(self):
        load = pltpu.make_async_copy(self.parts.at[:, :, :, self.core, :, self.lanes], self.own, self.local)
        return load, self.give_copy(self.parts.at[:, :, :, 1 - self.core, :, self.lanes])

    def core_start(self):
        load, give = self.core_copies()
        give.start()
        load.start()

    def core_finish(self):
        load, give = self.core_copies()
        load.wait()
        self.core_add(give)

    def first_copies(self):
        return [
            self.remote(self.own.at[pl.ds(0, 2), :, 1 - self.chip_x], self.from_first.at[0], 1, self.device(1)),
            self.remote(self.own.at[pl.ds(2, 2), 1 - self.chip_y], self.from_first.at[1], 2, self.device(2)),
        ]

    def second_copies(self):
        return [
            self.remote(self.middle.at[0, :, 1 - self.chip_y], self.from_second.at[0], 3, self.device(2)),
            self.remote(self.middle.at[1, :, 1 - self.chip_x], self.from_second.at[1], 4, self.device(1)),
        ]

    def chip_start(self):
        for copy in self.first_copies():
            copy.start()

    def chip_turn(self):
        for copy in self.first_copies():
            copy.wait()
        for j in range(2):
            mine = self.own[j, :, pl.ds(self.chip_x, 1)][:, 0]
            self.middle[0, j] = self.add(mine, self.from_first[0, j]).astype(self.middle.dtype)
            mine = self.own[2 + j, pl.ds(self.chip_y, 1)][0]
            self.middle[1, j] = self.add(mine, self.from_first[1, j]).astype(self.middle.dtype)
        for copy in self.second_copies():
            copy.start()

    def chip_finish(self):
        for copy in self.second_copies():
            copy.wait()
        for half, index in ((0, self.chip_y), (1, self.chip_x)):
            for j in range(2):
                mine = self.middle[half, j, pl.ds(index, 1)][0]
                self.total[2 * half + j] = self.add(mine, self.from_second[half, j]).astype(self.total.dtype)

    def plane_copies(self):
        return [
            self.remote(self.total.at[(self.plane + step) % 4], self.from_plane.at[step - 1], 4 + step,
                        (self.rank, (self.plane + step) % 4))
            for step in (1, 2, 3)
        ]

    def plane_start(self):
        for copy in self.plane_copies():
            copy.start()

    def plane_finish(self):
        for copy in self.plane_copies():
            copy.wait()
        value = self.total[pl.ds(self.plane, 1)][0].astype(jnp.float32)
        for slot in range(3):
            value = value + self.from_plane[slot].astype(jnp.float32)
        return value


def sum_scratch(rows, lanes, dtype=jnp.bfloat16):
    return [
        pltpu.VMEM((4, 2, 2, rows, lanes), dtype),
        pltpu.VMEM((4, 2, 2, rows, lanes), dtype),
        pltpu.VMEM((2, 2, 2, rows, lanes), dtype),
        pltpu.VMEM((2, 2, 2, rows, lanes), dtype),
        pltpu.VMEM((2, 2, rows, lanes), dtype),
        pltpu.VMEM((4, rows, lanes), dtype),
        pltpu.VMEM((3, rows, lanes), dtype),
        pltpu.SemaphoreType.DMA((8,)),
        pltpu.SemaphoreType.DMA((8,)),
        pltpu.SemaphoreType.DMA,
    ]


SUM_SCRATCH = 10


def table_sum(table_ref, table_out, from_core, from_chip, from_plane, held, send, recv):
    rank, plane, core, chip_x, chip_y = place()
    chip = chip_at(0, chip_x, chip_y)

    def remote(source, target, slot, device):
        return pltpu.make_async_remote_copy(
            src_ref=source, dst_ref=target, send_sem=send.at[slot], recv_sem=recv.at[slot],
            device_id=device, device_id_type=MESH)

    give = remote(table_ref.at[:, 1 - core], from_core, 0, (2 * chip + 1 - core, plane))
    give.start()
    yield
    give.wait()
    held[...] = table_ref[:, pl.ds(core, 1)][:, 0] + from_core[...]
    across = [remote(held.at[chip_at(step, chip_x, chip_y)], from_chip.at[step - 1], step,
                     (2 * chip_at(step, chip_x, chip_y) + core, plane)) for step in (1, 2, 3)]
    for copy in across:
        copy.start()
    yield
    for copy in across:
        copy.wait()
    own = held[pl.ds(chip, 1)][0] + from_chip[0] + from_chip[1] + from_chip[2]
    table_out[...] = own
    along = [remote(table_out, from_plane.at[step - 1], 3 + step, (rank, (plane + step) % 4)) for step in (1, 2, 3)]
    for copy in along:
        copy.start()
    yield
    for copy in along:
        copy.wait()
    table_out[...] = own + from_plane[0] + from_plane[1] + from_plane[2]
    yield


class Gather:
    def __init__(self, at, send, recv, base, parts):
        rank, plane, core, chip_x, chip_y = place()
        every, low, high = parts
        chips = [chip_at(step, chip_x, chip_y) for step in range(4)]
        over = [2 * chip + core for chip in chips]

        def copy(chip, lanes, slot, device):
            block = at(chip, core, lanes)
            return pltpu.make_async_remote_copy(
                src_ref=block, dst_ref=block, send_sem=send.at[base + slot], recv_sem=recv.at[base + slot],
                device_id=(device, plane), device_id_type=MESH)

        self.to_x, self.to_y = copy(chips[0], every, 0, over[1]), copy(chips[0], every, 1, over[2])
        self.on_y, self.on_x = copy(chips[1], low, 2, over[2]), copy(chips[2], high, 3, over[1])
        self.beside = [copy(chip, every, 4 + step, 2 * chips[0] + 1 - core) for step, chip in enumerate(chips)]

    def first(self):
        self.to_x.start()
        self.to_y.start()
        self.beside[0].start()

    def second(self):
        self.to_x.wait_recv()
        self.on_y.start()
        self.beside[1].start()
        self.to_y.wait_recv()
        self.on_x.start()
        self.beside[2].start()

    def third(self):
        self.on_y.wait_recv()
        self.on_x.wait_recv()
        self.beside[3].start()

    def landed(self):
        for copy in self.beside:
            copy.wait_recv()

    def sent(self):
        for copy in (self.to_x, self.to_y, self.on_y, self.on_x, *self.beside):
            copy.wait_send()

    def finish(self):
        self.landed()
        self.sent()


def split(values):
    top = values.astype(jnp.bfloat16)
    return top, (values - top.astype(jnp.float32)).astype(jnp.bfloat16)


def put_left(ref, values):
    width = values.shape[1]
    top, low = split(values)
    ref[:, :width] = top
    ref[:, width : 2 * width] = top
    ref[:, 2 * width :] = low


def put_right(ref, values):
    width = values.shape[0]
    top, low = split(values)
    ref[:width, :] = top
    ref[width : 2 * width, :] = low
    ref[2 * width :, :] = top


def tiles_of(width):
    first = width % 256
    edges = ([0] if first else []) + list(range(first, width + 1, 256))
    return list(zip(edges[:-1], edges[1:]))


def symmetric_product(out, left, right, tiles):
    for start, stop in tiles:
        block = nn(left[:stop, :], right[:, start:stop])
        out[:stop, start:stop] = block
        if start:
            out[start:stop, :start] = block[:start, :].T


def orthogonal_rows(whole, mine, gram, poly, temp, rows_s, left_gram, left_temp, right, write):
    width = gram.shape[0]
    tiles = tiles_of(width)
    parts = [whole[j].reshape(width, whole.shape[-1]) for j in range(4)]
    for start, stop in tiles:
        block = sum(nt(part[:stop, :], part[start:stop, :]) for part in parts)
        gram[:stop, start:stop] = block
        if start:
            gram[start:stop, :start] = block[:start, :].T
    diagonal = lax.broadcasted_iota(jnp.int32, (width, width), 0) == lax.broadcasted_iota(jnp.int32, (width, width), 1)
    norm_sq = jnp.sum(jnp.sum(jnp.where(diagonal, gram[...], 0.0), axis=1, keepdims=True), axis=0, keepdims=True) + 1e-07
    scale = lax.rsqrt(norm_sq)
    gram[...] = gram[...] * scale * scale

    def polynomial():
        put_left(left_gram, gram[...])
        put_right(right, gram[...])
        symmetric_product(temp, left_gram, right, tiles)
        poly[...] = jnp.where(diagonal, poly_linear, 0.0) + poly_square * gram[...] + poly_cubic * temp[...]
        put_right(right, poly[...])

    def next_gram():
        symmetric_product(temp, left_gram, right, tiles)
        put_left(left_temp, temp[...])
        symmetric_product(gram, left_temp, right, tiles)

    def thin(values):
        count = values.shape[0]
        top, low = split(values)
        both = nn(jnp.concatenate([top, low], axis=0), right[:width, :])
        return both[:count, :] + both[count:, :] + nn(top, right[width : 2 * width, :])

    polynomial()
    rows_s[...] = poly[mine, :]

    def iteration(step, carry):
        next_gram()
        polynomial()
        rows_s[...] = thin(rows_s[...])
        return carry

    lax.fori_loop(0, NS_ITERS - 2, iteration, 0)
    next_gram()
    put_right(right, gram[...])
    rows = rows_s[...]
    once = thin(rows)
    twice = thin(once)
    rows = (poly_linear * rows + poly_square * once + poly_cubic * twice) * lax.rsqrt(norm_sq)
    top, low = split(rows)
    for j, part in enumerate(parts):
        write(j, nn(top, part) + nn(low, part))


class PlaneStage:
    def __init__(self, total, from_plane, send, recv):
        rank, self.plane = place()[:2]
        self.total, self.from_plane = total, from_plane
        self.copies = [
            pltpu.make_async_remote_copy(
                src_ref=total.at[(self.plane + step) % 4], dst_ref=from_plane.at[step - 1],
                send_sem=send.at[step - 1], recv_sem=recv.at[step - 1],
                device_id=(rank, (self.plane + step) % 4), device_id_type=MESH)
            for step in (1, 2, 3)
        ]

    def start(self):
        for copy in self.copies:
            copy.start()

    def finish(self):
        for copy in self.copies:
            copy.wait()
        value = self.total[pl.ds(self.plane, 1)][0].astype(jnp.float32)
        for slot in range(3):
            value = value + self.from_plane[slot].astype(jnp.float32)
        return value


MATRIX_OF = (2, 0, 1, 3)
LANES_OF = (640, 512, 256, 640)
FIRST, LAST = (0, 3), (1, 2)
CUTS_A = ((0, 256), (256, 384))


def tail_kernel(
    sums_ref, table_ref, own_up_ref, total_b_ref, len_ref, *refs,
):
    moments, weights, small, large = refs[0:4], refs[4:8], refs[8:11], refs[11:19]
    refs = refs[19:]
    new_moments, new_weights, new_small, input_grad_hbm = refs[0:4], refs[4:8], refs[8:11], refs[11]
    table_out, pieces = refs[12:14]
    refs = refs[14:]
    early, late = (SumStages(None, refs[SUM_SCRATCH * n : SUM_SCRATCH * (n + 1)], None) for n in range(2))
    refs = refs[2 * SUM_SCRATCH :]
    table_scratch, refs = refs[:6], refs[6:]
    blocks, whole, gram, poly, temp, rows_s, left_gram, left_temp, right, from_plane_b = refs[:10]
    plane_send, plane_recv, gather_send, gather_recv, back_send, back_recv, b_send, b_recv, loads = refs[10:19]
    gives_s, (tiles_s, h1t_s, turned_s, stored), held = refs[19:21], refs[21:25], refs[25:]
    h1_ref, dq_ref, dk_ref, dv_ref, out_grad_ref, wt_s, after_s, x_s = held
    rank, plane, core, chip_x, chip_y = place()
    chip = chip_at(0, chip_x, chip_y)
    columns, lanes = blocks.shape[1:]
    tokens, width = h1_ref.shape
    rows_qkv, rows_out = moments[0].shape[1], moments[1].shape[0]
    last_b = PlaneStage(total_b_ref, from_plane_b, b_send, b_recv)
    loading = [pltpu.make_async_copy(source, target, loads.at[n]) for n, (source, target) in enumerate(zip(large, held))]
    for copy in loading:
        copy.start()

    @pl.when((plane == LAST[0]) | (plane == LAST[1]))
    def _():
        whole[...] = jnp.zeros_like(whole)

    call(all_partners())
    loading[0].wait()
    h1t_s[...] = h1_ref[...].T
    hear(all_partners())
    last_b.start()
    for copy in loading[1:5]:
        copy.wait()

    def half(which, targets):
        starts = [pl.multiple_of(columns * (2 * m + which), 16) for m in range(4)]
        left = jnp.concatenate([h1t_s[pl.ds(start, columns), :] for start in starts], axis=0)
        qkv = jnp.concatenate([nn(left, ref[...]).astype(jnp.bfloat16) for ref in (dq_ref, dk_ref, dv_ref)], axis=1)
        out = jnp.concatenate([out_grad_ref[pl.ds(start, columns), :] for start in starts], axis=0)
        for j in range(4):
            both = jnp.concatenate(
                [qkv[:, j * rows_qkv : (j + 1) * rows_qkv], out[:, j * rows_out : (j + 1) * rows_out]], axis=1)
            for target, (start, size) in zip(targets, CUTS_A):
                target[j] = both[:, start : start + size].reshape(2, 2, columns, size)

    half(1 - core, gives_s)
    gives = [stages.give_copy(source) for stages, source in zip((early, late), gives_s)]
    for give in gives:
        give.start()
    half(core, (early.own, late.own))
    early.core_add(gives[0])
    early.chip_start()
    late.core_add(gives[1])

    def momentum(x, gradient):
        rows = gradient.shape[1]
        slot = MATRIX_OF.index(x)
        if x == 1:
            new = moment_keep * moments[x][...].T + gradient
            new_moments[x][...] = new.T
        else:
            new = moment_keep * moments[x][...] + gradient
            new_moments[x][...] = new
        blocks[slot, :, :rows] = new.astype(jnp.bfloat16)
        if rows < lanes:
            blocks[slot, :, rows:] = jnp.zeros((columns, lanes - rows), jnp.bfloat16)

    def out_copy(step, target):
        part = pl.ds(0, LANES_OF[target])
        return pltpu.make_async_remote_copy(
            src_ref=blocks.at[target, :, part], dst_ref=whole.at[plane, chip, core, :, part],
            send_sem=plane_send.at[step - 1], recv_sem=plane_recv.at[step - 1],
            device_id=(rank, (plane + step) % 4), device_id_type=MESH)

    def when_target(targets, act):
        for step in (1, 2, 3):
            for target in targets:
                @pl.when((plane + step) % 4 == target)
                def _():
                    act(out_copy(step, target))

    def place_own(target):
        part = LANES_OF[target]
        whole[target, pl.ds(chip, 1), pl.ds(core, 1), :, :part] = blocks[target, :, :part][None, None]

    def gathers_of(target):
        filled = LANES_OF[target]
        low = (filled // LANES + 1) // 2 * LANES
        parts = pl.ds(0, filled), pl.ds(0, low), pl.ds(low, filled - low)
        ranges = [(target, 1), (0, target), (target + 1, 3 - target)]
        return [
            Gather(lambda m, c, part, cut=pl.ds(*cut): whole.at[cut, m, c, :, part], gather_send, gather_recv, 8 * n, parts)
            for n, cut in enumerate(ranges) if cut[1]
        ]

    def arrived(target):
        for step in (1, 2, 3):
            out_copy(step, target).wait_recv()

    for copy in loading[5:]:
        copy.wait()
    ends, offset = row_marks(len_ref)
    gain = table_ref[0:1, :]
    gain_sum = jnp.zeros((1, width), jnp.float32)
    shift_sum = jnp.zeros((1, width), jnp.float32)
    for r in range(0, tokens, 256):
        at = slice(r, r + 256)
        grad = sum(nt(ref[at, :], wt_s[:, part * width : (part + 1) * width])
                   for part, ref in enumerate((dq_ref, dk_ref, dv_ref)))
        values = x_s[at, :].astype(jnp.float32)
        center = values - jnp.mean(values, axis=-1, keepdims=True)
        rstd = lax.rsqrt(jnp.mean(center * center, axis=-1, keepdims=True) + norm_eps)
        xhat = center * rstd
        gain_sum += jnp.sum(grad * xhat, axis=0, keepdims=True)
        shift_sum += jnp.sum(grad, axis=0, keepdims=True)
        scaled = grad * gain
        after_s[at, :] += rstd * (scaled - jnp.mean(scaled, axis=-1, keepdims=True)
                                  - xhat * jnp.mean(scaled * xhat, axis=-1, keepdims=True))
        if r == 0:
            early.chip_turn()
            late.chip_start()
        if r == 512:
            early.chip_finish()
            early.plane_start()
        if r == 256:
            momentum(2, own_up_ref[...])
            momentum(3, last_b.finish())
            when_target(FIRST, lambda copy: copy.start())
    vector = jnp.concatenate(
        [gain_sum, shift_sum, sums_ref[2:4, :]]
        + [jnp.sum(ref[...].astype(jnp.float32), axis=0, keepdims=True) for ref in (dq_ref, dk_ref, dv_ref)]
        + [sums_ref[7:16, :]], axis=0)
    for block in range(8):
        part = vector[:, block * columns : (block + 1) * columns]
        tiles_s[block // 2, block % 2] = jnp.concatenate(
            [part, jnp.zeros((16, LANES - columns), jnp.float32)], axis=1)
    adding = table_sum(tiles_s, table_out, *table_scratch)
    late.chip_turn()
    next(adding)
    turned_s[...] = pltpu.roll(after_s[...], offset, 0)
    storing = pltpu.make_async_copy(turned_s, input_grad_hbm, stored)
    storing.start()
    late.chip_finish()
    late.plane_start()
    next(adding)
    for target in FIRST:
        @pl.when(plane == target)
        def _():
            place_own(target)
            own, *others = gathers_of(target)
            own.first()
            arrived(target)
            for gather in others:
                gather.first()
    next(adding)
    gradient = jnp.concatenate([early.plane_finish(), late.plane_finish()], axis=1)
    momentum(0, gradient[:, :rows_qkv])
    momentum(1, gradient[:, rows_qkv : rows_qkv + rows_out])
    when_target(LAST, lambda copy: copy.start())
    for target in FIRST:
        @pl.when(plane == target)
        def _():
            gathers = gathers_of(target)
            for gather in gathers:
                gather.second()
            for gather in gathers:
                gather.third()
            for gather in gathers:
                gather.landed()
    next(adding)
    first_fix = 1.0 - beta_first**STEP
    second_fix = 1.0 - beta_second**STEP
    n_vec = small[0].shape[0]
    vector_grad = table_out[:n_vec, :columns]
    vectors, vec_first, vec_second = (ref[...] for ref in small)
    new_first = beta_first * vec_first + (1.0 - beta_first) * vector_grad
    new_second = beta_second * vec_second + (1.0 - beta_second) * vector_grad * vector_grad
    new_small[0][...] = vectors - adam_rate * (new_first / first_fix) / (jnp.sqrt(new_second / second_fix) + adam_eps)
    new_small[1][...] = new_first
    new_small[2][...] = new_second
    for target in LAST:
        @pl.when(plane == target)
        def _():
            place_own(target)
            own, *others = gathers_of(target)
            own.first()
            arrived(target)
            for gather in others:
                gather.first()
            for gather in (own, *others):
                gather.second()
            for gather in (own, *others):
                gather.third()
            for gather in (own, *others):
                gather.landed()
    when_target((0, 1, 2, 3), lambda copy: copy.wait_send())

    def write(j, values):
        blocks[j] = values.astype(jnp.bfloat16)

    orthogonal_rows(whole, pl.ds(pl.multiple_of(rank * columns, 8), columns), gram, poly, temp, rows_s,
                    left_gram, left_temp, right, write)

    def home_copy(step, source):
        part = pl.ds(0, LANES_OF[source])
        return pltpu.make_async_remote_copy(
            src_ref=blocks.at[(plane + step) % 4, :, part], dst_ref=pieces.at[source, :, part],
            send_sem=back_send.at[step - 1], recv_sem=back_recv.at[step - 1],
            device_id=(rank, (plane + step) % 4), device_id_type=MESH)

    for source in range(4):
        @pl.when(plane == source)
        def _():
            for step in (1, 2, 3):
                home_copy(step, source).start()
            pieces[source] = blocks[source]

    def update(x):
        rows = moments[x].shape[0 if x == 1 else 1]
        scale = muon_rate * math.sqrt(max(1.0, rows * 4 / width))
        change = pieces[MATRIX_OF.index(x), :, :rows].astype(jnp.float32)
        new_weights[x][...] = (weights[x][...] * (1.0 - muon_rate * muon_decay)
                               - scale * (change.T if x == 1 else change))

    for source in (*FIRST, *reversed(LAST)):
        for step in (1, 2, 3):
            @pl.when((plane + 4 - source) % 4 == step)
            def _():
                home_copy(step, source).wait_recv()
        update(MATRIX_OF[source])
    for source in range(4):
        @pl.when(plane == source)
        def _():
            for step in (1, 2, 3):
                home_copy(step, source).wait_send()
            for gather in gathers_of(source):
                gather.sent()
    storing.wait()


def tail(h1, dq, dk, dv, out_grad, sums, table, own_up, total_b, lengths, moments, weights, small, wt_qkv, after_grad, x):
    tokens, width = h1.shape
    rows = width // 8
    large = (h1, dq, dk, dv, out_grad, wt_qkv, after_grad, x)
    vmem = pl.BlockSpec(memory_space=pltpu.VMEM)
    hbm = pl.BlockSpec(memory_space=pl.ANY)
    tile = (16, LANES)
    most = max(moments[n].shape[1] for n in (0, 2, 3))
    shape = jax.ShapeDtypeStruct
    f32, bf16 = jnp.float32, jnp.bfloat16
    square = pltpu.VMEM((width, width), f32)
    sems = lambda n: pltpu.SemaphoreType.DMA((n,))
    lanes_b = total_b.shape[-1]
    return pl.pallas_call(
        tail_kernel,
        in_specs=[vmem] * 4 + [pl.BlockSpec(memory_space=pltpu.SMEM)] + [vmem] * 11 + [hbm] * 8,
        out_specs=[vmem] * 11 + [hbm],
        out_shape=[shape(v.shape, f32) for v in (*moments, *weights, *small)] + [shape((tokens, width), f32)],
        scratch_shapes=[pltpu.VMEM(tile, f32), pltpu.VMEM((4, rows, most), bf16)]
        + [scratch for _, size in CUTS_A for scratch in sum_scratch(rows, size)]
        + [pltpu.VMEM((4, *tile), f32), pltpu.VMEM((3, *tile), f32),
           pltpu.VMEM((3, *tile), f32), pltpu.VMEM((4, *tile), f32), sems(7), sems(7)]
        + [pltpu.VMEM((4, rows, most), bf16), pltpu.VMEM((4, 4, 2, rows, most), bf16),
           square, square, square, pltpu.VMEM((rows, width), f32),
           pltpu.VMEM((width, 3 * width), bf16), pltpu.VMEM((width, 3 * width), bf16),
           pltpu.VMEM((3 * width, width), bf16), pltpu.VMEM((3, rows, lanes_b), bf16)]
        + [sems(3), sems(3), sems(24), sems(24), sems(3), sems(3), sems(3), sems(3), sems(8)]
        + [pltpu.VMEM((4, 2, 2, rows, size), bf16) for _, size in CUTS_A]
        + [pltpu.VMEM((4, 2, *tile), f32), pltpu.VMEM((width, tokens), bf16),
           pltpu.VMEM((tokens, width), f32), pltpu.SemaphoreType.DMA]
        + [pltpu.VMEM(v.shape, v.dtype) for v in large],
        compiler_params=pltpu.CompilerParams(collective_id=1, has_side_effects=True, vmem_limit_bytes=60 << 20),
        name="tail",
    )(sums, table, own_up, total_b, lengths, *moments, *weights, *small, *large)


def finish_kernel(*refs):
    count = len(refs) // 3
    sources, targets, held, loads, stores = refs[:count], refs[count : 2 * count], refs[2 * count : -2], refs[-2], refs[-1]
    loading, storing = [], []
    for n in sorted(range(count), key=lambda n: -sources[n].shape[0]):
        rows = sources[n].shape[0]
        parts = 8 if rows >= ROW_LEN else 1
        for p in range(parts):
            at = pl.ds(p * (rows // parts), rows // parts)
            slot = len(loading)
            loading.append(pltpu.make_async_copy(sources[n].at[at], held[n].at[at], loads.at[slot]))
            storing.append(pltpu.make_async_copy(held[n].at[at], targets[n].at[at], stores.at[slot]))
    for copy in loading:
        copy.start()
    for load, store in zip(loading, storing):
        load.wait()
        store.start()
    for copy in storing:
        copy.wait()


def finish(values):
    hbm = pl.BlockSpec(memory_space=pl.ANY)
    count = len(values)
    copies = sum(8 if x.shape[0] >= ROW_LEN else 1 for x in values)
    return pl.pallas_call(
        finish_kernel,
        in_specs=[hbm] * count,
        out_specs=[hbm] * count,
        out_shape=[jax.ShapeDtypeStruct(x.shape, x.dtype) for x in values],
        scratch_shapes=[pltpu.VMEM(x.shape, x.dtype) for x in values]
        + [pltpu.SemaphoreType.DMA((copies,)), pltpu.SemaphoreType.DMA((copies,))],
        compiler_params=pltpu.CompilerParams(vmem_limit_bytes=62 << 20),
        name="finish",
    )(*values)


def lane_parts(start, size):
    half = size // 2
    return pl.ds(start, size), pl.ds(start, half), pl.ds(start + half, half)


ROW_LEN = 1024
GATHERED = 512
CHUNK_A = 256
OUT_LANES = 256
CUTS_B = ((0, 512), (512, 768))


def row_marks(len_ref):
    ends = [len_ref[0, 0]]
    for slot in (1, 2):
        ends.append(ends[-1] + len_ref[0, slot])
    starts = [0, *ends]
    offset = starts[3]
    for slot in (2, 1, 0):
        offset = jnp.where(len_ref[0, slot] == LONGEST, starts[slot], offset)
    return ends, offset


def segment_of(index, ends, offset):
    where = index + offset
    where = jnp.where(where >= ROW_LEN, where - ROW_LEN, where)
    segment = sum((where >= end).astype(jnp.int32) for end in ends)
    return where, segment


def turned_rows(values, offset):
    return pltpu.roll(values.astype(jnp.float32), jnp.where(offset > 0, ROW_LEN - offset, 0), 0)


def same_rest(ends, offset):
    rest = ROW_LEN - LONGEST
    columns = lax.broadcasted_iota(jnp.int32, (rest, rest), 0) + LONGEST
    rows = lax.broadcasted_iota(jnp.int32, (rest, rest), 1) + LONGEST
    return segment_of(columns, ends, offset)[1] == segment_of(rows, ends, offset)[1]


def attention_jobs(tokens):
    blocks = [(start, 256, 0, LONGEST) for start in range(0, LONGEST, 256)] + [(LONGEST, tokens - LONGEST, LONGEST, tokens - LONGEST)]
    return [(h, *block) for h in range(LANES // HEAD_DIM) for block in blocks]


def attention_group(q, k_ref, v, same, ot_s, vt_s, lse_ref):
    tokens = q.shape[0]
    qt = q.T
    vt_s[...] = v.T
    row = lax.broadcasted_iota(jnp.int32, qt.shape, 0)
    jobs = attention_jobs(tokens)
    queries, scores, soft = {}, {}, {}

    def score(job):
        h, start, width, key_start, key_count = job
        if h not in queries:
            queries[h] = jnp.where(row // HEAD_DIM == h, qt, jnp.zeros((), jnp.bfloat16))
        out = nn(k_ref[key_start : key_start + key_count, :], queries[h][:, start : start + width])
        return jnp.where(same, out, masked_score) if start == LONGEST else out

    def soften(values):
        peak = jnp.max(values, axis=0, keepdims=True)
        raised = jnp.exp(values - peak)
        return raised.astype(jnp.bfloat16), peak, jnp.sum(raised, axis=0, keepdims=True)

    def collect(job, raised, peak, total):
        h, start, width, key_start, key_count = job
        rows = slice(h * HEAD_DIM, (h + 1) * HEAD_DIM)
        out = nn(vt_s[rows, key_start : key_start + key_count], raised)
        ot_s[rows, start : start + width] = out / total
        lse_ref[0, h : h + 1, start : start + width] = peak + jnp.log(total)

    count = len(jobs)
    for t in range(count + 2):
        if t < count:
            scores[t] = score(jobs[t])
        if 0 <= t - 1 < count:
            soft[t - 1] = soften(scores.pop(t - 1))
        if 0 <= t - 2:
            collect(jobs[t - 2], *soft.pop(t - 2))
    return ot_s[...].T.astype(jnp.bfloat16)


def head_kernel(
    len_ref, count_ref, tokens_ref, w_qkv_ref, w_up_ref, w_down_ref, w_out_ref, vectors_ref, cot_hbm,
    qr_ref, kr_ref, vr_ref, attn_ref, lse_ref, h1_hbm, x_hbm, cos_hbm, sin_hbm, wt_hbm, table_ref, full_b, full_o,
    incoming_hbm, dy_hbm, dyt_hbm, incoming_s, dy_s, dyt_s, cot_s,
    h1_ref, x_ref, cos_ref, sin_ref, wt_ref, stores, full_a, full_v, twice_s, q_s, k_s, v_s, ot_s, vt_s, slab_a, slab_b, slab_o,
    a_send, a_recv, az_send, az_recv, b_send, b_recv, bz_send, bz_recv, v_send, v_recv, local,
):
    group = pl.program_id(0)
    rank, plane, core, chip_x, chip_y = place()
    chip = chip_at(0, chip_x, chip_y)
    columns = slab_a.shape[0]
    chunks_a = GATHERED // CHUNK_A
    gather_a = [Gather(lambda m, c, lane: full_a.at[:, m, c, :, lane], a_send, a_recv, 8 * n,
                       lane_parts(CHUNK_A * n, CHUNK_A))
                for n in range(chunks_a)]
    gather_o = Gather(lambda m, c, lane: full_o.at[:, m, c, :, lane], b_send, b_recv, 0, lane_parts(0, OUT_LANES))
    gather_b = [Gather(lambda m, c, lane: full_b.at[pl.ds(0, 2), m, c, :, lane], b_send, b_recv, 8 + 8 * n,
                       lane_parts(*cut))
                for n, cut in enumerate(CUTS_B)]

    def along(slab, full, send, recv, n, start, size):
        lanes = pl.ds(start, size)
        return [
            pltpu.make_async_remote_copy(
                src_ref=slab.at[:, lanes], dst_ref=full.at[plane, chip, core, :, lanes],
                send_sem=send.at[3 * n + step - 1], recv_sem=recv.at[3 * n + step - 1],
                device_id=(rank, (plane + step) % 4), device_id_type=MESH)
            for step in (1, 2, 3)
        ]

    along_a = [along(slab_a, full_a, az_send, az_recv, n, CHUNK_A * n, CHUNK_A) for n in range(chunks_a)]
    along_o = along(slab_o, full_o, bz_send, bz_recv, 0, 0, OUT_LANES)
    along_b = [along(slab_b, full_b, bz_send, bz_recv, 1 + n, *cut) for n, cut in enumerate(CUTS_B)]
    own_b = [pltpu.make_async_copy(slab_b, full_b.at[plane, chip, core], local.at[0]),
             pltpu.make_async_copy(slab_o, full_o.at[plane, chip, core], local.at[1])]
    storing = [pltpu.make_async_copy(source, target, stores.at[n]) for n, (source, target) in enumerate(
        ((h1_ref, h1_hbm), (x_ref, x_hbm), (cos_ref, cos_hbm), (sin_ref, sin_hbm), (wt_ref, wt_hbm),
         (incoming_s, incoming_hbm), (dy_s, dy_hbm), (dyt_s, dyt_hbm)))]
    load_cot = pltpu.make_async_copy(cot_hbm, cot_s, local.at[2])
    ends, offset = row_marks(len_ref)

    def widen(values, lanes):
        return jnp.concatenate([values, jnp.zeros((values.shape[0], lanes - values.shape[1]), values.dtype)], axis=1)

    @pl.when(group == 0)
    def _():
        call(all_partners())
        load_cot.start()
        slab_a[...] = widen(w_qkv_ref[...].astype(jnp.bfloat16), GATHERED)
        n_vec, width = vectors_ref.shape[0], tokens_ref.shape[1]
        vectors = jnp.concatenate([vectors_ref[...], jnp.zeros((LANES - n_vec, columns), jnp.float32)], axis=0)
        vectors = vectors.astype(jnp.bfloat16).astype(jnp.float32)
        full_v[pl.ds(chip, 1), pl.ds(core, 1)] = widen(vectors, LANES).T[:columns, :][None, None]
        full_a[pl.ds(plane, 1), pl.ds(chip, 1), pl.ds(core, 1)] = slab_a[...][None, None, None]
        hear(all_partners())
        for copy in along_a[0]:
            copy.start()
        slab_b[:, :width] = w_up_ref[...].astype(jnp.bfloat16)
        slab_b[:, width:] = w_down_ref[...].astype(jnp.bfloat16)
        slab_o[...] = widen(w_out_ref[...].T.astype(jnp.bfloat16), OUT_LANES)
        for copy in own_b:
            copy.start()

        def vec_copy(m, slot, device):
            block = full_v.at[m, core]
            return pltpu.make_async_remote_copy(
                src_ref=block, dst_ref=block, send_sem=v_send.at[slot], recv_sem=v_recv.at[slot],
                device_id=(device, plane), device_id_type=MESH)

        chips = [chip_at(step, chip_x, chip_y) for step in range(4)]
        vec_over = [vec_copy(chip, step - 1, 2 * chips[step] + core) for step in (1, 2, 3)]
        vec_beside = [vec_copy(m, 3 + step, 2 * chip + 1 - core) for step, m in enumerate(chips)]
        for copy in (*vec_over, vec_beside[0]):
            copy.start()
        twice_s[...] = turned_rows(tokens_ref[...], offset)
        for copy in along_a[0]:
            copy.wait()
        for copy in along_a[1]:
            copy.start()
        gather_a[0].first()
        index = lax.broadcasted_iota(jnp.int32, (ROW_LEN, LANES), 0)
        where, segment = segment_of(index, ends, offset)
        start = jnp.where(segment == 0, 0, jnp.where(segment == 1, ends[0], jnp.where(segment == 2, ends[1], ends[2])))
        position = (where - start).astype(jnp.float32)
        lane = lax.broadcasted_iota(jnp.int32, (1, LANES), 1)
        inverse = jnp.exp((lane % (HEAD_DIM // 2)).astype(jnp.float32) * (-2.0 * math.log(10000.0) / HEAD_DIM))
        sign = jnp.where((lane % HEAD_DIM) < (HEAD_DIM // 2), -1.0, 1.0)
        angles = position * inverse
        for copy in along_a[1]:
            copy.wait()
        gather_a[1].first()
        for copies in (along_o, *along_b):
            for copy in copies:
                copy.start()
        cos_ref[...] = jnp.cos(angles)
        for step in range(3):
            vec_over[step].wait()
            vec_beside[step + 1].start()
        gather_a[0].second()
        sin_ref[...] = jnp.sin(angles) * sign
        for copy in vec_beside:
            copy.wait()
        table_t = jnp.concatenate([full_v[m, c] for m in range(4) for c in range(2)], axis=0)
        table_ref[...] = table_t.T[: table_ref.shape[0], :]
        gather_a[1].second()
        load_cot.wait()
        _, segment = segment_of(lax.broadcasted_iota(jnp.int32, (ROW_LEN, 1), 0), ends, offset)
        number = jnp.where(segment == 0, count_ref[0, 0], jnp.where(
            segment == 1, count_ref[0, 1], jnp.where(segment == 2, count_ref[0, 2], count_ref[0, 3])))
        incoming_s[...] = turned_rows(cot_s[...], offset) * (1.0 / number.astype(jnp.float32))
        dy_s[...] = incoming_s[...].astype(jnp.bfloat16)
        dyt_s[...] = dy_s[...].T
        gather_a[0].third()
        gather_a[1].third()
        gain, shift = table_ref[0:1, :], table_ref[1:2, :]
        for r in range(0, ROW_LEN, 256):
            values = twice_s[r : r + 256, :]
            x_ref[r : r + 256, :] = values.astype(jnp.bfloat16)
            h1_ref[r : r + 256, :] = layer_norm(values, gain, shift).astype(jnp.bfloat16)
        for gather in gather_a:
            gather.finish()
        for copy in (*own_b, *along_o):
            copy.wait()
        gather_o.first()
        rows = wt_ref.shape[1] // 4
        wt_ref[...] = jnp.concatenate(
            [full_a[j].reshape(width, GATHERED)[:, :rows] for j in range(4)], axis=1)
        first = _half_mask((256, LANES))
        bias = [table_ref[4 + part : 5 + part, :] for part in range(3)]
        for r in range(0, ROW_LEN, 256):
            at = slice(r, r + 256)
            project = nn(h1_ref[at, :], wt_ref[...])
            cosine, sine = cos_ref[at, :], sin_ref[at, :]
            for g in range(width // LANES):
                lanes = slice(g * LANES, (g + 1) * LANES)
                queries = (project[:, lanes] + bias[0][:, lanes]) * (1.0 / math.sqrt(HEAD_DIM))
                keys = project[:, width + g * LANES : width + (g + 1) * LANES] + bias[1][:, lanes]
                q_s[g, at, :] = (queries * cosine + _turn(queries, first) * sine).astype(jnp.bfloat16)
                k_s[g, at, :] = (keys * cosine + _turn(keys, first) * sine).astype(jnp.bfloat16)
                v_s[g, at, :] = (project[:, 2 * width + g * LANES : 2 * width + (g + 1) * LANES]
                                 + bias[2][:, lanes]).astype(jnp.bfloat16)
        for copy in storing:
            copy.start()
        for copy in along_b[0]:
            copy.wait()
        gather_b[0].first()
        gather_o.second()

    @pl.when(group == 1)
    def _():
        for copy in along_b[1]:
            copy.wait()
        gather_b[1].first()
        gather_o.third()

    @pl.when(group == 2)
    def _():
        gather_b[0].second()

    @pl.when(group == 4)
    def _():
        gather_b[1].second()
        gather_b[0].third()

    qr_ref[...] = q_s[group]
    kr_ref[...] = k_s[group]
    vr_ref[...] = v_s[group]
    attn_ref[...] = attention_group(q_s[group], kr_ref, v_s[group], same_rest(ends, offset), ot_s, vt_s, lse_ref)

    @pl.when(group == 4)
    def _():
        gather_b[1].third()
        for gather in (gather_o, *gather_b):
            gather.finish()
        for copy in storing:
            copy.wait()


def head(lengths, counts, tokens, cotangent, w_qkv_t, w_up_t, w_down_t, w_out, vectors):
    tokens_count, width = tokens.shape
    groups = width // LANES
    columns = w_qkv_t.shape[0]
    col = pl.BlockSpec((tokens_count, LANES), lambda g: (0, g))
    whole = lambda *shape: pl.BlockSpec(shape, lambda g: (0,) * len(shape))
    shape = jax.ShapeDtypeStruct
    bf16, f32 = jnp.bfloat16, jnp.float32
    sems = lambda n: pltpu.SemaphoreType.DMA((n,))
    na, nb = GATHERED // CHUNK_A, 1 + len(CUTS_B)
    return pl.pallas_call(
        head_kernel,
        grid=(groups,),
        in_specs=[pl.BlockSpec(memory_space=pltpu.SMEM)] * 2 + [whole(tokens_count, width), whole(*w_qkv_t.shape),
                  whole(columns, width), whole(columns, width), whole(*w_out.shape), whole(*vectors.shape),
                  pl.BlockSpec(memory_space=pl.ANY)],
        out_specs=[col] * 4 + [pl.BlockSpec((1, 4, tokens_count), lambda g: (g, 0, 0)),
                               *[pl.BlockSpec(memory_space=pl.ANY)] * 5, whole(16, width),
                               *[pl.BlockSpec(memory_space=pl.ANY)] * 5],
        out_shape=[shape((tokens_count, width), bf16)] * 4 + [shape((groups, 4, tokens_count), f32)]
        + [shape((tokens_count, width), bf16)] * 2 + [shape((tokens_count, LANES), f32)] * 2
        + [shape((width, 3 * width), bf16), shape((16, width), f32), shape((4, 4, 2, columns, 2 * width), bf16),
           shape((4, 4, 2, columns, OUT_LANES), bf16),
           shape((tokens_count, width), f32), shape((tokens_count, width), bf16), shape((width, tokens_count), bf16)],
        scratch_shapes=[
            pltpu.VMEM((tokens_count, width), f32),
            pltpu.VMEM((tokens_count, width), bf16),
            pltpu.VMEM((width, tokens_count), bf16),
            pltpu.VMEM((tokens_count, width), bf16),
            pltpu.VMEM((tokens_count, width), bf16),
            pltpu.VMEM((tokens_count, width), bf16),
            pltpu.VMEM((tokens_count, LANES), f32),
            pltpu.VMEM((tokens_count, LANES), f32),
            pltpu.VMEM((width, 3 * width), bf16),
            sems(8),
            pltpu.VMEM((4, 4, 2, columns, GATHERED), bf16),
            pltpu.VMEM((4, 2, columns, LANES), f32),
            pltpu.VMEM((tokens_count, width), f32),
            pltpu.VMEM((groups, tokens_count, LANES), bf16),
            pltpu.VMEM((groups, tokens_count, LANES), bf16),
            pltpu.VMEM((groups, tokens_count, LANES), bf16),
            pltpu.VMEM((LANES, tokens_count), f32),
            pltpu.VMEM((LANES, tokens_count), bf16),
            pltpu.VMEM((columns, GATHERED), bf16),
            pltpu.VMEM((columns, 2 * width), bf16),
            pltpu.VMEM((columns, OUT_LANES), bf16),
            sems(8 * na), sems(8 * na), sems(3 * na), sems(3 * na),
            sems(8 * nb), sems(8 * nb), sems(3 * nb), sems(3 * nb), sems(7), sems(7), sems(3),
        ],
        compiler_params=pltpu.CompilerParams(collective_id=2, has_side_effects=True, vmem_limit_bytes=58 << 20),
        name="head",
    )(lengths, counts, tokens, w_qkv_t, w_up_t, w_down_t, w_out, vectors, cotangent)


def middle_kernel(
    len_ref, table_ref, x_hbm, attn_hbm, incoming_hbm, dy_hbm, dyt_hbm, full_o_hbm, full_b,
    out_grad_ref, sums_ref, layer_hbm, after_hbm, attn_grad_hbm, parts_hbm,
    x_ref, attn_ref, cot_ref, full_o_ref, after_grad_ref, parts_s, stores,
    xhat_s, rstd_s, h2_s, h2t_s, dy_s, dyt_s, acc_s, back_s, act_s, pre_s, wt_out_s, w_s, send, recv, local,
):
    step = pl.program_id(0)
    tokens, width = x_ref.shape
    rank, plane, core, chip_x, chip_y = place()
    chip = chip_at(0, chip_x, chip_y)
    late = Gather(lambda m, c, lane: w_s.at[1, :, m, c, :, lane], send, recv, 0, lane_parts(0, 2 * width))
    loads = [pltpu.make_async_copy(full_b.at[pl.ds(2, 2), chip, core], w_s.at[1, :, chip, core], local.at[0]),
             pltpu.make_async_copy(full_o_hbm, full_o_ref, local.at[1]),
             pltpu.make_async_copy(attn_hbm, attn_ref, local.at[2]),
             pltpu.make_async_copy(x_hbm, x_ref, local.at[3]),
             pltpu.make_async_copy(full_b.at[pl.ds(0, 2)], w_s.at[0], local.at[4]),
             pltpu.make_async_copy(dy_hbm, dy_s, local.at[5]),
             pltpu.make_async_copy(dyt_hbm, dyt_s, local.at[6]),
             pltpu.make_async_copy(incoming_hbm, after_grad_ref, local.at[7])]
    ends, offset = row_marks(len_ref)
    chunk = 256
    cuts = [slice(r, r + chunk) for r in range(0, tokens, chunk)]

    @pl.when(step == 0)
    def _():
        beside = ([(2 * chip + 1 - core, plane)]
                  + [(2 * chip_at(other, chip_x, chip_y) + core, plane) for other in (1, 2)])
        call(beside)
        for load in loads[:6]:
            load.start()
        loads[0].wait()
        hear(beside)
        late.first()
        for load in loads[1:4]:
            load.wait()
        rows = width // 4
        wt_out_s[...] = jnp.concatenate([full_o_ref[p].reshape(width, OUT_LANES)[:, :rows] for p in range(4)], axis=1)
        sums_ref[...] = jnp.zeros_like(sums_ref)
        gain, shift = table_ref[2:3, :], table_ref[3:4, :]
        branch = {}
        for t in range(len(cuts) + 1):
            if t < len(cuts):
                branch[t] = nn(attn_ref[cuts[t], :], wt_out_s[...])
            if t == 0:
                continue
            at = cuts[t - 1]
            after = x_ref[at, :].astype(jnp.float32) + (branch.pop(t - 1) + table_ref[7:8, :])
            acc_s[at, :] = after + table_ref[8:9, :]
            center = after - jnp.mean(after, axis=-1, keepdims=True)
            rstd = lax.rsqrt(jnp.mean(center * center, axis=-1, keepdims=True) + norm_eps)
            xhat = center * rstd
            xhat_s[at, :] = xhat
            rstd_s[at, :] = rstd
            h2_s[at, :] = (xhat * gain + shift).astype(jnp.bfloat16)
        h2t_s[...] = h2_s[...].T
        back_s[...] = jnp.zeros_like(back_s)

    @pl.when(step == 0)
    def _():
        for load in loads[6:]:
            load.start()
        for load in loads[4:6]:
            load.wait()
        sums_ref[8:9, :] = jnp.sum(dy_s[...].astype(jnp.float32), axis=0, keepdims=True)

    @pl.when(step == 1)
    def _():
        late.finish()

    def weights(lanes):
        return jnp.concatenate([w_s[step, p, :, :, :, lanes].reshape(width, width) for p in range(2)], axis=1)

    up, down = (weights(slice(part * width, (part + 1) * width)) for part in range(2))
    bias = jnp.concatenate([table_ref[pl.ds(9 + 2 * step + p, 1), :] for p in range(2)], axis=1)

    def products(at):
        return nn(h2_s[at, :], up), nn(dy_s[at, :], down)

    def pointwise(at, pre, act_grad):
        pre = pre + bias
        cdf = 0.5 * (1.0 + lax.erf(pre * (1.0 / math.sqrt(2.0))))
        slope = cdf + pre * (jnp.exp(-0.5 * pre * pre) * (1.0 / math.sqrt(2.0 * math.pi)))
        act_s[at, :] = (pre * cdf).astype(jnp.bfloat16)
        pre_s[at, :] = (act_grad * slope).astype(jnp.bfloat16)

    def collect(at):
        acc_s[at, :] += nt(act_s[at, :], down)
        back_s[at, :] += nt(pre_s[at, :], up)

    held = {}
    for t in range(len(cuts) + 1):
        if t == 2:
            @pl.when(step == 0)
            def _():
                late.second()
                for load in loads[6:]:
                    load.wait()

        if t < len(cuts):
            held[t] = products(cuts[t])
        if t >= 1:
            pointwise(cuts[t - 1], *held.pop(t - 1))
            collect(cuts[t - 1])

    @pl.when(step == 0)
    def _():
        late.third()

    @pl.when(step == 1)
    def _():
        for part in range(2):
            lanes = pl.ds(part * width, width)
            pltpu.make_async_copy(parts_s.at[:, :, lanes], parts_hbm.at[pl.ds(0, 2), :, lanes],
                                  stores.at[0 if part == 0 else 10]).wait()

    store_parts = []
    for part, (left, right) in enumerate(((h2t_s, pre_s), (dyt_s, act_s))):
        grad = nn(left[...], right[...]).astype(jnp.bfloat16)
        for p in range(2):
            parts_s[p, :, part * width : (part + 1) * width] = grad[:, p * width : (p + 1) * width]
        lanes = pl.ds(part * width, width)
        store_parts.append(pltpu.make_async_copy(
            parts_s.at[:, :, lanes], parts_hbm.at[pl.ds(2 * step, 2), :, lanes], stores.at[0 if part == 0 else 10]))
        store_parts[part].start()
    bias_sum = jnp.sum(pre_s[...].astype(jnp.float32), axis=0, keepdims=True)
    for p in range(2):
        sums_ref[pl.ds(9 + 2 * step + p, 1), :] = bias_sum[:, p * width : (p + 1) * width]

    @pl.when(step == 1)
    def _():
        x_ref[...] = pltpu.roll(acc_s[...], offset, 0).astype(jnp.bfloat16)
        storing = [pltpu.make_async_copy(x_ref, layer_hbm, stores.at[1])]
        storing[0].start()
        gain = table_ref[2:3, :]
        gain_sum = jnp.zeros((1, width), jnp.float32)
        shift_sum = jnp.zeros((1, width), jnp.float32)
        branch_sum = jnp.zeros((1, width), jnp.float32)
        for n in range(len(cuts) + 1):
            if n >= 1:
                at = cuts[n - 1]
                cot_ref[at, :] = nt(dy_s[at, :], wt_out_s[...]).astype(jnp.bfloat16)
                rows = pl.ds(at.start, chunk)
                for source, target, slot in ((after_grad_ref, after_hbm, 1), (cot_ref, attn_grad_hbm, 5)):
                    copy = pltpu.make_async_copy(source.at[rows], target.at[rows], stores.at[slot + n])
                    copy.start()
                    storing.append(copy)
            if n == len(cuts):
                break
            at = cuts[n]
            grad, xhat = back_s[at, :], xhat_s[at, :]
            gain_sum += jnp.sum(grad * xhat, axis=0, keepdims=True)
            shift_sum += jnp.sum(grad, axis=0, keepdims=True)
            scaled = grad * gain
            resid = rstd_s[at, :] * (
                scaled - jnp.mean(scaled, axis=-1, keepdims=True)
                - xhat * jnp.mean(scaled * xhat, axis=-1, keepdims=True))
            after_grad = after_grad_ref[at, :] + resid
            after_grad_ref[at, :] = after_grad
            low = after_grad.astype(jnp.bfloat16)
            dy_s[at, :] = low
            branch_sum += jnp.sum(low.astype(jnp.float32), axis=0, keepdims=True)
        sums_ref[2:3, :] = gain_sum
        sums_ref[3:4, :] = shift_sum
        sums_ref[7:8, :] = branch_sum
        h2t_s[...] = attn_ref[...].T
        out_grad_ref[...] = nn(h2t_s[...], dy_s[...]).astype(jnp.bfloat16)
        for copy in (*store_parts, *storing):
            copy.wait()


def middle(lengths, x, attn, incoming, dy, dyt, table, full_o, full_b):
    tokens, width = x.shape
    columns = full_b.shape[3]
    whole = lambda *shape: pl.BlockSpec(shape, lambda j: (0,) * len(shape))
    smem = pl.BlockSpec(memory_space=pltpu.SMEM)
    hbm = pl.BlockSpec(memory_space=pl.ANY)
    shape = jax.ShapeDtypeStruct
    bf16, f32 = jnp.bfloat16, jnp.float32
    flat = pltpu.VMEM((tokens, width), bf16)
    double = pltpu.VMEM((tokens, 2 * width), bf16)
    wide = pltpu.VMEM((tokens, width), f32)
    turned = pltpu.VMEM((width, tokens), bf16)
    sems = lambda n: pltpu.SemaphoreType.DMA((n,))
    return pl.pallas_call(
        middle_kernel,
        grid=(2,),
        in_specs=[smem, whole(16, width)] + [hbm] * 7,
        out_specs=[whole(width, width), whole(16, width)] + [hbm] * 4,
        out_shape=[shape((width, width), bf16), shape((16, width), f32),
                   shape((tokens, width), bf16), shape((tokens, width), f32), shape((tokens, width), bf16),
                   shape((4, width, 2 * width), bf16)],
        scratch_shapes=[flat, flat, flat, pltpu.VMEM(full_o.shape, bf16), wide, pltpu.VMEM((2, width, 2 * width), bf16),
                        sems(11), wide, pltpu.VMEM((tokens, 1), f32), flat, turned, flat, turned, wide, wide, double, double,
                        pltpu.VMEM((width, width), bf16), pltpu.VMEM((2, 2, 4, 2, columns, 2 * width), bf16),
                        sems(8), sems(8), sems(8)],
        compiler_params=pltpu.CompilerParams(collective_id=3, has_side_effects=True, vmem_limit_bytes=62 << 20),
        name="middle",
    )(lengths, table, x, attn, incoming, dy, dyt, full_o, full_b)


def backward_group(between, qr_ref, kr_ref, vr_ref, do_ref, attn_ref, lse_ref, same, qt_s, dot_s, kt_s, delta_s, dqt_s, dk_s, dv_s):
    tokens = qr_ref.shape[0]
    qt_s[...] = qr_ref[...].T
    dot_s[...] = do_ref[...].T
    kt_s[...] = kr_ref[...].T
    heads = (lax.broadcasted_iota(jnp.int32, (8, LANES), 0)
             == lax.broadcasted_iota(jnp.int32, (8, LANES), 1) // HEAD_DIM).astype(jnp.float32).astype(jnp.bfloat16)
    top, low = split(do_ref[...].astype(jnp.float32) * attn_ref[...].astype(jnp.float32))
    delta_s[...] = nt(heads, top) + nt(heads, low)
    dk_s[...] = jnp.zeros_like(dk_s)
    dv_s[...] = jnp.zeros_like(dv_s)
    row = lax.broadcasted_iota(jnp.int32, (LANES, tokens), 0)
    lane = lax.broadcasted_iota(jnp.int32, (tokens, LANES), 1)
    zero = jnp.zeros((), jnp.bfloat16)
    jobs = attention_jobs(tokens)
    masked, held = {}, {}

    def products(job):
        h, start, width, key_start, key_count = job
        if h not in masked:
            masked[h] = (
                jnp.where(row // HEAD_DIM == h, qt_s[...], zero), jnp.where(row // HEAD_DIM == h, dot_s[...], zero),
                jnp.where(lane // HEAD_DIM == h, qr_ref[...], zero), jnp.where(lane // HEAD_DIM == h, do_ref[...], zero))
        at, keys = slice(start, start + width), slice(key_start, key_start + key_count)
        scores = nn(kr_ref[keys, :], masked[h][0][:, at])
        if start == LONGEST:
            scores = jnp.where(same, scores, masked_score)
        return scores, nn(vr_ref[keys, :], masked[h][1][:, at])

    def finish(job, scores, weight_grad):
        h, start, width, key_start, key_count = job
        at, keys = slice(start, start + width), slice(key_start, key_start + key_count)
        rows = slice(h * HEAD_DIM, (h + 1) * HEAD_DIM)
        soft = jnp.exp(scores - lse_ref[0, h : h + 1, at])
        score_grad = (soft * (weight_grad - delta_s[h : h + 1, at])).astype(jnp.bfloat16)
        dv_s[keys, :] += nn(soft.astype(jnp.bfloat16), masked[h][3][at, :])
        dk_s[keys, :] += nn(score_grad, masked[h][2][at, :])
        dqt_s[rows, at] = nn(kt_s[rows, keys], score_grad)

    for t in range(len(jobs) + 1):
        if t == len(jobs) // 2:
            between()
        if t < len(jobs):
            held[t] = products(jobs[t])
        if t >= 1:
            finish(jobs[t - 1], *held.pop(t - 1))


def backward_kernel(
    len_ref, qr_ref, kr_ref, vr_ref, do_ref, attn_ref, lse_ref, cos_ref, sin_ref, parts_ref,
    dq_ref, dk_ref, dv_ref, own_ref, total_ref, *scratch,
):
    group = pl.program_id(0)
    lanes = parts_ref.shape[-1] // 2
    halves = [SumStages(parts_ref, scratch[7 + SUM_SCRATCH * n : 7 + SUM_SCRATCH * (n + 1)], pl.ds(n * lanes, lanes))
              for n in range(2)]
    dqt_s, dk_s, dv_s = scratch[4:7]

    @pl.when(group == 0)
    def _():
        greet(all_partners())
        halves[0].core_start()

    @pl.when(group == 1)
    def _():
        halves[1].core_finish()

    def between():
        @pl.when(group == 0)
        def _():
            halves[0].core_finish()
            halves[0].chip_start()
            halves[1].core_start()

        @pl.when(group == 1)
        def _():
            halves[1].chip_start()

        @pl.when(group == 2)
        def _():
            halves[0].chip_turn()

        @pl.when(group == 3)
        def _():
            halves[0].chip_finish()
            halves[0].plane_start()
            halves[1].chip_turn()

        @pl.when(group == 4)
        def _():
            halves[1].chip_finish()
            total_ref[...] = halves[1].total[...]

    ends, offset = row_marks(len_ref)
    backward_group(between, qr_ref, kr_ref, vr_ref, do_ref, attn_ref, lse_ref, same_rest(ends, offset), *scratch[:7])
    first = _half_mask(cos_ref.shape)
    cosine, sine = cos_ref[...], sin_ref[...]

    def pull(values):
        return values * cosine + _turn(values * sine, first)

    dq_ref[...] = (pull(dqt_s[...].T) * (1.0 / math.sqrt(HEAD_DIM))).astype(jnp.bfloat16)
    dk_ref[...] = pull(dk_s[...]).astype(jnp.bfloat16)
    dv_ref[...] = dv_s[...].astype(jnp.bfloat16)

    @pl.when(group == 4)
    def _():
        own_ref[...] = halves[0].plane_finish()


def backward(lengths, qr, kr, vr, attn_grad, attn, lse, cosine, sine, parts):
    tokens, width = qr.shape
    groups = width // LANES
    rows, lanes = parts.shape[-2:]
    col = pl.BlockSpec((tokens, LANES), lambda g: (0, g))
    whole = lambda *shape: pl.BlockSpec(shape, lambda g: (0,) * len(shape))
    shape = jax.ShapeDtypeStruct
    bf16, f32 = jnp.bfloat16, jnp.float32
    return pl.pallas_call(
        backward_kernel,
        grid=(groups,),
        in_specs=[pl.BlockSpec(memory_space=pltpu.SMEM)] + [col] * 5
        + [pl.BlockSpec((1, 4, tokens), lambda g: (g, 0, 0)), whole(tokens, LANES), whole(tokens, LANES),
           pl.BlockSpec(memory_space=pl.ANY)],
        out_specs=[col] * 3 + [whole(rows, lanes // 2), whole(4, rows, lanes // 2)],
        out_shape=[shape((tokens, width), bf16)] * 3 + [shape((rows, lanes // 2), f32), shape((4, rows, lanes // 2), bf16)],
        scratch_shapes=[pltpu.VMEM((LANES, tokens), bf16)] * 3
        + [pltpu.VMEM((8, tokens), f32), pltpu.VMEM((LANES, tokens), f32), pltpu.VMEM((tokens, LANES), f32),
           pltpu.VMEM((tokens, LANES), f32)] + sum_scratch(rows, lanes // 2) * 2,
        compiler_params=pltpu.CompilerParams(collective_id=0, has_side_effects=True, vmem_limit_bytes=58 << 20),
        name="backward",
    )(lengths, qr, kr, vr, attn_grad, attn, lse, cosine, sine, parts)


def row_layout(lengths, counts, row_len):
    lens = lengths[0]
    slots = lens.shape[0]
    order = lax.broadcasted_iota(jnp.int32, (slots, slots), 0)
    upto = lax.broadcasted_iota(jnp.int32, (slots, slots), 1)
    starting = jnp.sum(jnp.where(upto < order, lens[None, :], 0), axis=1)
    slot = lax.broadcasted_iota(jnp.int32, (slots,), 0)
    which = jnp.min(jnp.where(lens == LONGEST, slot, slots))
    offset = jnp.sum(jnp.where(slot == which, starting, 0))
    places = lax.broadcasted_iota(jnp.int32, (row_len,), 0) + offset
    places = jnp.where(places >= row_len, places - row_len, places)
    endings = starting + lens
    segment = jnp.sum((places[:, None] >= endings[None, :]).astype(jnp.int32), axis=1)
    member = segment[:, None] == slot[None, :]
    first_place = jnp.sum(jnp.where(member, starting[None, :], 0), axis=1)
    position = (places - first_place).astype(jnp.float32)
    inverse_count = 1.0 / counts[0].astype(jnp.float32)
    share = jnp.sum(jnp.where(member, inverse_count[None, :], 0.0), axis=1)
    return offset, segment, position, share


def rotary_tables(position):
    lane = lax.broadcasted_iota(jnp.int32, (1, LANES), 1)
    indices = (lane % (HEAD_DIM // 2)).astype(jnp.float32)
    inverse = jnp.exp(indices * (-2.0 * math.log(10000.0) / HEAD_DIM))
    angles = position[:, None] * inverse
    sign = jnp.where((lane % HEAD_DIM) < (HEAD_DIM // 2), -1.0, 1.0)
    return jnp.cos(angles), jnp.sin(angles) * sign


def turn_rows(values, shift):
    twice = jnp.concatenate([values, values], axis=0)
    return lax.dynamic_slice_in_dim(twice, shift, values.shape[0], 0)


def high(left, right):
    return jnp.dot(left, right, precision=lax.Precision.HIGH, preferred_element_type=jnp.float32)


def shards_near(
    tokens, cotangent, lengths, counts,
    w_qkv, w_out, w_up, w_down,
    mom_qkv, mom_out, mom_up, mom_down,
    vectors, vec_first, vec_second,
):
    columns = w_qkv.shape[1]
    weights_t = [w_qkv.T, w_out, w_up.T, w_down.T]
    moments_t = [mom_qkv.T, mom_out, mom_up.T, mom_down.T]
    qr, kr, vr, attn, lse, normed_one, turned, cosine, sine, wt_qkv, table, full_b, full_o, incoming, dy, dyt = head(
        lengths, counts, tokens, cotangent, weights_t[0], weights_t[2], weights_t[3], w_out, vectors)
    out_grad, sums, layer_out, after_grad, attn_grad, parts_b = middle(
        lengths, turned, attn, incoming, dy, dyt, table, full_o, full_b)
    dq, dk, dv, own_up, total_down = backward(
        lengths, qr, kr, vr, attn_grad, attn, lse, cosine, sine, parts_b.reshape(4, 2, 2, 2, columns, -1))
    results = tail(
        normed_one, dq, dk, dv, out_grad, sums, table, own_up, total_down, lengths, moments_t, weights_t,
        (vectors, vec_first, vec_second), wt_qkv, after_grad, turned)
    results = finish([*results, layer_out])
    matrices = [v if x % 4 == 1 else v.T for x, v in enumerate(results[:8])]
    return (results[12], results[11], *matrices, *results[8:11])


def shards_far(
    tokens, cotangent, lengths, counts,
    w_qkv, w_out, w_up, w_down,
    mom_qkv, mom_out, mom_up, mom_down,
    vectors, vec_first, vec_second,
):
    both = ("fsdp", "dp")
    planes = lax.axis_size("fsdp")
    ranks = lax.axis_size("dp")
    row_len, width = tokens.shape
    columns = w_qkv.shape[1]
    old_weights = (w_qkv, w_out, w_up, w_down)
    old_moments = (mom_qkv, mom_out, mom_up, mom_down)
    counts_rows = [w.shape[0] for w in old_weights]
    n_vec = vectors.shape[0]

    slab_a = jnp.concatenate([w_qkv.T, w_out.T, vectors.T], axis=1).astype(jnp.bfloat16)
    slab_b = jnp.concatenate([w_up.T, w_down.T], axis=1).astype(jnp.bfloat16)
    full_a = lax.all_gather(slab_a, both, axis=0, tiled=True).reshape(planes, width, -1)
    full_b = lax.all_gather(slab_b, both, axis=0, tiled=True).reshape(planes, width, -1)
    r0, r1, r2, r3 = counts_rows
    wt_qkv = jnp.concatenate([full_a[j, :, :r0] for j in range(planes)], axis=1)
    wt_out = jnp.concatenate([full_a[j, :, r0 : r0 + r1] for j in range(planes)], axis=1)
    table = full_a[0, :, r0 + r1 :].T.astype(jnp.float32)
    wt_up = jnp.concatenate([full_b[j, :, :r2] for j in range(planes)], axis=1)
    wt_down = jnp.concatenate([full_b[j, :, r2:] for j in range(planes)], axis=1)

    offset, segment, position, share = row_layout(lengths, counts, row_len)
    cosine, sine = rotary_tables(position)
    seg_col, seg_row = segment[:, None], segment[None, :]
    inputs = turn_rows(tokens, offset).astype(jnp.float32)
    incoming = turn_rows(cotangent, offset).astype(jnp.float32) * share[:, None]

    normed_one, pull_one = jax.vjp(layer_norm, inputs, table[0], table[1])
    normed_one = normed_one.astype(jnp.bfloat16)
    project = nn(normed_one, wt_qkv) + table[4:7].reshape(-1)
    qr, kr, vr, attn, lse = attention_forward(project, cosine, sine, seg_col, seg_row)
    after = inputs + (nn(attn, wt_out) + table[7])
    normed_two, pull_two = jax.vjp(layer_norm, after, table[2], table[3])
    normed_two = normed_two.astype(jnp.bfloat16)
    hidden_pre = nn(normed_two, wt_up) + table[9:].reshape(-1)
    hidden, pull_hidden = jax.vjp(gelu_exact, hidden_pre)
    hidden = hidden.astype(jnp.bfloat16)
    layer_out = (after + (nt(hidden, wt_down) + table[8])).astype(jnp.bfloat16)

    grad_low = incoming.astype(jnp.bfloat16)
    grad_t_down = tn(grad_low, hidden)
    pre_grad = pull_hidden(nn(grad_low, wt_down))[0].astype(jnp.bfloat16)
    grad_t_up = tn(normed_two, pre_grad)
    resid_grad, gain_two, shift_two = pull_two(nt(pre_grad, wt_up))
    after_grad = incoming + resid_grad
    branch_low = after_grad.astype(jnp.bfloat16)
    grad_t_out = tn(attn, branch_low)
    attn_grad = nt(branch_low, wt_out).astype(jnp.bfloat16)
    dq, dk, dv = attention_backward(qr, kr, vr, attn_grad, attn, lse, cosine, sine, seg_col, seg_row)
    proj_grad = jnp.concatenate([dq, dk, dv], axis=1)
    grad_t_qkv = tn(normed_one, proj_grad)
    in_grad, gain_one, shift_one = pull_one(nt(proj_grad, wt_qkv))
    input_grad = after_grad + in_grad

    def column_sum(values):
        return jnp.sum(values.astype(jnp.float32), axis=0)

    vector_grad = jnp.concatenate(
        [gain_one[None], shift_one[None], gain_two[None], shift_two[None],
         column_sum(proj_grad).reshape(3, width), column_sum(branch_low)[None], column_sum(grad_low)[None],
         column_sum(pre_grad).reshape(-1, width)],
        axis=0,
    )
    back = jnp.where(offset > 0, row_len - offset, 0)
    layer_out = turn_rows(layer_out, back)
    input_grad = turn_rows(input_grad, back)

    def cut(values, j, rows):
        return values[:, j * rows : (j + 1) * rows]

    parts_b = jnp.stack([jnp.concatenate([cut(grad_t_up, j, r2), cut(grad_t_down, j, r3)], axis=1) for j in range(planes)])
    own_b = lax.psum_scatter(parts_b.reshape(planes * width, -1), both, scatter_dimension=0, tiled=True)
    parts_a = jnp.stack([jnp.concatenate([cut(grad_t_qkv, j, r0), cut(grad_t_out, j, r1), vector_grad.T], axis=1) for j in range(planes)])
    own_a = lax.psum_scatter(parts_a.reshape(planes * width, -1), both, scatter_dimension=0, tiled=True)
    grads_t = (own_a[:, :r0], own_a[:, r0 : r0 + r1], own_b[:, :r2], own_b[:, r2:])
    vector_grad = own_a[:, r0 + r1 :].T
    new_moments_t = [moment_keep * old.T + grad for old, grad in zip(old_moments, grads_t)]

    most = max(counts_rows)
    padded = [jnp.pad(m.astype(jnp.bfloat16), ((0, 0), (0, most - m.shape[1]))) for m in new_moments_t]
    sent = jnp.stack([padded[t % 4] for t in range(planes)])
    mine = lax.all_to_all(sent, "fsdp", 0, 0, tiled=True)
    mine = mine.transpose(1, 0, 2).reshape(columns, planes * most)
    whole = lax.all_gather(mine, "dp", axis=0, tiled=True)
    gram = nt(whole, whole)
    identity = jnp.eye(width, dtype=jnp.float32)
    norm_sq = jnp.trace(gram) + 1e-07
    gram = gram / norm_sq
    factor = None
    for iteration in range(NS_ITERS):
        poly = poly_linear * identity + poly_square * gram + poly_cubic * high(gram, gram)
        factor = poly if factor is None else high(factor, poly)
        if iteration + 1 < NS_ITERS:
            gram = high(high(gram, poly), poly)
    own_rows = lax.dynamic_slice_in_dim(factor, lax.axis_index("dp") * columns, columns, 0) * lax.rsqrt(norm_sq)
    own_orth = high(own_rows, whole.astype(jnp.float32))
    own_orth = own_orth.astype(jnp.bfloat16).reshape(columns, planes, most).transpose(1, 0, 2)
    pieces = lax.all_to_all(own_orth, "fsdp", 0, 0, tiled=True).astype(jnp.float32)

    new_weights = []
    for x, weight_old in enumerate(old_weights):
        rows = weight_old.shape[0]
        scale = muon_rate * math.sqrt(max(1.0, rows * planes / width))
        new_weights.append(weight_old * (1.0 - muon_rate * muon_decay) - scale * pieces[x, :, :rows].T)
    new_first = beta_first * vec_first + (1.0 - beta_first) * vector_grad
    new_second = beta_second * vec_second + (1.0 - beta_second) * vector_grad * vector_grad
    first_fix = 1.0 - beta_first**STEP
    second_fix = 1.0 - beta_second**STEP
    new_vectors = vectors - adam_rate * (new_first / first_fix) / (jnp.sqrt(new_second / second_fix) + adam_eps)
    return (layer_out, input_grad, *[m.T for m in new_moments_t], *new_weights, new_vectors, new_first, new_second)


def solution(mesh):
    rows, cells, table = P(("dp", "fsdp"), None), P("fsdp", "dp"), P(None, "dp")
    near = dict(mesh.shape) == {"dp": 8, "fsdp": 4}
    return jax.shard_map(
        shards_near if near else shards_far,
        mesh=mesh,
        in_specs=(rows,) * 4 + (cells,) * 8 + (table,) * 3,
        out_specs=(rows,) * 2 + (cells,) * 8 + (table,) * 3,
        check_vma=False,
    )
```
